128 devices in a mesh: row: 8 (over z, core), col: 16 (over y, x).
Axes of the slice: x: 4, y: 4, z: 4, core: 2. Of those that a mesh axis runs over, the one named last changes fastest.
Arguments:
- tile_values: bfloat16 [8, 16, 512, 128, 128], P('row', 'col'), may hold values from -0.046875 to 0.046875
- tile_rows: int32 [8, 16, 512], P('row', 'col'), may hold values from 0 to 63, as said below
- tile_cols: int32 [8, 16, 512], P('row', 'col'), may hold values from 0 to 31
- tile_count: int32 [8, 16], P('row', 'col'), may hold values from 64 to 512, as said below
- features: bfloat16 [65536, 256], P(('row', 'col')), may hold values from -6 to 6
- weight: bfloat16 [256, 256], replicated, may hold values from -0.375 to 0.375
- cotangent: bfloat16 [65536, 256], P(('row', 'col')), may hold values from -6 to 6
Outputs:
- output: bfloat16 [65536, 256], P(('row', 'col'))
- weight_grad: float32 [256, 256], replicated
- input_grad: float32 [65536, 256], P(('row', 'col'))
The draws below stay inside these ranges and needn't reach their ends.
Inputs may be any that keep to these rules, and one draw needn't show every extreme that they name: Within a cell, all slots hold distinct positions (tile_rows, tile_cols). `tile_count`: some cell holds exactly 512 tiles in every draw.
All inputs are finite; a program needn't handle non-finite values.
Results may differ from the reference program's by a relative error of at most 0.025.
Values may be sent and summed in bfloat16 or wider, within the bound.
A program may use at most 192 MiB of HBM per device.

```python
import math
import jax
import jax.numpy as jnp
from jax import lax

F = 256
TILE = 128
NODE_DEV = 512
TILE_MOST = 512
NODES = 65536
N_ROW = 8
N_COL = 16


def tile_layout(key):
    row_tiles = N_COL * NODE_DEV // TILE
    col_tiles = N_ROW * NODE_DEV // TILE
    cell_total = N_ROW * N_COL
    cell_keys = jax.random.split(jax.random.fold_in(key, 11), cell_total)
    positions = jax.vmap(lambda one_key: jax.random.permutation(one_key, row_tiles * col_tiles)[:TILE_MOST])(cell_keys)
    positions = positions.reshape(N_ROW, N_COL, TILE_MOST).astype(jnp.int32)
    return (positions // col_tiles, positions % col_tiles)


def draw_tile_rows(key, part):
    return tile_layout(key)[0]


def draw_tile_cols(key, part):
    return tile_layout(key)[1]


def draw_tile_count(key, part):
    cell_total = N_ROW * N_COL
    light_counts = jax.random.randint(jax.random.fold_in(key, 21), (cell_total,), TILE_MOST // 8, TILE_MOST // 2 + 1)
    heavy_cells = jax.random.randint(jax.random.fold_in(key, 22), (cell_total,), 0, 8) == 0
    chosen = jax.random.randint(jax.random.fold_in(key, 23), (), 0, cell_total)
    heavy_cells = heavy_cells | (jnp.arange(cell_total) == chosen)
    counts = jnp.where(heavy_cells, TILE_MOST, light_counts)
    return counts.reshape(N_ROW, N_COL).astype(jnp.int32)


def block_levels(rng, shape, pieces, least, top_value):
    level, own = 1.0, jax.random.fold_in(rng, 6)
    for axis_at, blocks in pieces:
        steps = jnp.exp(jax.random.uniform(jax.random.fold_in(own, axis_at), (blocks,), jnp.float32, least / len(pieces), top_value / len(pieces)))
        level = level * jnp.repeat(steps, shape[axis_at] // blocks).reshape([-1 if axis == axis_at else 1 for axis in range(len(shape))])
    return level


def bell_draw(rng, dims, width, most, shards=(), held_as=jnp.bfloat16):
    array = jax.random.normal(rng, dims, jnp.float32) * width
    if len(shards) > 0:
        array = block_levels(rng, dims, shards, -0.22, 0.18) * array
    return jnp.clip(array, min=-most, max=most).astype(held_as)


def setup_inputs(seed: int = 0) -> dict:
    splits = jax.random.split(jax.random.key(seed), 8)
    tile_values = bell_draw(splits[0], (N_ROW, N_COL, TILE_MOST, TILE, TILE), (TILE * TILE * TILE_MOST // NODE_DEV) ** -0.5, 0.046875, ((0, 8), (1, 16)))
    tile_rows = draw_tile_rows(jax.random.fold_in(splits[7], 71), 0)
    tile_cols = draw_tile_cols(jax.random.fold_in(splits[7], 71), 0)
    tile_count = draw_tile_count(jax.random.fold_in(splits[7], 71), 0)
    features = bell_draw(splits[4], (NODES, F), 1.0, 6.0, ((0, 128),))
    weight = bell_draw(splits[5], (F, F), F ** -0.5, 0.375)
    cotangent = bell_draw(splits[6], (NODES, F), 1.0, 6.0, ((0, 128),))
    return dict(tile_values=tile_values, tile_rows=tile_rows, tile_cols=tile_cols, tile_count=tile_count, features=features, weight=weight, cotangent=cotangent)


def cell_sum(block_vals, picked, add_index, live_count, segments, einsum_form):
    slot_ids = jnp.arange(block_vals.shape[0], dtype=jnp.int32)
    products = jnp.einsum(einsum_form, block_vals.astype(jnp.float32), picked.astype(jnp.float32), precision=lax.Precision.HIGHEST)
    products = jnp.where((slot_ids < live_count)[:, None, None], products, 0.0)
    return jax.ops.segment_sum(products, add_index, num_segments=segments)

def reference(tile_values, tile_rows, tile_cols, tile_count, features, weight, cotangent):
    feat_width = features.shape[1]
    row_tiles = N_COL * NODE_DEV // TILE
    col_tiles = N_ROW * NODE_DEV // TILE
    columns = features.reshape(N_ROW, N_COL, NODE_DEV, feat_width).transpose(1, 0, 2, 3).reshape(N_COL, col_tiles, TILE, feat_width)

    def forward_cell(cell_index, totals):
        grid_row = cell_index // N_COL
        grid_col = cell_index % N_COL
        picked = jnp.take(columns[grid_col], tile_cols[grid_row, grid_col], axis=0)
        summed = cell_sum(tile_values[grid_row, grid_col], picked, tile_rows[grid_row, grid_col], tile_count[grid_row, grid_col], row_tiles, 'kab,kbf->kaf')
        rounded = lax.optimization_barrier(summed.astype(jnp.bfloat16)).astype(totals.dtype)
        return totals.at[grid_row].add(rounded)
    zero_rows = jnp.zeros((N_ROW, row_tiles, TILE, feat_width), jnp.float32)
    totals = lax.fori_loop(0, N_ROW * N_COL, forward_cell, zero_rows)
    aggregated = totals.reshape(N_ROW * N_COL * NODE_DEV, feat_width).astype(jnp.bfloat16)
    hidden = jnp.dot(aggregated, weight, preferred_element_type=jnp.float32)
    sigmoid_value = jax.nn.sigmoid(hidden)
    output = (hidden * sigmoid_value).astype(jnp.bfloat16)
    silu_slope = sigmoid_value * (1.0 + hidden * (1.0 - sigmoid_value))
    hidden_grad = (cotangent.astype(jnp.float32) * silu_slope).astype(jnp.bfloat16)
    weight_grad = jnp.dot(aggregated.T, hidden_grad, preferred_element_type=jnp.float32) * (1.0 / math.sqrt(NODES))
    aggregated_grad = jnp.dot(hidden_grad, weight.T, preferred_element_type=jnp.float32).astype(jnp.bfloat16)
    grad_rows = aggregated_grad.reshape(N_ROW, row_tiles, TILE, feat_width)

    def backward_cell(cell_index, totals):
        grid_row = cell_index // N_COL
        grid_col = cell_index % N_COL
        picked = jnp.take(grad_rows[grid_row], tile_rows[grid_row, grid_col], axis=0)
        summed = cell_sum(tile_values[grid_row, grid_col], picked, tile_cols[grid_row, grid_col], tile_count[grid_row, grid_col], col_tiles, 'kab,kaf->kbf')
        return totals.at[grid_col].add(summed)
    zero_cols = jnp.zeros((N_COL, col_tiles, TILE, feat_width), jnp.float32)
    column_totals = lax.fori_loop(0, N_ROW * N_COL, backward_cell, zero_cols)
    input_grad = column_totals.reshape(N_COL, N_ROW, NODE_DEV, feat_width).transpose(1, 0, 2, 3).reshape(N_ROW * N_COL * NODE_DEV, feat_width)
    return (output, weight_grad, input_grad)
```

```python
import functools
import math

import jax
import jax.numpy as jnp
from jax import lax
from jax.experimental import pallas as pl
from jax.experimental.pallas import tpu as pltpu
from jax.sharding import PartitionSpec as P

SLOTS_PER_STEP = 32


def spmm_kernel(transpose, acc_index, src_index, count_ref, tiles_ref, src_ref, out_ref, acc_ref):
    step = pl.program_id(0)
    per_step = tiles_ref.shape[0]
    live = count_ref[0]
    acc_last = acc_ref.shape[0] - 1
    src_last = src_ref.shape[0] - 1

    @pl.when(step == 0)
    def _():
        acc_ref[...] = jnp.zeros_like(acc_ref)

    def one_slot(k, carry):
        slot = step * per_step + k

        @pl.when(slot < live)
        def _():
            target = jnp.clip(acc_index[slot], 0, acc_last)
            picked = jnp.clip(src_index[slot], 0, src_last)
            tile = tiles_ref[k]
            block = src_ref[picked]
            if transpose:
                product = lax.dot_general(
                    tile, block, (((0,), (0,)), ((), ())), preferred_element_type=jnp.float32
                )
            else:
                product = jnp.dot(tile, block, preferred_element_type=jnp.float32)
            acc_ref[target] += product

        return carry

    lax.fori_loop(0, per_step, one_slot, 0)

    @pl.when(step == pl.num_programs(0) - 1)
    def _():
        out_ref[...] = acc_ref[...].astype(out_ref.dtype)


def sparse_product(tile_block, acc_index, src_index, live_count, source, segments, transpose):
    slot_total, tile_edge, _ = tile_block.shape
    feat_width = source.shape[2]
    per_step = min(SLOTS_PER_STEP, slot_total)
    steps = slot_total // per_step

    def tile_map(step, acc_ref, src_ref, count_ref):
        last_live = jnp.maximum(count_ref[0] - 1, 0) // per_step
        return (jnp.minimum(step, last_live), 0, 0)

    grid_spec = pltpu.PrefetchScalarGridSpec(
        num_scalar_prefetch=3,
        grid=(steps,),
        in_specs=[
            pl.BlockSpec((per_step, tile_edge, tile_edge), tile_map),
            pl.BlockSpec(source.shape, lambda step, *_: (0, 0, 0)),
        ],
        out_specs=pl.BlockSpec((segments, tile_edge, feat_width), lambda step, *_: (0, 0, 0)),
        scratch_shapes=[pltpu.VMEM((segments, tile_edge, feat_width), jnp.float32)],
    )
    flops = 2 * slot_total * tile_edge * tile_edge * feat_width
    bytes_accessed = (
        tile_block.size * 2 + source.size * 2 + segments * tile_edge * feat_width * 2
    )
    return pl.pallas_call(
        functools.partial(spmm_kernel, transpose),
        out_shape=jax.ShapeDtypeStruct((segments, tile_edge, feat_width), jnp.bfloat16),
        grid_spec=grid_spec,
        compiler_params=pltpu.CompilerParams(
            dimension_semantics=("arbitrary",), vmem_limit_bytes=56 * 1024 * 1024
        ),
        cost_estimate=pl.CostEstimate(
            flops=flops, transcendentals=0, bytes_accessed=bytes_accessed
        ),
    )(acc_index, src_index, live_count, tile_block, source)


def activation(aggregated, weight, cot_rows):
    hidden = jnp.dot(aggregated, weight, preferred_element_type=jnp.float32)
    sigmoid_value = jax.nn.sigmoid(hidden)
    output = (hidden * sigmoid_value).astype(jnp.bfloat16)
    silu_slope = sigmoid_value * (1.0 + hidden * (1.0 - sigmoid_value))
    hidden_grad = (cot_rows.astype(jnp.float32) * silu_slope).astype(jnp.bfloat16)
    return (output, hidden_grad)


def per_device(tile_values, tile_rows, tile_cols, tile_count, features, weight, cotangent):
    slot_total = tile_values.shape[2]
    tile_edge = tile_values.shape[3]
    tile_block = tile_values.reshape(slot_total, tile_edge, tile_edge)
    row_index = tile_rows.reshape(slot_total)
    col_index = tile_cols.reshape(slot_total)
    live_count = tile_count.reshape(1)
    own_rows = features.shape[0]
    feat_width = features.shape[1]
    row_count = lax.axis_size("row")
    col_count = lax.axis_size("col")
    row_tiles = col_count * own_rows // tile_edge
    col_tiles = row_count * own_rows // tile_edge
    column_block = lax.all_gather(features, "row", axis=0, tiled=True)
    source = column_block.reshape(col_tiles, tile_edge, feat_width)
    partial_rows = sparse_product(
        tile_block, row_index, col_index, live_count, source, row_tiles, False
    )
    partial_flat = partial_rows.reshape(row_tiles * tile_edge, feat_width)
    node_total = row_count * col_count * own_rows
    aggregated = lax.psum_scatter(partial_flat, "col", scatter_dimension=0, tiled=True)
    output, hidden_grad = activation(aggregated, weight, cotangent)
    own_grad = lax.dot_general(
        hidden_grad, weight, (((1,), (1,)), ((), ())), preferred_element_type=jnp.float32
    ).astype(jnp.bfloat16)
    row_block = lax.all_gather(own_grad, "col", axis=0, tiled=True)
    local_grad = lax.dot_general(
        aggregated, hidden_grad, (((0,), (0,)), ((), ())), preferred_element_type=jnp.float32
    )
    weight_grad = lax.psum(local_grad, ("row", "col")) * (1.0 / math.sqrt(node_total))
    source_back = row_block.reshape(row_tiles, tile_edge, feat_width)
    partial_cols = sparse_product(
        tile_block, col_index, row_index, live_count, source_back, col_tiles, True
    )
    input_grad = lax.psum_scatter(
        partial_cols.reshape(col_tiles * tile_edge, feat_width),
        "row",
        scatter_dimension=0,
        tiled=True,
    ).astype(jnp.float32)
    return (output, weight_grad, input_grad)


def solution(mesh):
    placed = (
        P("row", "col", None, None, None),
        P("row", "col", None),
        P("row", "col", None),
        P("row", "col"),
        P(("row", "col"), None),
        P(),
        P(("row", "col"), None),
    )
    return jax.shard_map(
        per_device,
        mesh=mesh,
        in_specs=placed,
        out_specs=(P(("row", "col"), None), P(), P(("row", "col"), None)),
        check_vma=False,
    )
```

```python
import functools
import math

import jax
import jax.numpy as jnp
from jax import lax
from jax.experimental import pallas as pl
from jax.experimental.pallas import tpu as pltpu
from jax.sharding import PartitionSpec as P

SLOTS_PER_STEP = 32


def spmm_kernel(transpose, acc_index, src_index, count_ref, tiles_ref, src_ref, out_ref, acc_ref):
    step = pl.program_id(0)
    per_step = tiles_ref.shape[0]
    live = count_ref[0]
    acc_last = acc_ref.shape[0] - 1
    src_last = src_ref.shape[0] - 1

    @pl.when(step == 0)
    def _():
        acc_ref[...] = jnp.zeros_like(acc_ref)

    def one_slot(k, carry):
        slot = step * per_step + k

        @pl.when(slot < live)
        def _():
            target = jnp.clip(acc_index[slot], 0, acc_last)
            picked = jnp.clip(src_index[slot], 0, src_last)
            tile = tiles_ref[k]
            block = src_ref[picked]
            if transpose:
                product = lax.dot_general(
                    tile, block, (((0,), (0,)), ((), ())), preferred_element_type=jnp.float32
                )
            else:
                product = jnp.dot(tile, block, preferred_element_type=jnp.float32)
            acc_ref[target] += product

        return carry

    lax.fori_loop(0, per_step, one_slot, 0)

    @pl.when(step == pl.num_programs(0) - 1)
    def _():
        out_ref[...] = acc_ref[...].astype(out_ref.dtype)


def sparse_product(tile_block, acc_index, src_index, live_count, source, segments, transpose):
    slot_total, tile_edge, _ = tile_block.shape
    feat_width = source.shape[2]
    per_step = min(SLOTS_PER_STEP, slot_total)
    steps = slot_total // per_step

    def tile_map(step, acc_ref, src_ref, count_ref):
        last_live = jnp.maximum(count_ref[0] - 1, 0) // per_step
        return (jnp.minimum(step, last_live), 0, 0)

    grid_spec = pltpu.PrefetchScalarGridSpec(
        num_scalar_prefetch=3,
        grid=(steps,),
        in_specs=[
            pl.BlockSpec((per_step, tile_edge, tile_edge), tile_map),
            pl.BlockSpec(source.shape, lambda step, *_: (0, 0, 0)),
        ],
        out_specs=pl.BlockSpec((segments, tile_edge, feat_width), lambda step, *_: (0, 0, 0)),
        scratch_shapes=[pltpu.VMEM((segments, tile_edge, feat_width), jnp.float32)],
    )
    flops = 2 * slot_total * tile_edge * tile_edge * feat_width
    bytes_accessed = (
        tile_block.size * 2 + source.size * 2 + segments * tile_edge * feat_width * 2
    )
    return pl.pallas_call(
        functools.partial(spmm_kernel, transpose),
        out_shape=jax.ShapeDtypeStruct((segments, tile_edge, feat_width), jnp.bfloat16),
        grid_spec=grid_spec,
        compiler_params=pltpu.CompilerParams(
            dimension_semantics=("arbitrary",), vmem_limit_bytes=56 * 1024 * 1024
        ),
        cost_estimate=pl.CostEstimate(
            flops=flops, transcendentals=0, bytes_accessed=bytes_accessed
        ),
    )(acc_index, src_index, live_count, tile_block, source)


def peer_id(axis, other_axis, peer):
    if axis == "row":
        return (peer, lax.axis_index(other_axis))
    return (lax.axis_index(other_axis), peer)


def greet_all(axis, other_axis, n, me):
    barrier = pltpu.get_barrier_semaphore()
    for offset in range(1, n):
        peer = lax.rem(me + offset, n)
        pl.semaphore_signal(
            barrier, 1, device_id=peer_id(axis, other_axis, peer),
            device_id_type=pl.DeviceIdType.MESH,
        )
    pl.semaphore_wait(barrier, n - 1)


def scatter_sum_kernel(axis, other_axis, n, x_hbm, out_ref, recv, send_sems, recv_sems, own_sem):
    me = lax.axis_index(axis)
    greet_all(axis, other_axis, n, me)
    own = pltpu.make_async_copy(x_hbm.at[me], recv.at[me], own_sem)
    own.start()
    sends = []
    for offset in range(1, n):
        peer = lax.rem(me + offset, n)
        copy = pltpu.make_async_remote_copy(
            src_ref=x_hbm.at[peer],
            dst_ref=recv.at[me],
            send_sem=send_sems.at[offset],
            recv_sem=recv_sems.at[me],
            device_id=peer_id(axis, other_axis, peer),
            device_id_type=pl.DeviceIdType.MESH,
        )
        copy.start()
        sends.append(copy)
    own.wait()
    for offset in range(1, n):
        source = lax.rem(me + n - offset, n)
        pltpu.make_async_remote_copy(
            src_ref=x_hbm.at[source],
            dst_ref=recv.at[source],
            send_sem=send_sems.at[offset],
            recv_sem=recv_sems.at[source],
            device_id=peer_id(axis, other_axis, source),
            device_id_type=pl.DeviceIdType.MESH,
        ).wait_recv()
    total = recv[0].astype(jnp.float32)
    for j in range(1, n):
        total = total + recv[j].astype(jnp.float32)
    out_ref[...] = total.astype(out_ref.dtype)
    for copy in sends:
        copy.wait_send()


def scatter_sum(x, axis, other_axis, out_dtype, collective_id):
    n, rows, lanes = x.shape
    return pl.pallas_call(
        functools.partial(scatter_sum_kernel, axis, other_axis, n),
        out_shape=jax.ShapeDtypeStruct((rows, lanes), out_dtype),
        in_specs=[pl.BlockSpec(memory_space=pl.ANY)],
        out_specs=pl.BlockSpec(memory_space=pltpu.VMEM),
        scratch_shapes=[
            pltpu.VMEM((n, rows, lanes), x.dtype),
            pltpu.SemaphoreType.DMA((n,)),
            pltpu.SemaphoreType.DMA((n,)),
            pltpu.SemaphoreType.DMA(()),
        ],
        compiler_params=pltpu.CompilerParams(
            collective_id=collective_id, has_side_effects=True,
            vmem_limit_bytes=48 * 1024 * 1024,
        ),
    )(x)


def gather_all_kernel(axis, other_axis, n, x_ref, out_ref, recv, send_sems, recv_sems):
    me = lax.axis_index(axis)
    recv[me] = x_ref[...]
    greet_all(axis, other_axis, n, me)
    sends = []
    for offset in range(1, n):
        peer = lax.rem(me + offset, n)
        copy = pltpu.make_async_remote_copy(
            src_ref=x_ref,
            dst_ref=recv.at[me],
            send_sem=send_sems.at[offset],
            recv_sem=recv_sems.at[me],
            device_id=peer_id(axis, other_axis, peer),
            device_id_type=pl.DeviceIdType.MESH,
        )
        copy.start()
        sends.append(copy)
    for offset in range(1, n):
        source = lax.rem(me + n - offset, n)
        pltpu.make_async_remote_copy(
            src_ref=x_ref,
            dst_ref=recv.at[source],
            send_sem=send_sems.at[offset],
            recv_sem=recv_sems.at[source],
            device_id=peer_id(axis, other_axis, source),
            device_id_type=pl.DeviceIdType.MESH,
        ).wait_recv()
    out_ref[...] = recv[...]
    for copy in sends:
        copy.wait_send()


def gather_all(x, axis, other_axis, n, collective_id):
    rows, lanes = x.shape
    return pl.pallas_call(
        functools.partial(gather_all_kernel, axis, other_axis, n),
        out_shape=jax.ShapeDtypeStruct((n, rows, lanes), x.dtype),
        in_specs=[pl.BlockSpec(memory_space=pltpu.VMEM)],
        out_specs=pl.BlockSpec(memory_space=pltpu.VMEM),
        scratch_shapes=[
            pltpu.VMEM((n, rows, lanes), x.dtype),
            pltpu.SemaphoreType.DMA((n,)),
            pltpu.SemaphoreType.DMA((n,)),
        ],
        compiler_params=pltpu.CompilerParams(
            collective_id=collective_id, has_side_effects=True,
            vmem_limit_bytes=48 * 1024 * 1024,
        ),
    )(x)


def all_sum(local, collective_base):
    row_count = lax.axis_size("row")
    col_count = lax.axis_size("col")
    height, width = local.shape
    by_col = scatter_sum(
        local.reshape(col_count, height // col_count, width), "col", "row", jnp.float32,
        collective_base,
    )
    part = height // col_count
    by_row = scatter_sum(
        by_col.reshape(row_count, part // row_count, width), "row", "col", jnp.float32,
        collective_base + 1,
    )
    back_row = gather_all(by_row, "row", "col", row_count, collective_base + 2)
    back_col = gather_all(back_row.reshape(part, width), "col", "row", col_count, collective_base + 3)
    return back_col.reshape(height, width)


def activation(aggregated, weight, cot_rows):
    hidden = jnp.dot(aggregated, weight, preferred_element_type=jnp.float32)
    sigmoid_value = jax.nn.sigmoid(hidden)
    output = (hidden * sigmoid_value).astype(jnp.bfloat16)
    silu_slope = sigmoid_value * (1.0 + hidden * (1.0 - sigmoid_value))
    hidden_grad = (cot_rows.astype(jnp.float32) * silu_slope).astype(jnp.bfloat16)
    return (output, hidden_grad)


def per_device(tile_values, tile_rows, tile_cols, tile_count, features, weight, cotangent):
    slot_total = tile_values.shape[2]
    tile_edge = tile_values.shape[3]
    tile_block = tile_values.reshape(slot_total, tile_edge, tile_edge)
    row_index = tile_rows.reshape(slot_total)
    col_index = tile_cols.reshape(slot_total)
    live_count = tile_count.reshape(1)
    own_rows = features.shape[0]
    feat_width = features.shape[1]
    row_count = lax.axis_size("row")
    col_count = lax.axis_size("col")
    row_tiles = col_count * own_rows // tile_edge
    col_tiles = row_count * own_rows // tile_edge
    column_block = lax.all_gather(features, "row", axis=0, tiled=True)
    source = column_block.reshape(col_tiles, tile_edge, feat_width)
    partial_rows = sparse_product(
        tile_block, row_index, col_index, live_count, source, row_tiles, False
    )
    partial_flat = partial_rows.reshape(row_tiles * tile_edge, feat_width)
    node_total = row_count * col_count * own_rows
    aggregated = scatter_sum(
        partial_rows.reshape(col_count, own_rows, feat_width), "col", "row", jnp.bfloat16, 0
    )
    output, hidden_grad = activation(aggregated, weight, cotangent)
    own_grad = lax.dot_general(
        hidden_grad, weight, (((1,), (1,)), ((), ())), preferred_element_type=jnp.float32
    ).astype(jnp.bfloat16)
    row_block = lax.all_gather(own_grad, "col", axis=0, tiled=True)
    local_grad = lax.dot_general(
        aggregated, hidden_grad, (((0,), (0,)), ((), ())), preferred_element_type=jnp.float32
    )
    weight_grad = all_sum(local_grad, 1) * (1.0 / math.sqrt(node_total))
    source_back = row_block.reshape(row_tiles, tile_edge, feat_width)
    partial_cols = sparse_product(
        tile_block, col_index, row_index, live_count, source_back, col_tiles, True
    )
    input_grad = lax.psum_scatter(
        partial_cols.reshape(col_tiles * tile_edge, feat_width),
        "row",
        scatter_dimension=0,
        tiled=True,
    ).astype(jnp.float32)
    return (output, weight_grad, input_grad)


def solution(mesh):
    placed = (
        P("row", "col", None, None, None),
        P("row", "col", None),
        P("row", "col", None),
        P("row", "col"),
        P(("row", "col"), None),
        P(),
        P(("row", "col"), None),
    )
    return jax.shard_map(
        per_device,
        mesh=mesh,
        in_specs=placed,
        out_specs=(P(("row", "col"), None), P(), P(("row", "col"), None)),
        check_vma=False,
    )
```

```python
import functools
import math

import jax
import jax.numpy as jnp
from jax import lax
from jax.experimental import pallas as pl
from jax.experimental.pallas import tpu as pltpu
from jax.sharding import PartitionSpec as P

SLOTS_PER_STEP = 32
UNROLL = 32


def spmm_kernel(transpose, acc_index, src_index, count_ref, tiles_ref, src_ref, out_ref, acc_ref):
    step = pl.program_id(0)
    per_step = tiles_ref.shape[0]
    live = count_ref[0]
    acc_last = acc_ref.shape[0] - 1
    src_last = src_ref.shape[0] - 1

    @pl.when(step == 0)
    def _():
        acc_ref[...] = jnp.zeros_like(acc_ref)

    def one_slot(k, carry):
        slot = step * per_step + k
        target = jnp.clip(acc_index[slot], 0, acc_last)
        picked = jnp.clip(src_index[slot], 0, src_last)
        tile = tiles_ref[k]
        tile = jnp.where(slot < live, tile, jnp.zeros_like(tile))
        block = src_ref[picked]
        if transpose:
            product = lax.dot_general(
                tile, block, (((0,), (0,)), ((), ())), preferred_element_type=jnp.float32
            )
        else:
            product = jnp.dot(tile, block, preferred_element_type=jnp.float32)
        acc_ref[target] += product
        return carry

    lax.fori_loop(0, per_step, one_slot, 0, unroll=UNROLL)

    @pl.when(step == pl.num_programs(0) - 1)
    def _():
        out_ref[...] = acc_ref[...].astype(out_ref.dtype)


def sparse_product(tile_block, acc_index, src_index, live_count, source, segments, transpose):
    slot_total, tile_edge, _ = tile_block.shape
    feat_width = source.shape[2]
    per_step = min(SLOTS_PER_STEP, slot_total)
    steps = slot_total // per_step

    def tile_map(step, acc_ref, src_ref, count_ref):
        last_live = jnp.maximum(count_ref[0] - 1, 0) // per_step
        return (jnp.minimum(step, last_live), 0, 0)

    grid_spec = pltpu.PrefetchScalarGridSpec(
        num_scalar_prefetch=3,
        grid=(steps,),
        in_specs=[
            pl.BlockSpec((per_step, tile_edge, tile_edge), tile_map),
            pl.BlockSpec(source.shape, lambda step, *_: (0, 0, 0)),
        ],
        out_specs=pl.BlockSpec((segments, tile_edge, feat_width), lambda step, *_: (0, 0, 0)),
        scratch_shapes=[pltpu.VMEM((segments, tile_edge, feat_width), jnp.float32)],
    )
    flops = 2 * slot_total * tile_edge * tile_edge * feat_width
    bytes_accessed = (
        tile_block.size * 2 + source.size * 2 + segments * tile_edge * feat_width * 2
    )
    return pl.pallas_call(
        functools.partial(spmm_kernel, transpose),
        out_shape=jax.ShapeDtypeStruct((segments, tile_edge, feat_width), jnp.bfloat16),
        grid_spec=grid_spec,
        compiler_params=pltpu.CompilerParams(
            dimension_semantics=("arbitrary",), vmem_limit_bytes=56 * 1024 * 1024
        ),
        cost_estimate=pl.CostEstimate(
            flops=flops, transcendentals=0, bytes_accessed=bytes_accessed
        ),
    )(acc_index, src_index, live_count, tile_block, source)


def peer_id(axis, other_axis, peer):
    if axis == "row":
        return (peer, lax.axis_index(other_axis))
    return (lax.axis_index(other_axis), peer)


def greet_all(axis, other_axis, n, me):
    barrier = pltpu.get_barrier_semaphore()
    for offset in range(1, n):
        peer = lax.rem(me + offset, n)
        pl.semaphore_signal(
            barrier, 1, device_id=peer_id(axis, other_axis, peer),
            device_id_type=pl.DeviceIdType.MESH,
        )
    pl.semaphore_wait(barrier, n - 1)


def scatter_sum_kernel(axis, other_axis, n, x_hbm, out_ref, recv, send_sems, recv_sems, own_sem):
    me = lax.axis_index(axis)
    greet_all(axis, other_axis, n, me)
    own = pltpu.make_async_copy(x_hbm.at[me], recv.at[me], own_sem)
    own.start()
    sends = []
    for offset in range(1, n):
        peer = lax.rem(me + offset, n)
        copy = pltpu.make_async_remote_copy(
            src_ref=x_hbm.at[peer],
            dst_ref=recv.at[me],
            send_sem=send_sems.at[offset],
            recv_sem=recv_sems.at[me],
            device_id=peer_id(axis, other_axis, peer),
            device_id_type=pl.DeviceIdType.MESH,
        )
        copy.start()
        sends.append(copy)
    own.wait()
    for offset in range(1, n):
        source = lax.rem(me + n - offset, n)
        pltpu.make_async_remote_copy(
            src_ref=x_hbm.at[source],
            dst_ref=recv.at[source],
            send_sem=send_sems.at[offset],
            recv_sem=recv_sems.at[source],
            device_id=peer_id(axis, other_axis, source),
            device_id_type=pl.DeviceIdType.MESH,
        ).wait_recv()
    total = recv[0].astype(jnp.float32)
    for j in range(1, n):
        total = total + recv[j].astype(jnp.float32)
    out_ref[...] = total.astype(out_ref.dtype)
    for copy in sends:
        copy.wait_send()


def scatter_sum(x, axis, other_axis, out_dtype, collective_id):
    n, rows, lanes = x.shape
    return pl.pallas_call(
        functools.partial(scatter_sum_kernel, axis, other_axis, n),
        out_shape=jax.ShapeDtypeStruct((rows, lanes), out_dtype),
        in_specs=[pl.BlockSpec(memory_space=pl.ANY)],
        out_specs=pl.BlockSpec(memory_space=pltpu.VMEM),
        scratch_shapes=[
            pltpu.VMEM((n, rows, lanes), x.dtype),
            pltpu.SemaphoreType.DMA((n,)),
            pltpu.SemaphoreType.DMA((n,)),
            pltpu.SemaphoreType.DMA(()),
        ],
        compiler_params=pltpu.CompilerParams(
            collective_id=collective_id, has_side_effects=True,
            vmem_limit_bytes=48 * 1024 * 1024,
        ),
    )(x)


def gather_all_kernel(axis, other_axis, n, x_ref, out_ref, recv, send_sems, recv_sems):
    me = lax.axis_index(axis)
    recv[me] = x_ref[...]
    greet_all(axis, other_axis, n, me)
    sends = []
    for offset in range(1, n):
        peer = lax.rem(me + offset, n)
        copy = pltpu.make_async_remote_copy(
            src_ref=x_ref,
            dst_ref=recv.at[me],
            send_sem=send_sems.at[offset],
            recv_sem=recv_sems.at[me],
            device_id=peer_id(axis, other_axis, peer),
            device_id_type=pl.DeviceIdType.MESH,
        )
        copy.start()
        sends.append(copy)
    for offset in range(1, n):
        source = lax.rem(me + n - offset, n)
        pltpu.make_async_remote_copy(
            src_ref=x_ref,
            dst_ref=recv.at[source],
            send_sem=send_sems.at[offset],
            recv_sem=recv_sems.at[source],
            device_id=peer_id(axis, other_axis, source),
            device_id_type=pl.DeviceIdType.MESH,
        ).wait_recv()
    out_ref[...] = recv[...]
    for copy in sends:
        copy.wait_send()


def gather_all(x, axis, other_axis, n, collective_id):
    rows, lanes = x.shape
    return pl.pallas_call(
        functools.partial(gather_all_kernel, axis, other_axis, n),
        out_shape=jax.ShapeDtypeStruct((n, rows, lanes), x.dtype),
        in_specs=[pl.BlockSpec(memory_space=pltpu.VMEM)],
        out_specs=pl.BlockSpec(memory_space=pltpu.VMEM),
        scratch_shapes=[
            pltpu.VMEM((n, rows, lanes), x.dtype),
            pltpu.SemaphoreType.DMA((n,)),
            pltpu.SemaphoreType.DMA((n,)),
        ],
        compiler_params=pltpu.CompilerParams(
            collective_id=collective_id, has_side_effects=True,
            vmem_limit_bytes=48 * 1024 * 1024,
        ),
    )(x)


def all_sum(local, collective_base):
    row_count = lax.axis_size("row")
    col_count = lax.axis_size("col")
    height, width = local.shape
    by_col = scatter_sum(
        local.reshape(col_count, height // col_count, width), "col", "row", jnp.float32,
        collective_base,
    )
    part = height // col_count
    by_row = scatter_sum(
        by_col.reshape(row_count, part // row_count, width), "row", "col", jnp.float32,
        collective_base + 1,
    )
    back_row = gather_all(by_row, "row", "col", row_count, collective_base + 2)
    back_col = gather_all(back_row.reshape(part, width), "col", "row", col_count, collective_base + 3)
    return back_col.reshape(height, width)


def activation(aggregated, weight, cot_rows):
    hidden = jnp.dot(aggregated, weight, preferred_element_type=jnp.float32)
    sigmoid_value = jax.nn.sigmoid(hidden)
    output = (hidden * sigmoid_value).astype(jnp.bfloat16)
    silu_slope = sigmoid_value * (1.0 + hidden * (1.0 - sigmoid_value))
    hidden_grad = (cot_rows.astype(jnp.float32) * silu_slope).astype(jnp.bfloat16)
    return (output, hidden_grad)


def per_device(tile_values, tile_rows, tile_cols, tile_count, features, weight, cotangent):
    slot_total = tile_values.shape[2]
    tile_edge = tile_values.shape[3]
    tile_block = tile_values.reshape(slot_total, tile_edge, tile_edge)
    row_index = tile_rows.reshape(slot_total)
    col_index = tile_cols.reshape(slot_total)
    live_count = tile_count.reshape(1)
    own_rows = features.shape[0]
    feat_width = features.shape[1]
    row_count = lax.axis_size("row")
    col_count = lax.axis_size("col")
    row_tiles = col_count * own_rows // tile_edge
    col_tiles = row_count * own_rows // tile_edge
    column_block = lax.all_gather(features, "row", axis=0, tiled=True)
    source = column_block.reshape(col_tiles, tile_edge, feat_width)
    partial_rows = sparse_product(
        tile_block, row_index, col_index, live_count, source, row_tiles, False
    )
    partial_flat = partial_rows.reshape(row_tiles * tile_edge, feat_width)
    node_total = row_count * col_count * own_rows
    aggregated = scatter_sum(
        partial_rows.reshape(col_count, own_rows, feat_width), "col", "row", jnp.bfloat16, 0
    )
    output, hidden_grad = activation(aggregated, weight, cotangent)
    own_grad = lax.dot_general(
        hidden_grad, weight, (((1,), (1,)), ((), ())), preferred_element_type=jnp.float32
    ).astype(jnp.bfloat16)
    row_block = lax.all_gather(own_grad, "col", axis=0, tiled=True)
    local_grad = lax.dot_general(
        aggregated, hidden_grad, (((0,), (0,)), ((), ())), preferred_element_type=jnp.float32
    )
    weight_grad = all_sum(local_grad, 1) * (1.0 / math.sqrt(node_total))
    source_back = row_block.reshape(row_tiles, tile_edge, feat_width)
    partial_cols = sparse_product(
        tile_block, col_index, row_index, live_count, source_back, col_tiles, True
    )
    input_grad = lax.psum_scatter(
        partial_cols.reshape(col_tiles * tile_edge, feat_width),
        "row",
        scatter_dimension=0,
        tiled=True,
    ).astype(jnp.float32)
    return (output, weight_grad, input_grad)


def solution(mesh):
    placed = (
        P("row", "col", None, None, None),
        P("row", "col", None),
        P("row", "col", None),
        P("row", "col"),
        P(("row", "col"), None),
        P(),
        P(("row", "col"), None),
    )
    return jax.shard_map(
        per_device,
        mesh=mesh,
        in_specs=placed,
        out_specs=(P(("row", "col"), None), P(), P(("row", "col"), None)),
        check_vma=False,
    )
```

```python
import functools
import math

import jax
import jax.numpy as jnp
from jax import lax
from jax.experimental import pallas as pl
from jax.experimental.pallas import tpu as pltpu
from jax.sharding import PartitionSpec as P

SLOTS_PER_STEP = 32
UNROLL = 32


def spmm_kernel(transpose, acc_index, src_index, count_ref, tiles_ref, src_ref, out_ref, acc_ref):
    step = pl.program_id(0)
    per_step = tiles_ref.shape[0]
    live = count_ref[0]
    acc_last = acc_ref.shape[0] - 1
    src_last = src_ref.shape[0] - 1

    @pl.when(step == 0)
    def _():
        acc_ref[...] = jnp.zeros_like(acc_ref)

    def one_slot(k, carry):
        slot = step * per_step + k
        target = jnp.clip(acc_index[slot], 0, acc_last)
        picked = jnp.clip(src_index[slot], 0, src_last)
        tile = tiles_ref[k]
        tile = jnp.where(slot < live, tile, jnp.zeros_like(tile))
        block = src_ref[picked]
        if transpose:
            product = lax.dot_general(
                tile, block, (((0,), (0,)), ((), ())), preferred_element_type=jnp.float32
            )
        else:
            product = jnp.dot(tile, block, preferred_element_type=jnp.float32)
        acc_ref[target] += product
        return carry

    lax.fori_loop(0, per_step, one_slot, 0, unroll=UNROLL)

    @pl.when(step == pl.num_programs(0) - 1)
    def _():
        out_ref[...] = acc_ref[...].astype(out_ref.dtype)


def sparse_product(tile_block, acc_index, src_index, live_count, source, segments, transpose):
    slot_total, tile_edge, _ = tile_block.shape
    feat_width = source.shape[2]
    per_step = min(SLOTS_PER_STEP, slot_total)
    steps = slot_total // per_step

    def tile_map(step, acc_ref, src_ref, count_ref):
        last_live = jnp.maximum(count_ref[0] - 1, 0) // per_step
        return (jnp.minimum(step, last_live), 0, 0)

    grid_spec = pltpu.PrefetchScalarGridSpec(
        num_scalar_prefetch=3,
        grid=(steps,),
        in_specs=[
            pl.BlockSpec((per_step, tile_edge, tile_edge), tile_map),
            pl.BlockSpec(source.shape, lambda step, *_: (0, 0, 0)),
        ],
        out_specs=pl.BlockSpec((segments, tile_edge, feat_width), lambda step, *_: (0, 0, 0)),
        scratch_shapes=[pltpu.VMEM((segments, tile_edge, feat_width), jnp.float32)],
    )
    flops = 2 * slot_total * tile_edge * tile_edge * feat_width
    bytes_accessed = (
        tile_block.size * 2 + source.size * 2 + segments * tile_edge * feat_width * 2
    )
    return pl.pallas_call(
        functools.partial(spmm_kernel, transpose),
        out_shape=jax.ShapeDtypeStruct((segments, tile_edge, feat_width), jnp.bfloat16),
        grid_spec=grid_spec,
        compiler_params=pltpu.CompilerParams(
            dimension_semantics=("arbitrary",), vmem_limit_bytes=56 * 1024 * 1024
        ),
        cost_estimate=pl.CostEstimate(
            flops=flops, transcendentals=0, bytes_accessed=bytes_accessed
        ),
    )(acc_index, src_index, live_count, tile_block, source)


def peer_id(axis, other_axis, peer):
    if axis == "row":
        return (peer, lax.axis_index(other_axis))
    return (lax.axis_index(other_axis), peer)


def greet_all(axis, other_axis, n, me):
    barrier = pltpu.get_barrier_semaphore()
    for offset in range(1, n):
        peer = lax.rem(me + offset, n)
        pl.semaphore_signal(
            barrier, 1, device_id=peer_id(axis, other_axis, peer),
            device_id_type=pl.DeviceIdType.MESH,
        )
    pl.semaphore_wait(barrier, n - 1)


def scatter_sum_kernel(axis, other_axis, n, x_hbm, out_ref, recv, send_sems, recv_sems, own_sem):
    me = lax.axis_index(axis)
    greet_all(axis, other_axis, n, me)
    own = pltpu.make_async_copy(x_hbm.at[me], recv.at[me], own_sem)
    own.start()
    sends = []
    for offset in range(1, n):
        peer = lax.rem(me + offset, n)
        copy = pltpu.make_async_remote_copy(
            src_ref=x_hbm.at[peer],
            dst_ref=recv.at[me],
            send_sem=send_sems.at[offset],
            recv_sem=recv_sems.at[me],
            device_id=peer_id(axis, other_axis, peer),
            device_id_type=pl.DeviceIdType.MESH,
        )
        copy.start()
        sends.append(copy)
    own.wait()
    for offset in range(1, n):
        source = lax.rem(me + n - offset, n)
        pltpu.make_async_remote_copy(
            src_ref=x_hbm.at[source],
            dst_ref=recv.at[source],
            send_sem=send_sems.at[offset],
            recv_sem=recv_sems.at[source],
            device_id=peer_id(axis, other_axis, source),
            device_id_type=pl.DeviceIdType.MESH,
        ).wait_recv()
    total = recv[0].astype(jnp.float32)
    for j in range(1, n):
        total = total + recv[j].astype(jnp.float32)
    out_ref[...] = total.astype(out_ref.dtype)
    for copy in sends:
        copy.wait_send()


def scatter_sum(x, axis, other_axis, out_dtype, collective_id):
    n, rows, lanes = x.shape
    return pl.pallas_call(
        functools.partial(scatter_sum_kernel, axis, other_axis, n),
        out_shape=jax.ShapeDtypeStruct((rows, lanes), out_dtype),
        in_specs=[pl.BlockSpec(memory_space=pl.ANY)],
        out_specs=pl.BlockSpec(memory_space=pltpu.VMEM),
        scratch_shapes=[
            pltpu.VMEM((n, rows, lanes), x.dtype),
            pltpu.SemaphoreType.DMA((n,)),
            pltpu.SemaphoreType.DMA((n,)),
            pltpu.SemaphoreType.DMA(()),
        ],
        compiler_params=pltpu.CompilerParams(
            collective_id=collective_id, has_side_effects=True,
            vmem_limit_bytes=48 * 1024 * 1024,
        ),
        cost_estimate=pl.CostEstimate(
            flops=x.size, transcendentals=0, bytes_accessed=3 * x.size * x.dtype.itemsize
        ),
    )(x)


def gather_all_kernel(axis, other_axis, n, x_ref, out_ref, recv, send_sems, recv_sems):
    me = lax.axis_index(axis)
    recv[me] = x_ref[...]
    greet_all(axis, other_axis, n, me)
    sends = []
    for offset in range(1, n):
        peer = lax.rem(me + offset, n)
        copy = pltpu.make_async_remote_copy(
            src_ref=x_ref,
            dst_ref=recv.at[me],
            send_sem=send_sems.at[offset],
            recv_sem=recv_sems.at[me],
            device_id=peer_id(axis, other_axis, peer),
            device_id_type=pl.DeviceIdType.MESH,
        )
        copy.start()
        sends.append(copy)
    for offset in range(1, n):
        source = lax.rem(me + n - offset, n)
        pltpu.make_async_remote_copy(
            src_ref=x_ref,
            dst_ref=recv.at[source],
            send_sem=send_sems.at[offset],
            recv_sem=recv_sems.at[source],
            device_id=peer_id(axis, other_axis, source),
            device_id_type=pl.DeviceIdType.MESH,
        ).wait_recv()
    out_ref[...] = recv[...]
    for copy in sends:
        copy.wait_send()


def gather_all(x, axis, other_axis, n, collective_id):
    rows, lanes = x.shape
    return pl.pallas_call(
        functools.partial(gather_all_kernel, axis, other_axis, n),
        out_shape=jax.ShapeDtypeStruct((n, rows, lanes), x.dtype),
        in_specs=[pl.BlockSpec(memory_space=pltpu.VMEM)],
        out_specs=pl.BlockSpec(memory_space=pltpu.VMEM),
        scratch_shapes=[
            pltpu.VMEM((n, rows, lanes), x.dtype),
            pltpu.SemaphoreType.DMA((n,)),
            pltpu.SemaphoreType.DMA((n,)),
        ],
        compiler_params=pltpu.CompilerParams(
            collective_id=collective_id, has_side_effects=True,
            vmem_limit_bytes=48 * 1024 * 1024,
        ),
        cost_estimate=pl.CostEstimate(
            flops=0, transcendentals=0, bytes_accessed=3 * n * x.size * x.dtype.itemsize
        ),
    )(x)


def all_sum(local, collective_base):
    row_count = lax.axis_size("row")
    col_count = lax.axis_size("col")
    height, width = local.shape
    by_col = scatter_sum(
        local.reshape(col_count, height // col_count, width), "col", "row", jnp.float32,
        collective_base,
    )
    part = height // col_count
    by_row = scatter_sum(
        by_col.reshape(row_count, part // row_count, width), "row", "col", jnp.float32,
        collective_base + 1,
    )
    back_row = gather_all(by_row, "row", "col", row_count, collective_base + 2)
    back_col = gather_all(back_row.reshape(part, width), "col", "row", col_count, collective_base + 3)
    return back_col.reshape(height, width)


def activation(aggregated, weight, cot_rows):
    hidden = jnp.dot(aggregated, weight, preferred_element_type=jnp.float32)
    sigmoid_value = jax.nn.sigmoid(hidden)
    output = (hidden * sigmoid_value).astype(jnp.bfloat16)
    silu_slope = sigmoid_value * (1.0 + hidden * (1.0 - sigmoid_value))
    hidden_grad = (cot_rows.astype(jnp.float32) * silu_slope).astype(jnp.bfloat16)
    return (output, hidden_grad)


def per_device(tile_values, tile_rows, tile_cols, tile_count, features, weight, cotangent):
    slot_total = tile_values.shape[2]
    tile_edge = tile_values.shape[3]
    tile_block = tile_values.reshape(slot_total, tile_edge, tile_edge)
    row_index = tile_rows.reshape(slot_total)
    col_index = tile_cols.reshape(slot_total)
    live_count = tile_count.reshape(1)
    own_rows = features.shape[0]
    feat_width = features.shape[1]
    row_count = lax.axis_size("row")
    col_count = lax.axis_size("col")
    row_tiles = col_count * own_rows // tile_edge
    col_tiles = row_count * own_rows // tile_edge
    column_block = lax.all_gather(features, "row", axis=0, tiled=True)
    source = column_block.reshape(col_tiles, tile_edge, feat_width)
    partial_rows = sparse_product(
        tile_block, row_index, col_index, live_count, source, row_tiles, False
    )
    partial_flat = partial_rows.reshape(row_tiles * tile_edge, feat_width)
    node_total = row_count * col_count * own_rows
    aggregated = scatter_sum(
        partial_rows.reshape(col_count, own_rows, feat_width), "col", "row", jnp.bfloat16, 0
    )
    output, hidden_grad = activation(aggregated, weight, cotangent)
    own_grad = lax.dot_general(
        hidden_grad, weight, (((1,), (1,)), ((), ())), preferred_element_type=jnp.float32
    ).astype(jnp.bfloat16)
    row_block = lax.all_gather(own_grad, "col", axis=0, tiled=True)
    local_grad = lax.dot_general(
        aggregated, hidden_grad, (((0,), (0,)), ((), ())), preferred_element_type=jnp.float32
    )
    weight_grad = all_sum(local_grad, 1) * (1.0 / math.sqrt(node_total))
    row_block, weight_grad = lax.optimization_barrier((row_block, weight_grad))
    source_back = row_block.reshape(row_tiles, tile_edge, feat_width)
    partial_cols = sparse_product(
        tile_block, col_index, row_index, live_count, source_back, col_tiles, True
    )
    input_grad = lax.psum_scatter(
        partial_cols.reshape(col_tiles * tile_edge, feat_width),
        "row",
        scatter_dimension=0,
        tiled=True,
    ).astype(jnp.float32)
    return (output, weight_grad, input_grad)


def solution(mesh):
    placed = (
        P("row", "col", None, None, None),
        P("row", "col", None),
        P("row", "col", None),
        P("row", "col"),
        P(("row", "col"), None),
        P(),
        P(("row", "col"), None),
    )
    return jax.shard_map(
        per_device,
        mesh=mesh,
        in_specs=placed,
        out_specs=(P(("row", "col"), None), P(), P(("row", "col"), None)),
        check_vma=False,
    )
```

```python
import functools
import math

import jax
import jax.numpy as jnp
from jax import lax
from jax.experimental import pallas as pl
from jax.experimental.pallas import tpu as pltpu
from jax.sharding import PartitionSpec as P

SLOTS_PER_STEP = 32
UNROLL = 32
TORUS_X = 4


def spmm_kernel(transpose, acc_index, src_index, count_ref, tiles_ref, src_ref, out_ref, acc_ref):
    step = pl.program_id(0)
    per_step = tiles_ref.shape[0]
    live = count_ref[0]
    acc_last = acc_ref.shape[0] - 1
    src_last = src_ref.shape[0] - 1

    @pl.when(step == 0)
    def _():
        acc_ref[...] = jnp.zeros_like(acc_ref)

    def one_slot(k, carry):
        slot = step * per_step + k
        target = jnp.clip(acc_index[slot], 0, acc_last)
        picked = jnp.clip(src_index[slot], 0, src_last)
        tile = tiles_ref[k]
        tile = jnp.where(slot < live, tile, jnp.zeros_like(tile))
        block = src_ref[picked]
        if transpose:
            product = lax.dot_general(
                tile, block, (((0,), (0,)), ((), ())), preferred_element_type=jnp.float32
            )
        else:
            product = jnp.dot(tile, block, preferred_element_type=jnp.float32)
        acc_ref[target] += product
        return carry

    lax.fori_loop(0, per_step, one_slot, 0, unroll=UNROLL)

    @pl.when(step == pl.num_programs(0) - 1)
    def _():
        out_ref[...] = acc_ref[...].astype(out_ref.dtype)


def sparse_product(tile_block, acc_index, src_index, live_count, source, segments, transpose):
    slot_total, tile_edge, _ = tile_block.shape
    feat_width = source.shape[2]
    per_step = min(SLOTS_PER_STEP, slot_total)
    steps = slot_total // per_step

    def tile_map(step, acc_ref, src_ref, count_ref):
        last_live = jnp.maximum(count_ref[0] - 1, 0) // per_step
        return (jnp.minimum(step, last_live), 0, 0)

    grid_spec = pltpu.PrefetchScalarGridSpec(
        num_scalar_prefetch=3,
        grid=(steps,),
        in_specs=[
            pl.BlockSpec((per_step, tile_edge, tile_edge), tile_map),
            pl.BlockSpec(source.shape, lambda step, *_: (0, 0, 0)),
        ],
        out_specs=pl.BlockSpec((segments, tile_edge, feat_width), lambda step, *_: (0, 0, 0)),
        scratch_shapes=[pltpu.VMEM((segments, tile_edge, feat_width), jnp.float32)],
    )
    flops = 2 * slot_total * tile_edge * tile_edge * feat_width
    bytes_accessed = (
        tile_block.size * 2 + source.size * 2 + segments * tile_edge * feat_width * 2
    )
    return pl.pallas_call(
        functools.partial(spmm_kernel, transpose),
        out_shape=jax.ShapeDtypeStruct((segments, tile_edge, feat_width), jnp.bfloat16),
        grid_spec=grid_spec,
        compiler_params=pltpu.CompilerParams(
            dimension_semantics=("arbitrary",), vmem_limit_bytes=56 * 1024 * 1024
        ),
        cost_estimate=pl.CostEstimate(
            flops=flops, transcendentals=0, bytes_accessed=bytes_accessed
        ),
    )(acc_index, src_index, live_count, tile_block, source)


def peer_id(axis, other_axis, peer):
    if axis == "row":
        return (peer, lax.axis_index(other_axis))
    return (lax.axis_index(other_axis), peer)


def greet_all(axis, other_axis, n, me):
    barrier = pltpu.get_barrier_semaphore()
    for offset in range(1, n):
        peer = lax.rem(me + offset, n)
        pl.semaphore_signal(
            barrier, 1, device_id=peer_id(axis, other_axis, peer),
            device_id_type=pl.DeviceIdType.MESH,
        )
    pl.semaphore_wait(barrier, n - 1)


def scatter_sum_kernel(axis, other_axis, n, x_hbm, out_ref, recv, send_sems, recv_sems, own_sem):
    me = lax.axis_index(axis)
    greet_all(axis, other_axis, n, me)
    own = pltpu.make_async_copy(x_hbm.at[me], recv.at[me], own_sem)
    own.start()
    sends = []
    for offset in range(1, n):
        peer = lax.rem(me + offset, n)
        copy = pltpu.make_async_remote_copy(
            src_ref=x_hbm.at[peer],
            dst_ref=recv.at[me],
            send_sem=send_sems.at[offset],
            recv_sem=recv_sems.at[me],
            device_id=peer_id(axis, other_axis, peer),
            device_id_type=pl.DeviceIdType.MESH,
        )
        copy.start()
        sends.append(copy)
    own.wait()
    for offset in range(1, n):
        source = lax.rem(me + n - offset, n)
        pltpu.make_async_remote_copy(
            src_ref=x_hbm.at[source],
            dst_ref=recv.at[source],
            send_sem=send_sems.at[offset],
            recv_sem=recv_sems.at[source],
            device_id=peer_id(axis, other_axis, source),
            device_id_type=pl.DeviceIdType.MESH,
        ).wait_recv()
    total = recv[0].astype(jnp.float32)
    for j in range(1, n):
        total = total + recv[j].astype(jnp.float32)
    out_ref[...] = total.astype(out_ref.dtype)
    for copy in sends:
        copy.wait_send()


def scatter_sum(x, axis, other_axis, out_dtype, collective_id):
    n, rows, lanes = x.shape
    return pl.pallas_call(
        functools.partial(scatter_sum_kernel, axis, other_axis, n),
        out_shape=jax.ShapeDtypeStruct((rows, lanes), out_dtype),
        in_specs=[pl.BlockSpec(memory_space=pl.ANY)],
        out_specs=pl.BlockSpec(memory_space=pltpu.VMEM),
        scratch_shapes=[
            pltpu.VMEM((n, rows, lanes), x.dtype),
            pltpu.SemaphoreType.DMA((n,)),
            pltpu.SemaphoreType.DMA((n,)),
            pltpu.SemaphoreType.DMA(()),
        ],
        compiler_params=pltpu.CompilerParams(
            collective_id=collective_id, has_side_effects=True,
            vmem_limit_bytes=48 * 1024 * 1024,
        ),
        cost_estimate=pl.CostEstimate(
            flops=x.size, transcendentals=0, bytes_accessed=3 * x.size * x.dtype.itemsize
        ),
    )(x)


def gather_all_kernel(axis, other_axis, n, x_ref, out_ref, recv, send_sems, recv_sems):
    me = lax.axis_index(axis)
    recv[me] = x_ref[...]
    greet_all(axis, other_axis, n, me)
    sends = []
    for offset in range(1, n):
        peer = lax.rem(me + offset, n)
        copy = pltpu.make_async_remote_copy(
            src_ref=x_ref,
            dst_ref=recv.at[me],
            send_sem=send_sems.at[offset],
            recv_sem=recv_sems.at[me],
            device_id=peer_id(axis, other_axis, peer),
            device_id_type=pl.DeviceIdType.MESH,
        )
        copy.start()
        sends.append(copy)
    for offset in range(1, n):
        source = lax.rem(me + n - offset, n)
        pltpu.make_async_remote_copy(
            src_ref=x_ref,
            dst_ref=recv.at[source],
            send_sem=send_sems.at[offset],
            recv_sem=recv_sems.at[source],
            device_id=peer_id(axis, other_axis, source),
            device_id_type=pl.DeviceIdType.MESH,
        ).wait_recv()
    out_ref[...] = recv[...]
    for copy in sends:
        copy.wait_send()


def gather_all(x, axis, other_axis, n, collective_id):
    rows, lanes = x.shape
    return pl.pallas_call(
        functools.partial(gather_all_kernel, axis, other_axis, n),
        out_shape=jax.ShapeDtypeStruct((n, rows, lanes), x.dtype),
        in_specs=[pl.BlockSpec(memory_space=pltpu.VMEM)],
        out_specs=pl.BlockSpec(memory_space=pltpu.VMEM),
        scratch_shapes=[
            pltpu.VMEM((n, rows, lanes), x.dtype),
            pltpu.SemaphoreType.DMA((n,)),
            pltpu.SemaphoreType.DMA((n,)),
        ],
        compiler_params=pltpu.CompilerParams(
            collective_id=collective_id, has_side_effects=True,
            vmem_limit_bytes=48 * 1024 * 1024,
        ),
        cost_estimate=pl.CostEstimate(
            flops=0, transcendentals=0, bytes_accessed=3 * n * x.size * x.dtype.itemsize
        ),
    )(x)


def torus_peer(y, x, nx):
    return (lax.axis_index("row"), y * nx + x)


def scatter_sum_2d_kernel(nx, ny, x_hbm, out_ref, recv1, mid, recv2, sems):
    send1, got1, send2, got2, own_sems = sems
    me = lax.axis_index("col")
    my_y = me // nx
    my_x = lax.rem(me, nx)
    half = x_hbm.shape[2] // 2
    lower = pl.ds(0, half)
    upper = pl.ds(half, half)
    mesh_kind = pl.DeviceIdType.MESH

    barrier = pltpu.get_barrier_semaphore()
    for offset in range(1, nx):
        pl.semaphore_signal(barrier, 1, device_id=torus_peer(my_y, lax.rem(my_x + offset, nx), nx),
                            device_id_type=mesh_kind)
    for offset in range(1, ny):
        pl.semaphore_signal(barrier, 1, device_id=torus_peer(lax.rem(my_y + offset, ny), my_x, nx),
                            device_id_type=mesh_kind)
    pl.semaphore_wait(barrier, nx + ny - 2)

    own_a = pltpu.make_async_copy(x_hbm.at[:, my_x, lower], recv1.at[0, my_x], own_sems.at[0])
    own_b = pltpu.make_async_copy(x_hbm.at[my_y, :, upper], recv1.at[1, my_y], own_sems.at[1])
    own_a.start()
    own_b.start()
    sends = []
    for offset in range(1, nx):
        peer_x = lax.rem(my_x + offset, nx)
        copy = pltpu.make_async_remote_copy(
            src_ref=x_hbm.at[:, peer_x, lower], dst_ref=recv1.at[0, my_x],
            send_sem=send1.at[0, offset], recv_sem=got1.at[0, my_x],
            device_id=torus_peer(my_y, peer_x, nx), device_id_type=mesh_kind,
        )
        copy.start()
        sends.append(copy)
    for offset in range(1, ny):
        peer_y = lax.rem(my_y + offset, ny)
        copy = pltpu.make_async_remote_copy(
            src_ref=x_hbm.at[peer_y, :, upper], dst_ref=recv1.at[1, my_y],
            send_sem=send1.at[1, offset], recv_sem=got1.at[1, my_y],
            device_id=torus_peer(peer_y, my_x, nx), device_id_type=mesh_kind,
        )
        copy.start()
        sends.append(copy)
    own_a.wait()
    own_b.wait()
    for offset in range(1, nx):
        source_x = lax.rem(my_x + nx - offset, nx)
        pltpu.make_async_remote_copy(
            src_ref=x_hbm.at[:, source_x, lower], dst_ref=recv1.at[0, source_x],
            send_sem=send1.at[0, offset], recv_sem=got1.at[0, source_x],
            device_id=torus_peer(my_y, source_x, nx), device_id_type=mesh_kind,
        ).wait_recv()
    for offset in range(1, ny):
        source_y = lax.rem(my_y + ny - offset, ny)
        pltpu.make_async_remote_copy(
            src_ref=x_hbm.at[source_y, :, upper], dst_ref=recv1.at[1, source_y],
            send_sem=send1.at[1, offset], recv_sem=got1.at[1, source_y],
            device_id=torus_peer(source_y, my_x, nx), device_id_type=mesh_kind,
        ).wait_recv()

    def add_up(stack):
        total = stack[0].astype(jnp.float32)
        for j in range(1, stack.shape[0]):
            total = total + stack[j].astype(jnp.float32)
        return total

    for target in range(ny):
        mid[0, target] = add_up(recv1[0, :, target]).astype(mid.dtype)
    for target in range(nx):
        mid[1, target] = add_up(recv1[1, :, target]).astype(mid.dtype)
    recv2[0, my_y] = mid[0, my_y]
    recv2[1, my_x] = mid[1, my_x]

    for offset in range(1, ny):
        peer_y = lax.rem(my_y + offset, ny)
        copy = pltpu.make_async_remote_copy(
            src_ref=mid.at[0, peer_y], dst_ref=recv2.at[0, my_y],
            send_sem=send2.at[0, offset], recv_sem=got2.at[0, my_y],
            device_id=torus_peer(peer_y, my_x, nx), device_id_type=mesh_kind,
        )
        copy.start()
        sends.append(copy)
    for offset in range(1, nx):
        peer_x = lax.rem(my_x + offset, nx)
        copy = pltpu.make_async_remote_copy(
            src_ref=mid.at[1, peer_x], dst_ref=recv2.at[1, my_x],
            send_sem=send2.at[1, offset], recv_sem=got2.at[1, my_x],
            device_id=torus_peer(my_y, peer_x, nx), device_id_type=mesh_kind,
        )
        copy.start()
        sends.append(copy)
    for offset in range(1, ny):
        source_y = lax.rem(my_y + ny - offset, ny)
        pltpu.make_async_remote_copy(
            src_ref=mid.at[0, source_y], dst_ref=recv2.at[0, source_y],
            send_sem=send2.at[0, offset], recv_sem=got2.at[0, source_y],
            device_id=torus_peer(source_y, my_x, nx), device_id_type=mesh_kind,
        ).wait_recv()
    for offset in range(1, nx):
        source_x = lax.rem(my_x + nx - offset, nx)
        pltpu.make_async_remote_copy(
            src_ref=mid.at[1, source_x], dst_ref=recv2.at[1, source_x],
            send_sem=send2.at[1, offset], recv_sem=got2.at[1, source_x],
            device_id=torus_peer(my_y, source_x, nx), device_id_type=mesh_kind,
        ).wait_recv()
    out_ref[lower] = add_up(recv2[0]).astype(out_ref.dtype)
    out_ref[upper] = add_up(recv2[1]).astype(out_ref.dtype)
    for copy in sends:
        copy.wait_send()


def scatter_sum_2d(x, nx, out_dtype, collective_id):
    n, rows, lanes = x.shape
    ny = n // nx
    half = rows // 2
    side = max(nx, ny)
    return pl.pallas_call(
        functools.partial(scatter_sum_2d_kernel, nx, ny),
        out_shape=jax.ShapeDtypeStruct((rows, lanes), out_dtype),
        in_specs=[pl.BlockSpec(memory_space=pl.ANY)],
        out_specs=pl.BlockSpec(memory_space=pltpu.VMEM),
        scratch_shapes=[
            pltpu.VMEM((2, side, side, half, lanes), x.dtype),
            pltpu.VMEM((2, side, half, lanes), x.dtype),
            pltpu.VMEM((2, side, half, lanes), x.dtype),
            (
                pltpu.SemaphoreType.DMA((2, side)),
                pltpu.SemaphoreType.DMA((2, side)),
                pltpu.SemaphoreType.DMA((2, side)),
                pltpu.SemaphoreType.DMA((2, side)),
                pltpu.SemaphoreType.DMA((2,)),
            ),
        ],
        compiler_params=pltpu.CompilerParams(
            collective_id=collective_id, has_side_effects=True,
            vmem_limit_bytes=48 * 1024 * 1024,
        ),
        cost_estimate=pl.CostEstimate(
            flops=x.size, transcendentals=0, bytes_accessed=3 * x.size * x.dtype.itemsize
        ),
    )(x.reshape(ny, nx, rows, lanes))


def all_sum(local, collective_base):
    row_count = lax.axis_size("row")
    col_count = lax.axis_size("col")
    height, width = local.shape
    by_col = scatter_sum(
        local.reshape(col_count, height // col_count, width), "col", "row", jnp.float32,
        collective_base,
    )
    part = height // col_count
    by_row = scatter_sum(
        by_col.reshape(row_count, part // row_count, width), "row", "col", jnp.float32,
        collective_base + 1,
    )
    back_row = gather_all(by_row, "row", "col", row_count, collective_base + 2)
    back_col = gather_all(back_row.reshape(part, width), "col", "row", col_count, collective_base + 3)
    return back_col.reshape(height, width)


def activation(aggregated, weight, cot_rows):
    hidden = jnp.dot(aggregated, weight, preferred_element_type=jnp.float32)
    sigmoid_value = jax.nn.sigmoid(hidden)
    output = (hidden * sigmoid_value).astype(jnp.bfloat16)
    silu_slope = sigmoid_value * (1.0 + hidden * (1.0 - sigmoid_value))
    hidden_grad = (cot_rows.astype(jnp.float32) * silu_slope).astype(jnp.bfloat16)
    return (output, hidden_grad)


def per_device(tile_values, tile_rows, tile_cols, tile_count, features, weight, cotangent):
    slot_total = tile_values.shape[2]
    tile_edge = tile_values.shape[3]
    tile_block = tile_values.reshape(slot_total, tile_edge, tile_edge)
    row_index = tile_rows.reshape(slot_total)
    col_index = tile_cols.reshape(slot_total)
    live_count = tile_count.reshape(1)
    own_rows = features.shape[0]
    feat_width = features.shape[1]
    row_count = lax.axis_size("row")
    col_count = lax.axis_size("col")
    row_tiles = col_count * own_rows // tile_edge
    col_tiles = row_count * own_rows // tile_edge
    column_block = lax.all_gather(features, "row", axis=0, tiled=True)
    source = column_block.reshape(col_tiles, tile_edge, feat_width)
    partial_rows = sparse_product(
        tile_block, row_index, col_index, live_count, source, row_tiles, False
    )
    partial_flat = partial_rows.reshape(row_tiles * tile_edge, feat_width)
    node_total = row_count * col_count * own_rows
    aggregated = scatter_sum_2d(
        partial_rows.reshape(col_count, own_rows, feat_width), TORUS_X, jnp.bfloat16, 0
    )
    output, hidden_grad = activation(aggregated, weight, cotangent)
    own_grad = lax.dot_general(
        hidden_grad, weight, (((1,), (1,)), ((), ())), preferred_element_type=jnp.float32
    ).astype(jnp.bfloat16)
    row_block = lax.all_gather(own_grad, "col", axis=0, tiled=True)
    local_grad = lax.dot_general(
        aggregated, hidden_grad, (((0,), (0,)), ((), ())), preferred_element_type=jnp.float32
    )
    weight_grad = all_sum(local_grad, 1) * (1.0 / math.sqrt(node_total))
    row_block, weight_grad = lax.optimization_barrier((row_block, weight_grad))
    source_back = row_block.reshape(row_tiles, tile_edge, feat_width)
    partial_cols = sparse_product(
        tile_block, col_index, row_index, live_count, source_back, col_tiles, True
    )
    input_grad = lax.psum_scatter(
        partial_cols.reshape(col_tiles * tile_edge, feat_width),
        "row",
        scatter_dimension=0,
        tiled=True,
    ).astype(jnp.float32)
    return (output, weight_grad, input_grad)


def solution(mesh):
    placed = (
        P("row", "col", None, None, None),
        P("row", "col", None),
        P("row", "col", None),
        P("row", "col"),
        P(("row", "col"), None),
        P(),
        P(("row", "col"), None),
    )
    return jax.shard_map(
        per_device,
        mesh=mesh,
        in_specs=placed,
        out_specs=(P(("row", "col"), None), P(), P(("row", "col"), None)),
        check_vma=False,
    )
```

```python
import functools
import math

import jax
import jax.numpy as jnp
from jax import lax
from jax.experimental import pallas as pl
from jax.experimental.pallas import tpu as pltpu
from jax.sharding import PartitionSpec as P

SLOTS_PER_STEP = 32
UNROLL = 32
TORUS_X = 4


def spmm_kernel(transpose, acc_index, src_index, count_ref, tiles_ref, src_ref, out_ref, acc_ref):
    step = pl.program_id(0)
    per_step = tiles_ref.shape[0]
    live = count_ref[0]
    acc_last = acc_ref.shape[0] - 1
    src_last = src_ref.shape[0] - 1

    @pl.when(step == 0)
    def _():
        acc_ref[...] = jnp.zeros_like(acc_ref)

    def one_slot(k, carry):
        slot = step * per_step + k
        target = jnp.clip(acc_index[slot], 0, acc_last)
        picked = jnp.clip(src_index[slot], 0, src_last)
        tile = tiles_ref[k]
        tile = jnp.where(slot < live, tile, jnp.zeros_like(tile))
        block = src_ref[picked]
        if transpose:
            product = lax.dot_general(
                tile, block, (((0,), (0,)), ((), ())), preferred_element_type=jnp.float32
            )
        else:
            product = jnp.dot(tile, block, preferred_element_type=jnp.float32)
        acc_ref[target] += product
        return carry

    lax.fori_loop(0, per_step, one_slot, 0, unroll=UNROLL)

    @pl.when(step == pl.num_programs(0) - 1)
    def _():
        out_ref[...] = acc_ref[...].astype(out_ref.dtype)


def sparse_product(tile_block, acc_index, src_index, live_count, source, segments, transpose):
    slot_total, tile_edge, _ = tile_block.shape
    feat_width = source.shape[2]
    per_step = min(SLOTS_PER_STEP, slot_total)
    steps = slot_total // per_step

    def tile_map(step, acc_ref, src_ref, count_ref):
        last_live = jnp.maximum(count_ref[0] - 1, 0) // per_step
        return (jnp.minimum(step, last_live), 0, 0)

    grid_spec = pltpu.PrefetchScalarGridSpec(
        num_scalar_prefetch=3,
        grid=(steps,),
        in_specs=[
            pl.BlockSpec((per_step, tile_edge, tile_edge), tile_map),
            pl.BlockSpec(source.shape, lambda step, *_: (0, 0, 0)),
        ],
        out_specs=pl.BlockSpec((segments, tile_edge, feat_width), lambda step, *_: (0, 0, 0)),
        scratch_shapes=[pltpu.VMEM((segments, tile_edge, feat_width), jnp.float32)],
    )
    flops = 2 * slot_total * tile_edge * tile_edge * feat_width
    bytes_accessed = (
        tile_block.size * 2 + source.size * 2 + segments * tile_edge * feat_width * 2
    )
    return pl.pallas_call(
        functools.partial(spmm_kernel, transpose),
        out_shape=jax.ShapeDtypeStruct((segments, tile_edge, feat_width), jnp.bfloat16),
        grid_spec=grid_spec,
        compiler_params=pltpu.CompilerParams(
            dimension_semantics=("arbitrary",), vmem_limit_bytes=56 * 1024 * 1024
        ),
        cost_estimate=pl.CostEstimate(
            flops=flops, transcendentals=0, bytes_accessed=bytes_accessed
        ),
    )(acc_index, src_index, live_count, tile_block, source)


def peer_id(axis, other_axis, peer):
    if axis == "row":
        return (peer, lax.axis_index(other_axis))
    return (lax.axis_index(other_axis), peer)


def greet_all(axis, other_axis, n, me):
    barrier = pltpu.get_barrier_semaphore()
    for offset in range(1, n):
        peer = lax.rem(me + offset, n)
        pl.semaphore_signal(
            barrier, 1, device_id=peer_id(axis, other_axis, peer),
            device_id_type=pl.DeviceIdType.MESH,
        )
    pl.semaphore_wait(barrier, n - 1)


def scatter_sum_kernel(axis, other_axis, n, x_hbm, out_ref, recv, send_sems, recv_sems, own_sem):
    me = lax.axis_index(axis)
    greet_all(axis, other_axis, n, me)
    own = pltpu.make_async_copy(x_hbm.at[me], recv.at[me], own_sem)
    own.start()
    sends = []
    for offset in range(1, n):
        peer = lax.rem(me + offset, n)
        copy = pltpu.make_async_remote_copy(
            src_ref=x_hbm.at[peer],
            dst_ref=recv.at[me],
            send_sem=send_sems.at[offset],
            recv_sem=recv_sems.at[me],
            device_id=peer_id(axis, other_axis, peer),
            device_id_type=pl.DeviceIdType.MESH,
        )
        copy.start()
        sends.append(copy)
    own.wait()
    for offset in range(1, n):
        source = lax.rem(me + n - offset, n)
        pltpu.make_async_remote_copy(
            src_ref=x_hbm.at[source],
            dst_ref=recv.at[source],
            send_sem=send_sems.at[offset],
            recv_sem=recv_sems.at[source],
            device_id=peer_id(axis, other_axis, source),
            device_id_type=pl.DeviceIdType.MESH,
        ).wait_recv()
    total = recv[0].astype(jnp.float32)
    for j in range(1, n):
        total = total + recv[j].astype(jnp.float32)
    out_ref[...] = total.astype(out_ref.dtype)
    for copy in sends:
        copy.wait_send()


def scatter_sum(x, axis, other_axis, out_dtype, collective_id):
    n, rows, lanes = x.shape
    return pl.pallas_call(
        functools.partial(scatter_sum_kernel, axis, other_axis, n),
        out_shape=jax.ShapeDtypeStruct((rows, lanes), out_dtype),
        in_specs=[pl.BlockSpec(memory_space=pl.ANY)],
        out_specs=pl.BlockSpec(memory_space=pltpu.VMEM),
        scratch_shapes=[
            pltpu.VMEM((n, rows, lanes), x.dtype),
            pltpu.SemaphoreType.DMA((n,)),
            pltpu.SemaphoreType.DMA((n,)),
            pltpu.SemaphoreType.DMA(()),
        ],
        compiler_params=pltpu.CompilerParams(
            collective_id=collective_id, has_side_effects=True,
            vmem_limit_bytes=48 * 1024 * 1024,
        ),
        cost_estimate=pl.CostEstimate(
            flops=x.size, transcendentals=0, bytes_accessed=3 * x.size * x.dtype.itemsize
        ),
    )(x)


def gather_all_kernel(axis, other_axis, n, x_ref, out_ref, recv, send_sems, recv_sems):
    me = lax.axis_index(axis)
    recv[me] = x_ref[...]
    greet_all(axis, other_axis, n, me)
    sends = []
    for offset in range(1, n):
        peer = lax.rem(me + offset, n)
        copy = pltpu.make_async_remote_copy(
            src_ref=x_ref,
            dst_ref=recv.at[me],
            send_sem=send_sems.at[offset],
            recv_sem=recv_sems.at[me],
            device_id=peer_id(axis, other_axis, peer),
            device_id_type=pl.DeviceIdType.MESH,
        )
        copy.start()
        sends.append(copy)
    for offset in range(1, n):
        source = lax.rem(me + n - offset, n)
        pltpu.make_async_remote_copy(
            src_ref=x_ref,
            dst_ref=recv.at[source],
            send_sem=send_sems.at[offset],
            recv_sem=recv_sems.at[source],
            device_id=peer_id(axis, other_axis, source),
            device_id_type=pl.DeviceIdType.MESH,
        ).wait_recv()
    out_ref[...] = recv[...]
    for copy in sends:
        copy.wait_send()


def gather_all(x, axis, other_axis, n, collective_id):
    rows, lanes = x.shape
    return pl.pallas_call(
        functools.partial(gather_all_kernel, axis, other_axis, n),
        out_shape=jax.ShapeDtypeStruct((n, rows, lanes), x.dtype),
        in_specs=[pl.BlockSpec(memory_space=pltpu.VMEM)],
        out_specs=pl.BlockSpec(memory_space=pltpu.VMEM),
        scratch_shapes=[
            pltpu.VMEM((n, rows, lanes), x.dtype),
            pltpu.SemaphoreType.DMA((n,)),
            pltpu.SemaphoreType.DMA((n,)),
        ],
        compiler_params=pltpu.CompilerParams(
            collective_id=collective_id, has_side_effects=True,
            vmem_limit_bytes=48 * 1024 * 1024,
        ),
        cost_estimate=pl.CostEstimate(
            flops=0, transcendentals=0, bytes_accessed=3 * n * x.size * x.dtype.itemsize
        ),
    )(x)


def torus_peer(y, x, nx):
    return (lax.axis_index("row"), y * nx + x)


def scatter_sum_2d_kernel(nx, ny, x_hbm, out_ref, recv1, mid, recv2, sems):
    send1, got1, send2, got2, own_sems = sems
    me = lax.axis_index("col")
    my_y = me // nx
    my_x = lax.rem(me, nx)
    half = x_hbm.shape[2] // 2
    lower = pl.ds(0, half)
    upper = pl.ds(half, half)
    mesh_kind = pl.DeviceIdType.MESH

    barrier = pltpu.get_barrier_semaphore()
    for offset in range(1, nx):
        pl.semaphore_signal(barrier, 1, device_id=torus_peer(my_y, lax.rem(my_x + offset, nx), nx),
                            device_id_type=mesh_kind)
    for offset in range(1, ny):
        pl.semaphore_signal(barrier, 1, device_id=torus_peer(lax.rem(my_y + offset, ny), my_x, nx),
                            device_id_type=mesh_kind)
    pl.semaphore_wait(barrier, nx + ny - 2)

    own_a = pltpu.make_async_copy(x_hbm.at[:, my_x, lower], recv1.at[0, my_x], own_sems.at[0])
    own_b = pltpu.make_async_copy(x_hbm.at[my_y, :, upper], recv1.at[1, my_y], own_sems.at[1])
    own_a.start()
    own_b.start()
    sends = []
    for offset in range(1, nx):
        peer_x = lax.rem(my_x + offset, nx)
        copy = pltpu.make_async_remote_copy(
            src_ref=x_hbm.at[:, peer_x, lower], dst_ref=recv1.at[0, my_x],
            send_sem=send1.at[0, offset], recv_sem=got1.at[0, my_x],
            device_id=torus_peer(my_y, peer_x, nx), device_id_type=mesh_kind,
        )
        copy.start()
        sends.append(copy)
    for offset in range(1, ny):
        peer_y = lax.rem(my_y + offset, ny)
        copy = pltpu.make_async_remote_copy(
            src_ref=x_hbm.at[peer_y, :, upper], dst_ref=recv1.at[1, my_y],
            send_sem=send1.at[1, offset], recv_sem=got1.at[1, my_y],
            device_id=torus_peer(peer_y, my_x, nx), device_id_type=mesh_kind,
        )
        copy.start()
        sends.append(copy)
    own_a.wait()
    own_b.wait()
    for offset in range(1, nx):
        source_x = lax.rem(my_x + nx - offset, nx)
        pltpu.make_async_remote_copy(
            src_ref=x_hbm.at[:, source_x, lower], dst_ref=recv1.at[0, source_x],
            send_sem=send1.at[0, offset], recv_sem=got1.at[0, source_x],
            device_id=torus_peer(my_y, source_x, nx), device_id_type=mesh_kind,
        ).wait_recv()
    for offset in range(1, ny):
        source_y = lax.rem(my_y + ny - offset, ny)
        pltpu.make_async_remote_copy(
            src_ref=x_hbm.at[source_y, :, upper], dst_ref=recv1.at[1, source_y],
            send_sem=send1.at[1, offset], recv_sem=got1.at[1, source_y],
            device_id=torus_peer(source_y, my_x, nx), device_id_type=mesh_kind,
        ).wait_recv()

    def add_up(stack):
        total = stack[0].astype(jnp.float32)
        for j in range(1, stack.shape[0]):
            total = total + stack[j].astype(jnp.float32)
        return total

    for target in range(ny):
        mid[0, target] = add_up(recv1[0, :, target]).astype(mid.dtype)
    for target in range(nx):
        mid[1, target] = add_up(recv1[1, :, target]).astype(mid.dtype)
    recv2[0, my_y] = mid[0, my_y]
    recv2[1, my_x] = mid[1, my_x]

    for offset in range(1, ny):
        peer_y = lax.rem(my_y + offset, ny)
        copy = pltpu.make_async_remote_copy(
            src_ref=mid.at[0, peer_y], dst_ref=recv2.at[0, my_y],
            send_sem=send2.at[0, offset], recv_sem=got2.at[0, my_y],
            device_id=torus_peer(peer_y, my_x, nx), device_id_type=mesh_kind,
        )
        copy.start()
        sends.append(copy)
    for offset in range(1, nx):
        peer_x = lax.rem(my_x + offset, nx)
        copy = pltpu.make_async_remote_copy(
            src_ref=mid.at[1, peer_x], dst_ref=recv2.at[1, my_x],
            send_sem=send2.at[1, offset], recv_sem=got2.at[1, my_x],
            device_id=torus_peer(my_y, peer_x, nx), device_id_type=mesh_kind,
        )
        copy.start()
        sends.append(copy)
    for offset in range(1, ny):
        source_y = lax.rem(my_y + ny - offset, ny)
        pltpu.make_async_remote_copy(
            src_ref=mid.at[0, source_y], dst_ref=recv2.at[0, source_y],
            send_sem=send2.at[0, offset], recv_sem=got2.at[0, source_y],
            device_id=torus_peer(source_y, my_x, nx), device_id_type=mesh_kind,
        ).wait_recv()
    for offset in range(1, nx):
        source_x = lax.rem(my_x + nx - offset, nx)
        pltpu.make_async_remote_copy(
            src_ref=mid.at[1, source_x], dst_ref=recv2.at[1, source_x],
            send_sem=send2.at[1, offset], recv_sem=got2.at[1, source_x],
            device_id=torus_peer(my_y, source_x, nx), device_id_type=mesh_kind,
        ).wait_recv()
    out_ref[lower] = add_up(recv2[0]).astype(out_ref.dtype)
    out_ref[upper] = add_up(recv2[1]).astype(out_ref.dtype)
    for copy in sends:
        copy.wait_send()


def scatter_sum_2d(x, nx, out_dtype, collective_id):
    n, rows, lanes = x.shape
    ny = n // nx
    half = rows // 2
    side = max(nx, ny)
    return pl.pallas_call(
        functools.partial(scatter_sum_2d_kernel, nx, ny),
        out_shape=jax.ShapeDtypeStruct((rows, lanes), out_dtype),
        in_specs=[pl.BlockSpec(memory_space=pl.ANY)],
        out_specs=pl.BlockSpec(memory_space=pltpu.VMEM),
        scratch_shapes=[
            pltpu.VMEM((2, side, side, half, lanes), x.dtype),
            pltpu.VMEM((2, side, half, lanes), x.dtype),
            pltpu.VMEM((2, side, half, lanes), x.dtype),
            (
                pltpu.SemaphoreType.DMA((2, side)),
                pltpu.SemaphoreType.DMA((2, side)),
                pltpu.SemaphoreType.DMA((2, side)),
                pltpu.SemaphoreType.DMA((2, side)),
                pltpu.SemaphoreType.DMA((2,)),
            ),
        ],
        compiler_params=pltpu.CompilerParams(
            collective_id=collective_id, has_side_effects=True,
            vmem_limit_bytes=48 * 1024 * 1024,
        ),
        cost_estimate=pl.CostEstimate(
            flops=x.size, transcendentals=0, bytes_accessed=3 * x.size * x.dtype.itemsize
        ),
    )(x.reshape(ny, nx, rows, lanes))


def row_peer(index):
    return (index, lax.axis_index("col"))


def greet_row(my_z, my_core, nz):
    barrier = pltpu.get_barrier_semaphore()
    mesh_kind = pl.DeviceIdType.MESH
    pl.semaphore_signal(barrier, 1, device_id=row_peer(my_z * 2 + 1 - my_core), device_id_type=mesh_kind)
    for offset in range(1, nz):
        peer_z = lax.rem(my_z + offset, nz)
        pl.semaphore_signal(barrier, 1, device_id=row_peer(peer_z * 2 + my_core), device_id_type=mesh_kind)
    pl.semaphore_wait(barrier, nz)


def scatter_sum_row_kernel(nz, x_hbm, out_ref, own1, recv1, mid, recv2, sems):
    send1, got1, send2, got2, own_sem = sems
    mesh_kind = pl.DeviceIdType.MESH
    me = lax.axis_index("row")
    my_z = me // 2
    my_core = lax.rem(me, 2)
    other_core = 1 - my_core
    greet_row(my_z, my_core, nz)
    own = pltpu.make_async_copy(x_hbm.at[:, my_core], own1, own_sem.at[0])
    own.start()
    first = pltpu.make_async_remote_copy(
        src_ref=x_hbm.at[:, other_core], dst_ref=recv1,
        send_sem=send1.at[0], recv_sem=got1.at[0],
        device_id=row_peer(my_z * 2 + other_core), device_id_type=mesh_kind,
    )
    first.start()
    own.wait()
    first.wait_recv()
    for target in range(nz):
        mid[target] = (own1[target].astype(jnp.float32) + recv1[target].astype(jnp.float32)).astype(mid.dtype)
    sends = []
    for offset in range(1, nz):
        peer_z = lax.rem(my_z + offset, nz)
        copy = pltpu.make_async_remote_copy(
            src_ref=mid.at[peer_z], dst_ref=recv2.at[my_z],
            send_sem=send2.at[offset], recv_sem=got2.at[my_z],
            device_id=row_peer(peer_z * 2 + my_core), device_id_type=mesh_kind,
        )
        copy.start()
        sends.append(copy)
    total = mid[my_z].astype(jnp.float32)
    for offset in range(1, nz):
        source_z = lax.rem(my_z + nz - offset, nz)
        pltpu.make_async_remote_copy(
            src_ref=mid.at[source_z], dst_ref=recv2.at[source_z],
            send_sem=send2.at[offset], recv_sem=got2.at[source_z],
            device_id=row_peer(source_z * 2 + my_core), device_id_type=mesh_kind,
        ).wait_recv()
        total = total + recv2[source_z].astype(jnp.float32)
    out_ref[...] = total.astype(out_ref.dtype)
    first.wait_send()
    for copy in sends:
        copy.wait_send()


def scatter_sum_row(x, out_dtype, collective_id):
    n, rows, lanes = x.shape
    nz = n // 2
    return pl.pallas_call(
        functools.partial(scatter_sum_row_kernel, nz),
        out_shape=jax.ShapeDtypeStruct((rows, lanes), out_dtype),
        in_specs=[pl.BlockSpec(memory_space=pl.ANY)],
        out_specs=pl.BlockSpec(memory_space=pltpu.VMEM),
        scratch_shapes=[
            pltpu.VMEM((nz, rows, lanes), x.dtype),
            pltpu.VMEM((nz, rows, lanes), x.dtype),
            pltpu.VMEM((nz, rows, lanes), x.dtype),
            pltpu.VMEM((nz, rows, lanes), x.dtype),
            (
                pltpu.SemaphoreType.DMA((1,)),
                pltpu.SemaphoreType.DMA((1,)),
                pltpu.SemaphoreType.DMA((nz,)),
                pltpu.SemaphoreType.DMA((nz,)),
                pltpu.SemaphoreType.DMA((1,)),
            ),
        ],
        compiler_params=pltpu.CompilerParams(
            collective_id=collective_id, has_side_effects=True,
            vmem_limit_bytes=48 * 1024 * 1024,
        ),
        cost_estimate=pl.CostEstimate(
            flops=x.size, transcendentals=0, bytes_accessed=3 * x.size * x.dtype.itemsize
        ),
    )(x.reshape(nz, 2, rows, lanes))


def gather_row_kernel(nz, x_ref, out_ref, full, sems):
    send1, got1, send2, got2, own_sem = sems
    mesh_kind = pl.DeviceIdType.MESH
    me = lax.axis_index("row")
    my_z = me // 2
    my_core = lax.rem(me, 2)
    other_core = 1 - my_core
    greet_row(my_z, my_core, nz)
    own = pltpu.make_async_copy(x_ref, full.at[my_z, my_core], own_sem.at[0])
    own.start()
    sends = []
    for offset in range(1, nz):
        peer_z = lax.rem(my_z + offset, nz)
        copy = pltpu.make_async_remote_copy(
            src_ref=x_ref, dst_ref=full.at[my_z, my_core],
            send_sem=send1.at[offset], recv_sem=got1.at[my_z],
            device_id=row_peer(peer_z * 2 + my_core), device_id_type=mesh_kind,
        )
        copy.start()
        sends.append(copy)
    own.wait()
    for offset in range(1, nz):
        source_z = lax.rem(my_z + nz - offset, nz)
        pltpu.make_async_remote_copy(
            src_ref=x_ref, dst_ref=full.at[source_z, my_core],
            send_sem=send1.at[offset], recv_sem=got1.at[source_z],
            device_id=row_peer(source_z * 2 + my_core), device_id_type=mesh_kind,
        ).wait_recv()
    second = pltpu.make_async_remote_copy(
        src_ref=full.at[:, my_core], dst_ref=full.at[:, my_core],
        send_sem=send2.at[0], recv_sem=got2.at[0],
        device_id=row_peer(my_z * 2 + other_core), device_id_type=mesh_kind,
    )
    second.start()
    pltpu.make_async_remote_copy(
        src_ref=full.at[:, other_core], dst_ref=full.at[:, other_core],
        send_sem=send2.at[0], recv_sem=got2.at[0],
        device_id=row_peer(my_z * 2 + other_core), device_id_type=mesh_kind,
    ).wait_recv()
    for copy in sends:
        copy.wait_send()
    second.wait_send()
    out_ref[...] = full[...]


def gather_row(x, collective_id):
    rows, lanes = x.shape
    nz = lax.axis_size("row") // 2
    out = pl.pallas_call(
        functools.partial(gather_row_kernel, nz),
        out_shape=jax.ShapeDtypeStruct((nz, 2, rows, lanes), x.dtype),
        in_specs=[pl.BlockSpec(memory_space=pltpu.VMEM)],
        out_specs=pl.BlockSpec(memory_space=pltpu.VMEM),
        scratch_shapes=[
            pltpu.VMEM((nz, 2, rows, lanes), x.dtype),
            (
                pltpu.SemaphoreType.DMA((nz,)),
                pltpu.SemaphoreType.DMA((nz,)),
                pltpu.SemaphoreType.DMA((1,)),
                pltpu.SemaphoreType.DMA((1,)),
                pltpu.SemaphoreType.DMA((1,)),
            ),
        ],
        compiler_params=pltpu.CompilerParams(
            collective_id=collective_id, has_side_effects=True,
            vmem_limit_bytes=48 * 1024 * 1024,
        ),
        cost_estimate=pl.CostEstimate(
            flops=0, transcendentals=0, bytes_accessed=3 * 2 * nz * x.size * x.dtype.itemsize
        ),
    )(x)
    return out.reshape(2 * nz * rows, lanes)


def all_sum(local, collective_base):
    row_count = lax.axis_size("row")
    col_count = lax.axis_size("col")
    height, width = local.shape
    by_col = scatter_sum(
        local.reshape(col_count, height // col_count, width), "col", "row", jnp.float32,
        collective_base,
    )
    part = height // col_count
    by_row = scatter_sum(
        by_col.reshape(row_count, part // row_count, width), "row", "col", jnp.float32,
        collective_base + 1,
    )
    back_row = gather_all(by_row, "row", "col", row_count, collective_base + 2)
    back_col = gather_all(back_row.reshape(part, width), "col", "row", col_count, collective_base + 3)
    return back_col.reshape(height, width)


def activation(aggregated, weight, cot_rows):
    hidden = jnp.dot(aggregated, weight, preferred_element_type=jnp.float32)
    sigmoid_value = jax.nn.sigmoid(hidden)
    output = (hidden * sigmoid_value).astype(jnp.bfloat16)
    silu_slope = sigmoid_value * (1.0 + hidden * (1.0 - sigmoid_value))
    hidden_grad = (cot_rows.astype(jnp.float32) * silu_slope).astype(jnp.bfloat16)
    return (output, hidden_grad)


def per_device(tile_values, tile_rows, tile_cols, tile_count, features, weight, cotangent):
    slot_total = tile_values.shape[2]
    tile_edge = tile_values.shape[3]
    tile_block = tile_values.reshape(slot_total, tile_edge, tile_edge)
    row_index = tile_rows.reshape(slot_total)
    col_index = tile_cols.reshape(slot_total)
    live_count = tile_count.reshape(1)
    own_rows = features.shape[0]
    feat_width = features.shape[1]
    row_count = lax.axis_size("row")
    col_count = lax.axis_size("col")
    row_tiles = col_count * own_rows // tile_edge
    col_tiles = row_count * own_rows // tile_edge
    column_block = gather_row(features, 8)
    source = column_block.reshape(col_tiles, tile_edge, feat_width)
    partial_rows = sparse_product(
        tile_block, row_index, col_index, live_count, source, row_tiles, False
    )
    partial_flat = partial_rows.reshape(row_tiles * tile_edge, feat_width)
    node_total = row_count * col_count * own_rows
    aggregated = scatter_sum_2d(
        partial_rows.reshape(col_count, own_rows, feat_width), TORUS_X, jnp.bfloat16, 0
    )
    output, hidden_grad = activation(aggregated, weight, cotangent)
    own_grad = lax.dot_general(
        hidden_grad, weight, (((1,), (1,)), ((), ())), preferred_element_type=jnp.float32
    ).astype(jnp.bfloat16)
    row_block = lax.all_gather(own_grad, "col", axis=0, tiled=True)
    local_grad = lax.dot_general(
        aggregated, hidden_grad, (((0,), (0,)), ((), ())), preferred_element_type=jnp.float32
    )
    weight_grad = all_sum(local_grad, 1) * (1.0 / math.sqrt(node_total))
    row_block, weight_grad = lax.optimization_barrier((row_block, weight_grad))
    source_back = row_block.reshape(row_tiles, tile_edge, feat_width)
    partial_cols = sparse_product(
        tile_block, col_index, row_index, live_count, source_back, col_tiles, True
    )
    input_grad = scatter_sum_row(
        partial_cols.reshape(row_count, own_rows, feat_width), jnp.float32, 9
    )
    return (output, weight_grad, input_grad)


def solution(mesh):
    placed = (
        P("row", "col", None, None, None),
        P("row", "col", None),
        P("row", "col", None),
        P("row", "col"),
        P(("row", "col"), None),
        P(),
        P(("row", "col"), None),
    )
    return jax.shard_map(
        per_device,
        mesh=mesh,
        in_specs=placed,
        out_specs=(P(("row", "col"), None), P(), P(("row", "col"), None)),
        check_vma=False,
    )
```

```python
import functools
import math

import jax
import jax.numpy as jnp
from jax import lax
from jax.experimental import pallas as pl
from jax.experimental.pallas import tpu as pltpu
from jax.sharding import PartitionSpec as P

SLOTS_PER_STEP = 32
UNROLL = 32
TORUS_X = 4


def spmm_kernel(transpose, acc_index, src_index, count_ref, tiles_ref, src_ref, out_ref, acc_ref):
    step = pl.program_id(0)
    per_step = tiles_ref.shape[0]
    live = count_ref[0]
    acc_last = acc_ref.shape[0] - 1
    src_last = src_ref.shape[0] - 1

    @pl.when(step == 0)
    def _():
        acc_ref[...] = jnp.zeros_like(acc_ref)

    def one_slot(k, carry):
        slot = step * per_step + k
        target = jnp.clip(acc_index[slot], 0, acc_last)
        picked = jnp.clip(src_index[slot], 0, src_last)
        tile = tiles_ref[k]
        tile = jnp.where(slot < live, tile, jnp.zeros_like(tile))
        block = src_ref[picked]
        if transpose:
            product = lax.dot_general(
                tile, block, (((0,), (0,)), ((), ())), preferred_element_type=jnp.float32
            )
        else:
            product = jnp.dot(tile, block, preferred_element_type=jnp.float32)
        acc_ref[target] += product
        return carry

    lax.fori_loop(0, per_step, one_slot, 0, unroll=UNROLL)

    @pl.when(step == pl.num_programs(0) - 1)
    def _():
        out_ref[...] = acc_ref[...].astype(out_ref.dtype)


def sparse_product(tile_block, acc_index, src_index, live_count, source, segments, transpose):
    slot_total, tile_edge, _ = tile_block.shape
    feat_width = source.shape[2]
    per_step = min(SLOTS_PER_STEP, slot_total)
    steps = slot_total // per_step

    def tile_map(step, acc_ref, src_ref, count_ref):
        last_live = jnp.maximum(count_ref[0] - 1, 0) // per_step
        return (jnp.minimum(step, last_live), 0, 0)

    grid_spec = pltpu.PrefetchScalarGridSpec(
        num_scalar_prefetch=3,
        grid=(steps,),
        in_specs=[
            pl.BlockSpec((per_step, tile_edge, tile_edge), tile_map),
            pl.BlockSpec(source.shape, lambda step, *_: (0, 0, 0)),
        ],
        out_specs=pl.BlockSpec((segments, tile_edge, feat_width), lambda step, *_: (0, 0, 0)),
        scratch_shapes=[pltpu.VMEM((segments, tile_edge, feat_width), jnp.float32)],
    )
    flops = 2 * slot_total * tile_edge * tile_edge * feat_width
    bytes_accessed = (
        tile_block.size * 2 + source.size * 2 + segments * tile_edge * feat_width * 2
    )
    return pl.pallas_call(
        functools.partial(spmm_kernel, transpose),
        out_shape=jax.ShapeDtypeStruct((segments, tile_edge, feat_width), jnp.bfloat16),
        grid_spec=grid_spec,
        compiler_params=pltpu.CompilerParams(
            dimension_semantics=("arbitrary",), vmem_limit_bytes=56 * 1024 * 1024
        ),
        cost_estimate=pl.CostEstimate(
            flops=flops, transcendentals=0, bytes_accessed=bytes_accessed
        ),
    )(acc_index, src_index, live_count, tile_block, source)


def peer_id(axis, other_axis, peer):
    if axis == "row":
        return (peer, lax.axis_index(other_axis))
    return (lax.axis_index(other_axis), peer)


def greet_all(axis, other_axis, n, me):
    barrier = pltpu.get_barrier_semaphore()
    for offset in range(1, n):
        peer = lax.rem(me + offset, n)
        pl.semaphore_signal(
            barrier, 1, device_id=peer_id(axis, other_axis, peer),
            device_id_type=pl.DeviceIdType.MESH,
        )
    pl.semaphore_wait(barrier, n - 1)


def scatter_sum_kernel(axis, other_axis, n, x_hbm, out_ref, recv, send_sems, recv_sems, own_sem):
    me = lax.axis_index(axis)
    greet_all(axis, other_axis, n, me)
    own = pltpu.make_async_copy(x_hbm.at[me], recv.at[me], own_sem)
    own.start()
    sends = []
    for offset in range(1, n):
        peer = lax.rem(me + offset, n)
        copy = pltpu.make_async_remote_copy(
            src_ref=x_hbm.at[peer],
            dst_ref=recv.at[me],
            send_sem=send_sems.at[offset],
            recv_sem=recv_sems.at[me],
            device_id=peer_id(axis, other_axis, peer),
            device_id_type=pl.DeviceIdType.MESH,
        )
        copy.start()
        sends.append(copy)
    own.wait()
    for offset in range(1, n):
        source = lax.rem(me + n - offset, n)
        pltpu.make_async_remote_copy(
            src_ref=x_hbm.at[source],
            dst_ref=recv.at[source],
            send_sem=send_sems.at[offset],
            recv_sem=recv_sems.at[source],
            device_id=peer_id(axis, other_axis, source),
            device_id_type=pl.DeviceIdType.MESH,
        ).wait_recv()
    total = recv[0].astype(jnp.float32)
    for j in range(1, n):
        total = total + recv[j].astype(jnp.float32)
    out_ref[...] = total.astype(out_ref.dtype)
    for copy in sends:
        copy.wait_send()


def scatter_sum(x, axis, other_axis, out_dtype, collective_id):
    n, rows, lanes = x.shape
    return pl.pallas_call(
        functools.partial(scatter_sum_kernel, axis, other_axis, n),
        out_shape=jax.ShapeDtypeStruct((rows, lanes), out_dtype),
        in_specs=[pl.BlockSpec(memory_space=pl.ANY)],
        out_specs=pl.BlockSpec(memory_space=pltpu.VMEM),
        scratch_shapes=[
            pltpu.VMEM((n, rows, lanes), x.dtype),
            pltpu.SemaphoreType.DMA((n,)),
            pltpu.SemaphoreType.DMA((n,)),
            pltpu.SemaphoreType.DMA(()),
        ],
        compiler_params=pltpu.CompilerParams(
            collective_id=collective_id, has_side_effects=True,
            vmem_limit_bytes=48 * 1024 * 1024,
        ),
        cost_estimate=pl.CostEstimate(
            flops=x.size, transcendentals=0, bytes_accessed=3 * x.size * x.dtype.itemsize
        ),
    )(x)


def gather_all_kernel(axis, other_axis, n, x_ref, out_ref, recv, send_sems, recv_sems):
    me = lax.axis_index(axis)
    recv[me] = x_ref[...]
    greet_all(axis, other_axis, n, me)
    sends = []
    for offset in range(1, n):
        peer = lax.rem(me + offset, n)
        copy = pltpu.make_async_remote_copy(
            src_ref=x_ref,
            dst_ref=recv.at[me],
            send_sem=send_sems.at[offset],
            recv_sem=recv_sems.at[me],
            device_id=peer_id(axis, other_axis, peer),
            device_id_type=pl.DeviceIdType.MESH,
        )
        copy.start()
        sends.append(copy)
    for offset in range(1, n):
        source = lax.rem(me + n - offset, n)
        pltpu.make_async_remote_copy(
            src_ref=x_ref,
            dst_ref=recv.at[source],
            send_sem=send_sems.at[offset],
            recv_sem=recv_sems.at[source],
            device_id=peer_id(axis, other_axis, source),
            device_id_type=pl.DeviceIdType.MESH,
        ).wait_recv()
    out_ref[...] = recv[...]
    for copy in sends:
        copy.wait_send()


def gather_all(x, axis, other_axis, n, collective_id):
    rows, lanes = x.shape
    return pl.pallas_call(
        functools.partial(gather_all_kernel, axis, other_axis, n),
        out_shape=jax.ShapeDtypeStruct((n, rows, lanes), x.dtype),
        in_specs=[pl.BlockSpec(memory_space=pltpu.VMEM)],
        out_specs=pl.BlockSpec(memory_space=pltpu.VMEM),
        scratch_shapes=[
            pltpu.VMEM((n, rows, lanes), x.dtype),
            pltpu.SemaphoreType.DMA((n,)),
            pltpu.SemaphoreType.DMA((n,)),
        ],
        compiler_params=pltpu.CompilerParams(
            collective_id=collective_id, has_side_effects=True,
            vmem_limit_bytes=48 * 1024 * 1024,
        ),
        cost_estimate=pl.CostEstimate(
            flops=0, transcendentals=0, bytes_accessed=3 * n * x.size * x.dtype.itemsize
        ),
    )(x)


def torus_peer(y, x, nx):
    return (lax.axis_index("row"), y * nx + x)


def scatter_sum_2d_kernel(nx, ny, x_hbm, out_ref, recv1, mid, recv2, sems):
    send1, got1, send2, got2, own_sems = sems
    me = lax.axis_index("col")
    my_y = me // nx
    my_x = lax.rem(me, nx)
    half = x_hbm.shape[2] // 2
    lower = pl.ds(0, half)
    upper = pl.ds(half, half)
    mesh_kind = pl.DeviceIdType.MESH

    barrier = pltpu.get_barrier_semaphore()
    for offset in range(1, nx):
        pl.semaphore_signal(barrier, 1, device_id=torus_peer(my_y, lax.rem(my_x + offset, nx), nx),
                            device_id_type=mesh_kind)
    for offset in range(1, ny):
        pl.semaphore_signal(barrier, 1, device_id=torus_peer(lax.rem(my_y + offset, ny), my_x, nx),
                            device_id_type=mesh_kind)
    pl.semaphore_wait(barrier, nx + ny - 2)

    own_a = pltpu.make_async_copy(x_hbm.at[:, my_x, lower], recv1.at[0, my_x], own_sems.at[0])
    own_b = pltpu.make_async_copy(x_hbm.at[my_y, :, upper], recv1.at[1, my_y], own_sems.at[1])
    own_a.start()
    own_b.start()
    sends = []
    for offset in range(1, nx):
        peer_x = lax.rem(my_x + offset, nx)
        copy = pltpu.make_async_remote_copy(
            src_ref=x_hbm.at[:, peer_x, lower], dst_ref=recv1.at[0, my_x],
            send_sem=send1.at[0, offset], recv_sem=got1.at[0, my_x],
            device_id=torus_peer(my_y, peer_x, nx), device_id_type=mesh_kind,
        )
        copy.start()
        sends.append(copy)
    for offset in range(1, ny):
        peer_y = lax.rem(my_y + offset, ny)
        copy = pltpu.make_async_remote_copy(
            src_ref=x_hbm.at[peer_y, :, upper], dst_ref=recv1.at[1, my_y],
            send_sem=send1.at[1, offset], recv_sem=got1.at[1, my_y],
            device_id=torus_peer(peer_y, my_x, nx), device_id_type=mesh_kind,
        )
        copy.start()
        sends.append(copy)
    own_a.wait()
    own_b.wait()
    for offset in range(1, nx):
        source_x = lax.rem(my_x + nx - offset, nx)
        pltpu.make_async_remote_copy(
            src_ref=x_hbm.at[:, source_x, lower], dst_ref=recv1.at[0, source_x],
            send_sem=send1.at[0, offset], recv_sem=got1.at[0, source_x],
            device_id=torus_peer(my_y, source_x, nx), device_id_type=mesh_kind,
        ).wait_recv()
    for offset in range(1, ny):
        source_y = lax.rem(my_y + ny - offset, ny)
        pltpu.make_async_remote_copy(
            src_ref=x_hbm.at[source_y, :, upper], dst_ref=recv1.at[1, source_y],
            send_sem=send1.at[1, offset], recv_sem=got1.at[1, source_y],
            device_id=torus_peer(source_y, my_x, nx), device_id_type=mesh_kind,
        ).wait_recv()

    def add_up(stack):
        total = stack[0].astype(jnp.float32)
        for j in range(1, stack.shape[0]):
            total = total + stack[j].astype(jnp.float32)
        return total

    for target in range(ny):
        mid[0, target] = add_up(recv1[0, :, target]).astype(mid.dtype)
    for target in range(nx):
        mid[1, target] = add_up(recv1[1, :, target]).astype(mid.dtype)
    recv2[0, my_y] = mid[0, my_y]
    recv2[1, my_x] = mid[1, my_x]

    for offset in range(1, ny):
        peer_y = lax.rem(my_y + offset, ny)
        copy = pltpu.make_async_remote_copy(
            src_ref=mid.at[0, peer_y], dst_ref=recv2.at[0, my_y],
            send_sem=send2.at[0, offset], recv_sem=got2.at[0, my_y],
            device_id=torus_peer(peer_y, my_x, nx), device_id_type=mesh_kind,
        )
        copy.start()
        sends.append(copy)
    for offset in range(1, nx):
        peer_x = lax.rem(my_x + offset, nx)
        copy = pltpu.make_async_remote_copy(
            src_ref=mid.at[1, peer_x], dst_ref=recv2.at[1, my_x],
            send_sem=send2.at[1, offset], recv_sem=got2.at[1, my_x],
            device_id=torus_peer(my_y, peer_x, nx), device_id_type=mesh_kind,
        )
        copy.start()
        sends.append(copy)
    for offset in range(1, ny):
        source_y = lax.rem(my_y + ny - offset, ny)
        pltpu.make_async_remote_copy(
            src_ref=mid.at[0, source_y], dst_ref=recv2.at[0, source_y],
            send_sem=send2.at[0, offset], recv_sem=got2.at[0, source_y],
            device_id=torus_peer(source_y, my_x, nx), device_id_type=mesh_kind,
        ).wait_recv()
    for offset in range(1, nx):
        source_x = lax.rem(my_x + nx - offset, nx)
        pltpu.make_async_remote_copy(
            src_ref=mid.at[1, source_x], dst_ref=recv2.at[1, source_x],
            send_sem=send2.at[1, offset], recv_sem=got2.at[1, source_x],
            device_id=torus_peer(my_y, source_x, nx), device_id_type=mesh_kind,
        ).wait_recv()
    out_ref[lower] = add_up(recv2[0]).astype(out_ref.dtype)
    out_ref[upper] = add_up(recv2[1]).astype(out_ref.dtype)
    for copy in sends:
        copy.wait_send()


def scatter_sum_2d(x, nx, out_dtype, collective_id):
    n, rows, lanes = x.shape
    ny = n // nx
    half = rows // 2
    side = max(nx, ny)
    return pl.pallas_call(
        functools.partial(scatter_sum_2d_kernel, nx, ny),
        out_shape=jax.ShapeDtypeStruct((rows, lanes), out_dtype),
        in_specs=[pl.BlockSpec(memory_space=pl.ANY)],
        out_specs=pl.BlockSpec(memory_space=pltpu.VMEM),
        scratch_shapes=[
            pltpu.VMEM((2, side, side, half, lanes), x.dtype),
            pltpu.VMEM((2, side, half, lanes), x.dtype),
            pltpu.VMEM((2, side, half, lanes), x.dtype),
            (
                pltpu.SemaphoreType.DMA((2, side)),
                pltpu.SemaphoreType.DMA((2, side)),
                pltpu.SemaphoreType.DMA((2, side)),
                pltpu.SemaphoreType.DMA((2, side)),
                pltpu.SemaphoreType.DMA((2,)),
            ),
        ],
        compiler_params=pltpu.CompilerParams(
            collective_id=collective_id, has_side_effects=True,
            vmem_limit_bytes=48 * 1024 * 1024,
        ),
        cost_estimate=pl.CostEstimate(
            flops=x.size, transcendentals=0, bytes_accessed=3 * x.size * x.dtype.itemsize
        ),
    )(x.reshape(ny, nx, rows, lanes))


def row_peer(index):
    return (index, lax.axis_index("col"))


def greet_row(my_z, my_core, nz):
    barrier = pltpu.get_barrier_semaphore()
    mesh_kind = pl.DeviceIdType.MESH
    pl.semaphore_signal(barrier, 1, device_id=row_peer(my_z * 2 + 1 - my_core), device_id_type=mesh_kind)
    for offset in range(1, nz):
        peer_z = lax.rem(my_z + offset, nz)
        pl.semaphore_signal(barrier, 1, device_id=row_peer(peer_z * 2 + my_core), device_id_type=mesh_kind)
    pl.semaphore_wait(barrier, nz)


def scatter_sum_row_kernel(nz, x_hbm, out_ref, own1, recv1, mid, recv2, sems):
    send1, got1, send2, got2, own_sem = sems
    mesh_kind = pl.DeviceIdType.MESH
    me = lax.axis_index("row")
    my_z = me // 2
    my_core = lax.rem(me, 2)
    other_core = 1 - my_core
    greet_row(my_z, my_core, nz)
    own = pltpu.make_async_copy(x_hbm.at[:, my_core], own1, own_sem.at[0])
    own.start()
    first = pltpu.make_async_remote_copy(
        src_ref=x_hbm.at[:, other_core], dst_ref=recv1,
        send_sem=send1.at[0], recv_sem=got1.at[0],
        device_id=row_peer(my_z * 2 + other_core), device_id_type=mesh_kind,
    )
    first.start()
    own.wait()
    first.wait_recv()
    for target in range(nz):
        mid[target] = (own1[target].astype(jnp.float32) + recv1[target].astype(jnp.float32)).astype(mid.dtype)
    sends = []
    for offset in range(1, nz):
        peer_z = lax.rem(my_z + offset, nz)
        copy = pltpu.make_async_remote_copy(
            src_ref=mid.at[peer_z], dst_ref=recv2.at[my_z],
            send_sem=send2.at[offset], recv_sem=got2.at[my_z],
            device_id=row_peer(peer_z * 2 + my_core), device_id_type=mesh_kind,
        )
        copy.start()
        sends.append(copy)
    total = mid[my_z].astype(jnp.float32)
    for offset in range(1, nz):
        source_z = lax.rem(my_z + nz - offset, nz)
        pltpu.make_async_remote_copy(
            src_ref=mid.at[source_z], dst_ref=recv2.at[source_z],
            send_sem=send2.at[offset], recv_sem=got2.at[source_z],
            device_id=row_peer(source_z * 2 + my_core), device_id_type=mesh_kind,
        ).wait_recv()
        total = total + recv2[source_z].astype(jnp.float32)
    out_ref[...] = total.astype(out_ref.dtype)
    first.wait_send()
    for copy in sends:
        copy.wait_send()


def scatter_sum_row(x, out_dtype, collective_id):
    n, rows, lanes = x.shape
    nz = n // 2
    return pl.pallas_call(
        functools.partial(scatter_sum_row_kernel, nz),
        out_shape=jax.ShapeDtypeStruct((rows, lanes), out_dtype),
        in_specs=[pl.BlockSpec(memory_space=pl.ANY)],
        out_specs=pl.BlockSpec(memory_space=pltpu.VMEM),
        scratch_shapes=[
            pltpu.VMEM((nz, rows, lanes), x.dtype),
            pltpu.VMEM((nz, rows, lanes), x.dtype),
            pltpu.VMEM((nz, rows, lanes), x.dtype),
            pltpu.VMEM((nz, rows, lanes), x.dtype),
            (
                pltpu.SemaphoreType.DMA((1,)),
                pltpu.SemaphoreType.DMA((1,)),
                pltpu.SemaphoreType.DMA((nz,)),
                pltpu.SemaphoreType.DMA((nz,)),
                pltpu.SemaphoreType.DMA((1,)),
            ),
        ],
        compiler_params=pltpu.CompilerParams(
            collective_id=collective_id, has_side_effects=True,
            vmem_limit_bytes=48 * 1024 * 1024,
        ),
        cost_estimate=pl.CostEstimate(
            flops=x.size, transcendentals=0, bytes_accessed=3 * x.size * x.dtype.itemsize
        ),
    )(x.reshape(nz, 2, rows, lanes))


def gather_row_kernel(nz, x_ref, out_ref, full, sems):
    send1, got1, send2, got2, own_sem = sems
    mesh_kind = pl.DeviceIdType.MESH
    me = lax.axis_index("row")
    my_z = me // 2
    my_core = lax.rem(me, 2)
    other_core = 1 - my_core
    greet_row(my_z, my_core, nz)
    own = pltpu.make_async_copy(x_ref, full.at[my_z, my_core], own_sem.at[0])
    own.start()
    sends = []
    for offset in range(1, nz):
        peer_z = lax.rem(my_z + offset, nz)
        copy = pltpu.make_async_remote_copy(
            src_ref=x_ref, dst_ref=full.at[my_z, my_core],
            send_sem=send1.at[offset], recv_sem=got1.at[my_z],
            device_id=row_peer(peer_z * 2 + my_core), device_id_type=mesh_kind,
        )
        copy.start()
        sends.append(copy)
    own.wait()
    for offset in range(1, nz):
        source_z = lax.rem(my_z + nz - offset, nz)
        pltpu.make_async_remote_copy(
            src_ref=x_ref, dst_ref=full.at[source_z, my_core],
            send_sem=send1.at[offset], recv_sem=got1.at[source_z],
            device_id=row_peer(source_z * 2 + my_core), device_id_type=mesh_kind,
        ).wait_recv()
    second = pltpu.make_async_remote_copy(
        src_ref=full.at[:, my_core], dst_ref=full.at[:, my_core],
        send_sem=send2.at[0], recv_sem=got2.at[0],
        device_id=row_peer(my_z * 2 + other_core), device_id_type=mesh_kind,
    )
    second.start()
    pltpu.make_async_remote_copy(
        src_ref=full.at[:, other_core], dst_ref=full.at[:, other_core],
        send_sem=send2.at[0], recv_sem=got2.at[0],
        device_id=row_peer(my_z * 2 + other_core), device_id_type=mesh_kind,
    ).wait_recv()
    for copy in sends:
        copy.wait_send()
    second.wait_send()
    out_ref[...] = full[...]


def gather_row(x, collective_id):
    rows, lanes = x.shape
    nz = lax.axis_size("row") // 2
    out = pl.pallas_call(
        functools.partial(gather_row_kernel, nz),
        out_shape=jax.ShapeDtypeStruct((nz, 2, rows, lanes), x.dtype),
        in_specs=[pl.BlockSpec(memory_space=pltpu.VMEM)],
        out_specs=pl.BlockSpec(memory_space=pltpu.VMEM),
        scratch_shapes=[
            pltpu.VMEM((nz, 2, rows, lanes), x.dtype),
            (
                pltpu.SemaphoreType.DMA((nz,)),
                pltpu.SemaphoreType.DMA((nz,)),
                pltpu.SemaphoreType.DMA((1,)),
                pltpu.SemaphoreType.DMA((1,)),
                pltpu.SemaphoreType.DMA((1,)),
            ),
        ],
        compiler_params=pltpu.CompilerParams(
            collective_id=collective_id, has_side_effects=True,
            vmem_limit_bytes=48 * 1024 * 1024,
        ),
        cost_estimate=pl.CostEstimate(
            flops=0, transcendentals=0, bytes_accessed=3 * 2 * nz * x.size * x.dtype.itemsize
        ),
    )(x)
    return out.reshape(2 * nz * rows, lanes)


def gather_all_2d_kernel(nx, ny, x_ref, out_ref, full, sems):
    send, got, own_sem = sems
    mesh_kind = pl.DeviceIdType.MESH
    me = lax.axis_index("col")
    my_y = me // nx
    my_x = lax.rem(me, nx)
    half = x_ref.shape[0] // 2
    lower = pl.ds(0, half)
    upper = pl.ds(half, half)

    barrier = pltpu.get_barrier_semaphore()
    for offset in range(1, nx):
        pl.semaphore_signal(barrier, 1, device_id=torus_peer(my_y, lax.rem(my_x + offset, nx), nx),
                            device_id_type=mesh_kind)
    for offset in range(1, ny):
        pl.semaphore_signal(barrier, 1, device_id=torus_peer(lax.rem(my_y + offset, ny), my_x, nx),
                            device_id_type=mesh_kind)
    pl.semaphore_wait(barrier, nx + ny - 2)

    own = pltpu.make_async_copy(x_ref, full.at[my_y, my_x], own_sem.at[0])
    own.start()
    sends = []
    for offset in range(1, nx):
        peer_x = lax.rem(my_x + offset, nx)
        copy = pltpu.make_async_remote_copy(
            src_ref=x_ref.at[lower], dst_ref=full.at[my_y, my_x, lower],
            send_sem=send.at[0, offset], recv_sem=got.at[0, my_x],
            device_id=torus_peer(my_y, peer_x, nx), device_id_type=mesh_kind,
        )
        copy.start()
        sends.append(copy)
    for offset in range(1, ny):
        peer_y = lax.rem(my_y + offset, ny)
        copy = pltpu.make_async_remote_copy(
            src_ref=x_ref.at[upper], dst_ref=full.at[my_y, my_x, upper],
            send_sem=send.at[1, offset], recv_sem=got.at[1, my_y],
            device_id=torus_peer(peer_y, my_x, nx), device_id_type=mesh_kind,
        )
        copy.start()
        sends.append(copy)
    own.wait()
    for offset in range(1, nx):
        source_x = lax.rem(my_x + nx - offset, nx)
        pltpu.make_async_remote_copy(
            src_ref=x_ref.at[lower], dst_ref=full.at[my_y, source_x, lower],
            send_sem=send.at[0, offset], recv_sem=got.at[0, source_x],
            device_id=torus_peer(my_y, source_x, nx), device_id_type=mesh_kind,
        ).wait_recv()
    for offset in range(1, ny):
        peer_y = lax.rem(my_y + offset, ny)
        copy = pltpu.make_async_remote_copy(
            src_ref=full.at[my_y, :, lower], dst_ref=full.at[my_y, :, lower],
            send_sem=send.at[2, offset], recv_sem=got.at[2, my_y],
            device_id=torus_peer(peer_y, my_x, nx), device_id_type=mesh_kind,
        )
        copy.start()
        sends.append(copy)
    for offset in range(1, ny):
        source_y = lax.rem(my_y + ny - offset, ny)
        pltpu.make_async_remote_copy(
            src_ref=x_ref.at[upper], dst_ref=full.at[source_y, my_x, upper],
            send_sem=send.at[1, offset], recv_sem=got.at[1, source_y],
            device_id=torus_peer(source_y, my_x, nx), device_id_type=mesh_kind,
        ).wait_recv()
    for offset in range(1, nx):
        peer_x = lax.rem(my_x + offset, nx)
        copy = pltpu.make_async_remote_copy(
            src_ref=full.at[:, my_x, upper], dst_ref=full.at[:, my_x, upper],
            send_sem=send.at[3, offset], recv_sem=got.at[3, my_x],
            device_id=torus_peer(my_y, peer_x, nx), device_id_type=mesh_kind,
        )
        copy.start()
        sends.append(copy)
    for offset in range(1, ny):
        source_y = lax.rem(my_y + ny - offset, ny)
        pltpu.make_async_remote_copy(
            src_ref=full.at[source_y, :, lower], dst_ref=full.at[source_y, :, lower],
            send_sem=send.at[2, offset], recv_sem=got.at[2, source_y],
            device_id=torus_peer(source_y, my_x, nx), device_id_type=mesh_kind,
        ).wait_recv()
    for offset in range(1, nx):
        source_x = lax.rem(my_x + nx - offset, nx)
        pltpu.make_async_remote_copy(
            src_ref=full.at[:, source_x, upper], dst_ref=full.at[:, source_x, upper],
            send_sem=send.at[3, offset], recv_sem=got.at[3, source_x],
            device_id=torus_peer(my_y, source_x, nx), device_id_type=mesh_kind,
        ).wait_recv()
    for copy in sends:
        copy.wait_send()
    out_ref[...] = full[...]


def gather_all_2d(x, nx, collective_id):
    rows, lanes = x.shape
    n = lax.axis_size("col")
    ny = n // nx
    side = max(nx, ny)
    out = pl.pallas_call(
        functools.partial(gather_all_2d_kernel, nx, ny),
        out_shape=jax.ShapeDtypeStruct((ny, nx, rows, lanes), x.dtype),
        in_specs=[pl.BlockSpec(memory_space=pltpu.VMEM)],
        out_specs=pl.BlockSpec(memory_space=pltpu.VMEM),
        scratch_shapes=[
            pltpu.VMEM((ny, nx, rows, lanes), x.dtype),
            (
                pltpu.SemaphoreType.DMA((4, side)),
                pltpu.SemaphoreType.DMA((4, side)),
                pltpu.SemaphoreType.DMA((1,)),
            ),
        ],
        compiler_params=pltpu.CompilerParams(
            collective_id=collective_id, has_side_effects=True,
            vmem_limit_bytes=48 * 1024 * 1024,
        ),
        cost_estimate=pl.CostEstimate(
            flops=0, transcendentals=0, bytes_accessed=3 * n * x.size * x.dtype.itemsize
        ),
    )(x)
    return out.reshape(n, rows, lanes)


def all_sum(local, collective_base):
    row_count = lax.axis_size("row")
    col_count = lax.axis_size("col")
    height, width = local.shape
    by_col = scatter_sum(
        local.reshape(col_count, height // col_count, width), "col", "row", jnp.float32,
        collective_base,
    )
    part = height // col_count
    by_row = scatter_sum(
        by_col.reshape(row_count, part // row_count, width), "row", "col", jnp.float32,
        collective_base + 1,
    )
    back_row = gather_all(by_row, "row", "col", row_count, collective_base + 2)
    back_col = gather_all(back_row.reshape(part, width), "col", "row", col_count, collective_base + 3)
    return back_col.reshape(height, width)


def activation(aggregated, weight, cot_rows):
    hidden = jnp.dot(aggregated, weight, preferred_element_type=jnp.float32)
    sigmoid_value = jax.nn.sigmoid(hidden)
    output = (hidden * sigmoid_value).astype(jnp.bfloat16)
    silu_slope = sigmoid_value * (1.0 + hidden * (1.0 - sigmoid_value))
    hidden_grad = (cot_rows.astype(jnp.float32) * silu_slope).astype(jnp.bfloat16)
    return (output, hidden_grad)


def per_device(tile_values, tile_rows, tile_cols, tile_count, features, weight, cotangent):
    slot_total = tile_values.shape[2]
    tile_edge = tile_values.shape[3]
    tile_block = tile_values.reshape(slot_total, tile_edge, tile_edge)
    row_index = tile_rows.reshape(slot_total)
    col_index = tile_cols.reshape(slot_total)
    live_count = tile_count.reshape(1)
    own_rows = features.shape[0]
    feat_width = features.shape[1]
    row_count = lax.axis_size("row")
    col_count = lax.axis_size("col")
    row_tiles = col_count * own_rows // tile_edge
    col_tiles = row_count * own_rows // tile_edge
    column_block = gather_row(features, 8)
    source = column_block.reshape(col_tiles, tile_edge, feat_width)
    partial_rows = sparse_product(
        tile_block, row_index, col_index, live_count, source, row_tiles, False
    )
    partial_flat = partial_rows.reshape(row_tiles * tile_edge, feat_width)
    node_total = row_count * col_count * own_rows
    aggregated = scatter_sum_2d(
        partial_rows.reshape(col_count, own_rows, feat_width), TORUS_X, jnp.bfloat16, 0
    )
    output, hidden_grad = activation(aggregated, weight, cotangent)
    own_grad = lax.dot_general(
        hidden_grad, weight, (((1,), (1,)), ((), ())), preferred_element_type=jnp.float32
    ).astype(jnp.bfloat16)
    row_block = gather_all_2d(own_grad, TORUS_X, 7)
    local_grad = lax.dot_general(
        aggregated, hidden_grad, (((0,), (0,)), ((), ())), preferred_element_type=jnp.float32
    )
    weight_grad = lax.psum(local_grad, ("row", "col")) * (1.0 / math.sqrt(node_total))
    source_back = row_block.reshape(row_tiles, tile_edge, feat_width)
    partial_cols = sparse_product(
        tile_block, col_index, row_index, live_count, source_back, col_tiles, True
    )
    input_grad = scatter_sum_row(
        partial_cols.reshape(row_count, own_rows, feat_width), jnp.float32, 9
    )
    return (output, weight_grad, input_grad)


def solution(mesh):
    placed = (
        P("row", "col", None, None, None),
        P("row", "col", None),
        P("row", "col", None),
        P("row", "col"),
        P(("row", "col"), None),
        P(),
        P(("row", "col"), None),
    )
    return jax.shard_map(
        per_device,
        mesh=mesh,
        in_specs=placed,
        out_specs=(P(("row", "col"), None), P(), P(("row", "col"), None)),
        check_vma=False,
    )
```

```python
import functools
import math

import jax
import jax.numpy as jnp
from jax import lax
from jax.experimental import pallas as pl
from jax.experimental.pallas import tpu as pltpu
from jax.sharding import PartitionSpec as P

SLOTS_PER_STEP = 32
UNROLL = 32
TORUS_X = 4


def spmm_kernel(transpose, acc_index, src_index, count_ref, tiles_ref, src_ref, out_ref, acc_ref):
    step = pl.program_id(0)
    per_step = tiles_ref.shape[0]
    live = count_ref[0]
    acc_last = acc_ref.shape[0] - 1
    src_last = src_ref.shape[0] - 1

    @pl.when(step == 0)
    def _():
        acc_ref[...] = jnp.zeros_like(acc_ref)

    def one_slot(k, carry):
        slot = step * per_step + k
        target = jnp.clip(acc_index[slot], 0, acc_last)
        picked = jnp.clip(src_index[slot], 0, src_last)
        tile = tiles_ref[k]
        tile = jnp.where(slot < live, tile, jnp.zeros_like(tile))
        block = src_ref[picked]
        if transpose:
            product = lax.dot_general(
                tile, block, (((0,), (0,)), ((), ())), preferred_element_type=jnp.float32
            )
        else:
            product = jnp.dot(tile, block, preferred_element_type=jnp.float32)
        acc_ref[target] += product
        return carry

    lax.fori_loop(0, per_step, one_slot, 0, unroll=UNROLL)

    @pl.when(step == pl.num_programs(0) - 1)
    def _():
        out_ref[...] = acc_ref[...].astype(out_ref.dtype)


def sparse_product(tile_block, acc_index, src_index, live_count, source, segments, transpose):
    slot_total, tile_edge, _ = tile_block.shape
    feat_width = source.shape[2]
    per_step = min(SLOTS_PER_STEP, slot_total)
    steps = slot_total // per_step

    def tile_map(step, acc_ref, src_ref, count_ref):
        last_live = jnp.maximum(count_ref[0] - 1, 0) // per_step
        return (jnp.minimum(step, last_live), 0, 0)

    grid_spec = pltpu.PrefetchScalarGridSpec(
        num_scalar_prefetch=3,
        grid=(steps,),
        in_specs=[
            pl.BlockSpec((per_step, tile_edge, tile_edge), tile_map),
            pl.BlockSpec(source.shape, lambda step, *_: (0, 0, 0)),
        ],
        out_specs=pl.BlockSpec((segments, tile_edge, feat_width), lambda step, *_: (0, 0, 0)),
        scratch_shapes=[pltpu.VMEM((segments, tile_edge, feat_width), jnp.float32)],
    )
    flops = 2 * slot_total * tile_edge * tile_edge * feat_width
    bytes_accessed = (
        tile_block.size * 2 + source.size * 2 + segments * tile_edge * feat_width * 2
    )
    return pl.pallas_call(
        functools.partial(spmm_kernel, transpose),
        out_shape=jax.ShapeDtypeStruct((segments, tile_edge, feat_width), jnp.bfloat16),
        grid_spec=grid_spec,
        compiler_params=pltpu.CompilerParams(
            dimension_semantics=("arbitrary",), vmem_limit_bytes=56 * 1024 * 1024
        ),
        cost_estimate=pl.CostEstimate(
            flops=flops, transcendentals=0, bytes_accessed=bytes_accessed
        ),
    )(acc_index, src_index, live_count, tile_block, source)


def peer_id(axis, other_axis, peer):
    if axis == "row":
        return (peer, lax.axis_index(other_axis))
    return (lax.axis_index(other_axis), peer)


def greet_all(axis, other_axis, n, me):
    barrier = pltpu.get_barrier_semaphore()
    for offset in range(1, n):
        peer = lax.rem(me + offset, n)
        pl.semaphore_signal(
            barrier, 1, device_id=peer_id(axis, other_axis, peer),
            device_id_type=pl.DeviceIdType.MESH,
        )
    pl.semaphore_wait(barrier, n - 1)


def scatter_sum_kernel(axis, other_axis, n, x_hbm, out_ref, recv, send_sems, recv_sems, own_sem):
    me = lax.axis_index(axis)
    greet_all(axis, other_axis, n, me)
    own = pltpu.make_async_copy(x_hbm.at[me], recv.at[me], own_sem)
    own.start()
    sends = []
    for offset in range(1, n):
        peer = lax.rem(me + offset, n)
        copy = pltpu.make_async_remote_copy(
            src_ref=x_hbm.at[peer],
            dst_ref=recv.at[me],
            send_sem=send_sems.at[offset],
            recv_sem=recv_sems.at[me],
            device_id=peer_id(axis, other_axis, peer),
            device_id_type=pl.DeviceIdType.MESH,
        )
        copy.start()
        sends.append(copy)
    own.wait()
    for offset in range(1, n):
        source = lax.rem(me + n - offset, n)
        pltpu.make_async_remote_copy(
            src_ref=x_hbm.at[source],
            dst_ref=recv.at[source],
            send_sem=send_sems.at[offset],
            recv_sem=recv_sems.at[source],
            device_id=peer_id(axis, other_axis, source),
            device_id_type=pl.DeviceIdType.MESH,
        ).wait_recv()
    total = recv[0].astype(jnp.float32)
    for j in range(1, n):
        total = total + recv[j].astype(jnp.float32)
    out_ref[...] = total.astype(out_ref.dtype)
    for copy in sends:
        copy.wait_send()


def scatter_sum(x, axis, other_axis, out_dtype, collective_id):
    n, rows, lanes = x.shape
    return pl.pallas_call(
        functools.partial(scatter_sum_kernel, axis, other_axis, n),
        out_shape=jax.ShapeDtypeStruct((rows, lanes), out_dtype),
        in_specs=[pl.BlockSpec(memory_space=pl.ANY)],
        out_specs=pl.BlockSpec(memory_space=pltpu.VMEM),
        scratch_shapes=[
            pltpu.VMEM((n, rows, lanes), x.dtype),
            pltpu.SemaphoreType.DMA((n,)),
            pltpu.SemaphoreType.DMA((n,)),
            pltpu.SemaphoreType.DMA(()),
        ],
        compiler_params=pltpu.CompilerParams(
            collective_id=collective_id, has_side_effects=True,
            vmem_limit_bytes=48 * 1024 * 1024,
        ),
        cost_estimate=pl.CostEstimate(
            flops=x.size, transcendentals=0, bytes_accessed=3 * x.size * x.dtype.itemsize
        ),
    )(x)


def gather_all_kernel(axis, other_axis, n, x_ref, out_ref, recv, send_sems, recv_sems):
    me = lax.axis_index(axis)
    recv[me] = x_ref[...]
    greet_all(axis, other_axis, n, me)
    sends = []
    for offset in range(1, n):
        peer = lax.rem(me + offset, n)
        copy = pltpu.make_async_remote_copy(
            src_ref=x_ref,
            dst_ref=recv.at[me],
            send_sem=send_sems.at[offset],
            recv_sem=recv_sems.at[me],
            device_id=peer_id(axis, other_axis, peer),
            device_id_type=pl.DeviceIdType.MESH,
        )
        copy.start()
        sends.append(copy)
    for offset in range(1, n):
        source = lax.rem(me + n - offset, n)
        pltpu.make_async_remote_copy(
            src_ref=x_ref,
            dst_ref=recv.at[source],
            send_sem=send_sems.at[offset],
            recv_sem=recv_sems.at[source],
            device_id=peer_id(axis, other_axis, source),
            device_id_type=pl.DeviceIdType.MESH,
        ).wait_recv()
    out_ref[...] = recv[...]
    for copy in sends:
        copy.wait_send()


def gather_all(x, axis, other_axis, n, collective_id):
    rows, lanes = x.shape
    return pl.pallas_call(
        functools.partial(gather_all_kernel, axis, other_axis, n),
        out_shape=jax.ShapeDtypeStruct((n, rows, lanes), x.dtype),
        in_specs=[pl.BlockSpec(memory_space=pltpu.VMEM)],
        out_specs=pl.BlockSpec(memory_space=pltpu.VMEM),
        scratch_shapes=[
            pltpu.VMEM((n, rows, lanes), x.dtype),
            pltpu.SemaphoreType.DMA((n,)),
            pltpu.SemaphoreType.DMA((n,)),
        ],
        compiler_params=pltpu.CompilerParams(
            collective_id=collective_id, has_side_effects=True,
            vmem_limit_bytes=48 * 1024 * 1024,
        ),
        cost_estimate=pl.CostEstimate(
            flops=0, transcendentals=0, bytes_accessed=3 * n * x.size * x.dtype.itemsize
        ),
    )(x)


def torus_peer(y, x, nx):
    return (lax.axis_index("row"), y * nx + x)


def scatter_sum_2d_kernel(nx, ny, x_hbm, out_ref, recv1, mid, recv2, sems):
    send1, got1, send2, got2, own_sems = sems
    me = lax.axis_index("col")
    my_y = me // nx
    my_x = lax.rem(me, nx)
    half = x_hbm.shape[2] // 2
    lower = pl.ds(0, half)
    upper = pl.ds(half, half)
    mesh_kind = pl.DeviceIdType.MESH

    barrier = pltpu.get_barrier_semaphore()
    for offset in range(1, nx):
        pl.semaphore_signal(barrier, 1, device_id=torus_peer(my_y, lax.rem(my_x + offset, nx), nx),
                            device_id_type=mesh_kind)
    for offset in range(1, ny):
        pl.semaphore_signal(barrier, 1, device_id=torus_peer(lax.rem(my_y + offset, ny), my_x, nx),
                            device_id_type=mesh_kind)
    pl.semaphore_wait(barrier, nx + ny - 2)

    own_a = pltpu.make_async_copy(x_hbm.at[:, my_x, lower], recv1.at[0, my_x], own_sems.at[0])
    own_b = pltpu.make_async_copy(x_hbm.at[my_y, :, upper], recv1.at[1, my_y], own_sems.at[1])
    own_a.start()
    own_b.start()
    sends = []
    for offset in range(1, nx):
        peer_x = lax.rem(my_x + offset, nx)
        copy = pltpu.make_async_remote_copy(
            src_ref=x_hbm.at[:, peer_x, lower], dst_ref=recv1.at[0, my_x],
            send_sem=send1.at[0, offset], recv_sem=got1.at[0, my_x],
            device_id=torus_peer(my_y, peer_x, nx), device_id_type=mesh_kind,
        )
        copy.start()
        sends.append(copy)
    for offset in range(1, ny):
        peer_y = lax.rem(my_y + offset, ny)
        copy = pltpu.make_async_remote_copy(
            src_ref=x_hbm.at[peer_y, :, upper], dst_ref=recv1.at[1, my_y],
            send_sem=send1.at[1, offset], recv_sem=got1.at[1, my_y],
            device_id=torus_peer(peer_y, my_x, nx), device_id_type=mesh_kind,
        )
        copy.start()
        sends.append(copy)
    own_a.wait()
    own_b.wait()
    for offset in range(1, nx):
        source_x = lax.rem(my_x + nx - offset, nx)
        pltpu.make_async_remote_copy(
            src_ref=x_hbm.at[:, source_x, lower], dst_ref=recv1.at[0, source_x],
            send_sem=send1.at[0, offset], recv_sem=got1.at[0, source_x],
            device_id=torus_peer(my_y, source_x, nx), device_id_type=mesh_kind,
        ).wait_recv()
    for offset in range(1, ny):
        source_y = lax.rem(my_y + ny - offset, ny)
        pltpu.make_async_remote_copy(
            src_ref=x_hbm.at[source_y, :, upper], dst_ref=recv1.at[1, source_y],
            send_sem=send1.at[1, offset], recv_sem=got1.at[1, source_y],
            device_id=torus_peer(source_y, my_x, nx), device_id_type=mesh_kind,
        ).wait_recv()

    def add_up(stack):
        total = stack[0].astype(jnp.float32)
        for j in range(1, stack.shape[0]):
            total = total + stack[j].astype(jnp.float32)
        return total

    for target in range(ny):
        mid[0, target] = add_up(recv1[0, :, target]).astype(mid.dtype)
    for target in range(nx):
        mid[1, target] = add_up(recv1[1, :, target]).astype(mid.dtype)
    recv2[0, my_y] = mid[0, my_y]
    recv2[1, my_x] = mid[1, my_x]

    for offset in range(1, ny):
        peer_y = lax.rem(my_y + offset, ny)
        copy = pltpu.make_async_remote_copy(
            src_ref=mid.at[0, peer_y], dst_ref=recv2.at[0, my_y],
            send_sem=send2.at[0, offset], recv_sem=got2.at[0, my_y],
            device_id=torus_peer(peer_y, my_x, nx), device_id_type=mesh_kind,
        )
        copy.start()
        sends.append(copy)
    for offset in range(1, nx):
        peer_x = lax.rem(my_x + offset, nx)
        copy = pltpu.make_async_remote_copy(
            src_ref=mid.at[1, peer_x], dst_ref=recv2.at[1, my_x],
            send_sem=send2.at[1, offset], recv_sem=got2.at[1, my_x],
            device_id=torus_peer(my_y, peer_x, nx), device_id_type=mesh_kind,
        )
        copy.start()
        sends.append(copy)
    for offset in range(1, ny):
        source_y = lax.rem(my_y + ny - offset, ny)
        pltpu.make_async_remote_copy(
            src_ref=mid.at[0, source_y], dst_ref=recv2.at[0, source_y],
            send_sem=send2.at[0, offset], recv_sem=got2.at[0, source_y],
            device_id=torus_peer(source_y, my_x, nx), device_id_type=mesh_kind,
        ).wait_recv()
    for offset in range(1, nx):
        source_x = lax.rem(my_x + nx - offset, nx)
        pltpu.make_async_remote_copy(
            src_ref=mid.at[1, source_x], dst_ref=recv2.at[1, source_x],
            send_sem=send2.at[1, offset], recv_sem=got2.at[1, source_x],
            device_id=torus_peer(my_y, source_x, nx), device_id_type=mesh_kind,
        ).wait_recv()
    out_ref[lower] = add_up(recv2[0]).astype(out_ref.dtype)
    out_ref[upper] = add_up(recv2[1]).astype(out_ref.dtype)
    for copy in sends:
        copy.wait_send()


def scatter_sum_2d(x, nx, out_dtype, collective_id):
    n, rows, lanes = x.shape
    ny = n // nx
    half = rows // 2
    side = max(nx, ny)
    return pl.pallas_call(
        functools.partial(scatter_sum_2d_kernel, nx, ny),
        out_shape=jax.ShapeDtypeStruct((rows, lanes), out_dtype),
        in_specs=[pl.BlockSpec(memory_space=pl.ANY)],
        out_specs=pl.BlockSpec(memory_space=pltpu.VMEM),
        scratch_shapes=[
            pltpu.VMEM((2, side, side, half, lanes), x.dtype),
            pltpu.VMEM((2, side, half, lanes), x.dtype),
            pltpu.VMEM((2, side, half, lanes), x.dtype),
            (
                pltpu.SemaphoreType.DMA((2, side)),
                pltpu.SemaphoreType.DMA((2, side)),
                pltpu.SemaphoreType.DMA((2, side)),
                pltpu.SemaphoreType.DMA((2, side)),
                pltpu.SemaphoreType.DMA((2,)),
            ),
        ],
        compiler_params=pltpu.CompilerParams(
            collective_id=collective_id, has_side_effects=True,
            vmem_limit_bytes=48 * 1024 * 1024,
        ),
        cost_estimate=pl.CostEstimate(
            flops=x.size, transcendentals=0, bytes_accessed=3 * x.size * x.dtype.itemsize
        ),
    )(x.reshape(ny, nx, rows, lanes))


def row_peer(index):
    return (index, lax.axis_index("col"))


def greet_row(my_z, my_core, nz):
    barrier = pltpu.get_barrier_semaphore()
    mesh_kind = pl.DeviceIdType.MESH
    pl.semaphore_signal(barrier, 1, device_id=row_peer(my_z * 2 + 1 - my_core), device_id_type=mesh_kind)
    for offset in range(1, nz):
        peer_z = lax.rem(my_z + offset, nz)
        pl.semaphore_signal(barrier, 1, device_id=row_peer(peer_z * 2 + my_core), device_id_type=mesh_kind)
    pl.semaphore_wait(barrier, nz)


def scatter_sum_row_kernel(nz, x_hbm, out_ref, own1, recv1, mid, recv2, sems):
    send1, got1, send2, got2, own_sem = sems
    mesh_kind = pl.DeviceIdType.MESH
    me = lax.axis_index("row")
    my_z = me // 2
    my_core = lax.rem(me, 2)
    other_core = 1 - my_core
    greet_row(my_z, my_core, nz)
    own = pltpu.make_async_copy(x_hbm.at[:, my_core], own1, own_sem.at[0])
    own.start()
    first = pltpu.make_async_remote_copy(
        src_ref=x_hbm.at[:, other_core], dst_ref=recv1,
        send_sem=send1.at[0], recv_sem=got1.at[0],
        device_id=row_peer(my_z * 2 + other_core), device_id_type=mesh_kind,
    )
    first.start()
    own.wait()
    first.wait_recv()
    for target in range(nz):
        mid[target] = (own1[target].astype(jnp.float32) + recv1[target].astype(jnp.float32)).astype(mid.dtype)
    sends = []
    for offset in range(1, nz):
        peer_z = lax.rem(my_z + offset, nz)
        copy = pltpu.make_async_remote_copy(
            src_ref=mid.at[peer_z], dst_ref=recv2.at[my_z],
            send_sem=send2.at[offset], recv_sem=got2.at[my_z],
            device_id=row_peer(peer_z * 2 + my_core), device_id_type=mesh_kind,
        )
        copy.start()
        sends.append(copy)
    total = mid[my_z].astype(jnp.float32)
    for offset in range(1, nz):
        source_z = lax.rem(my_z + nz - offset, nz)
        pltpu.make_async_remote_copy(
            src_ref=mid.at[source_z], dst_ref=recv2.at[source_z],
            send_sem=send2.at[offset], recv_sem=got2.at[source_z],
            device_id=row_peer(source_z * 2 + my_core), device_id_type=mesh_kind,
        ).wait_recv()
        total = total + recv2[source_z].astype(jnp.float32)
    out_ref[...] = total.astype(out_ref.dtype)
    first.wait_send()
    for copy in sends:
        copy.wait_send()


def scatter_sum_row(x, out_dtype, collective_id):
    n, rows, lanes = x.shape
    nz = n // 2
    return pl.pallas_call(
        functools.partial(scatter_sum_row_kernel, nz),
        out_shape=jax.ShapeDtypeStruct((rows, lanes), out_dtype),
        in_specs=[pl.BlockSpec(memory_space=pl.ANY)],
        out_specs=pl.BlockSpec(memory_space=pltpu.VMEM),
        scratch_shapes=[
            pltpu.VMEM((nz, rows, lanes), x.dtype),
            pltpu.VMEM((nz, rows, lanes), x.dtype),
            pltpu.VMEM((nz, rows, lanes), x.dtype),
            pltpu.VMEM((nz, rows, lanes), x.dtype),
            (
                pltpu.SemaphoreType.DMA((1,)),
                pltpu.SemaphoreType.DMA((1,)),
                pltpu.SemaphoreType.DMA((nz,)),
                pltpu.SemaphoreType.DMA((nz,)),
                pltpu.SemaphoreType.DMA((1,)),
            ),
        ],
        compiler_params=pltpu.CompilerParams(
            collective_id=collective_id, has_side_effects=True,
            vmem_limit_bytes=48 * 1024 * 1024,
        ),
        cost_estimate=pl.CostEstimate(
            flops=x.size, transcendentals=0, bytes_accessed=3 * x.size * x.dtype.itemsize
        ),
    )(x.reshape(nz, 2, rows, lanes))


def gather_row_kernel(nz, x_ref, out_ref, full, sems):
    send1, got1, send2, got2, own_sem = sems
    mesh_kind = pl.DeviceIdType.MESH
    me = lax.axis_index("row")
    my_z = me // 2
    my_core = lax.rem(me, 2)
    other_core = 1 - my_core
    greet_row(my_z, my_core, nz)
    own = pltpu.make_async_copy(x_ref, full.at[my_z, my_core], own_sem.at[0])
    own.start()
    sends = []
    for offset in range(1, nz):
        peer_z = lax.rem(my_z + offset, nz)
        copy = pltpu.make_async_remote_copy(
            src_ref=x_ref, dst_ref=full.at[my_z, my_core],
            send_sem=send1.at[offset], recv_sem=got1.at[my_z],
            device_id=row_peer(peer_z * 2 + my_core), device_id_type=mesh_kind,
        )
        copy.start()
        sends.append(copy)
    own.wait()
    for offset in range(1, nz):
        source_z = lax.rem(my_z + nz - offset, nz)
        pltpu.make_async_remote_copy(
            src_ref=x_ref, dst_ref=full.at[source_z, my_core],
            send_sem=send1.at[offset], recv_sem=got1.at[source_z],
            device_id=row_peer(source_z * 2 + my_core), device_id_type=mesh_kind,
        ).wait_recv()
    second = pltpu.make_async_remote_copy(
        src_ref=full.at[:, my_core], dst_ref=full.at[:, my_core],
        send_sem=send2.at[0], recv_sem=got2.at[0],
        device_id=row_peer(my_z * 2 + other_core), device_id_type=mesh_kind,
    )
    second.start()
    pltpu.make_async_remote_copy(
        src_ref=full.at[:, other_core], dst_ref=full.at[:, other_core],
        send_sem=send2.at[0], recv_sem=got2.at[0],
        device_id=row_peer(my_z * 2 + other_core), device_id_type=mesh_kind,
    ).wait_recv()
    for copy in sends:
        copy.wait_send()
    second.wait_send()
    out_ref[...] = full[...]


def gather_row(x, collective_id):
    rows, lanes = x.shape
    nz = lax.axis_size("row") // 2
    out = pl.pallas_call(
        functools.partial(gather_row_kernel, nz),
        out_shape=jax.ShapeDtypeStruct((nz, 2, rows, lanes), x.dtype),
        in_specs=[pl.BlockSpec(memory_space=pltpu.VMEM)],
        out_specs=pl.BlockSpec(memory_space=pltpu.VMEM),
        scratch_shapes=[
            pltpu.VMEM((nz, 2, rows, lanes), x.dtype),
            (
                pltpu.SemaphoreType.DMA((nz,)),
                pltpu.SemaphoreType.DMA((nz,)),
                pltpu.SemaphoreType.DMA((1,)),
                pltpu.SemaphoreType.DMA((1,)),
                pltpu.SemaphoreType.DMA((1,)),
            ),
        ],
        compiler_params=pltpu.CompilerParams(
            collective_id=collective_id, has_side_effects=True,
            vmem_limit_bytes=48 * 1024 * 1024,
        ),
        cost_estimate=pl.CostEstimate(
            flops=0, transcendentals=0, bytes_accessed=3 * 2 * nz * x.size * x.dtype.itemsize
        ),
    )(x)
    return out.reshape(2 * nz * rows, lanes)


def gather_all_2d_kernel(nx, ny, x_ref, out_ref, full, sems):
    send, got, own_sem = sems
    mesh_kind = pl.DeviceIdType.MESH
    me = lax.axis_index("col")
    my_y = me // nx
    my_x = lax.rem(me, nx)
    half = x_ref.shape[0] // 2
    lower = pl.ds(0, half)
    upper = pl.ds(half, half)

    barrier = pltpu.get_barrier_semaphore()
    for offset in range(1, nx):
        pl.semaphore_signal(barrier, 1, device_id=torus_peer(my_y, lax.rem(my_x + offset, nx), nx),
                            device_id_type=mesh_kind)
    for offset in range(1, ny):
        pl.semaphore_signal(barrier, 1, device_id=torus_peer(lax.rem(my_y + offset, ny), my_x, nx),
                            device_id_type=mesh_kind)
    pl.semaphore_wait(barrier, nx + ny - 2)

    own = pltpu.make_async_copy(x_ref, full.at[my_y, my_x], own_sem.at[0])
    own.start()
    sends = []
    for offset in range(1, nx):
        peer_x = lax.rem(my_x + offset, nx)
        copy = pltpu.make_async_remote_copy(
            src_ref=x_ref.at[lower], dst_ref=full.at[my_y, my_x, lower],
            send_sem=send.at[0, offset], recv_sem=got.at[0, my_x],
            device_id=torus_peer(my_y, peer_x, nx), device_id_type=mesh_kind,
        )
        copy.start()
        sends.append(copy)
    for offset in range(1, ny):
        peer_y = lax.rem(my_y + offset, ny)
        copy = pltpu.make_async_remote_copy(
            src_ref=x_ref.at[upper], dst_ref=full.at[my_y, my_x, upper],
            send_sem=send.at[1, offset], recv_sem=got.at[1, my_y],
            device_id=torus_peer(peer_y, my_x, nx), device_id_type=mesh_kind,
        )
        copy.start()
        sends.append(copy)
    own.wait()
    for offset in range(1, nx):
        source_x = lax.rem(my_x + nx - offset, nx)
        pltpu.make_async_remote_copy(
            src_ref=x_ref.at[lower], dst_ref=full.at[my_y, source_x, lower],
            send_sem=send.at[0, offset], recv_sem=got.at[0, source_x],
            device_id=torus_peer(my_y, source_x, nx), device_id_type=mesh_kind,
        ).wait_recv()
    for offset in range(1, ny):
        peer_y = lax.rem(my_y + offset, ny)
        copy = pltpu.make_async_remote_copy(
            src_ref=full.at[my_y, :, lower], dst_ref=full.at[my_y, :, lower],
            send_sem=send.at[2, offset], recv_sem=got.at[2, my_y],
            device_id=torus_peer(peer_y, my_x, nx), device_id_type=mesh_kind,
        )
        copy.start()
        sends.append(copy)
    for offset in range(1, ny):
        source_y = lax.rem(my_y + ny - offset, ny)
        pltpu.make_async_remote_copy(
            src_ref=x_ref.at[upper], dst_ref=full.at[source_y, my_x, upper],
            send_sem=send.at[1, offset], recv_sem=got.at[1, source_y],
            device_id=torus_peer(source_y, my_x, nx), device_id_type=mesh_kind,
        ).wait_recv()
    for offset in range(1, nx):
        peer_x = lax.rem(my_x + offset, nx)
        copy = pltpu.make_async_remote_copy(
            src_ref=full.at[:, my_x, upper], dst_ref=full.at[:, my_x, upper],
            send_sem=send.at[3, offset], recv_sem=got.at[3, my_x],
            device_id=torus_peer(my_y, peer_x, nx), device_id_type=mesh_kind,
        )
        copy.start()
        sends.append(copy)
    for offset in range(1, ny):
        source_y = lax.rem(my_y + ny - offset, ny)
        pltpu.make_async_remote_copy(
            src_ref=full.at[source_y, :, lower], dst_ref=full.at[source_y, :, lower],
            send_sem=send.at[2, offset], recv_sem=got.at[2, source_y],
            device_id=torus_peer(source_y, my_x, nx), device_id_type=mesh_kind,
        ).wait_recv()
    for offset in range(1, nx):
        source_x = lax.rem(my_x + nx - offset, nx)
        pltpu.make_async_remote_copy(
            src_ref=full.at[:, source_x, upper], dst_ref=full.at[:, source_x, upper],
            send_sem=send.at[3, offset], recv_sem=got.at[3, source_x],
            device_id=torus_peer(my_y, source_x, nx), device_id_type=mesh_kind,
        ).wait_recv()
    for copy in sends:
        copy.wait_send()
    out_ref[...] = full[...]


def gather_all_2d(x, nx, collective_id):
    rows, lanes = x.shape
    n = lax.axis_size("col")
    ny = n // nx
    side = max(nx, ny)
    out = pl.pallas_call(
        functools.partial(gather_all_2d_kernel, nx, ny),
        out_shape=jax.ShapeDtypeStruct((ny, nx, rows, lanes), x.dtype),
        in_specs=[pl.BlockSpec(memory_space=pltpu.VMEM)],
        out_specs=pl.BlockSpec(memory_space=pltpu.VMEM),
        scratch_shapes=[
            pltpu.VMEM((ny, nx, rows, lanes), x.dtype),
            (
                pltpu.SemaphoreType.DMA((4, side)),
                pltpu.SemaphoreType.DMA((4, side)),
                pltpu.SemaphoreType.DMA((1,)),
            ),
        ],
        compiler_params=pltpu.CompilerParams(
            collective_id=collective_id, has_side_effects=True,
            vmem_limit_bytes=48 * 1024 * 1024,
        ),
        cost_estimate=pl.CostEstimate(
            flops=0, transcendentals=0, bytes_accessed=3 * n * x.size * x.dtype.itemsize
        ),
    )(x)
    return out.reshape(n, rows, lanes)


def all_sum(local, collective_base):
    row_count = lax.axis_size("row")
    col_count = lax.axis_size("col")
    height, width = local.shape
    by_col = scatter_sum(
        local.reshape(col_count, height // col_count, width), "col", "row", jnp.float32,
        collective_base,
    )
    part = height // col_count
    by_row = scatter_sum(
        by_col.reshape(row_count, part // row_count, width), "row", "col", jnp.float32,
        collective_base + 1,
    )
    back_row = gather_all(by_row, "row", "col", row_count, collective_base + 2)
    back_col = gather_all(back_row.reshape(part, width), "col", "row", col_count, collective_base + 3)
    return back_col.reshape(height, width)


def activation(aggregated, weight, cot_rows):
    hidden = jnp.dot(aggregated, weight, preferred_element_type=jnp.float32)
    sigmoid_value = jax.nn.sigmoid(hidden)
    output = (hidden * sigmoid_value).astype(jnp.bfloat16)
    silu_slope = sigmoid_value * (1.0 + hidden * (1.0 - sigmoid_value))
    hidden_grad = (cot_rows.astype(jnp.float32) * silu_slope).astype(jnp.bfloat16)
    return (output, hidden_grad)


def per_device(tile_values, tile_rows, tile_cols, tile_count, features, weight, cotangent):
    slot_total = tile_values.shape[2]
    tile_edge = tile_values.shape[3]
    tile_block = tile_values.reshape(slot_total, tile_edge, tile_edge)
    row_index = tile_rows.reshape(slot_total)
    col_index = tile_cols.reshape(slot_total)
    live_count = tile_count.reshape(1)
    own_rows = features.shape[0]
    feat_width = features.shape[1]
    row_count = lax.axis_size("row")
    col_count = lax.axis_size("col")
    row_tiles = col_count * own_rows // tile_edge
    col_tiles = row_count * own_rows // tile_edge
    column_block = gather_row(features, 8)
    source = column_block.reshape(col_tiles, tile_edge, feat_width)
    partial_rows = sparse_product(
        tile_block, row_index, col_index, live_count, source, row_tiles, False
    )
    partial_flat = partial_rows.reshape(row_tiles * tile_edge, feat_width)
    node_total = row_count * col_count * own_rows
    aggregated = scatter_sum_2d(
        partial_rows.reshape(col_count, own_rows, feat_width), TORUS_X, jnp.bfloat16, 0
    )
    output, hidden_grad = activation(aggregated, weight, cotangent)
    own_grad = lax.dot_general(
        hidden_grad, weight, (((1,), (1,)), ((), ())), preferred_element_type=jnp.float32
    ).astype(jnp.bfloat16)
    row_block = gather_all_2d(own_grad, TORUS_X, 7)
    local_grad = lax.dot_general(
        aggregated, hidden_grad, (((0,), (0,)), ((), ())), preferred_element_type=jnp.float32
    )
    weight_grad = lax.psum(lax.psum(local_grad, "row"), "col") * (1.0 / math.sqrt(node_total))
    source_back = row_block.reshape(row_tiles, tile_edge, feat_width)
    partial_cols = sparse_product(
        tile_block, col_index, row_index, live_count, source_back, col_tiles, True
    )
    input_grad = scatter_sum_row(
        partial_cols.reshape(row_count, own_rows, feat_width), jnp.float32, 9
    )
    return (output, weight_grad, input_grad)


def solution(mesh):
    placed = (
        P("row", "col", None, None, None),
        P("row", "col", None),
        P("row", "col", None),
        P("row", "col"),
        P(("row", "col"), None),
        P(),
        P(("row", "col"), None),
    )
    return jax.shard_map(
        per_device,
        mesh=mesh,
        in_specs=placed,
        out_specs=(P(("row", "col"), None), P(), P(("row", "col"), None)),
        check_vma=False,
    )
```

```python
import functools
import math

import jax
import jax.numpy as jnp
from jax import lax
from jax.experimental import pallas as pl
from jax.experimental.pallas import tpu as pltpu
from jax.sharding import PartitionSpec as P

SLOTS_PER_STEP = 32
UNROLL = 32
TORUS_X = 4


def spmm_kernel(transpose, acc_index, src_index, count_ref, tiles_ref, src_ref, out_ref, acc_ref):
    step = pl.program_id(0)
    per_step = tiles_ref.shape[0]
    live = count_ref[0]
    acc_last = acc_ref.shape[0] - 1
    src_last = src_ref.shape[0] - 1

    @pl.when(step == 0)
    def _():
        acc_ref[...] = jnp.zeros_like(acc_ref)

    def one_slot(k, carry):
        slot = step * per_step + k
        target = jnp.clip(acc_index[slot], 0, acc_last)
        picked = jnp.clip(src_index[slot], 0, src_last)
        tile = tiles_ref[k]
        tile = jnp.where(slot < live, tile, jnp.zeros_like(tile))
        block = src_ref[picked]
        if transpose:
            product = lax.dot_general(
                tile, block, (((0,), (0,)), ((), ())), preferred_element_type=jnp.float32
            )
        else:
            product = jnp.dot(tile, block, preferred_element_type=jnp.float32)
        acc_ref[target] += product
        return carry

    lax.fori_loop(0, per_step, one_slot, 0, unroll=UNROLL)

    @pl.when(step == pl.num_programs(0) - 1)
    def _():
        out_ref[...] = acc_ref[...].astype(out_ref.dtype)


def sparse_product(tile_block, acc_index, src_index, live_count, source, segments, transpose):
    slot_total, tile_edge, _ = tile_block.shape
    feat_width = source.shape[2]
    per_step = min(SLOTS_PER_STEP, slot_total)
    steps = slot_total // per_step

    def tile_map(step, acc_ref, src_ref, count_ref):
        last_live = jnp.maximum(count_ref[0] - 1, 0) // per_step
        return (jnp.minimum(step, last_live), 0, 0)

    grid_spec = pltpu.PrefetchScalarGridSpec(
        num_scalar_prefetch=3,
        grid=(steps,),
        in_specs=[
            pl.BlockSpec((per_step, tile_edge, tile_edge), tile_map),
            pl.BlockSpec(source.shape, lambda step, *_: (0, 0, 0)),
        ],
        out_specs=pl.BlockSpec((segments, tile_edge, feat_width), lambda step, *_: (0, 0, 0)),
        scratch_shapes=[pltpu.VMEM((segments, tile_edge, feat_width), jnp.float32)],
    )
    flops = 2 * slot_total * tile_edge * tile_edge * feat_width
    bytes_accessed = (
        tile_block.size * 2 + source.size * 2 + segments * tile_edge * feat_width * 2
    )
    return pl.pallas_call(
        functools.partial(spmm_kernel, transpose),
        out_shape=jax.ShapeDtypeStruct((segments, tile_edge, feat_width), jnp.bfloat16),
        grid_spec=grid_spec,
        compiler_params=pltpu.CompilerParams(
            dimension_semantics=("arbitrary",), vmem_limit_bytes=56 * 1024 * 1024
        ),
        cost_estimate=pl.CostEstimate(
            flops=flops, transcendentals=0, bytes_accessed=bytes_accessed
        ),
    )(acc_index, src_index, live_count, tile_block, source)


def peer_id(axis, other_axis, peer):
    if axis == "row":
        return (peer, lax.axis_index(other_axis))
    return (lax.axis_index(other_axis), peer)


def greet_all(axis, other_axis, n, me):
    barrier = pltpu.get_barrier_semaphore()
    for offset in range(1, n):
        peer = lax.rem(me + offset, n)
        pl.semaphore_signal(
            barrier, 1, device_id=peer_id(axis, other_axis, peer),
            device_id_type=pl.DeviceIdType.MESH,
        )
    pl.semaphore_wait(barrier, n - 1)


def scatter_sum_kernel(axis, other_axis, n, x_hbm, out_ref, recv, send_sems, recv_sems, own_sem):
    me = lax.axis_index(axis)
    greet_all(axis, other_axis, n, me)
    own = pltpu.make_async_copy(x_hbm.at[me], recv.at[me], own_sem)
    own.start()
    sends = []
    for offset in range(1, n):
        peer = lax.rem(me + offset, n)
        copy = pltpu.make_async_remote_copy(
            src_ref=x_hbm.at[peer],
            dst_ref=recv.at[me],
            send_sem=send_sems.at[offset],
            recv_sem=recv_sems.at[me],
            device_id=peer_id(axis, other_axis, peer),
            device_id_type=pl.DeviceIdType.MESH,
        )
        copy.start()
        sends.append(copy)
    own.wait()
    for offset in range(1, n):
        source = lax.rem(me + n - offset, n)
        pltpu.make_async_remote_copy(
            src_ref=x_hbm.at[source],
            dst_ref=recv.at[source],
            send_sem=send_sems.at[offset],
            recv_sem=recv_sems.at[source],
            device_id=peer_id(axis, other_axis, source),
            device_id_type=pl.DeviceIdType.MESH,
        ).wait_recv()
    total = recv[0].astype(jnp.float32)
    for j in range(1, n):
        total = total + recv[j].astype(jnp.float32)
    out_ref[...] = total.astype(out_ref.dtype)
    for copy in sends:
        copy.wait_send()


def scatter_sum(x, axis, other_axis, out_dtype, collective_id):
    n, rows, lanes = x.shape
    return pl.pallas_call(
        functools.partial(scatter_sum_kernel, axis, other_axis, n),
        out_shape=jax.ShapeDtypeStruct((rows, lanes), out_dtype),
        in_specs=[pl.BlockSpec(memory_space=pl.ANY)],
        out_specs=pl.BlockSpec(memory_space=pltpu.VMEM),
        scratch_shapes=[
            pltpu.VMEM((n, rows, lanes), x.dtype),
            pltpu.SemaphoreType.DMA((n,)),
            pltpu.SemaphoreType.DMA((n,)),
            pltpu.SemaphoreType.DMA(()),
        ],
        compiler_params=pltpu.CompilerParams(
            collective_id=collective_id, has_side_effects=True,
            vmem_limit_bytes=48 * 1024 * 1024,
        ),
        cost_estimate=pl.CostEstimate(
            flops=x.size, transcendentals=0, bytes_accessed=3 * x.size * x.dtype.itemsize
        ),
    )(x)


def gather_all_kernel(axis, other_axis, n, x_ref, out_ref, recv, send_sems, recv_sems):
    me = lax.axis_index(axis)
    recv[me] = x_ref[...]
    greet_all(axis, other_axis, n, me)
    sends = []
    for offset in range(1, n):
        peer = lax.rem(me + offset, n)
        copy = pltpu.make_async_remote_copy(
            src_ref=x_ref,
            dst_ref=recv.at[me],
            send_sem=send_sems.at[offset],
            recv_sem=recv_sems.at[me],
            device_id=peer_id(axis, other_axis, peer),
            device_id_type=pl.DeviceIdType.MESH,
        )
        copy.start()
        sends.append(copy)
    for offset in range(1, n):
        source = lax.rem(me + n - offset, n)
        pltpu.make_async_remote_copy(
            src_ref=x_ref,
            dst_ref=recv.at[source],
            send_sem=send_sems.at[offset],
            recv_sem=recv_sems.at[source],
            device_id=peer_id(axis, other_axis, source),
            device_id_type=pl.DeviceIdType.MESH,
        ).wait_recv()
    out_ref[...] = recv[...]
    for copy in sends:
        copy.wait_send()


def gather_all(x, axis, other_axis, n, collective_id):
    rows, lanes = x.shape
    return pl.pallas_call(
        functools.partial(gather_all_kernel, axis, other_axis, n),
        out_shape=jax.ShapeDtypeStruct((n, rows, lanes), x.dtype),
        in_specs=[pl.BlockSpec(memory_space=pltpu.VMEM)],
        out_specs=pl.BlockSpec(memory_space=pltpu.VMEM),
        scratch_shapes=[
            pltpu.VMEM((n, rows, lanes), x.dtype),
            pltpu.SemaphoreType.DMA((n,)),
            pltpu.SemaphoreType.DMA((n,)),
        ],
        compiler_params=pltpu.CompilerParams(
            collective_id=collective_id, has_side_effects=True,
            vmem_limit_bytes=48 * 1024 * 1024,
        ),
        cost_estimate=pl.CostEstimate(
            flops=0, transcendentals=0, bytes_accessed=3 * n * x.size * x.dtype.itemsize
        ),
    )(x)


def torus_peer(y, x, nx):
    return (lax.axis_index("row"), y * nx + x)


def scatter_sum_2d_kernel(nx, ny, x_hbm, out_ref, recv1, mid, recv2, sems):
    send1, got1, send2, got2, own_sems = sems
    me = lax.axis_index("col")
    my_y = me // nx
    my_x = lax.rem(me, nx)
    half = x_hbm.shape[2] // 2
    lower = pl.ds(0, half)
    upper = pl.ds(half, half)
    mesh_kind = pl.DeviceIdType.MESH

    barrier = pltpu.get_barrier_semaphore()
    for offset in range(1, nx):
        pl.semaphore_signal(barrier, 1, device_id=torus_peer(my_y, lax.rem(my_x + offset, nx), nx),
                            device_id_type=mesh_kind)
    for offset in range(1, ny):
        pl.semaphore_signal(barrier, 1, device_id=torus_peer(lax.rem(my_y + offset, ny), my_x, nx),
                            device_id_type=mesh_kind)
    pl.semaphore_wait(barrier, nx + ny - 2)

    own_a = pltpu.make_async_copy(x_hbm.at[:, my_x, lower], recv1.at[0, my_x], own_sems.at[0])
    own_b = pltpu.make_async_copy(x_hbm.at[my_y, :, upper], recv1.at[1, my_y], own_sems.at[1])
    own_a.start()
    own_b.start()
    sends = []
    for offset in range(1, nx):
        peer_x = lax.rem(my_x + offset, nx)
        copy = pltpu.make_async_remote_copy(
            src_ref=x_hbm.at[:, peer_x, lower], dst_ref=recv1.at[0, my_x],
            send_sem=send1.at[0, offset], recv_sem=got1.at[0, my_x],
            device_id=torus_peer(my_y, peer_x, nx), device_id_type=mesh_kind,
        )
        copy.start()
        sends.append(copy)
    for offset in range(1, ny):
        peer_y = lax.rem(my_y + offset, ny)
        copy = pltpu.make_async_remote_copy(
            src_ref=x_hbm.at[peer_y, :, upper], dst_ref=recv1.at[1, my_y],
            send_sem=send1.at[1, offset], recv_sem=got1.at[1, my_y],
            device_id=torus_peer(peer_y, my_x, nx), device_id_type=mesh_kind,
        )
        copy.start()
        sends.append(copy)
    own_a.wait()
    own_b.wait()
    for offset in range(1, nx):
        source_x = lax.rem(my_x + nx - offset, nx)
        pltpu.make_async_remote_copy(
            src_ref=x_hbm.at[:, source_x, lower], dst_ref=recv1.at[0, source_x],
            send_sem=send1.at[0, offset], recv_sem=got1.at[0, source_x],
            device_id=torus_peer(my_y, source_x, nx), device_id_type=mesh_kind,
        ).wait_recv()
    for offset in range(1, ny):
        source_y = lax.rem(my_y + ny - offset, ny)
        pltpu.make_async_remote_copy(
            src_ref=x_hbm.at[source_y, :, upper], dst_ref=recv1.at[1, source_y],
            send_sem=send1.at[1, offset], recv_sem=got1.at[1, source_y],
            device_id=torus_peer(source_y, my_x, nx), device_id_type=mesh_kind,
        ).wait_recv()

    def add_up(stack):
        total = stack[0].astype(jnp.float32)
        for j in range(1, stack.shape[0]):
            total = total + stack[j].astype(jnp.float32)
        return total

    for target in range(ny):
        mid[0, target] = add_up(recv1[0, :, target]).astype(mid.dtype)
    for target in range(nx):
        mid[1, target] = add_up(recv1[1, :, target]).astype(mid.dtype)
    recv2[0, my_y] = mid[0, my_y]
    recv2[1, my_x] = mid[1, my_x]

    for offset in range(1, ny):
        peer_y = lax.rem(my_y + offset, ny)
        copy = pltpu.make_async_remote_copy(
            src_ref=mid.at[0, peer_y], dst_ref=recv2.at[0, my_y],
            send_sem=send2.at[0, offset], recv_sem=got2.at[0, my_y],
            device_id=torus_peer(peer_y, my_x, nx), device_id_type=mesh_kind,
        )
        copy.start()
        sends.append(copy)
    for offset in range(1, nx):
        peer_x = lax.rem(my_x + offset, nx)
        copy = pltpu.make_async_remote_copy(
            src_ref=mid.at[1, peer_x], dst_ref=recv2.at[1, my_x],
            send_sem=send2.at[1, offset], recv_sem=got2.at[1, my_x],
            device_id=torus_peer(my_y, peer_x, nx), device_id_type=mesh_kind,
        )
        copy.start()
        sends.append(copy)
    for offset in range(1, ny):
        source_y = lax.rem(my_y + ny - offset, ny)
        pltpu.make_async_remote_copy(
            src_ref=mid.at[0, source_y], dst_ref=recv2.at[0, source_y],
            send_sem=send2.at[0, offset], recv_sem=got2.at[0, source_y],
            device_id=torus_peer(source_y, my_x, nx), device_id_type=mesh_kind,
        ).wait_recv()
    for offset in range(1, nx):
        source_x = lax.rem(my_x + nx - offset, nx)
        pltpu.make_async_remote_copy(
            src_ref=mid.at[1, source_x], dst_ref=recv2.at[1, source_x],
            send_sem=send2.at[1, offset], recv_sem=got2.at[1, source_x],
            device_id=torus_peer(my_y, source_x, nx), device_id_type=mesh_kind,
        ).wait_recv()
    out_ref[lower] = add_up(recv2[0]).astype(out_ref.dtype)
    out_ref[upper] = add_up(recv2[1]).astype(out_ref.dtype)
    for copy in sends:
        copy.wait_send()


def scatter_sum_2d(x, nx, out_dtype, collective_id):
    n, rows, lanes = x.shape
    ny = n // nx
    half = rows // 2
    side = max(nx, ny)
    return pl.pallas_call(
        functools.partial(scatter_sum_2d_kernel, nx, ny),
        out_shape=jax.ShapeDtypeStruct((rows, lanes), out_dtype),
        in_specs=[pl.BlockSpec(memory_space=pl.ANY)],
        out_specs=pl.BlockSpec(memory_space=pltpu.VMEM),
        scratch_shapes=[
            pltpu.VMEM((2, side, side, half, lanes), x.dtype),
            pltpu.VMEM((2, side, half, lanes), x.dtype),
            pltpu.VMEM((2, side, half, lanes), x.dtype),
            (
                pltpu.SemaphoreType.DMA((2, side)),
                pltpu.SemaphoreType.DMA((2, side)),
                pltpu.SemaphoreType.DMA((2, side)),
                pltpu.SemaphoreType.DMA((2, side)),
                pltpu.SemaphoreType.DMA((2,)),
            ),
        ],
        compiler_params=pltpu.CompilerParams(
            collective_id=collective_id, has_side_effects=True,
            vmem_limit_bytes=48 * 1024 * 1024,
        ),
        cost_estimate=pl.CostEstimate(
            flops=x.size, transcendentals=0, bytes_accessed=3 * x.size * x.dtype.itemsize
        ),
    )(x.reshape(ny, nx, rows, lanes))


def row_peer(index):
    return (index, lax.axis_index("col"))


def greet_row(my_z, my_core, nz):
    barrier = pltpu.get_barrier_semaphore()
    mesh_kind = pl.DeviceIdType.MESH
    pl.semaphore_signal(barrier, 1, device_id=row_peer(my_z * 2 + 1 - my_core), device_id_type=mesh_kind)
    for offset in range(1, nz):
        peer_z = lax.rem(my_z + offset, nz)
        pl.semaphore_signal(barrier, 1, device_id=row_peer(peer_z * 2 + my_core), device_id_type=mesh_kind)
    pl.semaphore_wait(barrier, nz)


def scatter_sum_row_kernel(nz, x_hbm, out_ref, own1, recv1, mid, recv2, sems):
    send1, got1, send2, got2, own_sem = sems
    mesh_kind = pl.DeviceIdType.MESH
    me = lax.axis_index("row")
    my_z = me // 2
    my_core = lax.rem(me, 2)
    other_core = 1 - my_core
    greet_row(my_z, my_core, nz)
    own = pltpu.make_async_copy(x_hbm.at[:, my_core], own1, own_sem.at[0])
    own.start()
    first = pltpu.make_async_remote_copy(
        src_ref=x_hbm.at[:, other_core], dst_ref=recv1,
        send_sem=send1.at[0], recv_sem=got1.at[0],
        device_id=row_peer(my_z * 2 + other_core), device_id_type=mesh_kind,
    )
    first.start()
    own.wait()
    first.wait_recv()
    for target in range(nz):
        mid[target] = (own1[target].astype(jnp.float32) + recv1[target].astype(jnp.float32)).astype(mid.dtype)
    sends = []
    for offset in range(1, nz):
        peer_z = lax.rem(my_z + offset, nz)
        copy = pltpu.make_async_remote_copy(
            src_ref=mid.at[peer_z], dst_ref=recv2.at[my_z],
            send_sem=send2.at[offset], recv_sem=got2.at[my_z],
            device_id=row_peer(peer_z * 2 + my_core), device_id_type=mesh_kind,
        )
        copy.start()
        sends.append(copy)
    total = mid[my_z].astype(jnp.float32)
    for offset in range(1, nz):
        source_z = lax.rem(my_z + nz - offset, nz)
        pltpu.make_async_remote_copy(
            src_ref=mid.at[source_z], dst_ref=recv2.at[source_z],
            send_sem=send2.at[offset], recv_sem=got2.at[source_z],
            device_id=row_peer(source_z * 2 + my_core), device_id_type=mesh_kind,
        ).wait_recv()
        total = total + recv2[source_z].astype(jnp.float32)
    out_ref[...] = total.astype(out_ref.dtype)
    first.wait_send()
    for copy in sends:
        copy.wait_send()


def scatter_sum_row(x, out_dtype, collective_id):
    n, rows, lanes = x.shape
    nz = n // 2
    return pl.pallas_call(
        functools.partial(scatter_sum_row_kernel, nz),
        out_shape=jax.ShapeDtypeStruct((rows, lanes), out_dtype),
        in_specs=[pl.BlockSpec(memory_space=pl.ANY)],
        out_specs=pl.BlockSpec(memory_space=pltpu.VMEM),
        scratch_shapes=[
            pltpu.VMEM((nz, rows, lanes), x.dtype),
            pltpu.VMEM((nz, rows, lanes), x.dtype),
            pltpu.VMEM((nz, rows, lanes), x.dtype),
            pltpu.VMEM((nz, rows, lanes), x.dtype),
            (
                pltpu.SemaphoreType.DMA((1,)),
                pltpu.SemaphoreType.DMA((1,)),
                pltpu.SemaphoreType.DMA((nz,)),
                pltpu.SemaphoreType.DMA((nz,)),
                pltpu.SemaphoreType.DMA((1,)),
            ),
        ],
        compiler_params=pltpu.CompilerParams(
            collective_id=collective_id, has_side_effects=True,
            vmem_limit_bytes=48 * 1024 * 1024,
        ),
        cost_estimate=pl.CostEstimate(
            flops=x.size, transcendentals=0, bytes_accessed=3 * x.size * x.dtype.itemsize
        ),
    )(x.reshape(nz, 2, rows, lanes))


def gather_row_kernel(nz, x_ref, out_ref, full, sems):
    send1, got1, send2, got2, own_sem = sems
    mesh_kind = pl.DeviceIdType.MESH
    me = lax.axis_index("row")
    my_z = me // 2
    my_core = lax.rem(me, 2)
    other_core = 1 - my_core
    greet_row(my_z, my_core, nz)
    own = pltpu.make_async_copy(x_ref, full.at[my_z, my_core], own_sem.at[0])
    own.start()
    sends = []
    for offset in range(1, nz):
        peer_z = lax.rem(my_z + offset, nz)
        copy = pltpu.make_async_remote_copy(
            src_ref=x_ref, dst_ref=full.at[my_z, my_core],
            send_sem=send1.at[offset], recv_sem=got1.at[my_z],
            device_id=row_peer(peer_z * 2 + my_core), device_id_type=mesh_kind,
        )
        copy.start()
        sends.append(copy)
    own.wait()
    for offset in range(1, nz):
        source_z = lax.rem(my_z + nz - offset, nz)
        pltpu.make_async_remote_copy(
            src_ref=x_ref, dst_ref=full.at[source_z, my_core],
            send_sem=send1.at[offset], recv_sem=got1.at[source_z],
            device_id=row_peer(source_z * 2 + my_core), device_id_type=mesh_kind,
        ).wait_recv()
    second = pltpu.make_async_remote_copy(
        src_ref=full.at[:, my_core], dst_ref=full.at[:, my_core],
        send_sem=send2.at[0], recv_sem=got2.at[0],
        device_id=row_peer(my_z * 2 + other_core), device_id_type=mesh_kind,
    )
    second.start()
    pltpu.make_async_remote_copy(
        src_ref=full.at[:, other_core], dst_ref=full.at[:, other_core],
        send_sem=send2.at[0], recv_sem=got2.at[0],
        device_id=row_peer(my_z * 2 + other_core), device_id_type=mesh_kind,
    ).wait_recv()
    for copy in sends:
        copy.wait_send()
    second.wait_send()
    out_ref[...] = full[...]


def gather_row(x, collective_id):
    rows, lanes = x.shape
    nz = lax.axis_size("row") // 2
    out = pl.pallas_call(
        functools.partial(gather_row_kernel, nz),
        out_shape=jax.ShapeDtypeStruct((nz, 2, rows, lanes), x.dtype),
        in_specs=[pl.BlockSpec(memory_space=pltpu.VMEM)],
        out_specs=pl.BlockSpec(memory_space=pltpu.VMEM),
        scratch_shapes=[
            pltpu.VMEM((nz, 2, rows, lanes), x.dtype),
            (
                pltpu.SemaphoreType.DMA((nz,)),
                pltpu.SemaphoreType.DMA((nz,)),
                pltpu.SemaphoreType.DMA((1,)),
                pltpu.SemaphoreType.DMA((1,)),
                pltpu.SemaphoreType.DMA((1,)),
            ),
        ],
        compiler_params=pltpu.CompilerParams(
            collective_id=collective_id, has_side_effects=True,
            vmem_limit_bytes=48 * 1024 * 1024,
        ),
        cost_estimate=pl.CostEstimate(
            flops=0, transcendentals=0, bytes_accessed=3 * 2 * nz * x.size * x.dtype.itemsize
        ),
    )(x)
    return out.reshape(2 * nz * rows, lanes)


def gather_all_2d_kernel(nx, ny, x_ref, out_ref, full, sems):
    send, got, own_sem = sems
    mesh_kind = pl.DeviceIdType.MESH
    me = lax.axis_index("col")
    my_y = me // nx
    my_x = lax.rem(me, nx)
    half = x_ref.shape[0] // 2
    lower = pl.ds(0, half)
    upper = pl.ds(half, half)

    barrier = pltpu.get_barrier_semaphore()
    for offset in range(1, nx):
        pl.semaphore_signal(barrier, 1, device_id=torus_peer(my_y, lax.rem(my_x + offset, nx), nx),
                            device_id_type=mesh_kind)
    for offset in range(1, ny):
        pl.semaphore_signal(barrier, 1, device_id=torus_peer(lax.rem(my_y + offset, ny), my_x, nx),
                            device_id_type=mesh_kind)
    pl.semaphore_wait(barrier, nx + ny - 2)

    own = pltpu.make_async_copy(x_ref, full.at[my_y, my_x], own_sem.at[0])
    own.start()
    sends = []
    for offset in range(1, nx):
        peer_x = lax.rem(my_x + offset, nx)
        copy = pltpu.make_async_remote_copy(
            src_ref=x_ref.at[lower], dst_ref=full.at[my_y, my_x, lower],
            send_sem=send.at[0, offset], recv_sem=got.at[0, my_x],
            device_id=torus_peer(my_y, peer_x, nx), device_id_type=mesh_kind,
        )
        copy.start()
        sends.append(copy)
    for offset in range(1, ny):
        peer_y = lax.rem(my_y + offset, ny)
        copy = pltpu.make_async_remote_copy(
            src_ref=x_ref.at[upper], dst_ref=full.at[my_y, my_x, upper],
            send_sem=send.at[1, offset], recv_sem=got.at[1, my_y],
            device_id=torus_peer(peer_y, my_x, nx), device_id_type=mesh_kind,
        )
        copy.start()
        sends.append(copy)
    own.wait()
    for offset in range(1, nx):
        source_x = lax.rem(my_x + nx - offset, nx)
        pltpu.make_async_remote_copy(
            src_ref=x_ref.at[lower], dst_ref=full.at[my_y, source_x, lower],
            send_sem=send.at[0, offset], recv_sem=got.at[0, source_x],
            device_id=torus_peer(my_y, source_x, nx), device_id_type=mesh_kind,
        ).wait_recv()
    for offset in range(1, ny):
        peer_y = lax.rem(my_y + offset, ny)
        copy = pltpu.make_async_remote_copy(
            src_ref=full.at[my_y, :, lower], dst_ref=full.at[my_y, :, lower],
            send_sem=send.at[2, offset], recv_sem=got.at[2, my_y],
            device_id=torus_peer(peer_y, my_x, nx), device_id_type=mesh_kind,
        )
        copy.start()
        sends.append(copy)
    for offset in range(1, ny):
        source_y = lax.rem(my_y + ny - offset, ny)
        pltpu.make_async_remote_copy(
            src_ref=x_ref.at[upper], dst_ref=full.at[source_y, my_x, upper],
            send_sem=send.at[1, offset], recv_sem=got.at[1, source_y],
            device_id=torus_peer(source_y, my_x, nx), device_id_type=mesh_kind,
        ).wait_recv()
    for offset in range(1, nx):
        peer_x = lax.rem(my_x + offset, nx)
        copy = pltpu.make_async_remote_copy(
            src_ref=full.at[:, my_x, upper], dst_ref=full.at[:, my_x, upper],
            send_sem=send.at[3, offset], recv_sem=got.at[3, my_x],
            device_id=torus_peer(my_y, peer_x, nx), device_id_type=mesh_kind,
        )
        copy.start()
        sends.append(copy)
    for offset in range(1, ny):
        source_y = lax.rem(my_y + ny - offset, ny)
        pltpu.make_async_remote_copy(
            src_ref=full.at[source_y, :, lower], dst_ref=full.at[source_y, :, lower],
            send_sem=send.at[2, offset], recv_sem=got.at[2, source_y],
            device_id=torus_peer(source_y, my_x, nx), device_id_type=mesh_kind,
        ).wait_recv()
    for offset in range(1, nx):
        source_x = lax.rem(my_x + nx - offset, nx)
        pltpu.make_async_remote_copy(
            src_ref=full.at[:, source_x, upper], dst_ref=full.at[:, source_x, upper],
            send_sem=send.at[3, offset], recv_sem=got.at[3, source_x],
            device_id=torus_peer(my_y, source_x, nx), device_id_type=mesh_kind,
        ).wait_recv()
    for copy in sends:
        copy.wait_send()
    out_ref[...] = full[...]


def gather_all_2d(x, nx, collective_id):
    rows, lanes = x.shape
    n = lax.axis_size("col")
    ny = n // nx
    side = max(nx, ny)
    out = pl.pallas_call(
        functools.partial(gather_all_2d_kernel, nx, ny),
        out_shape=jax.ShapeDtypeStruct((ny, nx, rows, lanes), x.dtype),
        in_specs=[pl.BlockSpec(memory_space=pltpu.VMEM)],
        out_specs=pl.BlockSpec(memory_space=pltpu.VMEM),
        scratch_shapes=[
            pltpu.VMEM((ny, nx, rows, lanes), x.dtype),
            (
                pltpu.SemaphoreType.DMA((4, side)),
                pltpu.SemaphoreType.DMA((4, side)),
                pltpu.SemaphoreType.DMA((1,)),
            ),
        ],
        compiler_params=pltpu.CompilerParams(
            collective_id=collective_id, has_side_effects=True,
            vmem_limit_bytes=48 * 1024 * 1024,
        ),
        cost_estimate=pl.CostEstimate(
            flops=0, transcendentals=0, bytes_accessed=3 * n * x.size * x.dtype.itemsize
        ),
    )(x)
    return out.reshape(n, rows, lanes)


def fused_sum_kernel(nr, nc, x_ref, out_ref, recv1, recv2, recv3, sems):
    send1, got1, send2, got2, send3, got3 = sems
    mesh_kind = pl.DeviceIdType.MESH
    my_r = lax.axis_index("row")
    my_c = lax.axis_index("col")
    barrier = pltpu.get_barrier_semaphore()
    for offset in range(1, nc):
        pl.semaphore_signal(barrier, 1, device_id=(my_r, lax.rem(my_c + offset, nc)),
                            device_id_type=mesh_kind)
    for offset in range(1, nr):
        pl.semaphore_signal(barrier, 1, device_id=(lax.rem(my_r + offset, nr), my_c),
                            device_id_type=mesh_kind)
    pl.semaphore_wait(barrier, nc + nr - 2)

    def exchange(peers, axis_count, src_of, dst, send, got, me_index):
        started = []
        for offset in range(1, axis_count):
            peer = lax.rem(me_index + offset, axis_count)
            copy = pltpu.make_async_remote_copy(
                src_ref=src_of(peer), dst_ref=dst.at[me_index],
                send_sem=send.at[offset], recv_sem=got.at[me_index],
                device_id=peers(peer), device_id_type=mesh_kind,
            )
            copy.start()
            started.append(copy)
        for offset in range(1, axis_count):
            source = lax.rem(me_index + axis_count - offset, axis_count)
            pltpu.make_async_remote_copy(
                src_ref=src_of(source), dst_ref=dst.at[source],
                send_sem=send.at[offset], recv_sem=got.at[source],
                device_id=peers(source), device_id_type=mesh_kind,
            ).wait_recv()
        return started

    along_col = lambda peer: (my_r, peer)
    along_row = lambda peer: (peer, my_c)
    recv1[my_c] = x_ref[my_c]
    sends = exchange(along_col, nc, lambda peer: x_ref.at[peer], recv1, send1, got1, my_c)
    part = recv1[0]
    for j in range(1, nc):
        part = part + recv1[j]
    recv2[my_r] = part
    sends += exchange(along_row, nr, lambda peer: recv2.at[my_r], recv2, send2, got2, my_r)
    total = recv2[0]
    for j in range(1, nr):
        total = total + recv2[j]
    recv3[my_c] = total
    sends += exchange(along_col, nc, lambda peer: recv3.at[my_c], recv3, send3, got3, my_c)
    out_ref[...] = recv3[...]
    for copy in sends:
        copy.wait_send()


def fused_sum(local, collective_id):
    nr = lax.axis_size("row")
    nc = lax.axis_size("col")
    height, width = local.shape
    part = height // nc
    out = pl.pallas_call(
        functools.partial(fused_sum_kernel, nr, nc),
        out_shape=jax.ShapeDtypeStruct((nc, part, width), local.dtype),
        in_specs=[pl.BlockSpec(memory_space=pltpu.VMEM)],
        out_specs=pl.BlockSpec(memory_space=pltpu.VMEM),
        scratch_shapes=[
            pltpu.VMEM((nc, part, width), local.dtype),
            pltpu.VMEM((nr, part, width), local.dtype),
            pltpu.VMEM((nc, part, width), local.dtype),
            (
                pltpu.SemaphoreType.DMA((nc,)),
                pltpu.SemaphoreType.DMA((nc,)),
                pltpu.SemaphoreType.DMA((nr,)),
                pltpu.SemaphoreType.DMA((nr,)),
                pltpu.SemaphoreType.DMA((nc,)),
                pltpu.SemaphoreType.DMA((nc,)),
            ),
        ],
        compiler_params=pltpu.CompilerParams(
            collective_id=collective_id, has_side_effects=True,
            vmem_limit_bytes=48 * 1024 * 1024,
        ),
        cost_estimate=pl.CostEstimate(
            flops=local.size, transcendentals=0, bytes_accessed=3 * local.size * 4
        ),
    )(local.reshape(nc, part, width))
    return out.reshape(height, width)


def all_sum(local, collective_base):
    row_count = lax.axis_size("row")
    col_count = lax.axis_size("col")
    height, width = local.shape
    by_col = scatter_sum(
        local.reshape(col_count, height // col_count, width), "col", "row", jnp.float32,
        collective_base,
    )
    part = height // col_count
    by_row = scatter_sum(
        by_col.reshape(row_count, part // row_count, width), "row", "col", jnp.float32,
        collective_base + 1,
    )
    back_row = gather_all(by_row, "row", "col", row_count, collective_base + 2)
    back_col = gather_all(back_row.reshape(part, width), "col", "row", col_count, collective_base + 3)
    return back_col.reshape(height, width)


def activation(aggregated, weight, cot_rows):
    hidden = jnp.dot(aggregated, weight, preferred_element_type=jnp.float32)
    sigmoid_value = jax.nn.sigmoid(hidden)
    output = (hidden * sigmoid_value).astype(jnp.bfloat16)
    silu_slope = sigmoid_value * (1.0 + hidden * (1.0 - sigmoid_value))
    hidden_grad = (cot_rows.astype(jnp.float32) * silu_slope).astype(jnp.bfloat16)
    return (output, hidden_grad)


def per_device(tile_values, tile_rows, tile_cols, tile_count, features, weight, cotangent):
    slot_total = tile_values.shape[2]
    tile_edge = tile_values.shape[3]
    tile_block = tile_values.reshape(slot_total, tile_edge, tile_edge)
    row_index = tile_rows.reshape(slot_total)
    col_index = tile_cols.reshape(slot_total)
    live_count = tile_count.reshape(1)
    own_rows = features.shape[0]
    feat_width = features.shape[1]
    row_count = lax.axis_size("row")
    col_count = lax.axis_size("col")
    row_tiles = col_count * own_rows // tile_edge
    col_tiles = row_count * own_rows // tile_edge
    column_block = gather_row(features, 8)
    source = column_block.reshape(col_tiles, tile_edge, feat_width)
    partial_rows = sparse_product(
        tile_block, row_index, col_index, live_count, source, row_tiles, False
    )
    partial_flat = partial_rows.reshape(row_tiles * tile_edge, feat_width)
    node_total = row_count * col_count * own_rows
    aggregated = scatter_sum_2d(
        partial_rows.reshape(col_count, own_rows, feat_width), TORUS_X, jnp.bfloat16, 0
    )
    output, hidden_grad = activation(aggregated, weight, cotangent)
    own_grad = lax.dot_general(
        hidden_grad, weight, (((1,), (1,)), ((), ())), preferred_element_type=jnp.float32
    ).astype(jnp.bfloat16)
    row_block = gather_all_2d(own_grad, TORUS_X, 7)
    local_grad = lax.dot_general(
        aggregated, hidden_grad, (((0,), (0,)), ((), ())), preferred_element_type=jnp.float32
    )
    weight_grad = fused_sum(local_grad, 1) * (1.0 / math.sqrt(node_total))
    source_back = row_block.reshape(row_tiles, tile_edge, feat_width)
    partial_cols = sparse_product(
        tile_block, col_index, row_index, live_count, source_back, col_tiles, True
    )
    input_grad = scatter_sum_row(
        partial_cols.reshape(row_count, own_rows, feat_width), jnp.float32, 9
    )
    return (output, weight_grad, input_grad)


def solution(mesh):
    placed = (
        P("row", "col", None, None, None),
        P("row", "col", None),
        P("row", "col", None),
        P("row", "col"),
        P(("row", "col"), None),
        P(),
        P(("row", "col"), None),
    )
    return jax.shard_map(
        per_device,
        mesh=mesh,
        in_specs=placed,
        out_specs=(P(("row", "col"), None), P(), P(("row", "col"), None)),
        check_vma=False,
    )
```

```python
import functools
import math

import jax
import jax.numpy as jnp
from jax import lax
from jax.experimental import pallas as pl
from jax.experimental.pallas import tpu as pltpu
from jax.sharding import PartitionSpec as P

SLOTS_PER_STEP = 32
UNROLL = 32
TORUS_X = 4


def spmm_kernel(transpose, acc_index, src_index, count_ref, tiles_ref, src_ref, out_ref, acc_ref):
    step = pl.program_id(0)
    per_step = tiles_ref.shape[0]
    live = count_ref[0]
    acc_last = acc_ref.shape[0] - 1
    src_last = src_ref.shape[0] - 1

    @pl.when(step == 0)
    def _():
        acc_ref[...] = jnp.zeros_like(acc_ref)

    def one_slot(k, carry):
        slot = step * per_step + k
        target = jnp.clip(acc_index[slot], 0, acc_last)
        picked = jnp.clip(src_index[slot], 0, src_last)
        tile = tiles_ref[k]
        tile = jnp.where(slot < live, tile, jnp.zeros_like(tile))
        block = src_ref[picked]
        if transpose:
            product = lax.dot_general(
                tile, block, (((0,), (0,)), ((), ())), preferred_element_type=jnp.float32
            )
        else:
            product = jnp.dot(tile, block, preferred_element_type=jnp.float32)
        acc_ref[target] += product
        return carry

    lax.fori_loop(0, per_step, one_slot, 0, unroll=UNROLL)

    @pl.when(step == pl.num_programs(0) - 1)
    def _():
        out_ref[...] = acc_ref[...].astype(out_ref.dtype)


def sparse_product(tile_block, acc_index, src_index, live_count, source, segments, transpose):
    slot_total, tile_edge, _ = tile_block.shape
    feat_width = source.shape[2]
    per_step = min(SLOTS_PER_STEP, slot_total)
    steps = slot_total // per_step

    def tile_map(step, acc_ref, src_ref, count_ref):
        last_live = jnp.maximum(count_ref[0] - 1, 0) // per_step
        return (jnp.minimum(step, last_live), 0, 0)

    grid_spec = pltpu.PrefetchScalarGridSpec(
        num_scalar_prefetch=3,
        grid=(steps,),
        in_specs=[
            pl.BlockSpec((per_step, tile_edge, tile_edge), tile_map),
            pl.BlockSpec(source.shape, lambda step, *_: (0, 0, 0)),
        ],
        out_specs=pl.BlockSpec((segments, tile_edge, feat_width), lambda step, *_: (0, 0, 0)),
        scratch_shapes=[pltpu.VMEM((segments, tile_edge, feat_width), jnp.float32)],
    )
    flops = 2 * slot_total * tile_edge * tile_edge * feat_width
    bytes_accessed = (
        tile_block.size * 2 + source.size * 2 + segments * tile_edge * feat_width * 2
    )
    return pl.pallas_call(
        functools.partial(spmm_kernel, transpose),
        out_shape=jax.ShapeDtypeStruct((segments, tile_edge, feat_width), jnp.bfloat16),
        grid_spec=grid_spec,
        compiler_params=pltpu.CompilerParams(
            dimension_semantics=("arbitrary",), vmem_limit_bytes=56 * 1024 * 1024
        ),
        cost_estimate=pl.CostEstimate(
            flops=flops, transcendentals=0, bytes_accessed=bytes_accessed
        ),
    )(acc_index, src_index, live_count, tile_block, source)


def peer_id(axis, other_axis, peer):
    if axis == "row":
        return (peer, lax.axis_index(other_axis))
    return (lax.axis_index(other_axis), peer)


def greet_all(axis, other_axis, n, me):
    barrier = pltpu.get_barrier_semaphore()
    for offset in range(1, n):
        peer = lax.rem(me + offset, n)
        pl.semaphore_signal(
            barrier, 1, device_id=peer_id(axis, other_axis, peer),
            device_id_type=pl.DeviceIdType.MESH,
        )
    pl.semaphore_wait(barrier, n - 1)


def scatter_sum_kernel(axis, other_axis, n, x_hbm, out_ref, recv, send_sems, recv_sems, own_sem):
    me = lax.axis_index(axis)
    greet_all(axis, other_axis, n, me)
    own = pltpu.make_async_copy(x_hbm.at[me], recv.at[me], own_sem)
    own.start()
    sends = []
    for offset in range(1, n):
        peer = lax.rem(me + offset, n)
        copy = pltpu.make_async_remote_copy(
            src_ref=x_hbm.at[peer],
            dst_ref=recv.at[me],
            send_sem=send_sems.at[offset],
            recv_sem=recv_sems.at[me],
            device_id=peer_id(axis, other_axis, peer),
            device_id_type=pl.DeviceIdType.MESH,
        )
        copy.start()
        sends.append(copy)
    own.wait()
    for offset in range(1, n):
        source = lax.rem(me + n - offset, n)
        pltpu.make_async_remote_copy(
            src_ref=x_hbm.at[source],
            dst_ref=recv.at[source],
            send_sem=send_sems.at[offset],
            recv_sem=recv_sems.at[source],
            device_id=peer_id(axis, other_axis, source),
            device_id_type=pl.DeviceIdType.MESH,
        ).wait_recv()
    total = recv[0].astype(jnp.float32)
    for j in range(1, n):
        total = total + recv[j].astype(jnp.float32)
    out_ref[...] = total.astype(out_ref.dtype)
    for copy in sends:
        copy.wait_send()


def scatter_sum(x, axis, other_axis, out_dtype, collective_id):
    n, rows, lanes = x.shape
    return pl.pallas_call(
        functools.partial(scatter_sum_kernel, axis, other_axis, n),
        out_shape=jax.ShapeDtypeStruct((rows, lanes), out_dtype),
        in_specs=[pl.BlockSpec(memory_space=pl.ANY)],
        out_specs=pl.BlockSpec(memory_space=pltpu.VMEM),
        scratch_shapes=[
            pltpu.VMEM((n, rows, lanes), x.dtype),
            pltpu.SemaphoreType.DMA((n,)),
            pltpu.SemaphoreType.DMA((n,)),
            pltpu.SemaphoreType.DMA(()),
        ],
        compiler_params=pltpu.CompilerParams(
            collective_id=collective_id, has_side_effects=True,
            vmem_limit_bytes=48 * 1024 * 1024,
        ),
        cost_estimate=pl.CostEstimate(
            flops=x.size, transcendentals=0, bytes_accessed=3 * x.size * x.dtype.itemsize
        ),
    )(x)


def gather_all_kernel(axis, other_axis, n, x_ref, out_ref, recv, send_sems, recv_sems):
    me = lax.axis_index(axis)
    recv[me] = x_ref[...]
    greet_all(axis, other_axis, n, me)
    sends = []
    for offset in range(1, n):
        peer = lax.rem(me + offset, n)
        copy = pltpu.make_async_remote_copy(
            src_ref=x_ref,
            dst_ref=recv.at[me],
            send_sem=send_sems.at[offset],
            recv_sem=recv_sems.at[me],
            device_id=peer_id(axis, other_axis, peer),
            device_id_type=pl.DeviceIdType.MESH,
        )
        copy.start()
        sends.append(copy)
    for offset in range(1, n):
        source = lax.rem(me + n - offset, n)
        pltpu.make_async_remote_copy(
            src_ref=x_ref,
            dst_ref=recv.at[source],
            send_sem=send_sems.at[offset],
            recv_sem=recv_sems.at[source],
            device_id=peer_id(axis, other_axis, source),
            device_id_type=pl.DeviceIdType.MESH,
        ).wait_recv()
    out_ref[...] = recv[...]
    for copy in sends:
        copy.wait_send()


def gather_all(x, axis, other_axis, n, collective_id):
    rows, lanes = x.shape
    return pl.pallas_call(
        functools.partial(gather_all_kernel, axis, other_axis, n),
        out_shape=jax.ShapeDtypeStruct((n, rows, lanes), x.dtype),
        in_specs=[pl.BlockSpec(memory_space=pltpu.VMEM)],
        out_specs=pl.BlockSpec(memory_space=pltpu.VMEM),
        scratch_shapes=[
            pltpu.VMEM((n, rows, lanes), x.dtype),
            pltpu.SemaphoreType.DMA((n,)),
            pltpu.SemaphoreType.DMA((n,)),
        ],
        compiler_params=pltpu.CompilerParams(
            collective_id=collective_id, has_side_effects=True,
            vmem_limit_bytes=48 * 1024 * 1024,
        ),
        cost_estimate=pl.CostEstimate(
            flops=0, transcendentals=0, bytes_accessed=3 * n * x.size * x.dtype.itemsize
        ),
    )(x)


def torus_peer(y, x, nx):
    return (lax.axis_index("row"), y * nx + x)


def scatter_sum_2d_kernel(nx, ny, x_hbm, out_ref, recv1, mid, recv2, sems):
    send1, got1, send2, got2, own_sems = sems
    me = lax.axis_index("col")
    my_y = me // nx
    my_x = lax.rem(me, nx)
    half = x_hbm.shape[2] // 2
    lower = pl.ds(0, half)
    upper = pl.ds(half, half)
    mesh_kind = pl.DeviceIdType.MESH

    barrier = pltpu.get_barrier_semaphore()
    for offset in range(1, nx):
        pl.semaphore_signal(barrier, 1, device_id=torus_peer(my_y, lax.rem(my_x + offset, nx), nx),
                            device_id_type=mesh_kind)
    for offset in range(1, ny):
        pl.semaphore_signal(barrier, 1, device_id=torus_peer(lax.rem(my_y + offset, ny), my_x, nx),
                            device_id_type=mesh_kind)
    pl.semaphore_wait(barrier, nx + ny - 2)

    own_a = pltpu.make_async_copy(x_hbm.at[:, my_x, lower], recv1.at[0, my_x], own_sems.at[0])
    own_b = pltpu.make_async_copy(x_hbm.at[my_y, :, upper], recv1.at[1, my_y], own_sems.at[1])
    own_a.start()
    own_b.start()
    sends = []
    for offset in range(1, nx):
        peer_x = lax.rem(my_x + offset, nx)
        copy = pltpu.make_async_remote_copy(
            src_ref=x_hbm.at[:, peer_x, lower], dst_ref=recv1.at[0, my_x],
            send_sem=send1.at[0, offset], recv_sem=got1.at[0, my_x],
            device_id=torus_peer(my_y, peer_x, nx), device_id_type=mesh_kind,
        )
        copy.start()
        sends.append(copy)
    for offset in range(1, ny):
        peer_y = lax.rem(my_y + offset, ny)
        copy = pltpu.make_async_remote_copy(
            src_ref=x_hbm.at[peer_y, :, upper], dst_ref=recv1.at[1, my_y],
            send_sem=send1.at[1, offset], recv_sem=got1.at[1, my_y],
            device_id=torus_peer(peer_y, my_x, nx), device_id_type=mesh_kind,
        )
        copy.start()
        sends.append(copy)
    own_a.wait()
    own_b.wait()
    for offset in range(1, nx):
        source_x = lax.rem(my_x + nx - offset, nx)
        pltpu.make_async_remote_copy(
            src_ref=x_hbm.at[:, source_x, lower], dst_ref=recv1.at[0, source_x],
            send_sem=send1.at[0, offset], recv_sem=got1.at[0, source_x],
            device_id=torus_peer(my_y, source_x, nx), device_id_type=mesh_kind,
        ).wait_recv()
    for offset in range(1, ny):
        source_y = lax.rem(my_y + ny - offset, ny)
        pltpu.make_async_remote_copy(
            src_ref=x_hbm.at[source_y, :, upper], dst_ref=recv1.at[1, source_y],
            send_sem=send1.at[1, offset], recv_sem=got1.at[1, source_y],
            device_id=torus_peer(source_y, my_x, nx), device_id_type=mesh_kind,
        ).wait_recv()

    def add_up(stack):
        total = stack[0].astype(jnp.float32)
        for j in range(1, stack.shape[0]):
            total = total + stack[j].astype(jnp.float32)
        return total

    for target in range(ny):
        mid[0, target] = add_up(recv1[0, :, target]).astype(mid.dtype)
    for target in range(nx):
        mid[1, target] = add_up(recv1[1, :, target]).astype(mid.dtype)
    recv2[0, my_y] = mid[0, my_y]
    recv2[1, my_x] = mid[1, my_x]

    for offset in range(1, ny):
        peer_y = lax.rem(my_y + offset, ny)
        copy = pltpu.make_async_remote_copy(
            src_ref=mid.at[0, peer_y], dst_ref=recv2.at[0, my_y],
            send_sem=send2.at[0, offset], recv_sem=got2.at[0, my_y],
            device_id=torus_peer(peer_y, my_x, nx), device_id_type=mesh_kind,
        )
        copy.start()
        sends.append(copy)
    for offset in range(1, nx):
        peer_x = lax.rem(my_x + offset, nx)
        copy = pltpu.make_async_remote_copy(
            src_ref=mid.at[1, peer_x], dst_ref=recv2.at[1, my_x],
            send_sem=send2.at[1, offset], recv_sem=got2.at[1, my_x],
            device_id=torus_peer(my_y, peer_x, nx), device_id_type=mesh_kind,
        )
        copy.start()
        sends.append(copy)
    for offset in range(1, ny):
        source_y = lax.rem(my_y + ny - offset, ny)
        pltpu.make_async_remote_copy(
            src_ref=mid.at[0, source_y], dst_ref=recv2.at[0, source_y],
            send_sem=send2.at[0, offset], recv_sem=got2.at[0, source_y],
            device_id=torus_peer(source_y, my_x, nx), device_id_type=mesh_kind,
        ).wait_recv()
    for offset in range(1, nx):
        source_x = lax.rem(my_x + nx - offset, nx)
        pltpu.make_async_remote_copy(
            src_ref=mid.at[1, source_x], dst_ref=recv2.at[1, source_x],
            send_sem=send2.at[1, offset], recv_sem=got2.at[1, source_x],
            device_id=torus_peer(my_y, source_x, nx), device_id_type=mesh_kind,
        ).wait_recv()
    out_ref[lower] = add_up(recv2[0]).astype(out_ref.dtype)
    out_ref[upper] = add_up(recv2[1]).astype(out_ref.dtype)
    for copy in sends:
        copy.wait_send()


def scatter_sum_2d(x, nx, out_dtype, collective_id):
    n, rows, lanes = x.shape
    ny = n // nx
    half = rows // 2
    side = max(nx, ny)
    return pl.pallas_call(
        functools.partial(scatter_sum_2d_kernel, nx, ny),
        out_shape=jax.ShapeDtypeStruct((rows, lanes), out_dtype),
        in_specs=[pl.BlockSpec(memory_space=pl.ANY)],
        out_specs=pl.BlockSpec(memory_space=pltpu.VMEM),
        scratch_shapes=[
            pltpu.VMEM((2, side, side, half, lanes), x.dtype),
            pltpu.VMEM((2, side, half, lanes), x.dtype),
            pltpu.VMEM((2, side, half, lanes), x.dtype),
            (
                pltpu.SemaphoreType.DMA((2, side)),
                pltpu.SemaphoreType.DMA((2, side)),
                pltpu.SemaphoreType.DMA((2, side)),
                pltpu.SemaphoreType.DMA((2, side)),
                pltpu.SemaphoreType.DMA((2,)),
            ),
        ],
        compiler_params=pltpu.CompilerParams(
            collective_id=collective_id, has_side_effects=True,
            vmem_limit_bytes=48 * 1024 * 1024,
        ),
        cost_estimate=pl.CostEstimate(
            flops=x.size, transcendentals=0, bytes_accessed=3 * x.size * x.dtype.itemsize
        ),
    )(x.reshape(ny, nx, rows, lanes))


def row_peer(index):
    return (index, lax.axis_index("col"))


def greet_row(my_z, my_core, nz):
    barrier = pltpu.get_barrier_semaphore()
    mesh_kind = pl.DeviceIdType.MESH
    pl.semaphore_signal(barrier, 1, device_id=row_peer(my_z * 2 + 1 - my_core), device_id_type=mesh_kind)
    for offset in range(1, nz):
        peer_z = lax.rem(my_z + offset, nz)
        pl.semaphore_signal(barrier, 1, device_id=row_peer(peer_z * 2 + my_core), device_id_type=mesh_kind)
    pl.semaphore_wait(barrier, nz)


def scatter_sum_row_kernel(nz, x_hbm, out_ref, own1, recv1, mid, recv2, sems):
    send1, got1, send2, got2, own_sem = sems
    mesh_kind = pl.DeviceIdType.MESH
    me = lax.axis_index("row")
    my_z = me // 2
    my_core = lax.rem(me, 2)
    other_core = 1 - my_core
    greet_row(my_z, my_core, nz)
    own = pltpu.make_async_copy(x_hbm.at[:, my_core], own1, own_sem.at[0])
    own.start()
    first = pltpu.make_async_remote_copy(
        src_ref=x_hbm.at[:, other_core], dst_ref=recv1,
        send_sem=send1.at[0], recv_sem=got1.at[0],
        device_id=row_peer(my_z * 2 + other_core), device_id_type=mesh_kind,
    )
    first.start()
    own.wait()
    first.wait_recv()
    for target in range(nz):
        mid[target] = (own1[target].astype(jnp.float32) + recv1[target].astype(jnp.float32)).astype(mid.dtype)
    sends = []
    for offset in range(1, nz):
        peer_z = lax.rem(my_z + offset, nz)
        copy = pltpu.make_async_remote_copy(
            src_ref=mid.at[peer_z], dst_ref=recv2.at[my_z],
            send_sem=send2.at[offset], recv_sem=got2.at[my_z],
            device_id=row_peer(peer_z * 2 + my_core), device_id_type=mesh_kind,
        )
        copy.start()
        sends.append(copy)
    total = mid[my_z].astype(jnp.float32)
    for offset in range(1, nz):
        source_z = lax.rem(my_z + nz - offset, nz)
        pltpu.make_async_remote_copy(
            src_ref=mid.at[source_z], dst_ref=recv2.at[source_z],
            send_sem=send2.at[offset], recv_sem=got2.at[source_z],
            device_id=row_peer(source_z * 2 + my_core), device_id_type=mesh_kind,
        ).wait_recv()
        total = total + recv2[source_z].astype(jnp.float32)
    out_ref[...] = total.astype(out_ref.dtype)
    first.wait_send()
    for copy in sends:
        copy.wait_send()


def scatter_sum_row(x, out_dtype, collective_id):
    n, rows, lanes = x.shape
    nz = n // 2
    return pl.pallas_call(
        functools.partial(scatter_sum_row_kernel, nz),
        out_shape=jax.ShapeDtypeStruct((rows, lanes), out_dtype),
        in_specs=[pl.BlockSpec(memory_space=pl.ANY)],
        out_specs=pl.BlockSpec(memory_space=pltpu.VMEM),
        scratch_shapes=[
            pltpu.VMEM((nz, rows, lanes), x.dtype),
            pltpu.VMEM((nz, rows, lanes), x.dtype),
            pltpu.VMEM((nz, rows, lanes), x.dtype),
            pltpu.VMEM((nz, rows, lanes), x.dtype),
            (
                pltpu.SemaphoreType.DMA((1,)),
                pltpu.SemaphoreType.DMA((1,)),
                pltpu.SemaphoreType.DMA((nz,)),
                pltpu.SemaphoreType.DMA((nz,)),
                pltpu.SemaphoreType.DMA((1,)),
            ),
        ],
        compiler_params=pltpu.CompilerParams(
            collective_id=collective_id, has_side_effects=True,
            vmem_limit_bytes=48 * 1024 * 1024,
        ),
        cost_estimate=pl.CostEstimate(
            flops=x.size, transcendentals=0, bytes_accessed=3 * x.size * x.dtype.itemsize
        ),
    )(x.reshape(nz, 2, rows, lanes))


def gather_row_kernel(nz, x_ref, out_ref, full, sems):
    send1, got1, send2, got2, own_sem = sems
    mesh_kind = pl.DeviceIdType.MESH
    me = lax.axis_index("row")
    my_z = me // 2
    my_core = lax.rem(me, 2)
    other_core = 1 - my_core
    greet_row(my_z, my_core, nz)
    own = pltpu.make_async_copy(x_ref, full.at[my_z, my_core], own_sem.at[0])
    own.start()
    sends = []
    for offset in range(1, nz):
        peer_z = lax.rem(my_z + offset, nz)
        copy = pltpu.make_async_remote_copy(
            src_ref=x_ref, dst_ref=full.at[my_z, my_core],
            send_sem=send1.at[offset], recv_sem=got1.at[my_z],
            device_id=row_peer(peer_z * 2 + my_core), device_id_type=mesh_kind,
        )
        copy.start()
        sends.append(copy)
    own.wait()
    for offset in range(1, nz):
        source_z = lax.rem(my_z + nz - offset, nz)
        pltpu.make_async_remote_copy(
            src_ref=x_ref, dst_ref=full.at[source_z, my_core],
            send_sem=send1.at[offset], recv_sem=got1.at[source_z],
            device_id=row_peer(source_z * 2 + my_core), device_id_type=mesh_kind,
        ).wait_recv()
    second = pltpu.make_async_remote_copy(
        src_ref=full.at[:, my_core], dst_ref=full.at[:, my_core],
        send_sem=send2.at[0], recv_sem=got2.at[0],
        device_id=row_peer(my_z * 2 + other_core), device_id_type=mesh_kind,
    )
    second.start()
    pltpu.make_async_remote_copy(
        src_ref=full.at[:, other_core], dst_ref=full.at[:, other_core],
        send_sem=send2.at[0], recv_sem=got2.at[0],
        device_id=row_peer(my_z * 2 + other_core), device_id_type=mesh_kind,
    ).wait_recv()
    for copy in sends:
        copy.wait_send()
    second.wait_send()
    out_ref[...] = full[...]


def gather_row(x, collective_id):
    rows, lanes = x.shape
    nz = lax.axis_size("row") // 2
    out = pl.pallas_call(
        functools.partial(gather_row_kernel, nz),
        out_shape=jax.ShapeDtypeStruct((nz, 2, rows, lanes), x.dtype),
        in_specs=[pl.BlockSpec(memory_space=pltpu.VMEM)],
        out_specs=pl.BlockSpec(memory_space=pltpu.VMEM),
        scratch_shapes=[
            pltpu.VMEM((nz, 2, rows, lanes), x.dtype),
            (
                pltpu.SemaphoreType.DMA((nz,)),
                pltpu.SemaphoreType.DMA((nz,)),
                pltpu.SemaphoreType.DMA((1,)),
                pltpu.SemaphoreType.DMA((1,)),
                pltpu.SemaphoreType.DMA((1,)),
            ),
        ],
        compiler_params=pltpu.CompilerParams(
            collective_id=collective_id, has_side_effects=True,
            vmem_limit_bytes=48 * 1024 * 1024,
        ),
        cost_estimate=pl.CostEstimate(
            flops=0, transcendentals=0, bytes_accessed=3 * 2 * nz * x.size * x.dtype.itemsize
        ),
    )(x)
    return out.reshape(2 * nz * rows, lanes)


def gather_all_2d_kernel(nx, ny, x_ref, out_ref, full, sems):
    send, got, own_sem = sems
    mesh_kind = pl.DeviceIdType.MESH
    me = lax.axis_index("col")
    my_y = me // nx
    my_x = lax.rem(me, nx)
    half = x_ref.shape[0] // 2
    lower = pl.ds(0, half)
    upper = pl.ds(half, half)

    barrier = pltpu.get_barrier_semaphore()
    for offset in range(1, nx):
        pl.semaphore_signal(barrier, 1, device_id=torus_peer(my_y, lax.rem(my_x + offset, nx), nx),
                            device_id_type=mesh_kind)
    for offset in range(1, ny):
        pl.semaphore_signal(barrier, 1, device_id=torus_peer(lax.rem(my_y + offset, ny), my_x, nx),
                            device_id_type=mesh_kind)
    pl.semaphore_wait(barrier, nx + ny - 2)

    own = pltpu.make_async_copy(x_ref, full.at[my_y, my_x], own_sem.at[0])
    own.start()
    sends = []
    for offset in range(1, nx):
        peer_x = lax.rem(my_x + offset, nx)
        copy = pltpu.make_async_remote_copy(
            src_ref=x_ref.at[lower], dst_ref=full.at[my_y, my_x, lower],
            send_sem=send.at[0, offset], recv_sem=got.at[0, my_x],
            device_id=torus_peer(my_y, peer_x, nx), device_id_type=mesh_kind,
        )
        copy.start()
        sends.append(copy)
    for offset in range(1, ny):
        peer_y = lax.rem(my_y + offset, ny)
        copy = pltpu.make_async_remote_copy(
            src_ref=x_ref.at[upper], dst_ref=full.at[my_y, my_x, upper],
            send_sem=send.at[1, offset], recv_sem=got.at[1, my_y],
            device_id=torus_peer(peer_y, my_x, nx), device_id_type=mesh_kind,
        )
        copy.start()
        sends.append(copy)
    own.wait()
    for offset in range(1, nx):
        source_x = lax.rem(my_x + nx - offset, nx)
        pltpu.make_async_remote_copy(
            src_ref=x_ref.at[lower], dst_ref=full.at[my_y, source_x, lower],
            send_sem=send.at[0, offset], recv_sem=got.at[0, source_x],
            device_id=torus_peer(my_y, source_x, nx), device_id_type=mesh_kind,
        ).wait_recv()
    for offset in range(1, ny):
        peer_y = lax.rem(my_y + offset, ny)
        copy = pltpu.make_async_remote_copy(
            src_ref=full.at[my_y, :, lower], dst_ref=full.at[my_y, :, lower],
            send_sem=send.at[2, offset], recv_sem=got.at[2, my_y],
            device_id=torus_peer(peer_y, my_x, nx), device_id_type=mesh_kind,
        )
        copy.start()
        sends.append(copy)
    for offset in range(1, ny):
        source_y = lax.rem(my_y + ny - offset, ny)
        pltpu.make_async_remote_copy(
            src_ref=x_ref.at[upper], dst_ref=full.at[source_y, my_x, upper],
            send_sem=send.at[1, offset], recv_sem=got.at[1, source_y],
            device_id=torus_peer(source_y, my_x, nx), device_id_type=mesh_kind,
        ).wait_recv()
    for offset in range(1, nx):
        peer_x = lax.rem(my_x + offset, nx)
        copy = pltpu.make_async_remote_copy(
            src_ref=full.at[:, my_x, upper], dst_ref=full.at[:, my_x, upper],
            send_sem=send.at[3, offset], recv_sem=got.at[3, my_x],
            device_id=torus_peer(my_y, peer_x, nx), device_id_type=mesh_kind,
        )
        copy.start()
        sends.append(copy)
    for offset in range(1, ny):
        source_y = lax.rem(my_y + ny - offset, ny)
        pltpu.make_async_remote_copy(
            src_ref=full.at[source_y, :, lower], dst_ref=full.at[source_y, :, lower],
            send_sem=send.at[2, offset], recv_sem=got.at[2, source_y],
            device_id=torus_peer(source_y, my_x, nx), device_id_type=mesh_kind,
        ).wait_recv()
    for offset in range(1, nx):
        source_x = lax.rem(my_x + nx - offset, nx)
        pltpu.make_async_remote_copy(
            src_ref=full.at[:, source_x, upper], dst_ref=full.at[:, source_x, upper],
            send_sem=send.at[3, offset], recv_sem=got.at[3, source_x],
            device_id=torus_peer(my_y, source_x, nx), device_id_type=mesh_kind,
        ).wait_recv()
    for copy in sends:
        copy.wait_send()
    out_ref[...] = full[...]


def gather_all_2d(x, nx, collective_id):
    rows, lanes = x.shape
    n = lax.axis_size("col")
    ny = n // nx
    side = max(nx, ny)
    out = pl.pallas_call(
        functools.partial(gather_all_2d_kernel, nx, ny),
        out_shape=jax.ShapeDtypeStruct((ny, nx, rows, lanes), x.dtype),
        in_specs=[pl.BlockSpec(memory_space=pltpu.VMEM)],
        out_specs=pl.BlockSpec(memory_space=pltpu.VMEM),
        scratch_shapes=[
            pltpu.VMEM((ny, nx, rows, lanes), x.dtype),
            (
                pltpu.SemaphoreType.DMA((4, side)),
                pltpu.SemaphoreType.DMA((4, side)),
                pltpu.SemaphoreType.DMA((1,)),
            ),
        ],
        compiler_params=pltpu.CompilerParams(
            collective_id=collective_id, has_side_effects=True,
            vmem_limit_bytes=48 * 1024 * 1024,
        ),
        cost_estimate=pl.CostEstimate(
            flops=0, transcendentals=0, bytes_accessed=3 * n * x.size * x.dtype.itemsize
        ),
    )(x)
    return out.reshape(n, rows, lanes)


def fused_sum_kernel(nr, nc, x_ref, out_ref, recv1, recv2, recv3, sems):
    send1, got1, send2, got2, send3, got3 = sems
    mesh_kind = pl.DeviceIdType.MESH
    my_r = lax.axis_index("row")
    my_c = lax.axis_index("col")
    barrier = pltpu.get_barrier_semaphore()
    for offset in range(1, nc):
        pl.semaphore_signal(barrier, 1, device_id=(my_r, lax.rem(my_c + offset, nc)),
                            device_id_type=mesh_kind)
    for offset in range(1, nr):
        pl.semaphore_signal(barrier, 1, device_id=(lax.rem(my_r + offset, nr), my_c),
                            device_id_type=mesh_kind)
    pl.semaphore_wait(barrier, nc + nr - 2)

    def exchange(peers, axis_count, src_of, dst, send, got, me_index):
        started = []
        for offset in range(1, axis_count):
            peer = lax.rem(me_index + offset, axis_count)
            copy = pltpu.make_async_remote_copy(
                src_ref=src_of(peer), dst_ref=dst.at[me_index],
                send_sem=send.at[offset], recv_sem=got.at[me_index],
                device_id=peers(peer), device_id_type=mesh_kind,
            )
            copy.start()
            started.append(copy)
        for offset in range(1, axis_count):
            source = lax.rem(me_index + axis_count - offset, axis_count)
            pltpu.make_async_remote_copy(
                src_ref=src_of(source), dst_ref=dst.at[source],
                send_sem=send.at[offset], recv_sem=got.at[source],
                device_id=peers(source), device_id_type=mesh_kind,
            ).wait_recv()
        return started

    along_col = lambda peer: (my_r, peer)
    along_row = lambda peer: (peer, my_c)
    recv1[my_c] = x_ref[my_c]
    sends = exchange(along_col, nc, lambda peer: x_ref.at[peer], recv1, send1, got1, my_c)
    part = recv1[0]
    for j in range(1, nc):
        part = part + recv1[j]
    recv2[my_r] = part
    sends += exchange(along_row, nr, lambda peer: recv2.at[my_r], recv2, send2, got2, my_r)
    total = recv2[0]
    for j in range(1, nr):
        total = total + recv2[j]
    recv3[my_c] = total
    sends += exchange(along_col, nc, lambda peer: recv3.at[my_c], recv3, send3, got3, my_c)
    out_ref[...] = recv3[...]
    for copy in sends:
        copy.wait_send()


def fused_sum(local, collective_id):
    nr = lax.axis_size("row")
    nc = lax.axis_size("col")
    height, width = local.shape
    part = height // nc
    out = pl.pallas_call(
        functools.partial(fused_sum_kernel, nr, nc),
        out_shape=jax.ShapeDtypeStruct((nc, part, width), local.dtype),
        in_specs=[pl.BlockSpec(memory_space=pltpu.VMEM)],
        out_specs=pl.BlockSpec(memory_space=pltpu.VMEM),
        scratch_shapes=[
            pltpu.VMEM((nc, part, width), local.dtype),
            pltpu.VMEM((nr, part, width), local.dtype),
            pltpu.VMEM((nc, part, width), local.dtype),
            (
                pltpu.SemaphoreType.DMA((nc,)),
                pltpu.SemaphoreType.DMA((nc,)),
                pltpu.SemaphoreType.DMA((nr,)),
                pltpu.SemaphoreType.DMA((nr,)),
                pltpu.SemaphoreType.DMA((nc,)),
                pltpu.SemaphoreType.DMA((nc,)),
            ),
        ],
        compiler_params=pltpu.CompilerParams(
            collective_id=collective_id, has_side_effects=True,
            vmem_limit_bytes=48 * 1024 * 1024,
        ),
        cost_estimate=pl.CostEstimate(
            flops=local.size, transcendentals=0, bytes_accessed=3 * local.size * 4
        ),
    )(local.reshape(nc, part, width))
    return out.reshape(height, width)


def gather_and_sum_kernel(nx, ny, nr, x_ref, w_ref, out_ref, wout_ref, full, recv1, recv2, recv3, sems):
    send, got, own_sem, wsend1, wgot1, wsend2, wgot2, wsend3, wgot3 = sems
    mesh_kind = pl.DeviceIdType.MESH
    nc = nx * ny
    me = lax.axis_index("col")
    my_r = lax.axis_index("row")
    my_y = me // nx
    my_x = lax.rem(me, nx)
    half = x_ref.shape[0] // 2
    lower = pl.ds(0, half)
    upper = pl.ds(half, half)
    along_col = lambda peer: (my_r, peer)
    along_row = lambda peer: (peer, me)

    barrier = pltpu.get_barrier_semaphore()
    for offset in range(1, nc):
        pl.semaphore_signal(barrier, 1, device_id=along_col(lax.rem(me + offset, nc)),
                            device_id_type=mesh_kind)
    for offset in range(1, nr):
        pl.semaphore_signal(barrier, 1, device_id=along_row(lax.rem(my_r + offset, nr)),
                            device_id_type=mesh_kind)
    pl.semaphore_wait(barrier, nc + nr - 2)

    def start_all(peers, count, me_index, src_of, dst, sem_send, sem_got):
        started = []
        for offset in range(1, count):
            peer = lax.rem(me_index + offset, count)
            copy = pltpu.make_async_remote_copy(
                src_ref=src_of(peer), dst_ref=dst.at[me_index],
                send_sem=sem_send.at[offset], recv_sem=sem_got.at[me_index],
                device_id=peers(peer), device_id_type=mesh_kind,
            )
            copy.start()
            started.append(copy)
        return started

    def wait_all(peers, count, me_index, src_of, dst, sem_send, sem_got):
        for offset in range(1, count):
            source = lax.rem(me_index + count - offset, count)
            pltpu.make_async_remote_copy(
                src_ref=src_of(source), dst_ref=dst.at[source],
                send_sem=sem_send.at[offset], recv_sem=sem_got.at[source],
                device_id=peers(source), device_id_type=mesh_kind,
            ).wait_recv()

    own = pltpu.make_async_copy(x_ref, full.at[my_y, my_x], own_sem.at[0])
    own.start()
    sends = []
    for offset in range(1, nx):
        peer_x = lax.rem(my_x + offset, nx)
        copy = pltpu.make_async_remote_copy(
            src_ref=x_ref.at[lower], dst_ref=full.at[my_y, my_x, lower],
            send_sem=send.at[0, offset], recv_sem=got.at[0, my_x],
            device_id=torus_peer(my_y, peer_x, nx), device_id_type=mesh_kind,
        )
        copy.start()
        sends.append(copy)
    for offset in range(1, ny):
        peer_y = lax.rem(my_y + offset, ny)
        copy = pltpu.make_async_remote_copy(
            src_ref=x_ref.at[upper], dst_ref=full.at[my_y, my_x, upper],
            send_sem=send.at[1, offset], recv_sem=got.at[1, my_y],
            device_id=torus_peer(peer_y, my_x, nx), device_id_type=mesh_kind,
        )
        copy.start()
        sends.append(copy)
    recv1[me] = w_ref[me]
    weight_src = lambda peer: w_ref.at[peer]
    sends += start_all(along_col, nc, me, weight_src, recv1, wsend1, wgot1)
    own.wait()
    for offset in range(1, nx):
        source_x = lax.rem(my_x + nx - offset, nx)
        pltpu.make_async_remote_copy(
            src_ref=x_ref.at[lower], dst_ref=full.at[my_y, source_x, lower],
            send_sem=send.at[0, offset], recv_sem=got.at[0, source_x],
            device_id=torus_peer(my_y, source_x, nx), device_id_type=mesh_kind,
        ).wait_recv()
    for offset in range(1, ny):
        peer_y = lax.rem(my_y + offset, ny)
        copy = pltpu.make_async_remote_copy(
            src_ref=full.at[my_y, :, lower], dst_ref=full.at[my_y, :, lower],
            send_sem=send.at[2, offset], recv_sem=got.at[2, my_y],
            device_id=torus_peer(peer_y, my_x, nx), device_id_type=mesh_kind,
        )
        copy.start()
        sends.append(copy)
    for offset in range(1, ny):
        source_y = lax.rem(my_y + ny - offset, ny)
        pltpu.make_async_remote_copy(
            src_ref=x_ref.at[upper], dst_ref=full.at[source_y, my_x, upper],
            send_sem=send.at[1, offset], recv_sem=got.at[1, source_y],
            device_id=torus_peer(source_y, my_x, nx), device_id_type=mesh_kind,
        ).wait_recv()
    for offset in range(1, nx):
        peer_x = lax.rem(my_x + offset, nx)
        copy = pltpu.make_async_remote_copy(
            src_ref=full.at[:, my_x, upper], dst_ref=full.at[:, my_x, upper],
            send_sem=send.at[3, offset], recv_sem=got.at[3, my_x],
            device_id=torus_peer(my_y, peer_x, nx), device_id_type=mesh_kind,
        )
        copy.start()
        sends.append(copy)

    wait_all(along_col, nc, me, weight_src, recv1, wsend1, wgot1)
    part = recv1[0]
    for j in range(1, nc):
        part = part + recv1[j]
    recv2[my_r] = part
    row_src = lambda peer: recv2.at[my_r]
    sends += start_all(along_row, nr, my_r, row_src, recv2, wsend2, wgot2)
    wait_all(along_row, nr, my_r, row_src, recv2, wsend2, wgot2)
    total = recv2[0]
    for j in range(1, nr):
        total = total + recv2[j]
    recv3[me] = total
    back_src = lambda peer: recv3.at[me]
    sends += start_all(along_col, nc, me, back_src, recv3, wsend3, wgot3)

    for offset in range(1, ny):
        source_y = lax.rem(my_y + ny - offset, ny)
        pltpu.make_async_remote_copy(
            src_ref=full.at[source_y, :, lower], dst_ref=full.at[source_y, :, lower],
            send_sem=send.at[2, offset], recv_sem=got.at[2, source_y],
            device_id=torus_peer(source_y, my_x, nx), device_id_type=mesh_kind,
        ).wait_recv()
    for offset in range(1, nx):
        source_x = lax.rem(my_x + nx - offset, nx)
        pltpu.make_async_remote_copy(
            src_ref=full.at[:, source_x, upper], dst_ref=full.at[:, source_x, upper],
            send_sem=send.at[3, offset], recv_sem=got.at[3, source_x],
            device_id=torus_peer(my_y, source_x, nx), device_id_type=mesh_kind,
        ).wait_recv()
    out_ref[...] = full[...]
    wait_all(along_col, nc, me, back_src, recv3, wsend3, wgot3)
    wout_ref[...] = recv3[...]
    for copy in sends:
        copy.wait_send()


def gather_and_sum(x, local, nx, collective_id):
    rows, lanes = x.shape
    nc = lax.axis_size("col")
    nr = lax.axis_size("row")
    ny = nc // nx
    side = max(nx, ny)
    height, width = local.shape
    part = height // nc
    out, summed = pl.pallas_call(
        functools.partial(gather_and_sum_kernel, nx, ny, nr),
        out_shape=(
            jax.ShapeDtypeStruct((ny, nx, rows, lanes), x.dtype),
            jax.ShapeDtypeStruct((nc, part, width), local.dtype),
        ),
        in_specs=[pl.BlockSpec(memory_space=pltpu.VMEM)] * 2,
        out_specs=(pl.BlockSpec(memory_space=pltpu.VMEM),) * 2,
        scratch_shapes=[
            pltpu.VMEM((ny, nx, rows, lanes), x.dtype),
            pltpu.VMEM((nc, part, width), local.dtype),
            pltpu.VMEM((nr, part, width), local.dtype),
            pltpu.VMEM((nc, part, width), local.dtype),
            (
                pltpu.SemaphoreType.DMA((4, side)),
                pltpu.SemaphoreType.DMA((4, side)),
                pltpu.SemaphoreType.DMA((1,)),
                pltpu.SemaphoreType.DMA((nc,)),
                pltpu.SemaphoreType.DMA((nc,)),
                pltpu.SemaphoreType.DMA((nr,)),
                pltpu.SemaphoreType.DMA((nr,)),
                pltpu.SemaphoreType.DMA((nc,)),
                pltpu.SemaphoreType.DMA((nc,)),
            ),
        ],
        compiler_params=pltpu.CompilerParams(
            collective_id=collective_id, has_side_effects=True,
            vmem_limit_bytes=48 * 1024 * 1024,
        ),
        cost_estimate=pl.CostEstimate(
            flops=local.size, transcendentals=0,
            bytes_accessed=3 * nc * x.size * x.dtype.itemsize + 3 * local.size * 4,
        ),
    )(x, local.reshape(nc, part, width))
    return out.reshape(nc, rows, lanes), summed.reshape(height, width)


def all_sum(local, collective_base):
    row_count = lax.axis_size("row")
    col_count = lax.axis_size("col")
    height, width = local.shape
    by_col = scatter_sum(
        local.reshape(col_count, height // col_count, width), "col", "row", jnp.float32,
        collective_base,
    )
    part = height // col_count
    by_row = scatter_sum(
        by_col.reshape(row_count, part // row_count, width), "row", "col", jnp.float32,
        collective_base + 1,
    )
    back_row = gather_all(by_row, "row", "col", row_count, collective_base + 2)
    back_col = gather_all(back_row.reshape(part, width), "col", "row", col_count, collective_base + 3)
    return back_col.reshape(height, width)


def activation(aggregated, weight, cot_rows):
    hidden = jnp.dot(aggregated, weight, preferred_element_type=jnp.float32)
    sigmoid_value = jax.nn.sigmoid(hidden)
    output = (hidden * sigmoid_value).astype(jnp.bfloat16)
    silu_slope = sigmoid_value * (1.0 + hidden * (1.0 - sigmoid_value))
    hidden_grad = (cot_rows.astype(jnp.float32) * silu_slope).astype(jnp.bfloat16)
    return (output, hidden_grad)


def per_device(tile_values, tile_rows, tile_cols, tile_count, features, weight, cotangent):
    slot_total = tile_values.shape[2]
    tile_edge = tile_values.shape[3]
    tile_block = tile_values.reshape(slot_total, tile_edge, tile_edge)
    row_index = tile_rows.reshape(slot_total)
    col_index = tile_cols.reshape(slot_total)
    live_count = tile_count.reshape(1)
    own_rows = features.shape[0]
    feat_width = features.shape[1]
    row_count = lax.axis_size("row")
    col_count = lax.axis_size("col")
    row_tiles = col_count * own_rows // tile_edge
    col_tiles = row_count * own_rows // tile_edge
    column_block = gather_row(features, 8)
    source = column_block.reshape(col_tiles, tile_edge, feat_width)
    partial_rows = sparse_product(
        tile_block, row_index, col_index, live_count, source, row_tiles, False
    )
    partial_flat = partial_rows.reshape(row_tiles * tile_edge, feat_width)
    node_total = row_count * col_count * own_rows
    aggregated = scatter_sum_2d(
        partial_rows.reshape(col_count, own_rows, feat_width), TORUS_X, jnp.bfloat16, 0
    )
    output, hidden_grad = activation(aggregated, weight, cotangent)
    own_grad = lax.dot_general(
        hidden_grad, weight, (((1,), (1,)), ((), ())), preferred_element_type=jnp.float32
    ).astype(jnp.bfloat16)
    local_grad = lax.dot_general(
        aggregated, hidden_grad, (((0,), (0,)), ((), ())), preferred_element_type=jnp.float32
    )
    row_block, summed_grad = gather_and_sum(own_grad, local_grad, TORUS_X, 7)
    weight_grad = summed_grad * (1.0 / math.sqrt(node_total))
    source_back = row_block.reshape(row_tiles, tile_edge, feat_width)
    partial_cols = sparse_product(
        tile_block, col_index, row_index, live_count, source_back, col_tiles, True
    )
    input_grad = scatter_sum_row(
        partial_cols.reshape(row_count, own_rows, feat_width), jnp.float32, 9
    )
    return (output, weight_grad, input_grad)


def solution(mesh):
    placed = (
        P("row", "col", None, None, None),
        P("row", "col", None),
        P("row", "col", None),
        P("row", "col"),
        P(("row", "col"), None),
        P(),
        P(("row", "col"), None),
    )
    return jax.shard_map(
        per_device,
        mesh=mesh,
        in_specs=placed,
        out_specs=(P(("row", "col"), None), P(), P(("row", "col"), None)),
        check_vma=False,
    )
```

```python
import functools
import math

import jax
import jax.numpy as jnp
from jax import lax
from jax.experimental import pallas as pl
from jax.experimental.pallas import tpu as pltpu
from jax.sharding import PartitionSpec as P

SLOTS_PER_STEP = 32
UNROLL = 32
TORUS_X = 4


def spmm_kernel(transpose, acc_index, src_index, count_ref, tiles_ref, src_ref, out_ref, acc_ref):
    step = pl.program_id(0)
    per_step = tiles_ref.shape[0]
    live = count_ref[0]
    acc_last = acc_ref.shape[0] - 1
    src_last = src_ref.shape[0] - 1

    @pl.when(step == 0)
    def _():
        acc_ref[...] = jnp.zeros_like(acc_ref)

    def one_slot(k, carry):
        slot = step * per_step + k
        target = jnp.clip(acc_index[slot], 0, acc_last)
        picked = jnp.clip(src_index[slot], 0, src_last)
        tile = tiles_ref[k]
        tile = jnp.where(slot < live, tile, jnp.zeros_like(tile))
        block = src_ref[picked]
        if transpose:
            product = lax.dot_general(
                tile, block, (((0,), (0,)), ((), ())), preferred_element_type=jnp.float32
            )
        else:
            product = jnp.dot(tile, block, preferred_element_type=jnp.float32)
        acc_ref[target] += product
        return carry

    lax.fori_loop(0, per_step, one_slot, 0, unroll=UNROLL)

    @pl.when(step == pl.num_programs(0) - 1)
    def _():
        out_ref[...] = acc_ref[...].astype(out_ref.dtype)


def sparse_product(tile_block, acc_index, src_index, live_count, source, segments, transpose):
    slot_total, tile_edge, _ = tile_block.shape
    feat_width = source.shape[2]
    per_step = min(SLOTS_PER_STEP, slot_total)
    steps = slot_total // per_step

    def tile_map(step, acc_ref, src_ref, count_ref):
        last_live = jnp.maximum(count_ref[0] - 1, 0) // per_step
        return (jnp.minimum(step, last_live), 0, 0)

    grid_spec = pltpu.PrefetchScalarGridSpec(
        num_scalar_prefetch=3,
        grid=(steps,),
        in_specs=[
            pl.BlockSpec((per_step, tile_edge, tile_edge), tile_map),
            pl.BlockSpec(source.shape, lambda step, *_: (0, 0, 0)),
        ],
        out_specs=pl.BlockSpec((segments, tile_edge, feat_width), lambda step, *_: (0, 0, 0)),
        scratch_shapes=[pltpu.VMEM((segments, tile_edge, feat_width), jnp.float32)],
    )
    flops = 2 * slot_total * tile_edge * tile_edge * feat_width
    bytes_accessed = (
        tile_block.size * 2 + source.size * 2 + segments * tile_edge * feat_width * 2
    )
    return pl.pallas_call(
        functools.partial(spmm_kernel, transpose),
        out_shape=jax.ShapeDtypeStruct((segments, tile_edge, feat_width), jnp.bfloat16),
        grid_spec=grid_spec,
        compiler_params=pltpu.CompilerParams(
            dimension_semantics=("arbitrary",), vmem_limit_bytes=56 * 1024 * 1024
        ),
        cost_estimate=pl.CostEstimate(
            flops=flops, transcendentals=0, bytes_accessed=bytes_accessed
        ),
    )(acc_index, src_index, live_count, tile_block, source)


def peer_id(axis, other_axis, peer):
    if axis == "row":
        return (peer, lax.axis_index(other_axis))
    return (lax.axis_index(other_axis), peer)


def greet_all(axis, other_axis, n, me):
    barrier = pltpu.get_barrier_semaphore()
    for offset in range(1, n):
        peer = lax.rem(me + offset, n)
        pl.semaphore_signal(
            barrier, 1, device_id=peer_id(axis, other_axis, peer),
            device_id_type=pl.DeviceIdType.MESH,
        )
    pl.semaphore_wait(barrier, n - 1)


def scatter_sum_kernel(axis, other_axis, n, x_hbm, out_ref, recv, send_sems, recv_sems, own_sem):
    me = lax.axis_index(axis)
    greet_all(axis, other_axis, n, me)
    own = pltpu.make_async_copy(x_hbm.at[me], recv.at[me], own_sem)
    own.start()
    sends = []
    for offset in range(1, n):
        peer = lax.rem(me + offset, n)
        copy = pltpu.make_async_remote_copy(
            src_ref=x_hbm.at[peer],
            dst_ref=recv.at[me],
            send_sem=send_sems.at[offset],
            recv_sem=recv_sems.at[me],
            device_id=peer_id(axis, other_axis, peer),
            device_id_type=pl.DeviceIdType.MESH,
        )
        copy.start()
        sends.append(copy)
    own.wait()
    for offset in range(1, n):
        source = lax.rem(me + n - offset, n)
        pltpu.make_async_remote_copy(
            src_ref=x_hbm.at[source],
            dst_ref=recv.at[source],
            send_sem=send_sems.at[offset],
            recv_sem=recv_sems.at[source],
            device_id=peer_id(axis, other_axis, source),
            device_id_type=pl.DeviceIdType.MESH,
        ).wait_recv()
    total = recv[0].astype(jnp.float32)
    for j in range(1, n):
        total = total + recv[j].astype(jnp.float32)
    out_ref[...] = total.astype(out_ref.dtype)
    for copy in sends:
        copy.wait_send()


def scatter_sum(x, axis, other_axis, out_dtype, collective_id):
    n, rows, lanes = x.shape
    return pl.pallas_call(
        functools.partial(scatter_sum_kernel, axis, other_axis, n),
        out_shape=jax.ShapeDtypeStruct((rows, lanes), out_dtype),
        in_specs=[pl.BlockSpec(memory_space=pl.ANY)],
        out_specs=pl.BlockSpec(memory_space=pltpu.VMEM),
        scratch_shapes=[
            pltpu.VMEM((n, rows, lanes), x.dtype),
            pltpu.SemaphoreType.DMA((n,)),
            pltpu.SemaphoreType.DMA((n,)),
            pltpu.SemaphoreType.DMA(()),
        ],
        compiler_params=pltpu.CompilerParams(
            collective_id=collective_id, has_side_effects=True,
            vmem_limit_bytes=48 * 1024 * 1024,
        ),
        cost_estimate=pl.CostEstimate(
            flops=x.size, transcendentals=0, bytes_accessed=3 * x.size * x.dtype.itemsize
        ),
    )(x)


def gather_all_kernel(axis, other_axis, n, x_ref, out_ref, recv, send_sems, recv_sems):
    me = lax.axis_index(axis)
    recv[me] = x_ref[...]
    greet_all(axis, other_axis, n, me)
    sends = []
    for offset in range(1, n):
        peer = lax.rem(me + offset, n)
        copy = pltpu.make_async_remote_copy(
            src_ref=x_ref,
            dst_ref=recv.at[me],
            send_sem=send_sems.at[offset],
            recv_sem=recv_sems.at[me],
            device_id=peer_id(axis, other_axis, peer),
            device_id_type=pl.DeviceIdType.MESH,
        )
        copy.start()
        sends.append(copy)
    for offset in range(1, n):
        source = lax.rem(me + n - offset, n)
        pltpu.make_async_remote_copy(
            src_ref=x_ref,
            dst_ref=recv.at[source],
            send_sem=send_sems.at[offset],
            recv_sem=recv_sems.at[source],
            device_id=peer_id(axis, other_axis, source),
            device_id_type=pl.DeviceIdType.MESH,
        ).wait_recv()
    out_ref[...] = recv[...]
    for copy in sends:
        copy.wait_send()


def gather_all(x, axis, other_axis, n, collective_id):
    rows, lanes = x.shape
    return pl.pallas_call(
        functools.partial(gather_all_kernel, axis, other_axis, n),
        out_shape=jax.ShapeDtypeStruct((n, rows, lanes), x.dtype),
        in_specs=[pl.BlockSpec(memory_space=pltpu.VMEM)],
        out_specs=pl.BlockSpec(memory_space=pltpu.VMEM),
        scratch_shapes=[
            pltpu.VMEM((n, rows, lanes), x.dtype),
            pltpu.SemaphoreType.DMA((n,)),
            pltpu.SemaphoreType.DMA((n,)),
        ],
        compiler_params=pltpu.CompilerParams(
            collective_id=collective_id, has_side_effects=True,
            vmem_limit_bytes=48 * 1024 * 1024,
        ),
        cost_estimate=pl.CostEstimate(
            flops=0, transcendentals=0, bytes_accessed=3 * n * x.size * x.dtype.itemsize
        ),
    )(x)


def torus_peer(y, x, nx):
    return (lax.axis_index("row"), y * nx + x)


def scatter_sum_2d_kernel(nx, ny, x_hbm, out_ref, recv1, mid, recv2, sems):
    send1, got1, send2, got2, own_sems = sems
    me = lax.axis_index("col")
    my_y = me // nx
    my_x = lax.rem(me, nx)
    half = x_hbm.shape[2] // 2
    lower = pl.ds(0, half)
    upper = pl.ds(half, half)
    mesh_kind = pl.DeviceIdType.MESH

    barrier = pltpu.get_barrier_semaphore()
    for offset in range(1, nx):
        pl.semaphore_signal(barrier, 1, device_id=torus_peer(my_y, lax.rem(my_x + offset, nx), nx),
                            device_id_type=mesh_kind)
    for offset in range(1, ny):
        pl.semaphore_signal(barrier, 1, device_id=torus_peer(lax.rem(my_y + offset, ny), my_x, nx),
                            device_id_type=mesh_kind)
    pl.semaphore_wait(barrier, nx + ny - 2)

    own_a = pltpu.make_async_copy(x_hbm.at[:, my_x, lower], recv1.at[0, my_x], own_sems.at[0])
    own_b = pltpu.make_async_copy(x_hbm.at[my_y, :, upper], recv1.at[1, my_y], own_sems.at[1])
    own_a.start()
    own_b.start()
    sends = []
    for offset in range(1, nx):
        peer_x = lax.rem(my_x + offset, nx)
        copy = pltpu.make_async_remote_copy(
            src_ref=x_hbm.at[:, peer_x, lower], dst_ref=recv1.at[0, my_x],
            send_sem=send1.at[0, offset], recv_sem=got1.at[0, my_x],
            device_id=torus_peer(my_y, peer_x, nx), device_id_type=mesh_kind,
        )
        copy.start()
        sends.append(copy)
    for offset in range(1, ny):
        peer_y = lax.rem(my_y + offset, ny)
        copy = pltpu.make_async_remote_copy(
            src_ref=x_hbm.at[peer_y, :, upper], dst_ref=recv1.at[1, my_y],
            send_sem=send1.at[1, offset], recv_sem=got1.at[1, my_y],
            device_id=torus_peer(peer_y, my_x, nx), device_id_type=mesh_kind,
        )
        copy.start()
        sends.append(copy)
    own_a.wait()
    own_b.wait()
    for offset in range(1, nx):
        source_x = lax.rem(my_x + nx - offset, nx)
        pltpu.make_async_remote_copy(
            src_ref=x_hbm.at[:, source_x, lower], dst_ref=recv1.at[0, source_x],
            send_sem=send1.at[0, offset], recv_sem=got1.at[0, source_x],
            device_id=torus_peer(my_y, source_x, nx), device_id_type=mesh_kind,
        ).wait_recv()

    def add_up(stack):
        total = stack[0].astype(jnp.float32)
        for j in range(1, stack.shape[0]):
            total = total + stack[j].astype(jnp.float32)
        return total

    for target in range(ny):
        mid[0, target] = add_up(recv1[0, :, target]).astype(mid.dtype)
    recv2[0, my_y] = mid[0, my_y]

    for offset in range(1, ny):
        peer_y = lax.rem(my_y + offset, ny)
        copy = pltpu.make_async_remote_copy(
            src_ref=mid.at[0, peer_y], dst_ref=recv2.at[0, my_y],
            send_sem=send2.at[0, offset], recv_sem=got2.at[0, my_y],
            device_id=torus_peer(peer_y, my_x, nx), device_id_type=mesh_kind,
        )
        copy.start()
        sends.append(copy)
    for offset in range(1, ny):
        source_y = lax.rem(my_y + ny - offset, ny)
        pltpu.make_async_remote_copy(
            src_ref=x_hbm.at[source_y, :, upper], dst_ref=recv1.at[1, source_y],
            send_sem=send1.at[1, offset], recv_sem=got1.at[1, source_y],
            device_id=torus_peer(source_y, my_x, nx), device_id_type=mesh_kind,
        ).wait_recv()
    for target in range(nx):
        mid[1, target] = add_up(recv1[1, :, target]).astype(mid.dtype)
    recv2[1, my_x] = mid[1, my_x]
    for offset in range(1, nx):
        peer_x = lax.rem(my_x + offset, nx)
        copy = pltpu.make_async_remote_copy(
            src_ref=mid.at[1, peer_x], dst_ref=recv2.at[1, my_x],
            send_sem=send2.at[1, offset], recv_sem=got2.at[1, my_x],
            device_id=torus_peer(my_y, peer_x, nx), device_id_type=mesh_kind,
        )
        copy.start()
        sends.append(copy)
    for offset in range(1, ny):
        source_y = lax.rem(my_y + ny - offset, ny)
        pltpu.make_async_remote_copy(
            src_ref=mid.at[0, source_y], dst_ref=recv2.at[0, source_y],
            send_sem=send2.at[0, offset], recv_sem=got2.at[0, source_y],
            device_id=torus_peer(source_y, my_x, nx), device_id_type=mesh_kind,
        ).wait_recv()
    out_ref[lower] = add_up(recv2[0]).astype(out_ref.dtype)
    for offset in range(1, nx):
        source_x = lax.rem(my_x + nx - offset, nx)
        pltpu.make_async_remote_copy(
            src_ref=mid.at[1, source_x], dst_ref=recv2.at[1, source_x],
            send_sem=send2.at[1, offset], recv_sem=got2.at[1, source_x],
            device_id=torus_peer(my_y, source_x, nx), device_id_type=mesh_kind,
        ).wait_recv()
    out_ref[upper] = add_up(recv2[1]).astype(out_ref.dtype)
    for copy in sends:
        copy.wait_send()


def scatter_sum_2d(x, nx, out_dtype, collective_id):
    n, rows, lanes = x.shape
    ny = n // nx
    half = rows // 2
    side = max(nx, ny)
    return pl.pallas_call(
        functools.partial(scatter_sum_2d_kernel, nx, ny),
        out_shape=jax.ShapeDtypeStruct((rows, lanes), out_dtype),
        in_specs=[pl.BlockSpec(memory_space=pl.ANY)],
        out_specs=pl.BlockSpec(memory_space=pltpu.VMEM),
        scratch_shapes=[
            pltpu.VMEM((2, side, side, half, lanes), x.dtype),
            pltpu.VMEM((2, side, half, lanes), x.dtype),
            pltpu.VMEM((2, side, half, lanes), x.dtype),
            (
                pltpu.SemaphoreType.DMA((2, side)),
                pltpu.SemaphoreType.DMA((2, side)),
                pltpu.SemaphoreType.DMA((2, side)),
                pltpu.SemaphoreType.DMA((2, side)),
                pltpu.SemaphoreType.DMA((2,)),
            ),
        ],
        compiler_params=pltpu.CompilerParams(
            collective_id=collective_id, has_side_effects=True,
            vmem_limit_bytes=48 * 1024 * 1024,
        ),
        cost_estimate=pl.CostEstimate(
            flops=x.size, transcendentals=0, bytes_accessed=3 * x.size * x.dtype.itemsize
        ),
    )(x.reshape(ny, nx, rows, lanes))


def row_peer(index):
    return (index, lax.axis_index("col"))


def greet_row(my_z, my_core, nz):
    barrier = pltpu.get_barrier_semaphore()
    mesh_kind = pl.DeviceIdType.MESH
    pl.semaphore_signal(barrier, 1, device_id=row_peer(my_z * 2 + 1 - my_core), device_id_type=mesh_kind)
    for offset in range(1, nz):
        peer_z = lax.rem(my_z + offset, nz)
        pl.semaphore_signal(barrier, 1, device_id=row_peer(peer_z * 2 + my_core), device_id_type=mesh_kind)
    pl.semaphore_wait(barrier, nz)


def scatter_sum_row_kernel(nz, x_hbm, out_ref, own1, recv1, mid, recv2, sems):
    send1, got1, send2, got2, own_sem = sems
    mesh_kind = pl.DeviceIdType.MESH
    me = lax.axis_index("row")
    my_z = me // 2
    my_core = lax.rem(me, 2)
    other_core = 1 - my_core
    greet_row(my_z, my_core, nz)
    own = pltpu.make_async_copy(x_hbm.at[:, my_core], own1, own_sem.at[0])
    own.start()
    first = pltpu.make_async_remote_copy(
        src_ref=x_hbm.at[:, other_core], dst_ref=recv1,
        send_sem=send1.at[0], recv_sem=got1.at[0],
        device_id=row_peer(my_z * 2 + other_core), device_id_type=mesh_kind,
    )
    first.start()
    own.wait()
    first.wait_recv()
    for target in range(nz):
        mid[target] = (own1[target].astype(jnp.float32) + recv1[target].astype(jnp.float32)).astype(mid.dtype)
    sends = []
    for offset in range(1, nz):
        peer_z = lax.rem(my_z + offset, nz)
        copy = pltpu.make_async_remote_copy(
            src_ref=mid.at[peer_z], dst_ref=recv2.at[my_z],
            send_sem=send2.at[offset], recv_sem=got2.at[my_z],
            device_id=row_peer(peer_z * 2 + my_core), device_id_type=mesh_kind,
        )
        copy.start()
        sends.append(copy)
    total = mid[my_z].astype(jnp.float32)
    for offset in range(1, nz):
        source_z = lax.rem(my_z + nz - offset, nz)
        pltpu.make_async_remote_copy(
            src_ref=mid.at[source_z], dst_ref=recv2.at[source_z],
            send_sem=send2.at[offset], recv_sem=got2.at[source_z],
            device_id=row_peer(source_z * 2 + my_core), device_id_type=mesh_kind,
        ).wait_recv()
        total = total + recv2[source_z].astype(jnp.float32)
    out_ref[...] = total.astype(out_ref.dtype)
    first.wait_send()
    for copy in sends:
        copy.wait_send()


def scatter_sum_row(x, out_dtype, collective_id):
    n, rows, lanes = x.shape
    nz = n // 2
    return pl.pallas_call(
        functools.partial(scatter_sum_row_kernel, nz),
        out_shape=jax.ShapeDtypeStruct((rows, lanes), out_dtype),
        in_specs=[pl.BlockSpec(memory_space=pl.ANY)],
        out_specs=pl.BlockSpec(memory_space=pltpu.VMEM),
        scratch_shapes=[
            pltpu.VMEM((nz, rows, lanes), x.dtype),
            pltpu.VMEM((nz, rows, lanes), x.dtype),
            pltpu.VMEM((nz, rows, lanes), x.dtype),
            pltpu.VMEM((nz, rows, lanes), x.dtype),
            (
                pltpu.SemaphoreType.DMA((1,)),
                pltpu.SemaphoreType.DMA((1,)),
                pltpu.SemaphoreType.DMA((nz,)),
                pltpu.SemaphoreType.DMA((nz,)),
                pltpu.SemaphoreType.DMA((1,)),
            ),
        ],
        compiler_params=pltpu.CompilerParams(
            collective_id=collective_id, has_side_effects=True,
            vmem_limit_bytes=48 * 1024 * 1024,
        ),
        cost_estimate=pl.CostEstimate(
            flops=x.size, transcendentals=0, bytes_accessed=3 * x.size * x.dtype.itemsize
        ),
    )(x.reshape(nz, 2, rows, lanes))


def gather_row_kernel(nz, x_ref, out_ref, full, sems):
    send1, got1, send2, got2, own_sem = sems
    mesh_kind = pl.DeviceIdType.MESH
    me = lax.axis_index("row")
    my_z = me // 2
    my_core = lax.rem(me, 2)
    other_core = 1 - my_core
    greet_row(my_z, my_core, nz)
    own = pltpu.make_async_copy(x_ref, full.at[my_z, my_core], own_sem.at[0])
    own.start()
    sends = []
    for offset in range(1, nz):
        peer_z = lax.rem(my_z + offset, nz)
        copy = pltpu.make_async_remote_copy(
            src_ref=x_ref, dst_ref=full.at[my_z, my_core],
            send_sem=send1.at[offset], recv_sem=got1.at[my_z],
            device_id=row_peer(peer_z * 2 + my_core), device_id_type=mesh_kind,
        )
        copy.start()
        sends.append(copy)
    own.wait()
    for offset in range(1, nz):
        source_z = lax.rem(my_z + nz - offset, nz)
        pltpu.make_async_remote_copy(
            src_ref=x_ref, dst_ref=full.at[source_z, my_core],
            send_sem=send1.at[offset], recv_sem=got1.at[source_z],
            device_id=row_peer(source_z * 2 + my_core), device_id_type=mesh_kind,
        ).wait_recv()
    second = pltpu.make_async_remote_copy(
        src_ref=full.at[:, my_core], dst_ref=full.at[:, my_core],
        send_sem=send2.at[0], recv_sem=got2.at[0],
        device_id=row_peer(my_z * 2 + other_core), device_id_type=mesh_kind,
    )
    second.start()
    pltpu.make_async_remote_copy(
        src_ref=full.at[:, other_core], dst_ref=full.at[:, other_core],
        send_sem=send2.at[0], recv_sem=got2.at[0],
        device_id=row_peer(my_z * 2 + other_core), device_id_type=mesh_kind,
    ).wait_recv()
    for copy in sends:
        copy.wait_send()
    second.wait_send()
    out_ref[...] = full[...]


def gather_row(x, collective_id):
    rows, lanes = x.shape
    nz = lax.axis_size("row") // 2
    out = pl.pallas_call(
        functools.partial(gather_row_kernel, nz),
        out_shape=jax.ShapeDtypeStruct((nz, 2, rows, lanes), x.dtype),
        in_specs=[pl.BlockSpec(memory_space=pltpu.VMEM)],
        out_specs=pl.BlockSpec(memory_space=pltpu.VMEM),
        scratch_shapes=[
            pltpu.VMEM((nz, 2, rows, lanes), x.dtype),
            (
                pltpu.SemaphoreType.DMA((nz,)),
                pltpu.SemaphoreType.DMA((nz,)),
                pltpu.SemaphoreType.DMA((1,)),
                pltpu.SemaphoreType.DMA((1,)),
                pltpu.SemaphoreType.DMA((1,)),
            ),
        ],
        compiler_params=pltpu.CompilerParams(
            collective_id=collective_id, has_side_effects=True,
            vmem_limit_bytes=48 * 1024 * 1024,
        ),
        cost_estimate=pl.CostEstimate(
            flops=0, transcendentals=0, bytes_accessed=3 * 2 * nz * x.size * x.dtype.itemsize
        ),
    )(x)
    return out.reshape(2 * nz * rows, lanes)


def gather_all_2d_kernel(nx, ny, x_ref, out_ref, full, sems):
    send, got, own_sem = sems
    mesh_kind = pl.DeviceIdType.MESH
    me = lax.axis_index("col")
    my_y = me // nx
    my_x = lax.rem(me, nx)
    half = x_ref.shape[0] // 2
    lower = pl.ds(0, half)
    upper = pl.ds(half, half)

    barrier = pltpu.get_barrier_semaphore()
    for offset in range(1, nx):
        pl.semaphore_signal(barrier, 1, device_id=torus_peer(my_y, lax.rem(my_x + offset, nx), nx),
                            device_id_type=mesh_kind)
    for offset in range(1, ny):
        pl.semaphore_signal(barrier, 1, device_id=torus_peer(lax.rem(my_y + offset, ny), my_x, nx),
                            device_id_type=mesh_kind)
    pl.semaphore_wait(barrier, nx + ny - 2)

    own = pltpu.make_async_copy(x_ref, full.at[my_y, my_x], own_sem.at[0])
    own.start()
    sends = []
    for offset in range(1, nx):
        peer_x = lax.rem(my_x + offset, nx)
        copy = pltpu.make_async_remote_copy(
            src_ref=x_ref.at[lower], dst_ref=full.at[my_y, my_x, lower],
            send_sem=send.at[0, offset], recv_sem=got.at[0, my_x],
            device_id=torus_peer(my_y, peer_x, nx), device_id_type=mesh_kind,
        )
        copy.start()
        sends.append(copy)
    for offset in range(1, ny):
        peer_y = lax.rem(my_y + offset, ny)
        copy = pltpu.make_async_remote_copy(
            src_ref=x_ref.at[upper], dst_ref=full.at[my_y, my_x, upper],
            send_sem=send.at[1, offset], recv_sem=got.at[1, my_y],
            device_id=torus_peer(peer_y, my_x, nx), device_id_type=mesh_kind,
        )
        copy.start()
        sends.append(copy)
    own.wait()
    for offset in range(1, nx):
        source_x = lax.rem(my_x + nx - offset, nx)
        pltpu.make_async_remote_copy(
            src_ref=x_ref.at[lower], dst_ref=full.at[my_y, source_x, lower],
            send_sem=send.at[0, offset], recv_sem=got.at[0, source_x],
            device_id=torus_peer(my_y, source_x, nx), device_id_type=mesh_kind,
        ).wait_recv()
    for offset in range(1, ny):
        peer_y = lax.rem(my_y + offset, ny)
        copy = pltpu.make_async_remote_copy(
            src_ref=full.at[my_y, :, lower], dst_ref=full.at[my_y, :, lower],
            send_sem=send.at[2, offset], recv_sem=got.at[2, my_y],
            device_id=torus_peer(peer_y, my_x, nx), device_id_type=mesh_kind,
        )
        copy.start()
        sends.append(copy)
    for offset in range(1, ny):
        source_y = lax.rem(my_y + ny - offset, ny)
        pltpu.make_async_remote_copy(
            src_ref=x_ref.at[upper], dst_ref=full.at[source_y, my_x, upper],
            send_sem=send.at[1, offset], recv_sem=got.at[1, source_y],
            device_id=torus_peer(source_y, my_x, nx), device_id_type=mesh_kind,
        ).wait_recv()
    for offset in range(1, nx):
        peer_x = lax.rem(my_x + offset, nx)
        copy = pltpu.make_async_remote_copy(
            src_ref=full.at[:, my_x, upper], dst_ref=full.at[:, my_x, upper],
            send_sem=send.at[3, offset], recv_sem=got.at[3, my_x],
            device_id=torus_peer(my_y, peer_x, nx), device_id_type=mesh_kind,
        )
        copy.start()
        sends.append(copy)
    for offset in range(1, ny):
        source_y = lax.rem(my_y + ny - offset, ny)
        pltpu.make_async_remote_copy(
            src_ref=full.at[source_y, :, lower], dst_ref=full.at[source_y, :, lower],
            send_sem=send.at[2, offset], recv_sem=got.at[2, source_y],
            device_id=torus_peer(source_y, my_x, nx), device_id_type=mesh_kind,
        ).wait_recv()
    for offset in range(1, nx):
        source_x = lax.rem(my_x + nx - offset, nx)
        pltpu.make_async_remote_copy(
            src_ref=full.at[:, source_x, upper], dst_ref=full.at[:, source_x, upper],
            send_sem=send.at[3, offset], recv_sem=got.at[3, source_x],
            device_id=torus_peer(my_y, source_x, nx), device_id_type=mesh_kind,
        ).wait_recv()
    for copy in sends:
        copy.wait_send()
    out_ref[...] = full[...]


def gather_all_2d(x, nx, collective_id):
    rows, lanes = x.shape
    n = lax.axis_size("col")
    ny = n // nx
    side = max(nx, ny)
    out = pl.pallas_call(
        functools.partial(gather_all_2d_kernel, nx, ny),
        out_shape=jax.ShapeDtypeStruct((ny, nx, rows, lanes), x.dtype),
        in_specs=[pl.BlockSpec(memory_space=pltpu.VMEM)],
        out_specs=pl.BlockSpec(memory_space=pltpu.VMEM),
        scratch_shapes=[
            pltpu.VMEM((ny, nx, rows, lanes), x.dtype),
            (
                pltpu.SemaphoreType.DMA((4, side)),
                pltpu.SemaphoreType.DMA((4, side)),
                pltpu.SemaphoreType.DMA((1,)),
            ),
        ],
        compiler_params=pltpu.CompilerParams(
            collective_id=collective_id, has_side_effects=True,
            vmem_limit_bytes=48 * 1024 * 1024,
        ),
        cost_estimate=pl.CostEstimate(
            flops=0, transcendentals=0, bytes_accessed=3 * n * x.size * x.dtype.itemsize
        ),
    )(x)
    return out.reshape(n, rows, lanes)


def fused_sum_kernel(nr, nc, x_ref, out_ref, recv1, recv2, recv3, sems):
    send1, got1, send2, got2, send3, got3 = sems
    mesh_kind = pl.DeviceIdType.MESH
    my_r = lax.axis_index("row")
    my_c = lax.axis_index("col")
    barrier = pltpu.get_barrier_semaphore()
    for offset in range(1, nc):
        pl.semaphore_signal(barrier, 1, device_id=(my_r, lax.rem(my_c + offset, nc)),
                            device_id_type=mesh_kind)
    for offset in range(1, nr):
        pl.semaphore_signal(barrier, 1, device_id=(lax.rem(my_r + offset, nr), my_c),
                            device_id_type=mesh_kind)
    pl.semaphore_wait(barrier, nc + nr - 2)

    def exchange(peers, axis_count, src_of, dst, send, got, me_index):
        started = []
        for offset in range(1, axis_count):
            peer = lax.rem(me_index + offset, axis_count)
            copy = pltpu.make_async_remote_copy(
                src_ref=src_of(peer), dst_ref=dst.at[me_index],
                send_sem=send.at[offset], recv_sem=got.at[me_index],
                device_id=peers(peer), device_id_type=mesh_kind,
            )
            copy.start()
            started.append(copy)
        for offset in range(1, axis_count):
            source = lax.rem(me_index + axis_count - offset, axis_count)
            pltpu.make_async_remote_copy(
                src_ref=src_of(source), dst_ref=dst.at[source],
                send_sem=send.at[offset], recv_sem=got.at[source],
                device_id=peers(source), device_id_type=mesh_kind,
            ).wait_recv()
        return started

    along_col = lambda peer: (my_r, peer)
    along_row = lambda peer: (peer, my_c)
    recv1[my_c] = x_ref[my_c]
    sends = exchange(along_col, nc, lambda peer: x_ref.at[peer], recv1, send1, got1, my_c)
    part = recv1[0]
    for j in range(1, nc):
        part = part + recv1[j]
    recv2[my_r] = part
    sends += exchange(along_row, nr, lambda peer: recv2.at[my_r], recv2, send2, got2, my_r)
    total = recv2[0]
    for j in range(1, nr):
        total = total + recv2[j]
    recv3[my_c] = total
    sends += exchange(along_col, nc, lambda peer: recv3.at[my_c], recv3, send3, got3, my_c)
    out_ref[...] = recv3[...]
    for copy in sends:
        copy.wait_send()


def fused_sum(local, collective_id):
    nr = lax.axis_size("row")
    nc = lax.axis_size("col")
    height, width = local.shape
    part = height // nc
    out = pl.pallas_call(
        functools.partial(fused_sum_kernel, nr, nc),
        out_shape=jax.ShapeDtypeStruct((nc, part, width), local.dtype),
        in_specs=[pl.BlockSpec(memory_space=pltpu.VMEM)],
        out_specs=pl.BlockSpec(memory_space=pltpu.VMEM),
        scratch_shapes=[
            pltpu.VMEM((nc, part, width), local.dtype),
            pltpu.VMEM((nr, part, width), local.dtype),
            pltpu.VMEM((nc, part, width), local.dtype),
            (
                pltpu.SemaphoreType.DMA((nc,)),
                pltpu.SemaphoreType.DMA((nc,)),
                pltpu.SemaphoreType.DMA((nr,)),
                pltpu.SemaphoreType.DMA((nr,)),
                pltpu.SemaphoreType.DMA((nc,)),
                pltpu.SemaphoreType.DMA((nc,)),
            ),
        ],
        compiler_params=pltpu.CompilerParams(
            collective_id=collective_id, has_side_effects=True,
            vmem_limit_bytes=48 * 1024 * 1024,
        ),
        cost_estimate=pl.CostEstimate(
            flops=local.size, transcendentals=0, bytes_accessed=3 * local.size * 4
        ),
    )(local.reshape(nc, part, width))
    return out.reshape(height, width)


def gather_and_sum_kernel(nx, ny, nr, x_ref, w_ref, out_ref, wout_ref, full, recv1, recv2, recv3, sems):
    send, got, own_sem, wsend1, wgot1, wsend2, wgot2, wsend3, wgot3 = sems
    mesh_kind = pl.DeviceIdType.MESH
    nc = nx * ny
    me = lax.axis_index("col")
    my_r = lax.axis_index("row")
    my_y = me // nx
    my_x = lax.rem(me, nx)
    half = x_ref.shape[0] // 2
    lower = pl.ds(0, half)
    upper = pl.ds(half, half)
    along_col = lambda peer: (my_r, peer)
    along_row = lambda peer: (peer, me)

    barrier = pltpu.get_barrier_semaphore()
    for offset in range(1, nc):
        pl.semaphore_signal(barrier, 1, device_id=along_col(lax.rem(me + offset, nc)),
                            device_id_type=mesh_kind)
    for offset in range(1, nr):
        pl.semaphore_signal(barrier, 1, device_id=along_row(lax.rem(my_r + offset, nr)),
                            device_id_type=mesh_kind)
    pl.semaphore_wait(barrier, nc + nr - 2)

    def start_all(peers, count, me_index, src_of, dst, sem_send, sem_got):
        started = []
        for offset in range(1, count):
            peer = lax.rem(me_index + offset, count)
            copy = pltpu.make_async_remote_copy(
                src_ref=src_of(peer), dst_ref=dst.at[me_index],
                send_sem=sem_send.at[offset], recv_sem=sem_got.at[me_index],
                device_id=peers(peer), device_id_type=mesh_kind,
            )
            copy.start()
            started.append(copy)
        return started

    def wait_all(peers, count, me_index, src_of, dst, sem_send, sem_got):
        for offset in range(1, count):
            source = lax.rem(me_index + count - offset, count)
            pltpu.make_async_remote_copy(
                src_ref=src_of(source), dst_ref=dst.at[source],
                send_sem=sem_send.at[offset], recv_sem=sem_got.at[source],
                device_id=peers(source), device_id_type=mesh_kind,
            ).wait_recv()

    own = pltpu.make_async_copy(x_ref, full.at[my_y, my_x], own_sem.at[0])
    own.start()
    sends = []
    for offset in range(1, nx):
        peer_x = lax.rem(my_x + offset, nx)
        copy = pltpu.make_async_remote_copy(
            src_ref=x_ref.at[lower], dst_ref=full.at[my_y, my_x, lower],
            send_sem=send.at[0, offset], recv_sem=got.at[0, my_x],
            device_id=torus_peer(my_y, peer_x, nx), device_id_type=mesh_kind,
        )
        copy.start()
        sends.append(copy)
    for offset in range(1, ny):
        peer_y = lax.rem(my_y + offset, ny)
        copy = pltpu.make_async_remote_copy(
            src_ref=x_ref.at[upper], dst_ref=full.at[my_y, my_x, upper],
            send_sem=send.at[1, offset], recv_sem=got.at[1, my_y],
            device_id=torus_peer(peer_y, my_x, nx), device_id_type=mesh_kind,
        )
        copy.start()
        sends.append(copy)
    recv1[me] = w_ref[me]
    weight_src = lambda peer: w_ref.at[peer]
    sends += start_all(along_col, nc, me, weight_src, recv1, wsend1, wgot1)
    own.wait()
    for offset in range(1, nx):
        source_x = lax.rem(my_x + nx - offset, nx)
        pltpu.make_async_remote_copy(
            src_ref=x_ref.at[lower], dst_ref=full.at[my_y, source_x, lower],
            send_sem=send.at[0, offset], recv_sem=got.at[0, source_x],
            device_id=torus_peer(my_y, source_x, nx), device_id_type=mesh_kind,
        ).wait_recv()
    for offset in range(1, ny):
        peer_y = lax.rem(my_y + offset, ny)
        copy = pltpu.make_async_remote_copy(
            src_ref=full.at[my_y, :, lower], dst_ref=full.at[my_y, :, lower],
            send_sem=send.at[2, offset], recv_sem=got.at[2, my_y],
            device_id=torus_peer(peer_y, my_x, nx), device_id_type=mesh_kind,
        )
        copy.start()
        sends.append(copy)
    for offset in range(1, ny):
        source_y = lax.rem(my_y + ny - offset, ny)
        pltpu.make_async_remote_copy(
            src_ref=x_ref.at[upper], dst_ref=full.at[source_y, my_x, upper],
            send_sem=send.at[1, offset], recv_sem=got.at[1, source_y],
            device_id=torus_peer(source_y, my_x, nx), device_id_type=mesh_kind,
        ).wait_recv()
    for offset in range(1, nx):
        peer_x = lax.rem(my_x + offset, nx)
        copy = pltpu.make_async_remote_copy(
            src_ref=full.at[:, my_x, upper], dst_ref=full.at[:, my_x, upper],
            send_sem=send.at[3, offset], recv_sem=got.at[3, my_x],
            device_id=torus_peer(my_y, peer_x, nx), device_id_type=mesh_kind,
        )
        copy.start()
        sends.append(copy)

    wait_all(along_col, nc, me, weight_src, recv1, wsend1, wgot1)
    part = recv1[0]
    for j in range(1, nc):
        part = part + recv1[j]
    recv2[my_r] = part
    row_src = lambda peer: recv2.at[my_r]
    sends += start_all(along_row, nr, my_r, row_src, recv2, wsend2, wgot2)
    wait_all(along_row, nr, my_r, row_src, recv2, wsend2, wgot2)
    total = recv2[0]
    for j in range(1, nr):
        total = total + recv2[j]
    recv3[me] = total
    back_src = lambda peer: recv3.at[me]
    sends += start_all(along_col, nc, me, back_src, recv3, wsend3, wgot3)

    for offset in range(1, ny):
        source_y = lax.rem(my_y + ny - offset, ny)
        pltpu.make_async_remote_copy(
            src_ref=full.at[source_y, :, lower], dst_ref=full.at[source_y, :, lower],
            send_sem=send.at[2, offset], recv_sem=got.at[2, source_y],
            device_id=torus_peer(source_y, my_x, nx), device_id_type=mesh_kind,
        ).wait_recv()
    for offset in range(1, nx):
        source_x = lax.rem(my_x + nx - offset, nx)
        pltpu.make_async_remote_copy(
            src_ref=full.at[:, source_x, upper], dst_ref=full.at[:, source_x, upper],
            send_sem=send.at[3, offset], recv_sem=got.at[3, source_x],
            device_id=torus_peer(my_y, source_x, nx), device_id_type=mesh_kind,
        ).wait_recv()
    out_ref[...] = full[...]
    wait_all(along_col, nc, me, back_src, recv3, wsend3, wgot3)
    wout_ref[...] = recv3[...]
    for copy in sends:
        copy.wait_send()


def gather_and_sum(x, local, nx, collective_id):
    rows, lanes = x.shape
    nc = lax.axis_size("col")
    nr = lax.axis_size("row")
    ny = nc // nx
    side = max(nx, ny)
    height, width = local.shape
    part = height // nc
    out, summed = pl.pallas_call(
        functools.partial(gather_and_sum_kernel, nx, ny, nr),
        out_shape=(
            jax.ShapeDtypeStruct((ny, nx, rows, lanes), x.dtype),
            jax.ShapeDtypeStruct((nc, part, width), local.dtype),
        ),
        in_specs=[pl.BlockSpec(memory_space=pltpu.VMEM)] * 2,
        out_specs=(pl.BlockSpec(memory_space=pltpu.VMEM),) * 2,
        scratch_shapes=[
            pltpu.VMEM((ny, nx, rows, lanes), x.dtype),
            pltpu.VMEM((nc, part, width), local.dtype),
            pltpu.VMEM((nr, part, width), local.dtype),
            pltpu.VMEM((nc, part, width), local.dtype),
            (
                pltpu.SemaphoreType.DMA((4, side)),
                pltpu.SemaphoreType.DMA((4, side)),
                pltpu.SemaphoreType.DMA((1,)),
                pltpu.SemaphoreType.DMA((nc,)),
                pltpu.SemaphoreType.DMA((nc,)),
                pltpu.SemaphoreType.DMA((nr,)),
                pltpu.SemaphoreType.DMA((nr,)),
                pltpu.SemaphoreType.DMA((nc,)),
                pltpu.SemaphoreType.DMA((nc,)),
            ),
        ],
        compiler_params=pltpu.CompilerParams(
            collective_id=collective_id, has_side_effects=True,
            vmem_limit_bytes=48 * 1024 * 1024,
        ),
        cost_estimate=pl.CostEstimate(
            flops=local.size, transcendentals=0,
            bytes_accessed=3 * nc * x.size * x.dtype.itemsize + 3 * local.size * 4,
        ),
    )(x, local.reshape(nc, part, width))
    return out.reshape(nc, rows, lanes), summed.reshape(height, width)


def all_sum(local, collective_base):
    row_count = lax.axis_size("row")
    col_count = lax.axis_size("col")
    height, width = local.shape
    by_col = scatter_sum(
        local.reshape(col_count, height // col_count, width), "col", "row", jnp.float32,
        collective_base,
    )
    part = height // col_count
    by_row = scatter_sum(
        by_col.reshape(row_count, part // row_count, width), "row", "col", jnp.float32,
        collective_base + 1,
    )
    back_row = gather_all(by_row, "row", "col", row_count, collective_base + 2)
    back_col = gather_all(back_row.reshape(part, width), "col", "row", col_count, collective_base + 3)
    return back_col.reshape(height, width)


def activation(aggregated, weight, cot_rows):
    hidden = jnp.dot(aggregated, weight, preferred_element_type=jnp.float32)
    sigmoid_value = jax.nn.sigmoid(hidden)
    output = (hidden * sigmoid_value).astype(jnp.bfloat16)
    silu_slope = sigmoid_value * (1.0 + hidden * (1.0 - sigmoid_value))
    hidden_grad = (cot_rows.astype(jnp.float32) * silu_slope).astype(jnp.bfloat16)
    return (output, hidden_grad)


def per_device(tile_values, tile_rows, tile_cols, tile_count, features, weight, cotangent):
    slot_total = tile_values.shape[2]
    tile_edge = tile_values.shape[3]
    tile_block = tile_values.reshape(slot_total, tile_edge, tile_edge)
    row_index = tile_rows.reshape(slot_total)
    col_index = tile_cols.reshape(slot_total)
    live_count = tile_count.reshape(1)
    own_rows = features.shape[0]
    feat_width = features.shape[1]
    row_count = lax.axis_size("row")
    col_count = lax.axis_size("col")
    row_tiles = col_count * own_rows // tile_edge
    col_tiles = row_count * own_rows // tile_edge
    column_block = gather_row(features, 8)
    source = column_block.reshape(col_tiles, tile_edge, feat_width)
    partial_rows = sparse_product(
        tile_block, row_index, col_index, live_count, source, row_tiles, False
    )
    partial_flat = partial_rows.reshape(row_tiles * tile_edge, feat_width)
    node_total = row_count * col_count * own_rows
    aggregated = scatter_sum_2d(
        partial_rows.reshape(col_count, own_rows, feat_width), TORUS_X, jnp.bfloat16, 0
    )
    output, hidden_grad = activation(aggregated, weight, cotangent)
    own_grad = lax.dot_general(
        hidden_grad, weight, (((1,), (1,)), ((), ())), preferred_element_type=jnp.float32
    ).astype(jnp.bfloat16)
    local_grad = lax.dot_general(
        aggregated, hidden_grad, (((0,), (0,)), ((), ())), preferred_element_type=jnp.float32
    )
    row_block, summed_grad = gather_and_sum(own_grad, local_grad, TORUS_X, 7)
    weight_grad = summed_grad * (1.0 / math.sqrt(node_total))
    source_back = row_block.reshape(row_tiles, tile_edge, feat_width)
    partial_cols = sparse_product(
        tile_block, col_index, row_index, live_count, source_back, col_tiles, True
    )
    input_grad = scatter_sum_row(
        partial_cols.reshape(row_count, own_rows, feat_width), jnp.float32, 9
    )
    return (output, weight_grad, input_grad)


def solution(mesh):
    placed = (
        P("row", "col", None, None, None),
        P("row", "col", None),
        P("row", "col", None),
        P("row", "col"),
        P(("row", "col"), None),
        P(),
        P(("row", "col"), None),
    )
    return jax.shard_map(
        per_device,
        mesh=mesh,
        in_specs=placed,
        out_specs=(P(("row", "col"), None), P(), P(("row", "col"), None)),
        check_vma=False,
    )
```

```python
import functools
import math

import jax
import jax.numpy as jnp
from jax import lax
from jax.experimental import pallas as pl
from jax.experimental.pallas import tpu as pltpu
from jax.sharding import PartitionSpec as P

SLOTS_PER_STEP = 32
UNROLL = 32
TORUS_X = 4


def spmm_kernel(transpose, acc_index, src_index, count_ref, tiles_ref, src_ref, out_ref, acc_ref):
    step = pl.program_id(0)
    per_step = tiles_ref.shape[0]
    live = count_ref[0]
    acc_last = acc_ref.shape[0] - 1
    src_last = src_ref.shape[0] - 1

    @pl.when(step == 0)
    def _():
        acc_ref[...] = jnp.zeros_like(acc_ref)

    def one_slot(k, carry):
        slot = step * per_step + k
        target = jnp.clip(acc_index[slot], 0, acc_last)
        picked = jnp.clip(src_index[slot], 0, src_last)
        tile = tiles_ref[k]
        tile = jnp.where(slot < live, tile, jnp.zeros_like(tile))
        block = src_ref[picked]
        if transpose:
            product = lax.dot_general(
                tile, block, (((0,), (0,)), ((), ())), preferred_element_type=jnp.float32
            )
        else:
            product = jnp.dot(tile, block, preferred_element_type=jnp.float32)
        acc_ref[target] += product
        return carry

    lax.fori_loop(0, per_step, one_slot, 0, unroll=UNROLL)

    @pl.when(step == pl.num_programs(0) - 1)
    def _():
        out_ref[...] = acc_ref[...].astype(out_ref.dtype)


def sparse_product(tile_block, acc_index, src_index, live_count, source, segments, transpose):
    slot_total, tile_edge, _ = tile_block.shape
    feat_width = source.shape[2]
    per_step = min(SLOTS_PER_STEP, slot_total)
    steps = slot_total // per_step

    def tile_map(step, acc_ref, src_ref, count_ref):
        last_live = jnp.maximum(count_ref[0] - 1, 0) // per_step
        return (jnp.minimum(step, last_live), 0, 0)

    grid_spec = pltpu.PrefetchScalarGridSpec(
        num_scalar_prefetch=3,
        grid=(steps,),
        in_specs=[
            pl.BlockSpec((per_step, tile_edge, tile_edge), tile_map),
            pl.BlockSpec(source.shape, lambda step, *_: (0, 0, 0)),
        ],
        out_specs=pl.BlockSpec((segments, tile_edge, feat_width), lambda step, *_: (0, 0, 0)),
        scratch_shapes=[pltpu.VMEM((segments, tile_edge, feat_width), jnp.float32)],
    )
    flops = 2 * slot_total * tile_edge * tile_edge * feat_width
    bytes_accessed = (
        tile_block.size * 2 + source.size * 2 + segments * tile_edge * feat_width * 2
    )
    return pl.pallas_call(
        functools.partial(spmm_kernel, transpose),
        out_shape=jax.ShapeDtypeStruct((segments, tile_edge, feat_width), jnp.bfloat16),
        grid_spec=grid_spec,
        compiler_params=pltpu.CompilerParams(
            dimension_semantics=("arbitrary",), vmem_limit_bytes=56 * 1024 * 1024
        ),
        cost_estimate=pl.CostEstimate(
            flops=flops, transcendentals=0, bytes_accessed=bytes_accessed
        ),
    )(acc_index, src_index, live_count, tile_block, source)


def peer_id(axis, other_axis, peer):
    if axis == "row":
        return (peer, lax.axis_index(other_axis))
    return (lax.axis_index(other_axis), peer)


def greet_all(axis, other_axis, n, me):
    barrier = pltpu.get_barrier_semaphore()
    for offset in range(1, n):
        peer = lax.rem(me + offset, n)
        pl.semaphore_signal(
            barrier, 1, device_id=peer_id(axis, other_axis, peer),
            device_id_type=pl.DeviceIdType.MESH,
        )
    pl.semaphore_wait(barrier, n - 1)


def scatter_sum_kernel(axis, other_axis, n, x_hbm, out_ref, recv, send_sems, recv_sems, own_sem):
    me = lax.axis_index(axis)
    greet_all(axis, other_axis, n, me)
    own = pltpu.make_async_copy(x_hbm.at[me], recv.at[me], own_sem)
    own.start()
    sends = []
    for offset in range(1, n):
        peer = lax.rem(me + offset, n)
        copy = pltpu.make_async_remote_copy(
            src_ref=x_hbm.at[peer],
            dst_ref=recv.at[me],
            send_sem=send_sems.at[offset],
            recv_sem=recv_sems.at[me],
            device_id=peer_id(axis, other_axis, peer),
            device_id_type=pl.DeviceIdType.MESH,
        )
        copy.start()
        sends.append(copy)
    own.wait()
    for offset in range(1, n):
        source = lax.rem(me + n - offset, n)
        pltpu.make_async_remote_copy(
            src_ref=x_hbm.at[source],
            dst_ref=recv.at[source],
            send_sem=send_sems.at[offset],
            recv_sem=recv_sems.at[source],
            device_id=peer_id(axis, other_axis, source),
            device_id_type=pl.DeviceIdType.MESH,
        ).wait_recv()
    total = recv[0].astype(jnp.float32)
    for j in range(1, n):
        total = total + recv[j].astype(jnp.float32)
    out_ref[...] = total.astype(out_ref.dtype)
    for copy in sends:
        copy.wait_send()


def scatter_sum(x, axis, other_axis, out_dtype, collective_id):
    n, rows, lanes = x.shape
    return pl.pallas_call(
        functools.partial(scatter_sum_kernel, axis, other_axis, n),
        out_shape=jax.ShapeDtypeStruct((rows, lanes), out_dtype),
        in_specs=[pl.BlockSpec(memory_space=pl.ANY)],
        out_specs=pl.BlockSpec(memory_space=pltpu.VMEM),
        scratch_shapes=[
            pltpu.VMEM((n, rows, lanes), x.dtype),
            pltpu.SemaphoreType.DMA((n,)),
            pltpu.SemaphoreType.DMA((n,)),
            pltpu.SemaphoreType.DMA(()),
        ],
        compiler_params=pltpu.CompilerParams(
            collective_id=collective_id, has_side_effects=True,
            vmem_limit_bytes=48 * 1024 * 1024,
        ),
        cost_estimate=pl.CostEstimate(
            flops=x.size, transcendentals=0, bytes_accessed=3 * x.size * x.dtype.itemsize
        ),
    )(x)


def gather_all_kernel(axis, other_axis, n, x_ref, out_ref, recv, send_sems, recv_sems):
    me = lax.axis_index(axis)
    recv[me] = x_ref[...]
    greet_all(axis, other_axis, n, me)
    sends = []
    for offset in range(1, n):
        peer = lax.rem(me + offset, n)
        copy = pltpu.make_async_remote_copy(
            src_ref=x_ref,
            dst_ref=recv.at[me],
            send_sem=send_sems.at[offset],
            recv_sem=recv_sems.at[me],
            device_id=peer_id(axis, other_axis, peer),
            device_id_type=pl.DeviceIdType.MESH,
        )
        copy.start()
        sends.append(copy)
    for offset in range(1, n):
        source = lax.rem(me + n - offset, n)
        pltpu.make_async_remote_copy(
            src_ref=x_ref,
            dst_ref=recv.at[source],
            send_sem=send_sems.at[offset],
            recv_sem=recv_sems.at[source],
            device_id=peer_id(axis, other_axis, source),
            device_id_type=pl.DeviceIdType.MESH,
        ).wait_recv()
    out_ref[...] = recv[...]
    for copy in sends:
        copy.wait_send()


def gather_all(x, axis, other_axis, n, collective_id):
    rows, lanes = x.shape
    return pl.pallas_call(
        functools.partial(gather_all_kernel, axis, other_axis, n),
        out_shape=jax.ShapeDtypeStruct((n, rows, lanes), x.dtype),
        in_specs=[pl.BlockSpec(memory_space=pltpu.VMEM)],
        out_specs=pl.BlockSpec(memory_space=pltpu.VMEM),
        scratch_shapes=[
            pltpu.VMEM((n, rows, lanes), x.dtype),
            pltpu.SemaphoreType.DMA((n,)),
            pltpu.SemaphoreType.DMA((n,)),
        ],
        compiler_params=pltpu.CompilerParams(
            collective_id=collective_id, has_side_effects=True,
            vmem_limit_bytes=48 * 1024 * 1024,
        ),
        cost_estimate=pl.CostEstimate(
            flops=0, transcendentals=0, bytes_accessed=3 * n * x.size * x.dtype.itemsize
        ),
    )(x)


def torus_peer(y, x, nx):
    return (lax.axis_index("row"), y * nx + x)


def scatter_sum_2d_kernel(nx, ny, x_hbm, out_ref, recv1, mid, recv2, sems):
    send1, got1, send2, got2, own_sems = sems
    me = lax.axis_index("col")
    my_y = me // nx
    my_x = lax.rem(me, nx)
    half = x_hbm.shape[2] // 2
    lower = pl.ds(0, half)
    upper = pl.ds(half, half)
    mesh_kind = pl.DeviceIdType.MESH

    barrier = pltpu.get_barrier_semaphore()
    for offset in range(1, nx):
        pl.semaphore_signal(barrier, 1, device_id=torus_peer(my_y, lax.rem(my_x + offset, nx), nx),
                            device_id_type=mesh_kind)
    for offset in range(1, ny):
        pl.semaphore_signal(barrier, 1, device_id=torus_peer(lax.rem(my_y + offset, ny), my_x, nx),
                            device_id_type=mesh_kind)
    pl.semaphore_wait(barrier, nx + ny - 2)

    own_a = pltpu.make_async_copy(x_hbm.at[:, my_x, lower], recv1.at[0, my_x], own_sems.at[0])
    own_b = pltpu.make_async_copy(x_hbm.at[my_y, :, upper], recv1.at[1, my_y], own_sems.at[1])
    own_a.start()
    own_b.start()
    sends = []
    for offset in range(1, nx):
        peer_x = lax.rem(my_x + offset, nx)
        copy = pltpu.make_async_remote_copy(
            src_ref=x_hbm.at[:, peer_x, lower], dst_ref=recv1.at[0, my_x],
            send_sem=send1.at[0, offset], recv_sem=got1.at[0, my_x],
            device_id=torus_peer(my_y, peer_x, nx), device_id_type=mesh_kind,
        )
        copy.start()
        sends.append(copy)
    for offset in range(1, ny):
        peer_y = lax.rem(my_y + offset, ny)
        copy = pltpu.make_async_remote_copy(
            src_ref=x_hbm.at[peer_y, :, upper], dst_ref=recv1.at[1, my_y],
            send_sem=send1.at[1, offset], recv_sem=got1.at[1, my_y],
            device_id=torus_peer(peer_y, my_x, nx), device_id_type=mesh_kind,
        )
        copy.start()
        sends.append(copy)
    own_a.wait()
    own_b.wait()
    for offset in range(1, nx):
        source_x = lax.rem(my_x + nx - offset, nx)
        pltpu.make_async_remote_copy(
            src_ref=x_hbm.at[:, source_x, lower], dst_ref=recv1.at[0, source_x],
            send_sem=send1.at[0, offset], recv_sem=got1.at[0, source_x],
            device_id=torus_peer(my_y, source_x, nx), device_id_type=mesh_kind,
        ).wait_recv()

    def add_up(stack):
        total = stack[0].astype(jnp.float32)
        for j in range(1, stack.shape[0]):
            total = total + stack[j].astype(jnp.float32)
        return total

    for target in range(ny):
        mid[0, target] = add_up(recv1[0, :, target]).astype(mid.dtype)
    recv2[0, my_y] = mid[0, my_y]

    for offset in range(1, ny):
        peer_y = lax.rem(my_y + offset, ny)
        copy = pltpu.make_async_remote_copy(
            src_ref=mid.at[0, peer_y], dst_ref=recv2.at[0, my_y],
            send_sem=send2.at[0, offset], recv_sem=got2.at[0, my_y],
            device_id=torus_peer(peer_y, my_x, nx), device_id_type=mesh_kind,
        )
        copy.start()
        sends.append(copy)
    for offset in range(1, ny):
        source_y = lax.rem(my_y + ny - offset, ny)
        pltpu.make_async_remote_copy(
            src_ref=x_hbm.at[source_y, :, upper], dst_ref=recv1.at[1, source_y],
            send_sem=send1.at[1, offset], recv_sem=got1.at[1, source_y],
            device_id=torus_peer(source_y, my_x, nx), device_id_type=mesh_kind,
        ).wait_recv()
    for target in range(nx):
        mid[1, target] = add_up(recv1[1, :, target]).astype(mid.dtype)
    recv2[1, my_x] = mid[1, my_x]
    for offset in range(1, nx):
        peer_x = lax.rem(my_x + offset, nx)
        copy = pltpu.make_async_remote_copy(
            src_ref=mid.at[1, peer_x], dst_ref=recv2.at[1, my_x],
            send_sem=send2.at[1, offset], recv_sem=got2.at[1, my_x],
            device_id=torus_peer(my_y, peer_x, nx), device_id_type=mesh_kind,
        )
        copy.start()
        sends.append(copy)
    for offset in range(1, ny):
        source_y = lax.rem(my_y + ny - offset, ny)
        pltpu.make_async_remote_copy(
            src_ref=mid.at[0, source_y], dst_ref=recv2.at[0, source_y],
            send_sem=send2.at[0, offset], recv_sem=got2.at[0, source_y],
            device_id=torus_peer(source_y, my_x, nx), device_id_type=mesh_kind,
        ).wait_recv()
    out_ref[lower] = add_up(recv2[0]).astype(out_ref.dtype)
    for offset in range(1, nx):
        source_x = lax.rem(my_x + nx - offset, nx)
        pltpu.make_async_remote_copy(
            src_ref=mid.at[1, source_x], dst_ref=recv2.at[1, source_x],
            send_sem=send2.at[1, offset], recv_sem=got2.at[1, source_x],
            device_id=torus_peer(my_y, source_x, nx), device_id_type=mesh_kind,
        ).wait_recv()
    out_ref[upper] = add_up(recv2[1]).astype(out_ref.dtype)
    for copy in sends:
        copy.wait_send()


def scatter_sum_2d(x, nx, out_dtype, collective_id):
    n, rows, lanes = x.shape
    ny = n // nx
    half = rows // 2
    side = max(nx, ny)
    return pl.pallas_call(
        functools.partial(scatter_sum_2d_kernel, nx, ny),
        out_shape=jax.ShapeDtypeStruct((rows, lanes), out_dtype),
        in_specs=[pl.BlockSpec(memory_space=pl.ANY)],
        out_specs=pl.BlockSpec(memory_space=pltpu.VMEM),
        scratch_shapes=[
            pltpu.VMEM((2, side, side, half, lanes), x.dtype),
            pltpu.VMEM((2, side, half, lanes), x.dtype),
            pltpu.VMEM((2, side, half, lanes), x.dtype),
            (
                pltpu.SemaphoreType.DMA((2, side)),
                pltpu.SemaphoreType.DMA((2, side)),
                pltpu.SemaphoreType.DMA((2, side)),
                pltpu.SemaphoreType.DMA((2, side)),
                pltpu.SemaphoreType.DMA((2,)),
            ),
        ],
        compiler_params=pltpu.CompilerParams(
            collective_id=collective_id, has_side_effects=True,
            vmem_limit_bytes=48 * 1024 * 1024,
        ),
        cost_estimate=pl.CostEstimate(
            flops=x.size, transcendentals=0, bytes_accessed=3 * x.size * x.dtype.itemsize
        ),
    )(x.reshape(ny, nx, rows, lanes))


def row_peer(index):
    return (index, lax.axis_index("col"))


def greet_row(my_z, my_core, nz):
    barrier = pltpu.get_barrier_semaphore()
    mesh_kind = pl.DeviceIdType.MESH
    pl.semaphore_signal(barrier, 1, device_id=row_peer(my_z * 2 + 1 - my_core), device_id_type=mesh_kind)
    for offset in range(1, nz):
        peer_z = lax.rem(my_z + offset, nz)
        pl.semaphore_signal(barrier, 1, device_id=row_peer(peer_z * 2 + my_core), device_id_type=mesh_kind)
    pl.semaphore_wait(barrier, nz)


def scatter_sum_row_kernel(nz, x_hbm, out_ref, own1, recv1, mid, recv2, sems):
    send1, got1, send2, got2, own_sem = sems
    mesh_kind = pl.DeviceIdType.MESH
    me = lax.axis_index("row")
    my_z = me // 2
    my_core = lax.rem(me, 2)
    other_core = 1 - my_core
    partner = row_peer(my_z * 2 + other_core)
    greet_row(my_z, my_core, nz)
    own = pltpu.make_async_copy(x_hbm.at[:, my_core], own1, own_sem.at[0])
    own.start()
    sends = []
    for offset in range(nz):
        target_z = lax.rem(my_z + offset + 1, nz)
        copy = pltpu.make_async_remote_copy(
            src_ref=x_hbm.at[target_z, other_core], dst_ref=recv1.at[target_z],
            send_sem=send1.at[offset], recv_sem=got1.at[target_z],
            device_id=partner, device_id_type=mesh_kind,
        )
        copy.start()
        sends.append(copy)
    own.wait()
    for offset in range(nz - 1):
        target_z = lax.rem(my_z + offset + 1, nz)
        pltpu.make_async_remote_copy(
            src_ref=x_hbm.at[target_z, other_core], dst_ref=recv1.at[target_z],
            send_sem=send1.at[offset], recv_sem=got1.at[target_z],
            device_id=partner, device_id_type=mesh_kind,
        ).wait_recv()
        mid[target_z] = (own1[target_z].astype(jnp.float32) + recv1[target_z].astype(jnp.float32)).astype(mid.dtype)
        copy = pltpu.make_async_remote_copy(
            src_ref=mid.at[target_z], dst_ref=recv2.at[my_z],
            send_sem=send2.at[offset + 1], recv_sem=got2.at[my_z],
            device_id=row_peer(target_z * 2 + my_core), device_id_type=mesh_kind,
        )
        copy.start()
        sends.append(copy)
    pltpu.make_async_remote_copy(
        src_ref=x_hbm.at[my_z, other_core], dst_ref=recv1.at[my_z],
        send_sem=send1.at[nz - 1], recv_sem=got1.at[my_z],
        device_id=partner, device_id_type=mesh_kind,
    ).wait_recv()
    total = own1[my_z].astype(jnp.float32) + recv1[my_z].astype(jnp.float32)
    for offset in range(1, nz):
        source_z = lax.rem(my_z + nz - offset, nz)
        pltpu.make_async_remote_copy(
            src_ref=mid.at[source_z], dst_ref=recv2.at[source_z],
            send_sem=send2.at[offset], recv_sem=got2.at[source_z],
            device_id=row_peer(source_z * 2 + my_core), device_id_type=mesh_kind,
        ).wait_recv()
        total = total + recv2[source_z].astype(jnp.float32)
    out_ref[...] = total.astype(out_ref.dtype)
    for copy in sends:
        copy.wait_send()


def scatter_sum_row(x, out_dtype, collective_id):
    n, rows, lanes = x.shape
    nz = n // 2
    return pl.pallas_call(
        functools.partial(scatter_sum_row_kernel, nz),
        out_shape=jax.ShapeDtypeStruct((rows, lanes), out_dtype),
        in_specs=[pl.BlockSpec(memory_space=pl.ANY)],
        out_specs=pl.BlockSpec(memory_space=pltpu.VMEM),
        scratch_shapes=[
            pltpu.VMEM((nz, rows, lanes), x.dtype),
            pltpu.VMEM((nz, rows, lanes), x.dtype),
            pltpu.VMEM((nz, rows, lanes), x.dtype),
            pltpu.VMEM((nz, rows, lanes), x.dtype),
            (
                pltpu.SemaphoreType.DMA((nz,)),
                pltpu.SemaphoreType.DMA((nz,)),
                pltpu.SemaphoreType.DMA((nz,)),
                pltpu.SemaphoreType.DMA((nz,)),
                pltpu.SemaphoreType.DMA((1,)),
            ),
        ],
        compiler_params=pltpu.CompilerParams(
            collective_id=collective_id, has_side_effects=True,
            vmem_limit_bytes=48 * 1024 * 1024,
        ),
        cost_estimate=pl.CostEstimate(
            flops=x.size, transcendentals=0, bytes_accessed=3 * x.size * x.dtype.itemsize
        ),
    )(x.reshape(nz, 2, rows, lanes))


def gather_row_kernel(nz, x_ref, out_ref, full, sems):
    send1, got1, send2, got2, own_sem = sems
    mesh_kind = pl.DeviceIdType.MESH
    me = lax.axis_index("row")
    my_z = me // 2
    my_core = lax.rem(me, 2)
    other_core = 1 - my_core
    greet_row(my_z, my_core, nz)
    own = pltpu.make_async_copy(x_ref, full.at[my_z, my_core], own_sem.at[0])
    own.start()
    sends = []
    for offset in range(1, nz):
        peer_z = lax.rem(my_z + offset, nz)
        copy = pltpu.make_async_remote_copy(
            src_ref=x_ref, dst_ref=full.at[my_z, my_core],
            send_sem=send1.at[offset], recv_sem=got1.at[my_z],
            device_id=row_peer(peer_z * 2 + my_core), device_id_type=mesh_kind,
        )
        copy.start()
        sends.append(copy)
    own.wait()
    for offset in range(1, nz):
        source_z = lax.rem(my_z + nz - offset, nz)
        pltpu.make_async_remote_copy(
            src_ref=x_ref, dst_ref=full.at[source_z, my_core],
            send_sem=send1.at[offset], recv_sem=got1.at[source_z],
            device_id=row_peer(source_z * 2 + my_core), device_id_type=mesh_kind,
        ).wait_recv()
    second = pltpu.make_async_remote_copy(
        src_ref=full.at[:, my_core], dst_ref=full.at[:, my_core],
        send_sem=send2.at[0], recv_sem=got2.at[0],
        device_id=row_peer(my_z * 2 + other_core), device_id_type=mesh_kind,
    )
    second.start()
    pltpu.make_async_remote_copy(
        src_ref=full.at[:, other_core], dst_ref=full.at[:, other_core],
        send_sem=send2.at[0], recv_sem=got2.at[0],
        device_id=row_peer(my_z * 2 + other_core), device_id_type=mesh_kind,
    ).wait_recv()
    for copy in sends:
        copy.wait_send()
    second.wait_send()
    out_ref[...] = full[...]


def gather_row(x, collective_id):
    rows, lanes = x.shape
    nz = lax.axis_size("row") // 2
    out = pl.pallas_call(
        functools.partial(gather_row_kernel, nz),
        out_shape=jax.ShapeDtypeStruct((nz, 2, rows, lanes), x.dtype),
        in_specs=[pl.BlockSpec(memory_space=pltpu.VMEM)],
        out_specs=pl.BlockSpec(memory_space=pltpu.VMEM),
        scratch_shapes=[
            pltpu.VMEM((nz, 2, rows, lanes), x.dtype),
            (
                pltpu.SemaphoreType.DMA((nz,)),
                pltpu.SemaphoreType.DMA((nz,)),
                pltpu.SemaphoreType.DMA((1,)),
                pltpu.SemaphoreType.DMA((1,)),
                pltpu.SemaphoreType.DMA((1,)),
            ),
        ],
        compiler_params=pltpu.CompilerParams(
            collective_id=collective_id, has_side_effects=True,
            vmem_limit_bytes=48 * 1024 * 1024,
        ),
        cost_estimate=pl.CostEstimate(
            flops=0, transcendentals=0, bytes_accessed=3 * 2 * nz * x.size * x.dtype.itemsize
        ),
    )(x)
    return out.reshape(2 * nz * rows, lanes)


def gather_all_2d_kernel(nx, ny, x_ref, out_ref, full, sems):
    send, got, own_sem = sems
    mesh_kind = pl.DeviceIdType.MESH
    me = lax.axis_index("col")
    my_y = me // nx
    my_x = lax.rem(me, nx)
    half = x_ref.shape[0] // 2
    lower = pl.ds(0, half)
    upper = pl.ds(half, half)

    barrier = pltpu.get_barrier_semaphore()
    for offset in range(1, nx):
        pl.semaphore_signal(barrier, 1, device_id=torus_peer(my_y, lax.rem(my_x + offset, nx), nx),
                            device_id_type=mesh_kind)
    for offset in range(1, ny):
        pl.semaphore_signal(barrier, 1, device_id=torus_peer(lax.rem(my_y + offset, ny), my_x, nx),
                            device_id_type=mesh_kind)
    pl.semaphore_wait(barrier, nx + ny - 2)

    own = pltpu.make_async_copy(x_ref, full.at[my_y, my_x], own_sem.at[0])
    own.start()
    sends = []
    for offset in range(1, nx):
        peer_x = lax.rem(my_x + offset, nx)
        copy = pltpu.make_async_remote_copy(
            src_ref=x_ref.at[lower], dst_ref=full.at[my_y, my_x, lower],
            send_sem=send.at[0, offset], recv_sem=got.at[0, my_x],
            device_id=torus_peer(my_y, peer_x, nx), device_id_type=mesh_kind,
        )
        copy.start()
        sends.append(copy)
    for offset in range(1, ny):
        peer_y = lax.rem(my_y + offset, ny)
        copy = pltpu.make_async_remote_copy(
            src_ref=x_ref.at[upper], dst_ref=full.at[my_y, my_x, upper],
            send_sem=send.at[1, offset], recv_sem=got.at[1, my_y],
            device_id=torus_peer(peer_y, my_x, nx), device_id_type=mesh_kind,
        )
        copy.start()
        sends.append(copy)
    own.wait()
    for offset in range(1, nx):
        source_x = lax.rem(my_x + nx - offset, nx)
        pltpu.make_async_remote_copy(
            src_ref=x_ref.at[lower], dst_ref=full.at[my_y, source_x, lower],
            send_sem=send.at[0, offset], recv_sem=got.at[0, source_x],
            device_id=torus_peer(my_y, source_x, nx), device_id_type=mesh_kind,
        ).wait_recv()
    for offset in range(1, ny):
        peer_y = lax.rem(my_y + offset, ny)
        copy = pltpu.make_async_remote_copy(
            src_ref=full.at[my_y, :, lower], dst_ref=full.at[my_y, :, lower],
            send_sem=send.at[2, offset], recv_sem=got.at[2, my_y],
            device_id=torus_peer(peer_y, my_x, nx), device_id_type=mesh_kind,
        )
        copy.start()
        sends.append(copy)
    for offset in range(1, ny):
        source_y = lax.rem(my_y + ny - offset, ny)
        pltpu.make_async_remote_copy(
            src_ref=x_ref.at[upper], dst_ref=full.at[source_y, my_x, upper],
            send_sem=send.at[1, offset], recv_sem=got.at[1, source_y],
            device_id=torus_peer(source_y, my_x, nx), device_id_type=mesh_kind,
        ).wait_recv()
    for offset in range(1, nx):
        peer_x = lax.rem(my_x + offset, nx)
        copy = pltpu.make_async_remote_copy(
            src_ref=full.at[:, my_x, upper], dst_ref=full.at[:, my_x, upper],
            send_sem=send.at[3, offset], recv_sem=got.at[3, my_x],
            device_id=torus_peer(my_y, peer_x, nx), device_id_type=mesh_kind,
        )
        copy.start()
        sends.append(copy)
    for offset in range(1, ny):
        source_y = lax.rem(my_y + ny - offset, ny)
        pltpu.make_async_remote_copy(
            src_ref=full.at[source_y, :, lower], dst_ref=full.at[source_y, :, lower],
            send_sem=send.at[2, offset], recv_sem=got.at[2, source_y],
            device_id=torus_peer(source_y, my_x, nx), device_id_type=mesh_kind,
        ).wait_recv()
    for offset in range(1, nx):
        source_x = lax.rem(my_x + nx - offset, nx)
        pltpu.make_async_remote_copy(
            src_ref=full.at[:, source_x, upper], dst_ref=full.at[:, source_x, upper],
            send_sem=send.at[3, offset], recv_sem=got.at[3, source_x],
            device_id=torus_peer(my_y, source_x, nx), device_id_type=mesh_kind,
        ).wait_recv()
    for copy in sends:
        copy.wait_send()
    out_ref[...] = full[...]


def gather_all_2d(x, nx, collective_id):
    rows, lanes = x.shape
    n = lax.axis_size("col")
    ny = n // nx
    side = max(nx, ny)
    out = pl.pallas_call(
        functools.partial(gather_all_2d_kernel, nx, ny),
        out_shape=jax.ShapeDtypeStruct((ny, nx, rows, lanes), x.dtype),
        in_specs=[pl.BlockSpec(memory_space=pltpu.VMEM)],
        out_specs=pl.BlockSpec(memory_space=pltpu.VMEM),
        scratch_shapes=[
            pltpu.VMEM((ny, nx, rows, lanes), x.dtype),
            (
                pltpu.SemaphoreType.DMA((4, side)),
                pltpu.SemaphoreType.DMA((4, side)),
                pltpu.SemaphoreType.DMA((1,)),
            ),
        ],
        compiler_params=pltpu.CompilerParams(
            collective_id=collective_id, has_side_effects=True,
            vmem_limit_bytes=48 * 1024 * 1024,
        ),
        cost_estimate=pl.CostEstimate(
            flops=0, transcendentals=0, bytes_accessed=3 * n * x.size * x.dtype.itemsize
        ),
    )(x)
    return out.reshape(n, rows, lanes)


def fused_sum_kernel(nr, nc, x_ref, out_ref, recv1, recv2, recv3, sems):
    send1, got1, send2, got2, send3, got3 = sems
    mesh_kind = pl.DeviceIdType.MESH
    my_r = lax.axis_index("row")
    my_c = lax.axis_index("col")
    barrier = pltpu.get_barrier_semaphore()
    for offset in range(1, nc):
        pl.semaphore_signal(barrier, 1, device_id=(my_r, lax.rem(my_c + offset, nc)),
                            device_id_type=mesh_kind)
    for offset in range(1, nr):
        pl.semaphore_signal(barrier, 1, device_id=(lax.rem(my_r + offset, nr), my_c),
                            device_id_type=mesh_kind)
    pl.semaphore_wait(barrier, nc + nr - 2)

    def exchange(peers, axis_count, src_of, dst, send, got, me_index):
        started = []
        for offset in range(1, axis_count):
            peer = lax.rem(me_index + offset, axis_count)
            copy = pltpu.make_async_remote_copy(
                src_ref=src_of(peer), dst_ref=dst.at[me_index],
                send_sem=send.at[offset], recv_sem=got.at[me_index],
                device_id=peers(peer), device_id_type=mesh_kind,
            )
            copy.start()
            started.append(copy)
        for offset in range(1, axis_count):
            source = lax.rem(me_index + axis_count - offset, axis_count)
            pltpu.make_async_remote_copy(
                src_ref=src_of(source), dst_ref=dst.at[source],
                send_sem=send.at[offset], recv_sem=got.at[source],
                device_id=peers(source), device_id_type=mesh_kind,
            ).wait_recv()
        return started

    along_col = lambda peer: (my_r, peer)
    along_row = lambda peer: (peer, my_c)
    recv1[my_c] = x_ref[my_c]
    sends = exchange(along_col, nc, lambda peer: x_ref.at[peer], recv1, send1, got1, my_c)
    part = recv1[0]
    for j in range(1, nc):
        part = part + recv1[j]
    recv2[my_r] = part
    sends += exchange(along_row, nr, lambda peer: recv2.at[my_r], recv2, send2, got2, my_r)
    total = recv2[0]
    for j in range(1, nr):
        total = total + recv2[j]
    recv3[my_c] = total
    sends += exchange(along_col, nc, lambda peer: recv3.at[my_c], recv3, send3, got3, my_c)
    out_ref[...] = recv3[...]
    for copy in sends:
        copy.wait_send()


def fused_sum(local, collective_id):
    nr = lax.axis_size("row")
    nc = lax.axis_size("col")
    height, width = local.shape
    part = height // nc
    out = pl.pallas_call(
        functools.partial(fused_sum_kernel, nr, nc),
        out_shape=jax.ShapeDtypeStruct((nc, part, width), local.dtype),
        in_specs=[pl.BlockSpec(memory_space=pltpu.VMEM)],
        out_specs=pl.BlockSpec(memory_space=pltpu.VMEM),
        scratch_shapes=[
            pltpu.VMEM((nc, part, width), local.dtype),
            pltpu.VMEM((nr, part, width), local.dtype),
            pltpu.VMEM((nc, part, width), local.dtype),
            (
                pltpu.SemaphoreType.DMA((nc,)),
                pltpu.SemaphoreType.DMA((nc,)),
                pltpu.SemaphoreType.DMA((nr,)),
                pltpu.SemaphoreType.DMA((nr,)),
                pltpu.SemaphoreType.DMA((nc,)),
                pltpu.SemaphoreType.DMA((nc,)),
            ),
        ],
        compiler_params=pltpu.CompilerParams(
            collective_id=collective_id, has_side_effects=True,
            vmem_limit_bytes=48 * 1024 * 1024,
        ),
        cost_estimate=pl.CostEstimate(
            flops=local.size, transcendentals=0, bytes_accessed=3 * local.size * 4
        ),
    )(local.reshape(nc, part, width))
    return out.reshape(height, width)


def gather_and_sum_kernel(nx, ny, nr, x_ref, w_ref, out_ref, wout_ref, full, recv1, recv2, recv3, sems):
    send, got, own_sem, wsend1, wgot1, wsend2, wgot2, wsend3, wgot3 = sems
    mesh_kind = pl.DeviceIdType.MESH
    nc = nx * ny
    me = lax.axis_index("col")
    my_r = lax.axis_index("row")
    my_y = me // nx
    my_x = lax.rem(me, nx)
    half = x_ref.shape[0] // 2
    lower = pl.ds(0, half)
    upper = pl.ds(half, half)
    along_col = lambda peer: (my_r, peer)
    along_row = lambda peer: (peer, me)

    barrier = pltpu.get_barrier_semaphore()
    for offset in range(1, nc):
        pl.semaphore_signal(barrier, 1, device_id=along_col(lax.rem(me + offset, nc)),
                            device_id_type=mesh_kind)
    for offset in range(1, nr):
        pl.semaphore_signal(barrier, 1, device_id=along_row(lax.rem(my_r + offset, nr)),
                            device_id_type=mesh_kind)
    pl.semaphore_wait(barrier, nc + nr - 2)

    def start_all(peers, count, me_index, src_of, dst, sem_send, sem_got):
        started = []
        for offset in range(1, count):
            peer = lax.rem(me_index + offset, count)
            copy = pltpu.make_async_remote_copy(
                src_ref=src_of(peer), dst_ref=dst.at[me_index],
                send_sem=sem_send.at[offset], recv_sem=sem_got.at[me_index],
                device_id=peers(peer), device_id_type=mesh_kind,
            )
            copy.start()
            started.append(copy)
        return started

    def wait_all(peers, count, me_index, src_of, dst, sem_send, sem_got):
        for offset in range(1, count):
            source = lax.rem(me_index + count - offset, count)
            pltpu.make_async_remote_copy(
                src_ref=src_of(source), dst_ref=dst.at[source],
                send_sem=sem_send.at[offset], recv_sem=sem_got.at[source],
                device_id=peers(source), device_id_type=mesh_kind,
            ).wait_recv()

    own = pltpu.make_async_copy(x_ref, full.at[my_y, my_x], own_sem.at[0])
    own.start()
    sends = []
    for offset in range(1, nx):
        peer_x = lax.rem(my_x + offset, nx)
        copy = pltpu.make_async_remote_copy(
            src_ref=x_ref.at[lower], dst_ref=full.at[my_y, my_x, lower],
            send_sem=send.at[0, offset], recv_sem=got.at[0, my_x],
            device_id=torus_peer(my_y, peer_x, nx), device_id_type=mesh_kind,
        )
        copy.start()
        sends.append(copy)
    for offset in range(1, ny):
        peer_y = lax.rem(my_y + offset, ny)
        copy = pltpu.make_async_remote_copy(
            src_ref=x_ref.at[upper], dst_ref=full.at[my_y, my_x, upper],
            send_sem=send.at[1, offset], recv_sem=got.at[1, my_y],
            device_id=torus_peer(peer_y, my_x, nx), device_id_type=mesh_kind,
        )
        copy.start()
        sends.append(copy)
    recv1[me] = w_ref[me]
    weight_src = lambda peer: w_ref.at[peer]
    sends += start_all(along_col, nc, me, weight_src, recv1, wsend1, wgot1)
    own.wait()
    for offset in range(1, nx):
        source_x = lax.rem(my_x + nx - offset, nx)
        pltpu.make_async_remote_copy(
            src_ref=x_ref.at[lower], dst_ref=full.at[my_y, source_x, lower],
            send_sem=send.at[0, offset], recv_sem=got.at[0, source_x],
            device_id=torus_peer(my_y, source_x, nx), device_id_type=mesh_kind,
        ).wait_recv()
    for offset in range(1, ny):
        peer_y = lax.rem(my_y + offset, ny)
        copy = pltpu.make_async_remote_copy(
            src_ref=full.at[my_y, :, lower], dst_ref=full.at[my_y, :, lower],
            send_sem=send.at[2, offset], recv_sem=got.at[2, my_y],
            device_id=torus_peer(peer_y, my_x, nx), device_id_type=mesh_kind,
        )
        copy.start()
        sends.append(copy)
    for offset in range(1, ny):
        source_y = lax.rem(my_y + ny - offset, ny)
        pltpu.make_async_remote_copy(
            src_ref=x_ref.at[upper], dst_ref=full.at[source_y, my_x, upper],
            send_sem=send.at[1, offset], recv_sem=got.at[1, source_y],
            device_id=torus_peer(source_y, my_x, nx), device_id_type=mesh_kind,
        ).wait_recv()
    for offset in range(1, nx):
        peer_x = lax.rem(my_x + offset, nx)
        copy = pltpu.make_async_remote_copy(
            src_ref=full.at[:, my_x, upper], dst_ref=full.at[:, my_x, upper],
            send_sem=send.at[3, offset], recv_sem=got.at[3, my_x],
            device_id=torus_peer(my_y, peer_x, nx), device_id_type=mesh_kind,
        )
        copy.start()
        sends.append(copy)

    wait_all(along_col, nc, me, weight_src, recv1, wsend1, wgot1)
    part = recv1[0]
    for j in range(1, nc):
        part = part + recv1[j]
    recv2[my_r] = part
    row_src = lambda peer: recv2.at[my_r]
    sends += start_all(along_row, nr, my_r, row_src, recv2, wsend2, wgot2)
    wait_all(along_row, nr, my_r, row_src, recv2, wsend2, wgot2)
    total = recv2[0]
    for j in range(1, nr):
        total = total + recv2[j]
    recv3[me] = total
    back_src = lambda peer: recv3.at[me]
    sends += start_all(along_col, nc, me, back_src, recv3, wsend3, wgot3)

    for offset in range(1, ny):
        source_y = lax.rem(my_y + ny - offset, ny)
        pltpu.make_async_remote_copy(
            src_ref=full.at[source_y, :, lower], dst_ref=full.at[source_y, :, lower],
            send_sem=send.at[2, offset], recv_sem=got.at[2, source_y],
            device_id=torus_peer(source_y, my_x, nx), device_id_type=mesh_kind,
        ).wait_recv()
    for offset in range(1, nx):
        source_x = lax.rem(my_x + nx - offset, nx)
        pltpu.make_async_remote_copy(
            src_ref=full.at[:, source_x, upper], dst_ref=full.at[:, source_x, upper],
            send_sem=send.at[3, offset], recv_sem=got.at[3, source_x],
            device_id=torus_peer(my_y, source_x, nx), device_id_type=mesh_kind,
        ).wait_recv()
    out_ref[...] = full[...]
    wait_all(along_col, nc, me, back_src, recv3, wsend3, wgot3)
    wout_ref[...] = recv3[...]
    for copy in sends:
        copy.wait_send()


def gather_and_sum(x, local, nx, collective_id):
    rows, lanes = x.shape
    nc = lax.axis_size("col")
    nr = lax.axis_size("row")
    ny = nc // nx
    side = max(nx, ny)
    height, width = local.shape
    part = height // nc
    out, summed = pl.pallas_call(
        functools.partial(gather_and_sum_kernel, nx, ny, nr),
        out_shape=(
            jax.ShapeDtypeStruct((ny, nx, rows, lanes), x.dtype),
            jax.ShapeDtypeStruct((nc, part, width), local.dtype),
        ),
        in_specs=[pl.BlockSpec(memory_space=pltpu.VMEM)] * 2,
        out_specs=(pl.BlockSpec(memory_space=pltpu.VMEM),) * 2,
        scratch_shapes=[
            pltpu.VMEM((ny, nx, rows, lanes), x.dtype),
            pltpu.VMEM((nc, part, width), local.dtype),
            pltpu.VMEM((nr, part, width), local.dtype),
            pltpu.VMEM((nc, part, width), local.dtype),
            (
                pltpu.SemaphoreType.DMA((4, side)),
                pltpu.SemaphoreType.DMA((4, side)),
                pltpu.SemaphoreType.DMA((1,)),
                pltpu.SemaphoreType.DMA((nc,)),
                pltpu.SemaphoreType.DMA((nc,)),
                pltpu.SemaphoreType.DMA((nr,)),
                pltpu.SemaphoreType.DMA((nr,)),
                pltpu.SemaphoreType.DMA((nc,)),
                pltpu.SemaphoreType.DMA((nc,)),
            ),
        ],
        compiler_params=pltpu.CompilerParams(
            collective_id=collective_id, has_side_effects=True,
            vmem_limit_bytes=48 * 1024 * 1024,
        ),
        cost_estimate=pl.CostEstimate(
            flops=local.size, transcendentals=0,
            bytes_accessed=3 * nc * x.size * x.dtype.itemsize + 3 * local.size * 4,
        ),
    )(x, local.reshape(nc, part, width))
    return out.reshape(nc, rows, lanes), summed.reshape(height, width)


def all_sum(local, collective_base):
    row_count = lax.axis_size("row")
    col_count = lax.axis_size("col")
    height, width = local.shape
    by_col = scatter_sum(
        local.reshape(col_count, height // col_count, width), "col", "row", jnp.float32,
        collective_base,
    )
    part = height // col_count
    by_row = scatter_sum(
        by_col.reshape(row_count, part // row_count, width), "row", "col", jnp.float32,
        collective_base + 1,
    )
    back_row = gather_all(by_row, "row", "col", row_count, collective_base + 2)
    back_col = gather_all(back_row.reshape(part, width), "col", "row", col_count, collective_base + 3)
    return back_col.reshape(height, width)


def activation(aggregated, weight, cot_rows):
    hidden = jnp.dot(aggregated, weight, preferred_element_type=jnp.float32)
    sigmoid_value = jax.nn.sigmoid(hidden)
    output = (hidden * sigmoid_value).astype(jnp.bfloat16)
    silu_slope = sigmoid_value * (1.0 + hidden * (1.0 - sigmoid_value))
    hidden_grad = (cot_rows.astype(jnp.float32) * silu_slope).astype(jnp.bfloat16)
    return (output, hidden_grad)


def per_device(tile_values, tile_rows, tile_cols, tile_count, features, weight, cotangent):
    slot_total = tile_values.shape[2]
    tile_edge = tile_values.shape[3]
    tile_block = tile_values.reshape(slot_total, tile_edge, tile_edge)
    row_index = tile_rows.reshape(slot_total)
    col_index = tile_cols.reshape(slot_total)
    live_count = tile_count.reshape(1)
    own_rows = features.shape[0]
    feat_width = features.shape[1]
    row_count = lax.axis_size("row")
    col_count = lax.axis_size("col")
    row_tiles = col_count * own_rows // tile_edge
    col_tiles = row_count * own_rows // tile_edge
    column_block = gather_row(features, 8)
    source = column_block.reshape(col_tiles, tile_edge, feat_width)
    partial_rows = sparse_product(
        tile_block, row_index, col_index, live_count, source, row_tiles, False
    )
    partial_flat = partial_rows.reshape(row_tiles * tile_edge, feat_width)
    node_total = row_count * col_count * own_rows
    aggregated = scatter_sum_2d(
        partial_rows.reshape(col_count, own_rows, feat_width), TORUS_X, jnp.bfloat16, 0
    )
    output, hidden_grad = activation(aggregated, weight, cotangent)
    own_grad = lax.dot_general(
        hidden_grad, weight, (((1,), (1,)), ((), ())), preferred_element_type=jnp.float32
    ).astype(jnp.bfloat16)
    local_grad = lax.dot_general(
        aggregated, hidden_grad, (((0,), (0,)), ((), ())), preferred_element_type=jnp.float32
    )
    row_block, summed_grad = gather_and_sum(own_grad, local_grad, TORUS_X, 7)
    weight_grad = summed_grad * (1.0 / math.sqrt(node_total))
    source_back = row_block.reshape(row_tiles, tile_edge, feat_width)
    partial_cols = sparse_product(
        tile_block, col_index, row_index, live_count, source_back, col_tiles, True
    )
    input_grad = scatter_sum_row(
        partial_cols.reshape(row_count, own_rows, feat_width), jnp.float32, 9
    )
    return (output, weight_grad, input_grad)


def solution(mesh):
    placed = (
        P("row", "col", None, None, None),
        P("row", "col", None),
        P("row", "col", None),
        P("row", "col"),
        P(("row", "col"), None),
        P(),
        P(("row", "col"), None),
    )
    return jax.shard_map(
        per_device,
        mesh=mesh,
        in_specs=placed,
        out_specs=(P(("row", "col"), None), P(), P(("row", "col"), None)),
        check_vma=False,
    )
```

```python
import functools
import math

import jax
import jax.numpy as jnp
from jax import lax
from jax.experimental import pallas as pl
from jax.experimental.pallas import tpu as pltpu
from jax.sharding import PartitionSpec as P

SLOTS_PER_STEP = 32
UNROLL = 32
TORUS_X = 4


def spmm_kernel(transpose, acc_index, src_index, count_ref, tiles_ref, src_ref, out_ref, acc_ref):
    step = pl.program_id(0)
    per_step = tiles_ref.shape[0]
    live = count_ref[0]
    acc_last = acc_ref.shape[0] - 1
    src_last = src_ref.shape[0] - 1

    @pl.when(step == 0)
    def _():
        acc_ref[...] = jnp.zeros_like(acc_ref)

    def one_slot(k, carry):
        slot = step * per_step + k
        target = jnp.clip(acc_index[slot], 0, acc_last)
        picked = jnp.clip(src_index[slot], 0, src_last)
        tile = tiles_ref[k]
        tile = jnp.where(slot < live, tile, jnp.zeros_like(tile))
        block = src_ref[picked]
        if transpose:
            product = lax.dot_general(
                tile, block, (((0,), (0,)), ((), ())), preferred_element_type=jnp.float32
            )
        else:
            product = jnp.dot(tile, block, preferred_element_type=jnp.float32)
        acc_ref[target] += product
        return carry

    lax.fori_loop(0, per_step, one_slot, 0, unroll=UNROLL)

    @pl.when(step == pl.num_programs(0) - 1)
    def _():
        out_ref[...] = acc_ref[...].astype(out_ref.dtype)


def sparse_product(tile_block, acc_index, src_index, live_count, source, segments, transpose):
    slot_total, tile_edge, _ = tile_block.shape
    feat_width = source.shape[2]
    per_step = min(SLOTS_PER_STEP, slot_total)
    steps = slot_total // per_step

    def tile_map(step, acc_ref, src_ref, count_ref):
        last_live = jnp.maximum(count_ref[0] - 1, 0) // per_step
        return (jnp.minimum(step, last_live), 0, 0)

    grid_spec = pltpu.PrefetchScalarGridSpec(
        num_scalar_prefetch=3,
        grid=(steps,),
        in_specs=[
            pl.BlockSpec((per_step, tile_edge, tile_edge), tile_map),
            pl.BlockSpec(source.shape, lambda step, *_: (0, 0, 0)),
        ],
        out_specs=pl.BlockSpec((segments, tile_edge, feat_width), lambda step, *_: (0, 0, 0)),
        scratch_shapes=[pltpu.VMEM((segments, tile_edge, feat_width), jnp.float32)],
    )
    flops = 2 * slot_total * tile_edge * tile_edge * feat_width
    bytes_accessed = (
        tile_block.size * 2 + source.size * 2 + segments * tile_edge * feat_width * 2
    )
    return pl.pallas_call(
        functools.partial(spmm_kernel, transpose),
        out_shape=jax.ShapeDtypeStruct((segments, tile_edge, feat_width), jnp.bfloat16),
        grid_spec=grid_spec,
        compiler_params=pltpu.CompilerParams(
            dimension_semantics=("arbitrary",), vmem_limit_bytes=56 * 1024 * 1024
        ),
        cost_estimate=pl.CostEstimate(
            flops=flops, transcendentals=0, bytes_accessed=bytes_accessed
        ),
    )(acc_index, src_index, live_count, tile_block, source)


def peer_id(axis, other_axis, peer):
    if axis == "row":
        return (peer, lax.axis_index(other_axis))
    return (lax.axis_index(other_axis), peer)


def greet_all(axis, other_axis, n, me):
    barrier = pltpu.get_barrier_semaphore()
    for offset in range(1, n):
        peer = lax.rem(me + offset, n)
        pl.semaphore_signal(
            barrier, 1, device_id=peer_id(axis, other_axis, peer),
            device_id_type=pl.DeviceIdType.MESH,
        )
    pl.semaphore_wait(barrier, n - 1)


def scatter_sum_kernel(axis, other_axis, n, x_hbm, out_ref, recv, send_sems, recv_sems, own_sem):
    me = lax.axis_index(axis)
    greet_all(axis, other_axis, n, me)
    own = pltpu.make_async_copy(x_hbm.at[me], recv.at[me], own_sem)
    own.start()
    sends = []
    for offset in range(1, n):
        peer = lax.rem(me + offset, n)
        copy = pltpu.make_async_remote_copy(
            src_ref=x_hbm.at[peer],
            dst_ref=recv.at[me],
            send_sem=send_sems.at[offset],
            recv_sem=recv_sems.at[me],
            device_id=peer_id(axis, other_axis, peer),
            device_id_type=pl.DeviceIdType.MESH,
        )
        copy.start()
        sends.append(copy)
    own.wait()
    for offset in range(1, n):
        source = lax.rem(me + n - offset, n)
        pltpu.make_async_remote_copy(
            src_ref=x_hbm.at[source],
            dst_ref=recv.at[source],
            send_sem=send_sems.at[offset],
            recv_sem=recv_sems.at[source],
            device_id=peer_id(axis, other_axis, source),
            device_id_type=pl.DeviceIdType.MESH,
        ).wait_recv()
    total = recv[0].astype(jnp.float32)
    for j in range(1, n):
        total = total + recv[j].astype(jnp.float32)
    out_ref[...] = total.astype(out_ref.dtype)
    for copy in sends:
        copy.wait_send()


def scatter_sum(x, axis, other_axis, out_dtype, collective_id):
    n, rows, lanes = x.shape
    return pl.pallas_call(
        functools.partial(scatter_sum_kernel, axis, other_axis, n),
        out_shape=jax.ShapeDtypeStruct((rows, lanes), out_dtype),
        in_specs=[pl.BlockSpec(memory_space=pl.ANY)],
        out_specs=pl.BlockSpec(memory_space=pltpu.VMEM),
        scratch_shapes=[
            pltpu.VMEM((n, rows, lanes), x.dtype),
            pltpu.SemaphoreType.DMA((n,)),
            pltpu.SemaphoreType.DMA((n,)),
            pltpu.SemaphoreType.DMA(()),
        ],
        compiler_params=pltpu.CompilerParams(
            collective_id=collective_id, has_side_effects=True,
            vmem_limit_bytes=48 * 1024 * 1024,
        ),
        cost_estimate=pl.CostEstimate(
            flops=x.size, transcendentals=0, bytes_accessed=3 * x.size * x.dtype.itemsize
        ),
    )(x)


def gather_all_kernel(axis, other_axis, n, x_ref, out_ref, recv, send_sems, recv_sems):
    me = lax.axis_index(axis)
    recv[me] = x_ref[...]
    greet_all(axis, other_axis, n, me)
    sends = []
    for offset in range(1, n):
        peer = lax.rem(me + offset, n)
        copy = pltpu.make_async_remote_copy(
            src_ref=x_ref,
            dst_ref=recv.at[me],
            send_sem=send_sems.at[offset],
            recv_sem=recv_sems.at[me],
            device_id=peer_id(axis, other_axis, peer),
            device_id_type=pl.DeviceIdType.MESH,
        )
        copy.start()
        sends.append(copy)
    for offset in range(1, n):
        source = lax.rem(me + n - offset, n)
        pltpu.make_async_remote_copy(
            src_ref=x_ref,
            dst_ref=recv.at[source],
            send_sem=send_sems.at[offset],
            recv_sem=recv_sems.at[source],
            device_id=peer_id(axis, other_axis, source),
            device_id_type=pl.DeviceIdType.MESH,
        ).wait_recv()
    out_ref[...] = recv[...]
    for copy in sends:
        copy.wait_send()


def gather_all(x, axis, other_axis, n, collective_id):
    rows, lanes = x.shape
    return pl.pallas_call(
        functools.partial(gather_all_kernel, axis, other_axis, n),
        out_shape=jax.ShapeDtypeStruct((n, rows, lanes), x.dtype),
        in_specs=[pl.BlockSpec(memory_space=pltpu.VMEM)],
        out_specs=pl.BlockSpec(memory_space=pltpu.VMEM),
        scratch_shapes=[
            pltpu.VMEM((n, rows, lanes), x.dtype),
            pltpu.SemaphoreType.DMA((n,)),
            pltpu.SemaphoreType.DMA((n,)),
        ],
        compiler_params=pltpu.CompilerParams(
            collective_id=collective_id, has_side_effects=True,
            vmem_limit_bytes=48 * 1024 * 1024,
        ),
        cost_estimate=pl.CostEstimate(
            flops=0, transcendentals=0, bytes_accessed=3 * n * x.size * x.dtype.itemsize
        ),
    )(x)


def torus_peer(y, x, nx):
    return (lax.axis_index("row"), y * nx + x)


def scatter_sum_2d_kernel(nx, ny, x_hbm, out_ref, recv1, mid, recv2, sems):
    send1, got1, send2, got2, own_sems = sems
    me = lax.axis_index("col")
    my_y = me // nx
    my_x = lax.rem(me, nx)
    half = x_hbm.shape[2] // 2
    lower = pl.ds(0, half)
    upper = pl.ds(half, half)
    mesh_kind = pl.DeviceIdType.MESH

    barrier = pltpu.get_barrier_semaphore()
    for offset in range(1, nx):
        pl.semaphore_signal(barrier, 1, device_id=torus_peer(my_y, lax.rem(my_x + offset, nx), nx),
                            device_id_type=mesh_kind)
    for offset in range(1, ny):
        pl.semaphore_signal(barrier, 1, device_id=torus_peer(lax.rem(my_y + offset, ny), my_x, nx),
                            device_id_type=mesh_kind)
    pl.semaphore_wait(barrier, nx + ny - 2)

    own_a = pltpu.make_async_copy(x_hbm.at[:, my_x, lower], recv1.at[0, my_x], own_sems.at[0])
    own_b = pltpu.make_async_copy(x_hbm.at[my_y, :, upper], recv1.at[1, my_y], own_sems.at[1])
    own_a.start()
    own_b.start()
    sends = []
    for offset in range(1, nx):
        peer_x = lax.rem(my_x + offset, nx)
        copy = pltpu.make_async_remote_copy(
            src_ref=x_hbm.at[:, peer_x, lower], dst_ref=recv1.at[0, my_x],
            send_sem=send1.at[0, offset], recv_sem=got1.at[0, my_x],
            device_id=torus_peer(my_y, peer_x, nx), device_id_type=mesh_kind,
        )
        copy.start()
        sends.append(copy)
    for offset in range(1, ny):
        peer_y = lax.rem(my_y + offset, ny)
        copy = pltpu.make_async_remote_copy(
            src_ref=x_hbm.at[peer_y, :, upper], dst_ref=recv1.at[1, my_y],
            send_sem=send1.at[1, offset], recv_sem=got1.at[1, my_y],
            device_id=torus_peer(peer_y, my_x, nx), device_id_type=mesh_kind,
        )
        copy.start()
        sends.append(copy)
    own_a.wait()
    own_b.wait()
    for offset in range(1, nx):
        source_x = lax.rem(my_x + nx - offset, nx)
        pltpu.make_async_remote_copy(
            src_ref=x_hbm.at[:, source_x, lower], dst_ref=recv1.at[0, source_x],
            send_sem=send1.at[0, offset], recv_sem=got1.at[0, source_x],
            device_id=torus_peer(my_y, source_x, nx), device_id_type=mesh_kind,
        ).wait_recv()

    def add_up(stack):
        total = stack[0].astype(jnp.float32)
        for j in range(1, stack.shape[0]):
            total = total + stack[j].astype(jnp.float32)
        return total

    for target in range(ny):
        mid[0, target] = add_up(recv1[0, :, target]).astype(mid.dtype)
    recv2[0, my_y] = mid[0, my_y]

    for offset in range(1, ny):
        peer_y = lax.rem(my_y + offset, ny)
        copy = pltpu.make_async_remote_copy(
            src_ref=mid.at[0, peer_y], dst_ref=recv2.at[0, my_y],
            send_sem=send2.at[0, offset], recv_sem=got2.at[0, my_y],
            device_id=torus_peer(peer_y, my_x, nx), device_id_type=mesh_kind,
        )
        copy.start()
        sends.append(copy)
    for offset in range(1, ny):
        source_y = lax.rem(my_y + ny - offset, ny)
        pltpu.make_async_remote_copy(
            src_ref=x_hbm.at[source_y, :, upper], dst_ref=recv1.at[1, source_y],
            send_sem=send1.at[1, offset], recv_sem=got1.at[1, source_y],
            device_id=torus_peer(source_y, my_x, nx), device_id_type=mesh_kind,
        ).wait_recv()
    for target in range(nx):
        mid[1, target] = add_up(recv1[1, :, target]).astype(mid.dtype)
    recv2[1, my_x] = mid[1, my_x]
    for offset in range(1, nx):
        peer_x = lax.rem(my_x + offset, nx)
        copy = pltpu.make_async_remote_copy(
            src_ref=mid.at[1, peer_x], dst_ref=recv2.at[1, my_x],
            send_sem=send2.at[1, offset], recv_sem=got2.at[1, my_x],
            device_id=torus_peer(my_y, peer_x, nx), device_id_type=mesh_kind,
        )
        copy.start()
        sends.append(copy)
    for offset in range(1, ny):
        source_y = lax.rem(my_y + ny - offset, ny)
        pltpu.make_async_remote_copy(
            src_ref=mid.at[0, source_y], dst_ref=recv2.at[0, source_y],
            send_sem=send2.at[0, offset], recv_sem=got2.at[0, source_y],
            device_id=torus_peer(source_y, my_x, nx), device_id_type=mesh_kind,
        ).wait_recv()
    out_ref[lower] = add_up(recv2[0]).astype(out_ref.dtype)
    for offset in range(1, nx):
        source_x = lax.rem(my_x + nx - offset, nx)
        pltpu.make_async_remote_copy(
            src_ref=mid.at[1, source_x], dst_ref=recv2.at[1, source_x],
            send_sem=send2.at[1, offset], recv_sem=got2.at[1, source_x],
            device_id=torus_peer(my_y, source_x, nx), device_id_type=mesh_kind,
        ).wait_recv()
    out_ref[upper] = add_up(recv2[1]).astype(out_ref.dtype)
    for copy in sends:
        copy.wait_send()


def scatter_sum_2d(x, nx, out_dtype, collective_id):
    n, rows, lanes = x.shape
    ny = n // nx
    half = rows // 2
    side = max(nx, ny)
    return pl.pallas_call(
        functools.partial(scatter_sum_2d_kernel, nx, ny),
        out_shape=jax.ShapeDtypeStruct((rows, lanes), out_dtype),
        in_specs=[pl.BlockSpec(memory_space=pl.ANY)],
        out_specs=pl.BlockSpec(memory_space=pltpu.VMEM),
        scratch_shapes=[
            pltpu.VMEM((2, side, side, half, lanes), x.dtype),
            pltpu.VMEM((2, side, half, lanes), x.dtype),
            pltpu.VMEM((2, side, half, lanes), x.dtype),
            (
                pltpu.SemaphoreType.DMA((2, side)),
                pltpu.SemaphoreType.DMA((2, side)),
                pltpu.SemaphoreType.DMA((2, side)),
                pltpu.SemaphoreType.DMA((2, side)),
                pltpu.SemaphoreType.DMA((2,)),
            ),
        ],
        compiler_params=pltpu.CompilerParams(
            collective_id=collective_id, has_side_effects=True,
            vmem_limit_bytes=48 * 1024 * 1024,
        ),
        cost_estimate=pl.CostEstimate(
            flops=x.size, transcendentals=0, bytes_accessed=3 * x.size * x.dtype.itemsize
        ),
    )(x.reshape(ny, nx, rows, lanes))


def row_peer(index):
    return (index, lax.axis_index("col"))


def greet_row(my_z, my_core, nz):
    barrier = pltpu.get_barrier_semaphore()
    mesh_kind = pl.DeviceIdType.MESH
    pl.semaphore_signal(barrier, 1, device_id=row_peer(my_z * 2 + 1 - my_core), device_id_type=mesh_kind)
    for offset in range(1, nz):
        peer_z = lax.rem(my_z + offset, nz)
        pl.semaphore_signal(barrier, 1, device_id=row_peer(peer_z * 2 + my_core), device_id_type=mesh_kind)
    pl.semaphore_wait(barrier, nz)


def scatter_sum_row_kernel(nz, x_hbm, out_ref, own1, recv1, mid, recv2, sems):
    send1, got1, send2, got2, own_sem = sems
    mesh_kind = pl.DeviceIdType.MESH
    me = lax.axis_index("row")
    my_z = me // 2
    my_core = lax.rem(me, 2)
    other_core = 1 - my_core
    partner = row_peer(my_z * 2 + other_core)
    greet_row(my_z, my_core, nz)
    own = pltpu.make_async_copy(x_hbm.at[:, my_core], own1, own_sem.at[0])
    own.start()
    sends = []
    for offset in range(nz):
        target_z = lax.rem(my_z + offset + 1, nz)
        copy = pltpu.make_async_remote_copy(
            src_ref=x_hbm.at[target_z, other_core], dst_ref=recv1.at[target_z],
            send_sem=send1.at[offset], recv_sem=got1.at[target_z],
            device_id=partner, device_id_type=mesh_kind,
        )
        copy.start()
        sends.append(copy)
    own.wait()
    for offset in range(nz - 1):
        target_z = lax.rem(my_z + offset + 1, nz)
        pltpu.make_async_remote_copy(
            src_ref=x_hbm.at[target_z, other_core], dst_ref=recv1.at[target_z],
            send_sem=send1.at[offset], recv_sem=got1.at[target_z],
            device_id=partner, device_id_type=mesh_kind,
        ).wait_recv()
        mid[target_z] = (own1[target_z].astype(jnp.float32) + recv1[target_z].astype(jnp.float32)).astype(mid.dtype)
        copy = pltpu.make_async_remote_copy(
            src_ref=mid.at[target_z], dst_ref=recv2.at[my_z],
            send_sem=send2.at[offset + 1], recv_sem=got2.at[my_z],
            device_id=row_peer(target_z * 2 + my_core), device_id_type=mesh_kind,
        )
        copy.start()
        sends.append(copy)
    pltpu.make_async_remote_copy(
        src_ref=x_hbm.at[my_z, other_core], dst_ref=recv1.at[my_z],
        send_sem=send1.at[nz - 1], recv_sem=got1.at[my_z],
        device_id=partner, device_id_type=mesh_kind,
    ).wait_recv()
    total = own1[my_z].astype(jnp.float32) + recv1[my_z].astype(jnp.float32)
    for offset in range(1, nz):
        source_z = lax.rem(my_z + nz - offset, nz)
        pltpu.make_async_remote_copy(
            src_ref=mid.at[source_z], dst_ref=recv2.at[source_z],
            send_sem=send2.at[offset], recv_sem=got2.at[source_z],
            device_id=row_peer(source_z * 2 + my_core), device_id_type=mesh_kind,
        ).wait_recv()
        total = total + recv2[source_z].astype(jnp.float32)
    out_ref[...] = total.astype(out_ref.dtype)
    for copy in sends:
        copy.wait_send()


def scatter_sum_row(x, out_dtype, collective_id):
    n, rows, lanes = x.shape
    nz = n // 2
    return pl.pallas_call(
        functools.partial(scatter_sum_row_kernel, nz),
        out_shape=jax.ShapeDtypeStruct((rows, lanes), out_dtype),
        in_specs=[pl.BlockSpec(memory_space=pl.ANY)],
        out_specs=pl.BlockSpec(memory_space=pltpu.VMEM),
        scratch_shapes=[
            pltpu.VMEM((nz, rows, lanes), x.dtype),
            pltpu.VMEM((nz, rows, lanes), x.dtype),
            pltpu.VMEM((nz, rows, lanes), x.dtype),
            pltpu.VMEM((nz, rows, lanes), x.dtype),
            (
                pltpu.SemaphoreType.DMA((nz,)),
                pltpu.SemaphoreType.DMA((nz,)),
                pltpu.SemaphoreType.DMA((nz,)),
                pltpu.SemaphoreType.DMA((nz,)),
                pltpu.SemaphoreType.DMA((1,)),
            ),
        ],
        compiler_params=pltpu.CompilerParams(
            collective_id=collective_id, has_side_effects=True,
            vmem_limit_bytes=48 * 1024 * 1024,
        ),
        cost_estimate=pl.CostEstimate(
            flops=x.size, transcendentals=0, bytes_accessed=3 * x.size * x.dtype.itemsize
        ),
    )(x.reshape(nz, 2, rows, lanes))


def gather_row_kernel(nz, x_ref, out_ref, full, sems):
    send1, got1, send2, got2, own_sem = sems
    mesh_kind = pl.DeviceIdType.MESH
    me = lax.axis_index("row")
    my_z = me // 2
    my_core = lax.rem(me, 2)
    other_core = 1 - my_core
    partner = row_peer(my_z * 2 + other_core)
    greet_row(my_z, my_core, nz)
    own = pltpu.make_async_copy(x_ref, full.at[my_z, my_core], own_sem.at[0])
    own.start()
    sends = []
    for offset in range(1, nz):
        peer_z = lax.rem(my_z + offset, nz)
        copy = pltpu.make_async_remote_copy(
            src_ref=x_ref, dst_ref=full.at[my_z, my_core],
            send_sem=send1.at[offset], recv_sem=got1.at[my_z],
            device_id=row_peer(peer_z * 2 + my_core), device_id_type=mesh_kind,
        )
        copy.start()
        sends.append(copy)

    def forward(block_z, slot):
        copy = pltpu.make_async_remote_copy(
            src_ref=full.at[block_z, my_core], dst_ref=full.at[block_z, my_core],
            send_sem=send2.at[slot], recv_sem=got2.at[block_z],
            device_id=partner, device_id_type=mesh_kind,
        )
        copy.start()
        sends.append(copy)

    own.wait()
    forward(my_z, 0)
    for offset in range(1, nz):
        source_z = lax.rem(my_z + nz - offset, nz)
        pltpu.make_async_remote_copy(
            src_ref=x_ref, dst_ref=full.at[source_z, my_core],
            send_sem=send1.at[offset], recv_sem=got1.at[source_z],
            device_id=row_peer(source_z * 2 + my_core), device_id_type=mesh_kind,
        ).wait_recv()
        forward(source_z, offset)
    for offset in range(nz):
        block_z = lax.rem(my_z + nz - offset, nz)
        pltpu.make_async_remote_copy(
            src_ref=full.at[block_z, other_core], dst_ref=full.at[block_z, other_core],
            send_sem=send2.at[offset], recv_sem=got2.at[block_z],
            device_id=partner, device_id_type=mesh_kind,
        ).wait_recv()
    for copy in sends:
        copy.wait_send()
    out_ref[...] = full[...]


def gather_row(x, collective_id):
    rows, lanes = x.shape
    nz = lax.axis_size("row") // 2
    out = pl.pallas_call(
        functools.partial(gather_row_kernel, nz),
        out_shape=jax.ShapeDtypeStruct((nz, 2, rows, lanes), x.dtype),
        in_specs=[pl.BlockSpec(memory_space=pltpu.VMEM)],
        out_specs=pl.BlockSpec(memory_space=pltpu.VMEM),
        scratch_shapes=[
            pltpu.VMEM((nz, 2, rows, lanes), x.dtype),
            (
                pltpu.SemaphoreType.DMA((nz,)),
                pltpu.SemaphoreType.DMA((nz,)),
                pltpu.SemaphoreType.DMA((nz,)),
                pltpu.SemaphoreType.DMA((nz,)),
                pltpu.SemaphoreType.DMA((1,)),
            ),
        ],
        compiler_params=pltpu.CompilerParams(
            collective_id=collective_id, has_side_effects=True,
            vmem_limit_bytes=48 * 1024 * 1024,
        ),
        cost_estimate=pl.CostEstimate(
            flops=0, transcendentals=0, bytes_accessed=3 * 2 * nz * x.size * x.dtype.itemsize
        ),
    )(x)
    return out.reshape(2 * nz * rows, lanes)


def gather_all_2d_kernel(nx, ny, x_ref, out_ref, full, sems):
    send, got, own_sem = sems
    mesh_kind = pl.DeviceIdType.MESH
    me = lax.axis_index("col")
    my_y = me // nx
    my_x = lax.rem(me, nx)
    half = x_ref.shape[0] // 2
    lower = pl.ds(0, half)
    upper = pl.ds(half, half)

    barrier = pltpu.get_barrier_semaphore()
    for offset in range(1, nx):
        pl.semaphore_signal(barrier, 1, device_id=torus_peer(my_y, lax.rem(my_x + offset, nx), nx),
                            device_id_type=mesh_kind)
    for offset in range(1, ny):
        pl.semaphore_signal(barrier, 1, device_id=torus_peer(lax.rem(my_y + offset, ny), my_x, nx),
                            device_id_type=mesh_kind)
    pl.semaphore_wait(barrier, nx + ny - 2)

    own = pltpu.make_async_copy(x_ref, full.at[my_y, my_x], own_sem.at[0])
    own.start()
    sends = []
    for offset in range(1, nx):
        peer_x = lax.rem(my_x + offset, nx)
        copy = pltpu.make_async_remote_copy(
            src_ref=x_ref.at[lower], dst_ref=full.at[my_y, my_x, lower],
            send_sem=send.at[0, offset], recv_sem=got.at[0, my_x],
            device_id=torus_peer(my_y, peer_x, nx), device_id_type=mesh_kind,
        )
        copy.start()
        sends.append(copy)
    for offset in range(1, ny):
        peer_y = lax.rem(my_y + offset, ny)
        copy = pltpu.make_async_remote_copy(
            src_ref=x_ref.at[upper], dst_ref=full.at[my_y, my_x, upper],
            send_sem=send.at[1, offset], recv_sem=got.at[1, my_y],
            device_id=torus_peer(peer_y, my_x, nx), device_id_type=mesh_kind,
        )
        copy.start()
        sends.append(copy)
    own.wait()
    for offset in range(1, nx):
        source_x = lax.rem(my_x + nx - offset, nx)
        pltpu.make_async_remote_copy(
            src_ref=x_ref.at[lower], dst_ref=full.at[my_y, source_x, lower],
            send_sem=send.at[0, offset], recv_sem=got.at[0, source_x],
            device_id=torus_peer(my_y, source_x, nx), device_id_type=mesh_kind,
        ).wait_recv()
    for offset in range(1, ny):
        peer_y = lax.rem(my_y + offset, ny)
        copy = pltpu.make_async_remote_copy(
            src_ref=full.at[my_y, :, lower], dst_ref=full.at[my_y, :, lower],
            send_sem=send.at[2, offset], recv_sem=got.at[2, my_y],
            device_id=torus_peer(peer_y, my_x, nx), device_id_type=mesh_kind,
        )
        copy.start()
        sends.append(copy)
    for offset in range(1, ny):
        source_y = lax.rem(my_y + ny - offset, ny)
        pltpu.make_async_remote_copy(
            src_ref=x_ref.at[upper], dst_ref=full.at[source_y, my_x, upper],
            send_sem=send.at[1, offset], recv_sem=got.at[1, source_y],
            device_id=torus_peer(source_y, my_x, nx), device_id_type=mesh_kind,
        ).wait_recv()
    for offset in range(1, nx):
        peer_x = lax.rem(my_x + offset, nx)
        copy = pltpu.make_async_remote_copy(
            src_ref=full.at[:, my_x, upper], dst_ref=full.at[:, my_x, upper],
            send_sem=send.at[3, offset], recv_sem=got.at[3, my_x],
            device_id=torus_peer(my_y, peer_x, nx), device_id_type=mesh_kind,
        )
        copy.start()
        sends.append(copy)
    for offset in range(1, ny):
        source_y = lax.rem(my_y + ny - offset, ny)
        pltpu.make_async_remote_copy(
            src_ref=full.at[source_y, :, lower], dst_ref=full.at[source_y, :, lower],
            send_sem=send.at[2, offset], recv_sem=got.at[2, source_y],
            device_id=torus_peer(source_y, my_x, nx), device_id_type=mesh_kind,
        ).wait_recv()
    for offset in range(1, nx):
        source_x = lax.rem(my_x + nx - offset, nx)
        pltpu.make_async_remote_copy(
            src_ref=full.at[:, source_x, upper], dst_ref=full.at[:, source_x, upper],
            send_sem=send.at[3, offset], recv_sem=got.at[3, source_x],
            device_id=torus_peer(my_y, source_x, nx), device_id_type=mesh_kind,
        ).wait_recv()
    for copy in sends:
        copy.wait_send()
    out_ref[...] = full[...]


def gather_all_2d(x, nx, collective_id):
    rows, lanes = x.shape
    n = lax.axis_size("col")
    ny = n // nx
    side = max(nx, ny)
    out = pl.pallas_call(
        functools.partial(gather_all_2d_kernel, nx, ny),
        out_shape=jax.ShapeDtypeStruct((ny, nx, rows, lanes), x.dtype),
        in_specs=[pl.BlockSpec(memory_space=pltpu.VMEM)],
        out_specs=pl.BlockSpec(memory_space=pltpu.VMEM),
        scratch_shapes=[
            pltpu.VMEM((ny, nx, rows, lanes), x.dtype),
            (
                pltpu.SemaphoreType.DMA((4, side)),
                pltpu.SemaphoreType.DMA((4, side)),
                pltpu.SemaphoreType.DMA((1,)),
            ),
        ],
        compiler_params=pltpu.CompilerParams(
            collective_id=collective_id, has_side_effects=True,
            vmem_limit_bytes=48 * 1024 * 1024,
        ),
        cost_estimate=pl.CostEstimate(
            flops=0, transcendentals=0, bytes_accessed=3 * n * x.size * x.dtype.itemsize
        ),
    )(x)
    return out.reshape(n, rows, lanes)


def fused_sum_kernel(nr, nc, x_ref, out_ref, recv1, recv2, recv3, sems):
    send1, got1, send2, got2, send3, got3 = sems
    mesh_kind = pl.DeviceIdType.MESH
    my_r = lax.axis_index("row")
    my_c = lax.axis_index("col")
    barrier = pltpu.get_barrier_semaphore()
    for offset in range(1, nc):
        pl.semaphore_signal(barrier, 1, device_id=(my_r, lax.rem(my_c + offset, nc)),
                            device_id_type=mesh_kind)
    for offset in range(1, nr):
        pl.semaphore_signal(barrier, 1, device_id=(lax.rem(my_r + offset, nr), my_c),
                            device_id_type=mesh_kind)
    pl.semaphore_wait(barrier, nc + nr - 2)

    def exchange(peers, axis_count, src_of, dst, send, got, me_index):
        started = []
        for offset in range(1, axis_count):
            peer = lax.rem(me_index + offset, axis_count)
            copy = pltpu.make_async_remote_copy(
                src_ref=src_of(peer), dst_ref=dst.at[me_index],
                send_sem=send.at[offset], recv_sem=got.at[me_index],
                device_id=peers(peer), device_id_type=mesh_kind,
            )
            copy.start()
            started.append(copy)
        for offset in range(1, axis_count):
            source = lax.rem(me_index + axis_count - offset, axis_count)
            pltpu.make_async_remote_copy(
                src_ref=src_of(source), dst_ref=dst.at[source],
                send_sem=send.at[offset], recv_sem=got.at[source],
                device_id=peers(source), device_id_type=mesh_kind,
            ).wait_recv()
        return started

    along_col = lambda peer: (my_r, peer)
    along_row = lambda peer: (peer, my_c)
    recv1[my_c] = x_ref[my_c]
    sends = exchange(along_col, nc, lambda peer: x_ref.at[peer], recv1, send1, got1, my_c)
    part = recv1[0]
    for j in range(1, nc):
        part = part + recv1[j]
    recv2[my_r] = part
    sends += exchange(along_row, nr, lambda peer: recv2.at[my_r], recv2, send2, got2, my_r)
    total = recv2[0]
    for j in range(1, nr):
        total = total + recv2[j]
    recv3[my_c] = total
    sends += exchange(along_col, nc, lambda peer: recv3.at[my_c], recv3, send3, got3, my_c)
    out_ref[...] = recv3[...]
    for copy in sends:
        copy.wait_send()


def fused_sum(local, collective_id):
    nr = lax.axis_size("row")
    nc = lax.axis_size("col")
    height, width = local.shape
    part = height // nc
    out = pl.pallas_call(
        functools.partial(fused_sum_kernel, nr, nc),
        out_shape=jax.ShapeDtypeStruct((nc, part, width), local.dtype),
        in_specs=[pl.BlockSpec(memory_space=pltpu.VMEM)],
        out_specs=pl.BlockSpec(memory_space=pltpu.VMEM),
        scratch_shapes=[
            pltpu.VMEM((nc, part, width), local.dtype),
            pltpu.VMEM((nr, part, width), local.dtype),
            pltpu.VMEM((nc, part, width), local.dtype),
            (
                pltpu.SemaphoreType.DMA((nc,)),
                pltpu.SemaphoreType.DMA((nc,)),
                pltpu.SemaphoreType.DMA((nr,)),
                pltpu.SemaphoreType.DMA((nr,)),
                pltpu.SemaphoreType.DMA((nc,)),
                pltpu.SemaphoreType.DMA((nc,)),
            ),
        ],
        compiler_params=pltpu.CompilerParams(
            collective_id=collective_id, has_side_effects=True,
            vmem_limit_bytes=48 * 1024 * 1024,
        ),
        cost_estimate=pl.CostEstimate(
            flops=local.size, transcendentals=0, bytes_accessed=3 * local.size * 4
        ),
    )(local.reshape(nc, part, width))
    return out.reshape(height, width)


def gather_and_sum_kernel(nx, ny, nr, x_ref, w_ref, out_ref, wout_ref, full, recv1, recv2, recv3, sems):
    send, got, own_sem, wsend1, wgot1, wsend2, wgot2, wsend3, wgot3 = sems
    mesh_kind = pl.DeviceIdType.MESH
    nc = nx * ny
    me = lax.axis_index("col")
    my_r = lax.axis_index("row")
    my_y = me // nx
    my_x = lax.rem(me, nx)
    half = x_ref.shape[0] // 2
    lower = pl.ds(0, half)
    upper = pl.ds(half, half)
    along_col = lambda peer: (my_r, peer)
    along_row = lambda peer: (peer, me)

    barrier = pltpu.get_barrier_semaphore()
    for offset in range(1, nc):
        pl.semaphore_signal(barrier, 1, device_id=along_col(lax.rem(me + offset, nc)),
                            device_id_type=mesh_kind)
    for offset in range(1, nr):
        pl.semaphore_signal(barrier, 1, device_id=along_row(lax.rem(my_r + offset, nr)),
                            device_id_type=mesh_kind)
    pl.semaphore_wait(barrier, nc + nr - 2)

    def start_all(peers, count, me_index, src_of, dst, sem_send, sem_got):
        started = []
        for offset in range(1, count):
            peer = lax.rem(me_index + offset, count)
            copy = pltpu.make_async_remote_copy(
                src_ref=src_of(peer), dst_ref=dst.at[me_index],
                send_sem=sem_send.at[offset], recv_sem=sem_got.at[me_index],
                device_id=peers(peer), device_id_type=mesh_kind,
            )
            copy.start()
            started.append(copy)
        return started

    def wait_all(peers, count, me_index, src_of, dst, sem_send, sem_got):
        for offset in range(1, count):
            source = lax.rem(me_index + count - offset, count)
            pltpu.make_async_remote_copy(
                src_ref=src_of(source), dst_ref=dst.at[source],
                send_sem=sem_send.at[offset], recv_sem=sem_got.at[source],
                device_id=peers(source), device_id_type=mesh_kind,
            ).wait_recv()

    own = pltpu.make_async_copy(x_ref, full.at[my_y, my_x], own_sem.at[0])
    own.start()
    sends = []
    for offset in range(1, nx):
        peer_x = lax.rem(my_x + offset, nx)
        copy = pltpu.make_async_remote_copy(
            src_ref=x_ref.at[lower], dst_ref=full.at[my_y, my_x, lower],
            send_sem=send.at[0, offset], recv_sem=got.at[0, my_x],
            device_id=torus_peer(my_y, peer_x, nx), device_id_type=mesh_kind,
        )
        copy.start()
        sends.append(copy)
    for offset in range(1, ny):
        peer_y = lax.rem(my_y + offset, ny)
        copy = pltpu.make_async_remote_copy(
            src_ref=x_ref.at[upper], dst_ref=full.at[my_y, my_x, upper],
            send_sem=send.at[1, offset], recv_sem=got.at[1, my_y],
            device_id=torus_peer(peer_y, my_x, nx), device_id_type=mesh_kind,
        )
        copy.start()
        sends.append(copy)
    recv1[me] = w_ref[me]
    weight_src = lambda peer: w_ref.at[peer]
    sends += start_all(along_col, nc, me, weight_src, recv1, wsend1, wgot1)
    own.wait()
    for offset in range(1, nx):
        source_x = lax.rem(my_x + nx - offset, nx)
        pltpu.make_async_remote_copy(
            src_ref=x_ref.at[lower], dst_ref=full.at[my_y, source_x, lower],
            send_sem=send.at[0, offset], recv_sem=got.at[0, source_x],
            device_id=torus_peer(my_y, source_x, nx), device_id_type=mesh_kind,
        ).wait_recv()
    for offset in range(1, ny):
        peer_y = lax.rem(my_y + offset, ny)
        copy = pltpu.make_async_remote_copy(
            src_ref=full.at[my_y, :, lower], dst_ref=full.at[my_y, :, lower],
            send_sem=send.at[2, offset], recv_sem=got.at[2, my_y],
            device_id=torus_peer(peer_y, my_x, nx), device_id_type=mesh_kind,
        )
        copy.start()
        sends.append(copy)
    for offset in range(1, ny):
        source_y = lax.rem(my_y + ny - offset, ny)
        pltpu.make_async_remote_copy(
            src_ref=x_ref.at[upper], dst_ref=full.at[source_y, my_x, upper],
            send_sem=send.at[1, offset], recv_sem=got.at[1, source_y],
            device_id=torus_peer(source_y, my_x, nx), device_id_type=mesh_kind,
        ).wait_recv()
    for offset in range(1, nx):
        peer_x = lax.rem(my_x + offset, nx)
        copy = pltpu.make_async_remote_copy(
            src_ref=full.at[:, my_x, upper], dst_ref=full.at[:, my_x, upper],
            send_sem=send.at[3, offset], recv_sem=got.at[3, my_x],
            device_id=torus_peer(my_y, peer_x, nx), device_id_type=mesh_kind,
        )
        copy.start()
        sends.append(copy)

    wait_all(along_col, nc, me, weight_src, recv1, wsend1, wgot1)
    part = recv1[0]
    for j in range(1, nc):
        part = part + recv1[j]
    recv2[my_r] = part
    row_src = lambda peer: recv2.at[my_r]
    sends += start_all(along_row, nr, my_r, row_src, recv2, wsend2, wgot2)
    wait_all(along_row, nr, my_r, row_src, recv2, wsend2, wgot2)
    total = recv2[0]
    for j in range(1, nr):
        total = total + recv2[j]
    recv3[me] = total
    back_src = lambda peer: recv3.at[me]
    sends += start_all(along_col, nc, me, back_src, recv3, wsend3, wgot3)

    for offset in range(1, ny):
        source_y = lax.rem(my_y + ny - offset, ny)
        pltpu.make_async_remote_copy(
            src_ref=full.at[source_y, :, lower], dst_ref=full.at[source_y, :, lower],
            send_sem=send.at[2, offset], recv_sem=got.at[2, source_y],
            device_id=torus_peer(source_y, my_x, nx), device_id_type=mesh_kind,
        ).wait_recv()
    for offset in range(1, nx):
        source_x = lax.rem(my_x + nx - offset, nx)
        pltpu.make_async_remote_copy(
            src_ref=full.at[:, source_x, upper], dst_ref=full.at[:, source_x, upper],
            send_sem=send.at[3, offset], recv_sem=got.at[3, source_x],
            device_id=torus_peer(my_y, source_x, nx), device_id_type=mesh_kind,
        ).wait_recv()
    out_ref[...] = full[...]
    wait_all(along_col, nc, me, back_src, recv3, wsend3, wgot3)
    wout_ref[...] = recv3[...]
    for copy in sends:
        copy.wait_send()


def gather_and_sum(x, local, nx, collective_id):
    rows, lanes = x.shape
    nc = lax.axis_size("col")
    nr = lax.axis_size("row")
    ny = nc // nx
    side = max(nx, ny)
    height, width = local.shape
    part = height // nc
    out, summed = pl.pallas_call(
        functools.partial(gather_and_sum_kernel, nx, ny, nr),
        out_shape=(
            jax.ShapeDtypeStruct((ny, nx, rows, lanes), x.dtype),
            jax.ShapeDtypeStruct((nc, part, width), local.dtype),
        ),
        in_specs=[pl.BlockSpec(memory_space=pltpu.VMEM)] * 2,
        out_specs=(pl.BlockSpec(memory_space=pltpu.VMEM),) * 2,
        scratch_shapes=[
            pltpu.VMEM((ny, nx, rows, lanes), x.dtype),
            pltpu.VMEM((nc, part, width), local.dtype),
            pltpu.VMEM((nr, part, width), local.dtype),
            pltpu.VMEM((nc, part, width), local.dtype),
            (
                pltpu.SemaphoreType.DMA((4, side)),
                pltpu.SemaphoreType.DMA((4, side)),
                pltpu.SemaphoreType.DMA((1,)),
                pltpu.SemaphoreType.DMA((nc,)),
                pltpu.SemaphoreType.DMA((nc,)),
                pltpu.SemaphoreType.DMA((nr,)),
                pltpu.SemaphoreType.DMA((nr,)),
                pltpu.SemaphoreType.DMA((nc,)),
                pltpu.SemaphoreType.DMA((nc,)),
            ),
        ],
        compiler_params=pltpu.CompilerParams(
            collective_id=collective_id, has_side_effects=True,
            vmem_limit_bytes=48 * 1024 * 1024,
        ),
        cost_estimate=pl.CostEstimate(
            flops=local.size, transcendentals=0,
            bytes_accessed=3 * nc * x.size * x.dtype.itemsize + 3 * local.size * 4,
        ),
    )(x, local.reshape(nc, part, width))
    return out.reshape(nc, rows, lanes), summed.reshape(height, width)


def all_sum(local, collective_base):
    row_count = lax.axis_size("row")
    col_count = lax.axis_size("col")
    height, width = local.shape
    by_col = scatter_sum(
        local.reshape(col_count, height // col_count, width), "col", "row", jnp.float32,
        collective_base,
    )
    part = height // col_count
    by_row = scatter_sum(
        by_col.reshape(row_count, part // row_count, width), "row", "col", jnp.float32,
        collective_base + 1,
    )
    back_row = gather_all(by_row, "row", "col", row_count, collective_base + 2)
    back_col = gather_all(back_row.reshape(part, width), "col", "row", col_count, collective_base + 3)
    return back_col.reshape(height, width)


def activation(aggregated, weight, cot_rows):
    hidden = jnp.dot(aggregated, weight, preferred_element_type=jnp.float32)
    sigmoid_value = jax.nn.sigmoid(hidden)
    output = (hidden * sigmoid_value).astype(jnp.bfloat16)
    silu_slope = sigmoid_value * (1.0 + hidden * (1.0 - sigmoid_value))
    hidden_grad = (cot_rows.astype(jnp.float32) * silu_slope).astype(jnp.bfloat16)
    return (output, hidden_grad)


def per_device(tile_values, tile_rows, tile_cols, tile_count, features, weight, cotangent):
    slot_total = tile_values.shape[2]
    tile_edge = tile_values.shape[3]
    tile_block = tile_values.reshape(slot_total, tile_edge, tile_edge)
    row_index = tile_rows.reshape(slot_total)
    col_index = tile_cols.reshape(slot_total)
    live_count = tile_count.reshape(1)
    own_rows = features.shape[0]
    feat_width = features.shape[1]
    row_count = lax.axis_size("row")
    col_count = lax.axis_size("col")
    row_tiles = col_count * own_rows // tile_edge
    col_tiles = row_count * own_rows // tile_edge
    column_block = gather_row(features, 8)
    source = column_block.reshape(col_tiles, tile_edge, feat_width)
    partial_rows = sparse_product(
        tile_block, row_index, col_index, live_count, source, row_tiles, False
    )
    partial_flat = partial_rows.reshape(row_tiles * tile_edge, feat_width)
    node_total = row_count * col_count * own_rows
    aggregated = scatter_sum_2d(
        partial_rows.reshape(col_count, own_rows, feat_width), TORUS_X, jnp.bfloat16, 0
    )
    output, hidden_grad = activation(aggregated, weight, cotangent)
    own_grad = lax.dot_general(
        hidden_grad, weight, (((1,), (1,)), ((), ())), preferred_element_type=jnp.float32
    ).astype(jnp.bfloat16)
    local_grad = lax.dot_general(
        aggregated, hidden_grad, (((0,), (0,)), ((), ())), preferred_element_type=jnp.float32
    )
    row_block, summed_grad = gather_and_sum(own_grad, local_grad, TORUS_X, 7)
    weight_grad = summed_grad * (1.0 / math.sqrt(node_total))
    source_back = row_block.reshape(row_tiles, tile_edge, feat_width)
    partial_cols = sparse_product(
        tile_block, col_index, row_index, live_count, source_back, col_tiles, True
    )
    input_grad = scatter_sum_row(
        partial_cols.reshape(row_count, own_rows, feat_width), jnp.float32, 9
    )
    return (output, weight_grad, input_grad)


def solution(mesh):
    placed = (
        P("row", "col", None, None, None),
        P("row", "col", None),
        P("row", "col", None),
        P("row", "col"),
        P(("row", "col"), None),
        P(),
        P(("row", "col"), None),
    )
    return jax.shard_map(
        per_device,
        mesh=mesh,
        in_specs=placed,
        out_specs=(P(("row", "col"), None), P(), P(("row", "col"), None)),
        check_vma=False,
    )
```

```python
import functools
import math

import jax
import jax.numpy as jnp
from jax import lax
from jax.experimental import pallas as pl
from jax.experimental.pallas import tpu as pltpu
from jax.sharding import PartitionSpec as P

SLOTS_PER_STEP = 64
UNROLL = 64
TORUS_X = 4


def spmm_kernel(transpose, acc_index, src_index, count_ref, tiles_ref, src_ref, out_ref, acc_ref):
    step = pl.program_id(0)
    per_step = tiles_ref.shape[0]
    live = count_ref[0]
    acc_last = acc_ref.shape[0] - 1
    src_last = src_ref.shape[0] - 1

    @pl.when(step == 0)
    def _():
        acc_ref[...] = jnp.zeros_like(acc_ref)

    def one_slot(k, carry):
        slot = step * per_step + k
        target = jnp.clip(acc_index[slot], 0, acc_last)
        picked = jnp.clip(src_index[slot], 0, src_last)
        tile = tiles_ref[k]
        tile = jnp.where(slot < live, tile, jnp.zeros_like(tile))
        block = src_ref[picked]
        if transpose:
            product = lax.dot_general(
                tile, block, (((0,), (0,)), ((), ())), preferred_element_type=jnp.float32
            )
        else:
            product = jnp.dot(tile, block, preferred_element_type=jnp.float32)
        acc_ref[target] += product
        return carry

    lax.fori_loop(0, per_step, one_slot, 0, unroll=UNROLL)

    @pl.when(step == pl.num_programs(0) - 1)
    def _():
        out_ref[...] = acc_ref[...].astype(out_ref.dtype)


def sparse_product(tile_block, acc_index, src_index, live_count, source, segments, transpose):
    slot_total, tile_edge, _ = tile_block.shape
    feat_width = source.shape[2]
    per_step = min(SLOTS_PER_STEP, slot_total)
    steps = slot_total // per_step

    def tile_map(step, acc_ref, src_ref, count_ref):
        last_live = jnp.maximum(count_ref[0] - 1, 0) // per_step
        return (jnp.minimum(step, last_live), 0, 0)

    grid_spec = pltpu.PrefetchScalarGridSpec(
        num_scalar_prefetch=3,
        grid=(steps,),
        in_specs=[
            pl.BlockSpec((per_step, tile_edge, tile_edge), tile_map),
            pl.BlockSpec(source.shape, lambda step, *_: (0, 0, 0)),
        ],
        out_specs=pl.BlockSpec((segments, tile_edge, feat_width), lambda step, *_: (0, 0, 0)),
        scratch_shapes=[pltpu.VMEM((segments, tile_edge, feat_width), jnp.float32)],
    )
    flops = 2 * slot_total * tile_edge * tile_edge * feat_width
    bytes_accessed = (
        tile_block.size * 2 + source.size * 2 + segments * tile_edge * feat_width * 2
    )
    return pl.pallas_call(
        functools.partial(spmm_kernel, transpose),
        out_shape=jax.ShapeDtypeStruct((segments, tile_edge, feat_width), jnp.bfloat16),
        grid_spec=grid_spec,
        compiler_params=pltpu.CompilerParams(
            dimension_semantics=("arbitrary",), vmem_limit_bytes=56 * 1024 * 1024
        ),
        cost_estimate=pl.CostEstimate(
            flops=flops, transcendentals=0, bytes_accessed=bytes_accessed
        ),
    )(acc_index, src_index, live_count, tile_block, source)


def peer_id(axis, other_axis, peer):
    if axis == "row":
        return (peer, lax.axis_index(other_axis))
    return (lax.axis_index(other_axis), peer)


def greet_all(axis, other_axis, n, me):
    barrier = pltpu.get_barrier_semaphore()
    for offset in range(1, n):
        peer = lax.rem(me + offset, n)
        pl.semaphore_signal(
            barrier, 1, device_id=peer_id(axis, other_axis, peer),
            device_id_type=pl.DeviceIdType.MESH,
        )
    pl.semaphore_wait(barrier, n - 1)


def scatter_sum_kernel(axis, other_axis, n, x_hbm, out_ref, recv, send_sems, recv_sems, own_sem):
    me = lax.axis_index(axis)
    greet_all(axis, other_axis, n, me)
    own = pltpu.make_async_copy(x_hbm.at[me], recv.at[me], own_sem)
    own.start()
    sends = []
    for offset in range(1, n):
        peer = lax.rem(me + offset, n)
        copy = pltpu.make_async_remote_copy(
            src_ref=x_hbm.at[peer],
            dst_ref=recv.at[me],
            send_sem=send_sems.at[offset],
            recv_sem=recv_sems.at[me],
            device_id=peer_id(axis, other_axis, peer),
            device_id_type=pl.DeviceIdType.MESH,
        )
        copy.start()
        sends.append(copy)
    own.wait()
    for offset in range(1, n):
        source = lax.rem(me + n - offset, n)
        pltpu.make_async_remote_copy(
            src_ref=x_hbm.at[source],
            dst_ref=recv.at[source],
            send_sem=send_sems.at[offset],
            recv_sem=recv_sems.at[source],
            device_id=peer_id(axis, other_axis, source),
            device_id_type=pl.DeviceIdType.MESH,
        ).wait_recv()
    total = recv[0].astype(jnp.float32)
    for j in range(1, n):
        total = total + recv[j].astype(jnp.float32)
    out_ref[...] = total.astype(out_ref.dtype)
    for copy in sends:
        copy.wait_send()


def scatter_sum(x, axis, other_axis, out_dtype, collective_id):
    n, rows, lanes = x.shape
    return pl.pallas_call(
        functools.partial(scatter_sum_kernel, axis, other_axis, n),
        out_shape=jax.ShapeDtypeStruct((rows, lanes), out_dtype),
        in_specs=[pl.BlockSpec(memory_space=pl.ANY)],
        out_specs=pl.BlockSpec(memory_space=pltpu.VMEM),
        scratch_shapes=[
            pltpu.VMEM((n, rows, lanes), x.dtype),
            pltpu.SemaphoreType.DMA((n,)),
            pltpu.SemaphoreType.DMA((n,)),
            pltpu.SemaphoreType.DMA(()),
        ],
        compiler_params=pltpu.CompilerParams(
            collective_id=collective_id, has_side_effects=True,
            vmem_limit_bytes=48 * 1024 * 1024,
        ),
        cost_estimate=pl.CostEstimate(
            flops=x.size, transcendentals=0, bytes_accessed=3 * x.size * x.dtype.itemsize
        ),
    )(x)


def gather_all_kernel(axis, other_axis, n, x_ref, out_ref, recv, send_sems, recv_sems):
    me = lax.axis_index(axis)
    recv[me] = x_ref[...]
    greet_all(axis, other_axis, n, me)
    sends = []
    for offset in range(1, n):
        peer = lax.rem(me + offset, n)
        copy = pltpu.make_async_remote_copy(
            src_ref=x_ref,
            dst_ref=recv.at[me],
            send_sem=send_sems.at[offset],
            recv_sem=recv_sems.at[me],
            device_id=peer_id(axis, other_axis, peer),
            device_id_type=pl.DeviceIdType.MESH,
        )
        copy.start()
        sends.append(copy)
    for offset in range(1, n):
        source = lax.rem(me + n - offset, n)
        pltpu.make_async_remote_copy(
            src_ref=x_ref,
            dst_ref=recv.at[source],
            send_sem=send_sems.at[offset],
            recv_sem=recv_sems.at[source],
            device_id=peer_id(axis, other_axis, source),
            device_id_type=pl.DeviceIdType.MESH,
        ).wait_recv()
    out_ref[...] = recv[...]
    for copy in sends:
        copy.wait_send()


def gather_all(x, axis, other_axis, n, collective_id):
    rows, lanes = x.shape
    return pl.pallas_call(
        functools.partial(gather_all_kernel, axis, other_axis, n),
        out_shape=jax.ShapeDtypeStruct((n, rows, lanes), x.dtype),
        in_specs=[pl.BlockSpec(memory_space=pltpu.VMEM)],
        out_specs=pl.BlockSpec(memory_space=pltpu.VMEM),
        scratch_shapes=[
            pltpu.VMEM((n, rows, lanes), x.dtype),
            pltpu.SemaphoreType.DMA((n,)),
            pltpu.SemaphoreType.DMA((n,)),
        ],
        compiler_params=pltpu.CompilerParams(
            collective_id=collective_id, has_side_effects=True,
            vmem_limit_bytes=48 * 1024 * 1024,
        ),
        cost_estimate=pl.CostEstimate(
            flops=0, transcendentals=0, bytes_accessed=3 * n * x.size * x.dtype.itemsize
        ),
    )(x)


def torus_peer(y, x, nx):
    return (lax.axis_index("row"), y * nx + x)


def scatter_sum_2d_kernel(nx, ny, x_hbm, out_ref, recv1, mid, recv2, sems):
    send1, got1, send2, got2, own_sems = sems
    me = lax.axis_index("col")
    my_y = me // nx
    my_x = lax.rem(me, nx)
    half = x_hbm.shape[2] // 2
    lower = pl.ds(0, half)
    upper = pl.ds(half, half)
    mesh_kind = pl.DeviceIdType.MESH

    barrier = pltpu.get_barrier_semaphore()
    for offset in range(1, nx):
        pl.semaphore_signal(barrier, 1, device_id=torus_peer(my_y, lax.rem(my_x + offset, nx), nx),
                            device_id_type=mesh_kind)
    for offset in range(1, ny):
        pl.semaphore_signal(barrier, 1, device_id=torus_peer(lax.rem(my_y + offset, ny), my_x, nx),
                            device_id_type=mesh_kind)
    pl.semaphore_wait(barrier, nx + ny - 2)

    own_a = pltpu.make_async_copy(x_hbm.at[:, my_x, lower], recv1.at[0, my_x], own_sems.at[0])
    own_b = pltpu.make_async_copy(x_hbm.at[my_y, :, upper], recv1.at[1, my_y], own_sems.at[1])
    own_a.start()
    own_b.start()
    sends = []
    for offset in range(1, nx):
        peer_x = lax.rem(my_x + offset, nx)
        copy = pltpu.make_async_remote_copy(
            src_ref=x_hbm.at[:, peer_x, lower], dst_ref=recv1.at[0, my_x],
            send_sem=send1.at[0, offset], recv_sem=got1.at[0, my_x],
            device_id=torus_peer(my_y, peer_x, nx), device_id_type=mesh_kind,
        )
        copy.start()
        sends.append(copy)
    for offset in range(1, ny):
        peer_y = lax.rem(my_y + offset, ny)
        copy = pltpu.make_async_remote_copy(
            src_ref=x_hbm.at[peer_y, :, upper], dst_ref=recv1.at[1, my_y],
            send_sem=send1.at[1, offset], recv_sem=got1.at[1, my_y],
            device_id=torus_peer(peer_y, my_x, nx), device_id_type=mesh_kind,
        )
        copy.start()
        sends.append(copy)
    own_a.wait()
    own_b.wait()
    for offset in range(1, nx):
        source_x = lax.rem(my_x + nx - offset, nx)
        pltpu.make_async_remote_copy(
            src_ref=x_hbm.at[:, source_x, lower], dst_ref=recv1.at[0, source_x],
            send_sem=send1.at[0, offset], recv_sem=got1.at[0, source_x],
            device_id=torus_peer(my_y, source_x, nx), device_id_type=mesh_kind,
        ).wait_recv()

    def add_up(stack):
        total = stack[0].astype(jnp.float32)
        for j in range(1, stack.shape[0]):
            total = total + stack[j].astype(jnp.float32)
        return total

    for target in range(ny):
        mid[0, target] = add_up(recv1[0, :, target]).astype(mid.dtype)
    recv2[0, my_y] = mid[0, my_y]

    for offset in range(1, ny):
        peer_y = lax.rem(my_y + offset, ny)
        copy = pltpu.make_async_remote_copy(
            src_ref=mid.at[0, peer_y], dst_ref=recv2.at[0, my_y],
            send_sem=send2.at[0, offset], recv_sem=got2.at[0, my_y],
            device_id=torus_peer(peer_y, my_x, nx), device_id_type=mesh_kind,
        )
        copy.start()
        sends.append(copy)
    for offset in range(1, ny):
        source_y = lax.rem(my_y + ny - offset, ny)
        pltpu.make_async_remote_copy(
            src_ref=x_hbm.at[source_y, :, upper], dst_ref=recv1.at[1, source_y],
            send_sem=send1.at[1, offset], recv_sem=got1.at[1, source_y],
            device_id=torus_peer(source_y, my_x, nx), device_id_type=mesh_kind,
        ).wait_recv()
    for target in range(nx):
        mid[1, target] = add_up(recv1[1, :, target]).astype(mid.dtype)
    recv2[1, my_x] = mid[1, my_x]
    for offset in range(1, nx):
        peer_x = lax.rem(my_x + offset, nx)
        copy = pltpu.make_async_remote_copy(
            src_ref=mid.at[1, peer_x], dst_ref=recv2.at[1, my_x],
            send_sem=send2.at[1, offset], recv_sem=got2.at[1, my_x],
            device_id=torus_peer(my_y, peer_x, nx), device_id_type=mesh_kind,
        )
        copy.start()
        sends.append(copy)
    for offset in range(1, ny):
        source_y = lax.rem(my_y + ny - offset, ny)
        pltpu.make_async_remote_copy(
            src_ref=mid.at[0, source_y], dst_ref=recv2.at[0, source_y],
            send_sem=send2.at[0, offset], recv_sem=got2.at[0, source_y],
            device_id=torus_peer(source_y, my_x, nx), device_id_type=mesh_kind,
        ).wait_recv()
    out_ref[lower] = add_up(recv2[0]).astype(out_ref.dtype)
    for offset in range(1, nx):
        source_x = lax.rem(my_x + nx - offset, nx)
        pltpu.make_async_remote_copy(
            src_ref=mid.at[1, source_x], dst_ref=recv2.at[1, source_x],
            send_sem=send2.at[1, offset], recv_sem=got2.at[1, source_x],
            device_id=torus_peer(my_y, source_x, nx), device_id_type=mesh_kind,
        ).wait_recv()
    out_ref[upper] = add_up(recv2[1]).astype(out_ref.dtype)
    for copy in sends:
        copy.wait_send()


def scatter_sum_2d(x, nx, out_dtype, collective_id):
    n, rows, lanes = x.shape
    ny = n // nx
    half = rows // 2
    side = max(nx, ny)
    return pl.pallas_call(
        functools.partial(scatter_sum_2d_kernel, nx, ny),
        out_shape=jax.ShapeDtypeStruct((rows, lanes), out_dtype),
        in_specs=[pl.BlockSpec(memory_space=pl.ANY)],
        out_specs=pl.BlockSpec(memory_space=pltpu.VMEM),
        scratch_shapes=[
            pltpu.VMEM((2, side, side, half, lanes), x.dtype),
            pltpu.VMEM((2, side, half, lanes), x.dtype),
            pltpu.VMEM((2, side, half, lanes), x.dtype),
            (
                pltpu.SemaphoreType.DMA((2, side)),
                pltpu.SemaphoreType.DMA((2, side)),
                pltpu.SemaphoreType.DMA((2, side)),
                pltpu.SemaphoreType.DMA((2, side)),
                pltpu.SemaphoreType.DMA((2,)),
            ),
        ],
        compiler_params=pltpu.CompilerParams(
            collective_id=collective_id, has_side_effects=True,
            vmem_limit_bytes=48 * 1024 * 1024,
        ),
        cost_estimate=pl.CostEstimate(
            flops=x.size, transcendentals=0, bytes_accessed=3 * x.size * x.dtype.itemsize
        ),
    )(x.reshape(ny, nx, rows, lanes))


def row_peer(index):
    return (index, lax.axis_index("col"))


def greet_row(my_z, my_core, nz):
    barrier = pltpu.get_barrier_semaphore()
    mesh_kind = pl.DeviceIdType.MESH
    pl.semaphore_signal(barrier, 1, device_id=row_peer(my_z * 2 + 1 - my_core), device_id_type=mesh_kind)
    for offset in range(1, nz):
        peer_z = lax.rem(my_z + offset, nz)
        pl.semaphore_signal(barrier, 1, device_id=row_peer(peer_z * 2 + my_core), device_id_type=mesh_kind)
    pl.semaphore_wait(barrier, nz)


def scatter_sum_row_kernel(nz, x_hbm, out_ref, own1, recv1, mid, recv2, sems):
    send1, got1, send2, got2, own_sem = sems
    mesh_kind = pl.DeviceIdType.MESH
    me = lax.axis_index("row")
    my_z = me // 2
    my_core = lax.rem(me, 2)
    other_core = 1 - my_core
    partner = row_peer(my_z * 2 + other_core)
    greet_row(my_z, my_core, nz)
    own = pltpu.make_async_copy(x_hbm.at[:, my_core], own1, own_sem.at[0])
    own.start()
    sends = []
    for offset in range(nz):
        target_z = lax.rem(my_z + offset + 1, nz)
        copy = pltpu.make_async_remote_copy(
            src_ref=x_hbm.at[target_z, other_core], dst_ref=recv1.at[target_z],
            send_sem=send1.at[offset], recv_sem=got1.at[target_z],
            device_id=partner, device_id_type=mesh_kind,
        )
        copy.start()
        sends.append(copy)
    own.wait()
    for offset in range(nz - 1):
        target_z = lax.rem(my_z + offset + 1, nz)
        pltpu.make_async_remote_copy(
            src_ref=x_hbm.at[target_z, other_core], dst_ref=recv1.at[target_z],
            send_sem=send1.at[offset], recv_sem=got1.at[target_z],
            device_id=partner, device_id_type=mesh_kind,
        ).wait_recv()
        mid[target_z] = (own1[target_z].astype(jnp.float32) + recv1[target_z].astype(jnp.float32)).astype(mid.dtype)
        copy = pltpu.make_async_remote_copy(
            src_ref=mid.at[target_z], dst_ref=recv2.at[my_z],
            send_sem=send2.at[offset + 1], recv_sem=got2.at[my_z],
            device_id=row_peer(target_z * 2 + my_core), device_id_type=mesh_kind,
        )
        copy.start()
        sends.append(copy)
    pltpu.make_async_remote_copy(
        src_ref=x_hbm.at[my_z, other_core], dst_ref=recv1.at[my_z],
        send_sem=send1.at[nz - 1], recv_sem=got1.at[my_z],
        device_id=partner, device_id_type=mesh_kind,
    ).wait_recv()
    total = own1[my_z].astype(jnp.float32) + recv1[my_z].astype(jnp.float32)
    for offset in range(1, nz):
        source_z = lax.rem(my_z + nz - offset, nz)
        pltpu.make_async_remote_copy(
            src_ref=mid.at[source_z], dst_ref=recv2.at[source_z],
            send_sem=send2.at[offset], recv_sem=got2.at[source_z],
            device_id=row_peer(source_z * 2 + my_core), device_id_type=mesh_kind,
        ).wait_recv()
        total = total + recv2[source_z].astype(jnp.float32)
    out_ref[...] = total.astype(out_ref.dtype)
    for copy in sends:
        copy.wait_send()


def scatter_sum_row(x, out_dtype, collective_id):
    n, rows, lanes = x.shape
    nz = n // 2
    return pl.pallas_call(
        functools.partial(scatter_sum_row_kernel, nz),
        out_shape=jax.ShapeDtypeStruct((rows, lanes), out_dtype),
        in_specs=[pl.BlockSpec(memory_space=pl.ANY)],
        out_specs=pl.BlockSpec(memory_space=pltpu.VMEM),
        scratch_shapes=[
            pltpu.VMEM((nz, rows, lanes), x.dtype),
            pltpu.VMEM((nz, rows, lanes), x.dtype),
            pltpu.VMEM((nz, rows, lanes), x.dtype),
            pltpu.VMEM((nz, rows, lanes), x.dtype),
            (
                pltpu.SemaphoreType.DMA((nz,)),
                pltpu.SemaphoreType.DMA((nz,)),
                pltpu.SemaphoreType.DMA((nz,)),
                pltpu.SemaphoreType.DMA((nz,)),
                pltpu.SemaphoreType.DMA((1,)),
            ),
        ],
        compiler_params=pltpu.CompilerParams(
            collective_id=collective_id, has_side_effects=True,
            vmem_limit_bytes=48 * 1024 * 1024,
        ),
        cost_estimate=pl.CostEstimate(
            flops=x.size, transcendentals=0, bytes_accessed=3 * x.size * x.dtype.itemsize
        ),
    )(x.reshape(nz, 2, rows, lanes))


def gather_row_kernel(nz, x_ref, out_ref, full, sems):
    send1, got1, send2, got2, own_sem = sems
    mesh_kind = pl.DeviceIdType.MESH
    me = lax.axis_index("row")
    my_z = me // 2
    my_core = lax.rem(me, 2)
    other_core = 1 - my_core
    partner = row_peer(my_z * 2 + other_core)
    greet_row(my_z, my_core, nz)
    own = pltpu.make_async_copy(x_ref, full.at[my_z, my_core], own_sem.at[0])
    own.start()
    sends = []
    for offset in range(1, nz):
        peer_z = lax.rem(my_z + offset, nz)
        copy = pltpu.make_async_remote_copy(
            src_ref=x_ref, dst_ref=full.at[my_z, my_core],
            send_sem=send1.at[offset], recv_sem=got1.at[my_z],
            device_id=row_peer(peer_z * 2 + my_core), device_id_type=mesh_kind,
        )
        copy.start()
        sends.append(copy)

    def forward(block_z, slot):
        copy = pltpu.make_async_remote_copy(
            src_ref=full.at[block_z, my_core], dst_ref=full.at[block_z, my_core],
            send_sem=send2.at[slot], recv_sem=got2.at[block_z],
            device_id=partner, device_id_type=mesh_kind,
        )
        copy.start()
        sends.append(copy)

    own.wait()
    forward(my_z, 0)
    for offset in range(1, nz):
        source_z = lax.rem(my_z + nz - offset, nz)
        pltpu.make_async_remote_copy(
            src_ref=x_ref, dst_ref=full.at[source_z, my_core],
            send_sem=send1.at[offset], recv_sem=got1.at[source_z],
            device_id=row_peer(source_z * 2 + my_core), device_id_type=mesh_kind,
        ).wait_recv()
        forward(source_z, offset)
    for offset in range(nz):
        block_z = lax.rem(my_z + nz - offset, nz)
        pltpu.make_async_remote_copy(
            src_ref=full.at[block_z, other_core], dst_ref=full.at[block_z, other_core],
            send_sem=send2.at[offset], recv_sem=got2.at[block_z],
            device_id=partner, device_id_type=mesh_kind,
        ).wait_recv()
    for copy in sends:
        copy.wait_send()
    out_ref[...] = full[...]


def gather_row(x, collective_id):
    rows, lanes = x.shape
    nz = lax.axis_size("row") // 2
    out = pl.pallas_call(
        functools.partial(gather_row_kernel, nz),
        out_shape=jax.ShapeDtypeStruct((nz, 2, rows, lanes), x.dtype),
        in_specs=[pl.BlockSpec(memory_space=pltpu.VMEM)],
        out_specs=pl.BlockSpec(memory_space=pltpu.VMEM),
        scratch_shapes=[
            pltpu.VMEM((nz, 2, rows, lanes), x.dtype),
            (
                pltpu.SemaphoreType.DMA((nz,)),
                pltpu.SemaphoreType.DMA((nz,)),
                pltpu.SemaphoreType.DMA((nz,)),
                pltpu.SemaphoreType.DMA((nz,)),
                pltpu.SemaphoreType.DMA((1,)),
            ),
        ],
        compiler_params=pltpu.CompilerParams(
            collective_id=collective_id, has_side_effects=True,
            vmem_limit_bytes=48 * 1024 * 1024,
        ),
        cost_estimate=pl.CostEstimate(
            flops=0, transcendentals=0, bytes_accessed=3 * 2 * nz * x.size * x.dtype.itemsize
        ),
    )(x)
    return out.reshape(2 * nz * rows, lanes)


def gather_all_2d_kernel(nx, ny, x_ref, out_ref, full, sems):
    send, got, own_sem = sems
    mesh_kind = pl.DeviceIdType.MESH
    me = lax.axis_index("col")
    my_y = me // nx
    my_x = lax.rem(me, nx)
    half = x_ref.shape[0] // 2
    lower = pl.ds(0, half)
    upper = pl.ds(half, half)

    barrier = pltpu.get_barrier_semaphore()
    for offset in range(1, nx):
        pl.semaphore_signal(barrier, 1, device_id=torus_peer(my_y, lax.rem(my_x + offset, nx), nx),
                            device_id_type=mesh_kind)
    for offset in range(1, ny):
        pl.semaphore_signal(barrier, 1, device_id=torus_peer(lax.rem(my_y + offset, ny), my_x, nx),
                            device_id_type=mesh_kind)
    pl.semaphore_wait(barrier, nx + ny - 2)

    own = pltpu.make_async_copy(x_ref, full.at[my_y, my_x], own_sem.at[0])
    own.start()
    sends = []
    for offset in range(1, nx):
        peer_x = lax.rem(my_x + offset, nx)
        copy = pltpu.make_async_remote_copy(
            src_ref=x_ref.at[lower], dst_ref=full.at[my_y, my_x, lower],
            send_sem=send.at[0, offset], recv_sem=got.at[0, my_x],
            device_id=torus_peer(my_y, peer_x, nx), device_id_type=mesh_kind,
        )
        copy.start()
        sends.append(copy)
    for offset in range(1, ny):
        peer_y = lax.rem(my_y + offset, ny)
        copy = pltpu.make_async_remote_copy(
            src_ref=x_ref.at[upper], dst_ref=full.at[my_y, my_x, upper],
            send_sem=send.at[1, offset], recv_sem=got.at[1, my_y],
            device_id=torus_peer(peer_y, my_x, nx), device_id_type=mesh_kind,
        )
        copy.start()
        sends.append(copy)
    own.wait()
    for offset in range(1, nx):
        source_x = lax.rem(my_x + nx - offset, nx)
        pltpu.make_async_remote_copy(
            src_ref=x_ref.at[lower], dst_ref=full.at[my_y, source_x, lower],
            send_sem=send.at[0, offset], recv_sem=got.at[0, source_x],
            device_id=torus_peer(my_y, source_x, nx), device_id_type=mesh_kind,
        ).wait_recv()
    for offset in range(1, ny):
        peer_y = lax.rem(my_y + offset, ny)
        copy = pltpu.make_async_remote_copy(
            src_ref=full.at[my_y, :, lower], dst_ref=full.at[my_y, :, lower],
            send_sem=send.at[2, offset], recv_sem=got.at[2, my_y],
            device_id=torus_peer(peer_y, my_x, nx), device_id_type=mesh_kind,
        )
        copy.start()
        sends.append(copy)
    for offset in range(1, ny):
        source_y = lax.rem(my_y + ny - offset, ny)
        pltpu.make_async_remote_copy(
            src_ref=x_ref.at[upper], dst_ref=full.at[source_y, my_x, upper],
            send_sem=send.at[1, offset], recv_sem=got.at[1, source_y],
            device_id=torus_peer(source_y, my_x, nx), device_id_type=mesh_kind,
        ).wait_recv()
    for offset in range(1, nx):
        peer_x = lax.rem(my_x + offset, nx)
        copy = pltpu.make_async_remote_copy(
            src_ref=full.at[:, my_x, upper], dst_ref=full.at[:, my_x, upper],
            send_sem=send.at[3, offset], recv_sem=got.at[3, my_x],
            device_id=torus_peer(my_y, peer_x, nx), device_id_type=mesh_kind,
        )
        copy.start()
        sends.append(copy)
    for offset in range(1, ny):
        source_y = lax.rem(my_y + ny - offset, ny)
        pltpu.make_async_remote_copy(
            src_ref=full.at[source_y, :, lower], dst_ref=full.at[source_y, :, lower],
            send_sem=send.at[2, offset], recv_sem=got.at[2, source_y],
            device_id=torus_peer(source_y, my_x, nx), device_id_type=mesh_kind,
        ).wait_recv()
    for offset in range(1, nx):
        source_x = lax.rem(my_x + nx - offset, nx)
        pltpu.make_async_remote_copy(
            src_ref=full.at[:, source_x, upper], dst_ref=full.at[:, source_x, upper],
            send_sem=send.at[3, offset], recv_sem=got.at[3, source_x],
            device_id=torus_peer(my_y, source_x, nx), device_id_type=mesh_kind,
        ).wait_recv()
    for copy in sends:
        copy.wait_send()
    out_ref[...] = full[...]


def gather_all_2d(x, nx, collective_id):
    rows, lanes = x.shape
    n = lax.axis_size("col")
    ny = n // nx
    side = max(nx, ny)
    out = pl.pallas_call(
        functools.partial(gather_all_2d_kernel, nx, ny),
        out_shape=jax.ShapeDtypeStruct((ny, nx, rows, lanes), x.dtype),
        in_specs=[pl.BlockSpec(memory_space=pltpu.VMEM)],
        out_specs=pl.BlockSpec(memory_space=pltpu.VMEM),
        scratch_shapes=[
            pltpu.VMEM((ny, nx, rows, lanes), x.dtype),
            (
                pltpu.SemaphoreType.DMA((4, side)),
                pltpu.SemaphoreType.DMA((4, side)),
                pltpu.SemaphoreType.DMA((1,)),
            ),
        ],
        compiler_params=pltpu.CompilerParams(
            collective_id=collective_id, has_side_effects=True,
            vmem_limit_bytes=48 * 1024 * 1024,
        ),
        cost_estimate=pl.CostEstimate(
            flops=0, transcendentals=0, bytes_accessed=3 * n * x.size * x.dtype.itemsize
        ),
    )(x)
    return out.reshape(n, rows, lanes)


def fused_sum_kernel(nr, nc, x_ref, out_ref, recv1, recv2, recv3, sems):
    send1, got1, send2, got2, send3, got3 = sems
    mesh_kind = pl.DeviceIdType.MESH
    my_r = lax.axis_index("row")
    my_c = lax.axis_index("col")
    barrier = pltpu.get_barrier_semaphore()
    for offset in range(1, nc):
        pl.semaphore_signal(barrier, 1, device_id=(my_r, lax.rem(my_c + offset, nc)),
                            device_id_type=mesh_kind)
    for offset in range(1, nr):
        pl.semaphore_signal(barrier, 1, device_id=(lax.rem(my_r + offset, nr), my_c),
                            device_id_type=mesh_kind)
    pl.semaphore_wait(barrier, nc + nr - 2)

    def exchange(peers, axis_count, src_of, dst, send, got, me_index):
        started = []
        for offset in range(1, axis_count):
            peer = lax.rem(me_index + offset, axis_count)
            copy = pltpu.make_async_remote_copy(
                src_ref=src_of(peer), dst_ref=dst.at[me_index],
                send_sem=send.at[offset], recv_sem=got.at[me_index],
                device_id=peers(peer), device_id_type=mesh_kind,
            )
            copy.start()
            started.append(copy)
        for offset in range(1, axis_count):
            source = lax.rem(me_index + axis_count - offset, axis_count)
            pltpu.make_async_remote_copy(
                src_ref=src_of(source), dst_ref=dst.at[source],
                send_sem=send.at[offset], recv_sem=got.at[source],
                device_id=peers(source), device_id_type=mesh_kind,
            ).wait_recv()
        return started

    along_col = lambda peer: (my_r, peer)
    along_row = lambda peer: (peer, my_c)
    recv1[my_c] = x_ref[my_c]
    sends = exchange(along_col, nc, lambda peer: x_ref.at[peer], recv1, send1, got1, my_c)
    part = recv1[0]
    for j in range(1, nc):
        part = part + recv1[j]
    recv2[my_r] = part
    sends += exchange(along_row, nr, lambda peer: recv2.at[my_r], recv2, send2, got2, my_r)
    total = recv2[0]
    for j in range(1, nr):
        total = total + recv2[j]
    recv3[my_c] = total
    sends += exchange(along_col, nc, lambda peer: recv3.at[my_c], recv3, send3, got3, my_c)
    out_ref[...] = recv3[...]
    for copy in sends:
        copy.wait_send()


def fused_sum(local, collective_id):
    nr = lax.axis_size("row")
    nc = lax.axis_size("col")
    height, width = local.shape
    part = height // nc
    out = pl.pallas_call(
        functools.partial(fused_sum_kernel, nr, nc),
        out_shape=jax.ShapeDtypeStruct((nc, part, width), local.dtype),
        in_specs=[pl.BlockSpec(memory_space=pltpu.VMEM)],
        out_specs=pl.BlockSpec(memory_space=pltpu.VMEM),
        scratch_shapes=[
            pltpu.VMEM((nc, part, width), local.dtype),
            pltpu.VMEM((nr, part, width), local.dtype),
            pltpu.VMEM((nc, part, width), local.dtype),
            (
                pltpu.SemaphoreType.DMA((nc,)),
                pltpu.SemaphoreType.DMA((nc,)),
                pltpu.SemaphoreType.DMA((nr,)),
                pltpu.SemaphoreType.DMA((nr,)),
                pltpu.SemaphoreType.DMA((nc,)),
                pltpu.SemaphoreType.DMA((nc,)),
            ),
        ],
        compiler_params=pltpu.CompilerParams(
            collective_id=collective_id, has_side_effects=True,
            vmem_limit_bytes=48 * 1024 * 1024,
        ),
        cost_estimate=pl.CostEstimate(
            flops=local.size, transcendentals=0, bytes_accessed=3 * local.size * 4
        ),
    )(local.reshape(nc, part, width))
    return out.reshape(height, width)


def gather_and_sum_kernel(nx, ny, nr, x_ref, w_ref, out_ref, wout_ref, full, recv1, recv2, recv3, sems):
    send, got, own_sem, wsend1, wgot1, wsend2, wgot2, wsend3, wgot3 = sems
    mesh_kind = pl.DeviceIdType.MESH
    nc = nx * ny
    me = lax.axis_index("col")
    my_r = lax.axis_index("row")
    my_y = me // nx
    my_x = lax.rem(me, nx)
    half = x_ref.shape[0] // 2
    lower = pl.ds(0, half)
    upper = pl.ds(half, half)
    along_col = lambda peer: (my_r, peer)
    along_row = lambda peer: (peer, me)

    barrier = pltpu.get_barrier_semaphore()
    for offset in range(1, nc):
        pl.semaphore_signal(barrier, 1, device_id=along_col(lax.rem(me + offset, nc)),
                            device_id_type=mesh_kind)
    for offset in range(1, nr):
        pl.semaphore_signal(barrier, 1, device_id=along_row(lax.rem(my_r + offset, nr)),
                            device_id_type=mesh_kind)
    pl.semaphore_wait(barrier, nc + nr - 2)

    def start_all(peers, count, me_index, src_of, dst, sem_send, sem_got):
        started = []
        for offset in range(1, count):
            peer = lax.rem(me_index + offset, count)
            copy = pltpu.make_async_remote_copy(
                src_ref=src_of(peer), dst_ref=dst.at[me_index],
                send_sem=sem_send.at[offset], recv_sem=sem_got.at[me_index],
                device_id=peers(peer), device_id_type=mesh_kind,
            )
            copy.start()
            started.append(copy)
        return started

    def wait_all(peers, count, me_index, src_of, dst, sem_send, sem_got):
        for offset in range(1, count):
            source = lax.rem(me_index + count - offset, count)
            pltpu.make_async_remote_copy(
                src_ref=src_of(source), dst_ref=dst.at[source],
                send_sem=sem_send.at[offset], recv_sem=sem_got.at[source],
                device_id=peers(source), device_id_type=mesh_kind,
            ).wait_recv()

    own = pltpu.make_async_copy(x_ref, full.at[my_y, my_x], own_sem.at[0])
    own.start()
    sends = []
    for offset in range(1, nx):
        peer_x = lax.rem(my_x + offset, nx)
        copy = pltpu.make_async_remote_copy(
            src_ref=x_ref.at[lower], dst_ref=full.at[my_y, my_x, lower],
            send_sem=send.at[0, offset], recv_sem=got.at[0, my_x],
            device_id=torus_peer(my_y, peer_x, nx), device_id_type=mesh_kind,
        )
        copy.start()
        sends.append(copy)
    for offset in range(1, ny):
        peer_y = lax.rem(my_y + offset, ny)
        copy = pltpu.make_async_remote_copy(
            src_ref=x_ref.at[upper], dst_ref=full.at[my_y, my_x, upper],
            send_sem=send.at[1, offset], recv_sem=got.at[1, my_y],
            device_id=torus_peer(peer_y, my_x, nx), device_id_type=mesh_kind,
        )
        copy.start()
        sends.append(copy)
    recv1[me] = w_ref[me]
    weight_src = lambda peer: w_ref.at[peer]
    sends += start_all(along_col, nc, me, weight_src, recv1, wsend1, wgot1)
    own.wait()
    for offset in range(1, nx):
        source_x = lax.rem(my_x + nx - offset, nx)
        pltpu.make_async_remote_copy(
            src_ref=x_ref.at[lower], dst_ref=full.at[my_y, source_x, lower],
            send_sem=send.at[0, offset], recv_sem=got.at[0, source_x],
            device_id=torus_peer(my_y, source_x, nx), device_id_type=mesh_kind,
        ).wait_recv()
    for offset in range(1, ny):
        peer_y = lax.rem(my_y + offset, ny)
        copy = pltpu.make_async_remote_copy(
            src_ref=full.at[my_y, :, lower], dst_ref=full.at[my_y, :, lower],
            send_sem=send.at[2, offset], recv_sem=got.at[2, my_y],
            device_id=torus_peer(peer_y, my_x, nx), device_id_type=mesh_kind,
        )
        copy.start()
        sends.append(copy)
    for offset in range(1, ny):
        source_y = lax.rem(my_y + ny - offset, ny)
        pltpu.make_async_remote_copy(
            src_ref=x_ref.at[upper], dst_ref=full.at[source_y, my_x, upper],
            send_sem=send.at[1, offset], recv_sem=got.at[1, source_y],
            device_id=torus_peer(source_y, my_x, nx), device_id_type=mesh_kind,
        ).wait_recv()
    for offset in range(1, nx):
        peer_x = lax.rem(my_x + offset, nx)
        copy = pltpu.make_async_remote_copy(
            src_ref=full.at[:, my_x, upper], dst_ref=full.at[:, my_x, upper],
            send_sem=send.at[3, offset], recv_sem=got.at[3, my_x],
            device_id=torus_peer(my_y, peer_x, nx), device_id_type=mesh_kind,
        )
        copy.start()
        sends.append(copy)

    wait_all(along_col, nc, me, weight_src, recv1, wsend1, wgot1)
    part = recv1[0]
    for j in range(1, nc):
        part = part + recv1[j]
    recv2[my_r] = part
    row_src = lambda peer: recv2.at[my_r]
    sends += start_all(along_row, nr, my_r, row_src, recv2, wsend2, wgot2)
    wait_all(along_row, nr, my_r, row_src, recv2, wsend2, wgot2)
    total = recv2[0]
    for j in range(1, nr):
        total = total + recv2[j]
    recv3[me] = total
    back_src = lambda peer: recv3.at[me]
    sends += start_all(along_col, nc, me, back_src, recv3, wsend3, wgot3)

    for offset in range(1, ny):
        source_y = lax.rem(my_y + ny - offset, ny)
        pltpu.make_async_remote_copy(
            src_ref=full.at[source_y, :, lower], dst_ref=full.at[source_y, :, lower],
            send_sem=send.at[2, offset], recv_sem=got.at[2, source_y],
            device_id=torus_peer(source_y, my_x, nx), device_id_type=mesh_kind,
        ).wait_recv()
    for offset in range(1, nx):
        source_x = lax.rem(my_x + nx - offset, nx)
        pltpu.make_async_remote_copy(
            src_ref=full.at[:, source_x, upper], dst_ref=full.at[:, source_x, upper],
            send_sem=send.at[3, offset], recv_sem=got.at[3, source_x],
            device_id=torus_peer(my_y, source_x, nx), device_id_type=mesh_kind,
        ).wait_recv()
    out_ref[...] = full[...]
    wait_all(along_col, nc, me, back_src, recv3, wsend3, wgot3)
    wout_ref[...] = recv3[...]
    for copy in sends:
        copy.wait_send()


def gather_and_sum(x, local, nx, collective_id):
    rows, lanes = x.shape
    nc = lax.axis_size("col")
    nr = lax.axis_size("row")
    ny = nc // nx
    side = max(nx, ny)
    height, width = local.shape
    part = height // nc
    out, summed = pl.pallas_call(
        functools.partial(gather_and_sum_kernel, nx, ny, nr),
        out_shape=(
            jax.ShapeDtypeStruct((ny, nx, rows, lanes), x.dtype),
            jax.ShapeDtypeStruct((nc, part, width), local.dtype),
        ),
        in_specs=[pl.BlockSpec(memory_space=pltpu.VMEM)] * 2,
        out_specs=(pl.BlockSpec(memory_space=pltpu.VMEM),) * 2,
        scratch_shapes=[
            pltpu.VMEM((ny, nx, rows, lanes), x.dtype),
            pltpu.VMEM((nc, part, width), local.dtype),
            pltpu.VMEM((nr, part, width), local.dtype),
            pltpu.VMEM((nc, part, width), local.dtype),
            (
                pltpu.SemaphoreType.DMA((4, side)),
                pltpu.SemaphoreType.DMA((4, side)),
                pltpu.SemaphoreType.DMA((1,)),
                pltpu.SemaphoreType.DMA((nc,)),
                pltpu.SemaphoreType.DMA((nc,)),
                pltpu.SemaphoreType.DMA((nr,)),
                pltpu.SemaphoreType.DMA((nr,)),
                pltpu.SemaphoreType.DMA((nc,)),
                pltpu.SemaphoreType.DMA((nc,)),
            ),
        ],
        compiler_params=pltpu.CompilerParams(
            collective_id=collective_id, has_side_effects=True,
            vmem_limit_bytes=48 * 1024 * 1024,
        ),
        cost_estimate=pl.CostEstimate(
            flops=local.size, transcendentals=0,
            bytes_accessed=3 * nc * x.size * x.dtype.itemsize + 3 * local.size * 4,
        ),
    )(x, local.reshape(nc, part, width))
    return out.reshape(nc, rows, lanes), summed.reshape(height, width)


def all_sum(local, collective_base):
    row_count = lax.axis_size("row")
    col_count = lax.axis_size("col")
    height, width = local.shape
    by_col = scatter_sum(
        local.reshape(col_count, height // col_count, width), "col", "row", jnp.float32,
        collective_base,
    )
    part = height // col_count
    by_row = scatter_sum(
        by_col.reshape(row_count, part // row_count, width), "row", "col", jnp.float32,
        collective_base + 1,
    )
    back_row = gather_all(by_row, "row", "col", row_count, collective_base + 2)
    back_col = gather_all(back_row.reshape(part, width), "col", "row", col_count, collective_base + 3)
    return back_col.reshape(height, width)


def activation(aggregated, weight, cot_rows):
    hidden = jnp.dot(aggregated, weight, preferred_element_type=jnp.float32)
    sigmoid_value = jax.nn.sigmoid(hidden)
    output = (hidden * sigmoid_value).astype(jnp.bfloat16)
    silu_slope = sigmoid_value * (1.0 + hidden * (1.0 - sigmoid_value))
    hidden_grad = (cot_rows.astype(jnp.float32) * silu_slope).astype(jnp.bfloat16)
    return (output, hidden_grad)


def per_device(tile_values, tile_rows, tile_cols, tile_count, features, weight, cotangent):
    slot_total = tile_values.shape[2]
    tile_edge = tile_values.shape[3]
    tile_block = tile_values.reshape(slot_total, tile_edge, tile_edge)
    row_index = tile_rows.reshape(slot_total)
    col_index = tile_cols.reshape(slot_total)
    live_count = tile_count.reshape(1)
    own_rows = features.shape[0]
    feat_width = features.shape[1]
    row_count = lax.axis_size("row")
    col_count = lax.axis_size("col")
    row_tiles = col_count * own_rows // tile_edge
    col_tiles = row_count * own_rows // tile_edge
    column_block = gather_row(features, 8)
    source = column_block.reshape(col_tiles, tile_edge, feat_width)
    partial_rows = sparse_product(
        tile_block, row_index, col_index, live_count, source, row_tiles, False
    )
    partial_flat = partial_rows.reshape(row_tiles * tile_edge, feat_width)
    node_total = row_count * col_count * own_rows
    aggregated = scatter_sum_2d(
        partial_rows.reshape(col_count, own_rows, feat_width), TORUS_X, jnp.bfloat16, 0
    )
    output, hidden_grad = activation(aggregated, weight, cotangent)
    own_grad = lax.dot_general(
        hidden_grad, weight, (((1,), (1,)), ((), ())), preferred_element_type=jnp.float32
    ).astype(jnp.bfloat16)
    local_grad = lax.dot_general(
        aggregated, hidden_grad, (((0,), (0,)), ((), ())), preferred_element_type=jnp.float32
    )
    row_block, summed_grad = gather_and_sum(own_grad, local_grad, TORUS_X, 7)
    weight_grad = summed_grad * (1.0 / math.sqrt(node_total))
    source_back = row_block.reshape(row_tiles, tile_edge, feat_width)
    partial_cols = sparse_product(
        tile_block, col_index, row_index, live_count, source_back, col_tiles, True
    )
    input_grad = scatter_sum_row(
        partial_cols.reshape(row_count, own_rows, feat_width), jnp.float32, 9
    )
    return (output, weight_grad, input_grad)


def solution(mesh):
    placed = (
        P("row", "col", None, None, None),
        P("row", "col", None),
        P("row", "col", None),
        P("row", "col"),
        P(("row", "col"), None),
        P(),
        P(("row", "col"), None),
    )
    return jax.shard_map(
        per_device,
        mesh=mesh,
        in_specs=placed,
        out_specs=(P(("row", "col"), None), P(), P(("row", "col"), None)),
        check_vma=False,
    )
```

```python
import functools
import math

import jax
import jax.numpy as jnp
from jax import lax
from jax.experimental import pallas as pl
from jax.experimental.pallas import tpu as pltpu
from jax.sharding import PartitionSpec as P

SLOTS_PER_STEP = 128
UNROLL = 128
TORUS_X = 4


def spmm_kernel(transpose, acc_index, src_index, count_ref, tiles_ref, src_ref, out_ref, acc_ref):
    step = pl.program_id(0)
    per_step = tiles_ref.shape[0]
    live = count_ref[0]
    acc_last = acc_ref.shape[0] - 1
    src_last = src_ref.shape[0] - 1

    @pl.when(step == 0)
    def _():
        acc_ref[...] = jnp.zeros_like(acc_ref)

    def one_slot(k, carry):
        slot = step * per_step + k
        target = jnp.clip(acc_index[slot], 0, acc_last)
        picked = jnp.clip(src_index[slot], 0, src_last)
        tile = tiles_ref[k]
        tile = jnp.where(slot < live, tile, jnp.zeros_like(tile))
        block = src_ref[picked]
        if transpose:
            product = lax.dot_general(
                tile, block, (((0,), (0,)), ((), ())), preferred_element_type=jnp.float32
            )
        else:
            product = jnp.dot(tile, block, preferred_element_type=jnp.float32)
        acc_ref[target] += product
        return carry

    lax.fori_loop(0, per_step, one_slot, 0, unroll=UNROLL)

    @pl.when(step == pl.num_programs(0) - 1)
    def _():
        out_ref[...] = acc_ref[...].astype(out_ref.dtype)


def sparse_product(tile_block, acc_index, src_index, live_count, source, segments, transpose):
    slot_total, tile_edge, _ = tile_block.shape
    feat_width = source.shape[2]
    per_step = min(SLOTS_PER_STEP, slot_total)
    steps = slot_total // per_step

    def tile_map(step, acc_ref, src_ref, count_ref):
        last_live = jnp.maximum(count_ref[0] - 1, 0) // per_step
        return (jnp.minimum(step, last_live), 0, 0)

    grid_spec = pltpu.PrefetchScalarGridSpec(
        num_scalar_prefetch=3,
        grid=(steps,),
        in_specs=[
            pl.BlockSpec((per_step, tile_edge, tile_edge), tile_map),
            pl.BlockSpec(source.shape, lambda step, *_: (0, 0, 0)),
        ],
        out_specs=pl.BlockSpec((segments, tile_edge, feat_width), lambda step, *_: (0, 0, 0)),
        scratch_shapes=[pltpu.VMEM((segments, tile_edge, feat_width), jnp.float32)],
    )
    flops = 2 * slot_total * tile_edge * tile_edge * feat_width
    bytes_accessed = (
        tile_block.size * 2 + source.size * 2 + segments * tile_edge * feat_width * 2
    )
    return pl.pallas_call(
        functools.partial(spmm_kernel, transpose),
        out_shape=jax.ShapeDtypeStruct((segments, tile_edge, feat_width), jnp.bfloat16),
        grid_spec=grid_spec,
        compiler_params=pltpu.CompilerParams(
            dimension_semantics=("arbitrary",), vmem_limit_bytes=56 * 1024 * 1024
        ),
        cost_estimate=pl.CostEstimate(
            flops=flops, transcendentals=0, bytes_accessed=bytes_accessed
        ),
    )(acc_index, src_index, live_count, tile_block, source)


def peer_id(axis, other_axis, peer):
    if axis == "row":
        return (peer, lax.axis_index(other_axis))
    return (lax.axis_index(other_axis), peer)


def greet_all(axis, other_axis, n, me):
    barrier = pltpu.get_barrier_semaphore()
    for offset in range(1, n):
        peer = lax.rem(me + offset, n)
        pl.semaphore_signal(
            barrier, 1, device_id=peer_id(axis, other_axis, peer),
            device_id_type=pl.DeviceIdType.MESH,
        )
    pl.semaphore_wait(barrier, n - 1)


def scatter_sum_kernel(axis, other_axis, n, x_hbm, out_ref, recv, send_sems, recv_sems, own_sem):
    me = lax.axis_index(axis)
    greet_all(axis, other_axis, n, me)
    own = pltpu.make_async_copy(x_hbm.at[me], recv.at[me], own_sem)
    own.start()
    sends = []
    for offset in range(1, n):
        peer = lax.rem(me + offset, n)
        copy = pltpu.make_async_remote_copy(
            src_ref=x_hbm.at[peer],
            dst_ref=recv.at[me],
            send_sem=send_sems.at[offset],
            recv_sem=recv_sems.at[me],
            device_id=peer_id(axis, other_axis, peer),
            device_id_type=pl.DeviceIdType.MESH,
        )
        copy.start()
        sends.append(copy)
    own.wait()
    for offset in range(1, n):
        source = lax.rem(me + n - offset, n)
        pltpu.make_async_remote_copy(
            src_ref=x_hbm.at[source],
            dst_ref=recv.at[source],
            send_sem=send_sems.at[offset],
            recv_sem=recv_sems.at[source],
            device_id=peer_id(axis, other_axis, source),
            device_id_type=pl.DeviceIdType.MESH,
        ).wait_recv()
    total = recv[0].astype(jnp.float32)
    for j in range(1, n):
        total = total + recv[j].astype(jnp.float32)
    out_ref[...] = total.astype(out_ref.dtype)
    for copy in sends:
        copy.wait_send()


def scatter_sum(x, axis, other_axis, out_dtype, collective_id):
    n, rows, lanes = x.shape
    return pl.pallas_call(
        functools.partial(scatter_sum_kernel, axis, other_axis, n),
        out_shape=jax.ShapeDtypeStruct((rows, lanes), out_dtype),
        in_specs=[pl.BlockSpec(memory_space=pl.ANY)],
        out_specs=pl.BlockSpec(memory_space=pltpu.VMEM),
        scratch_shapes=[
            pltpu.VMEM((n, rows, lanes), x.dtype),
            pltpu.SemaphoreType.DMA((n,)),
            pltpu.SemaphoreType.DMA((n,)),
            pltpu.SemaphoreType.DMA(()),
        ],
        compiler_params=pltpu.CompilerParams(
            collective_id=collective_id, has_side_effects=True,
            vmem_limit_bytes=48 * 1024 * 1024,
        ),
        cost_estimate=pl.CostEstimate(
            flops=x.size, transcendentals=0, bytes_accessed=3 * x.size * x.dtype.itemsize
        ),
    )(x)


def gather_all_kernel(axis, other_axis, n, x_ref, out_ref, recv, send_sems, recv_sems):
    me = lax.axis_index(axis)
    recv[me] = x_ref[...]
    greet_all(axis, other_axis, n, me)
    sends = []
    for offset in range(1, n):
        peer = lax.rem(me + offset, n)
        copy = pltpu.make_async_remote_copy(
            src_ref=x_ref,
            dst_ref=recv.at[me],
            send_sem=send_sems.at[offset],
            recv_sem=recv_sems.at[me],
            device_id=peer_id(axis, other_axis, peer),
            device_id_type=pl.DeviceIdType.MESH,
        )
        copy.start()
        sends.append(copy)
    for offset in range(1, n):
        source = lax.rem(me + n - offset, n)
        pltpu.make_async_remote_copy(
            src_ref=x_ref,
            dst_ref=recv.at[source],
            send_sem=send_sems.at[offset],
            recv_sem=recv_sems.at[source],
            device_id=peer_id(axis, other_axis, source),
            device_id_type=pl.DeviceIdType.MESH,
        ).wait_recv()
    out_ref[...] = recv[...]
    for copy in sends:
        copy.wait_send()


def gather_all(x, axis, other_axis, n, collective_id):
    rows, lanes = x.shape
    return pl.pallas_call(
        functools.partial(gather_all_kernel, axis, other_axis, n),
        out_shape=jax.ShapeDtypeStruct((n, rows, lanes), x.dtype),
        in_specs=[pl.BlockSpec(memory_space=pltpu.VMEM)],
        out_specs=pl.BlockSpec(memory_space=pltpu.VMEM),
        scratch_shapes=[
            pltpu.VMEM((n, rows, lanes), x.dtype),
            pltpu.SemaphoreType.DMA((n,)),
            pltpu.SemaphoreType.DMA((n,)),
        ],
        compiler_params=pltpu.CompilerParams(
            collective_id=collective_id, has_side_effects=True,
            vmem_limit_bytes=48 * 1024 * 1024,
        ),
        cost_estimate=pl.CostEstimate(
            flops=0, transcendentals=0, bytes_accessed=3 * n * x.size * x.dtype.itemsize
        ),
    )(x)


def torus_peer(y, x, nx):
    return (lax.axis_index("row"), y * nx + x)


def scatter_sum_2d_kernel(nx, ny, x_hbm, out_ref, recv1, mid, recv2, sems):
    send1, got1, send2, got2, own_sems = sems
    me = lax.axis_index("col")
    my_y = me // nx
    my_x = lax.rem(me, nx)
    half = x_hbm.shape[2] // 2
    lower = pl.ds(0, half)
    upper = pl.ds(half, half)
    mesh_kind = pl.DeviceIdType.MESH

    barrier = pltpu.get_barrier_semaphore()
    for offset in range(1, nx):
        pl.semaphore_signal(barrier, 1, device_id=torus_peer(my_y, lax.rem(my_x + offset, nx), nx),
                            device_id_type=mesh_kind)
    for offset in range(1, ny):
        pl.semaphore_signal(barrier, 1, device_id=torus_peer(lax.rem(my_y + offset, ny), my_x, nx),
                            device_id_type=mesh_kind)
    pl.semaphore_wait(barrier, nx + ny - 2)

    own_a = pltpu.make_async_copy(x_hbm.at[:, my_x, lower], recv1.at[0, my_x], own_sems.at[0])
    own_b = pltpu.make_async_copy(x_hbm.at[my_y, :, upper], recv1.at[1, my_y], own_sems.at[1])
    own_a.start()
    own_b.start()
    sends = []
    for offset in range(1, nx):
        peer_x = lax.rem(my_x + offset, nx)
        copy = pltpu.make_async_remote_copy(
            src_ref=x_hbm.at[:, peer_x, lower], dst_ref=recv1.at[0, my_x],
            send_sem=send1.at[0, offset], recv_sem=got1.at[0, my_x],
            device_id=torus_peer(my_y, peer_x, nx), device_id_type=mesh_kind,
        )
        copy.start()
        sends.append(copy)
    for offset in range(1, ny):
        peer_y = lax.rem(my_y + offset, ny)
        copy = pltpu.make_async_remote_copy(
            src_ref=x_hbm.at[peer_y, :, upper], dst_ref=recv1.at[1, my_y],
            send_sem=send1.at[1, offset], recv_sem=got1.at[1, my_y],
            device_id=torus_peer(peer_y, my_x, nx), device_id_type=mesh_kind,
        )
        copy.start()
        sends.append(copy)
    own_a.wait()
    own_b.wait()
    for offset in range(1, nx):
        source_x = lax.rem(my_x + nx - offset, nx)
        pltpu.make_async_remote_copy(
            src_ref=x_hbm.at[:, source_x, lower], dst_ref=recv1.at[0, source_x],
            send_sem=send1.at[0, offset], recv_sem=got1.at[0, source_x],
            device_id=torus_peer(my_y, source_x, nx), device_id_type=mesh_kind,
        ).wait_recv()

    def add_up(stack):
        total = stack[0].astype(jnp.float32)
        for j in range(1, stack.shape[0]):
            total = total + stack[j].astype(jnp.float32)
        return total

    for target in range(ny):
        mid[0, target] = add_up(recv1[0, :, target]).astype(mid.dtype)
    recv2[0, my_y] = mid[0, my_y]

    for offset in range(1, ny):
        peer_y = lax.rem(my_y + offset, ny)
        copy = pltpu.make_async_remote_copy(
            src_ref=mid.at[0, peer_y], dst_ref=recv2.at[0, my_y],
            send_sem=send2.at[0, offset], recv_sem=got2.at[0, my_y],
            device_id=torus_peer(peer_y, my_x, nx), device_id_type=mesh_kind,
        )
        copy.start()
        sends.append(copy)
    for offset in range(1, ny):
        source_y = lax.rem(my_y + ny - offset, ny)
        pltpu.make_async_remote_copy(
            src_ref=x_hbm.at[source_y, :, upper], dst_ref=recv1.at[1, source_y],
            send_sem=send1.at[1, offset], recv_sem=got1.at[1, source_y],
            device_id=torus_peer(source_y, my_x, nx), device_id_type=mesh_kind,
        ).wait_recv()
    for target in range(nx):
        mid[1, target] = add_up(recv1[1, :, target]).astype(mid.dtype)
    recv2[1, my_x] = mid[1, my_x]
    for offset in range(1, nx):
        peer_x = lax.rem(my_x + offset, nx)
        copy = pltpu.make_async_remote_copy(
            src_ref=mid.at[1, peer_x], dst_ref=recv2.at[1, my_x],
            send_sem=send2.at[1, offset], recv_sem=got2.at[1, my_x],
            device_id=torus_peer(my_y, peer_x, nx), device_id_type=mesh_kind,
        )
        copy.start()
        sends.append(copy)
    for offset in range(1, ny):
        source_y = lax.rem(my_y + ny - offset, ny)
        pltpu.make_async_remote_copy(
            src_ref=mid.at[0, source_y], dst_ref=recv2.at[0, source_y],
            send_sem=send2.at[0, offset], recv_sem=got2.at[0, source_y],
            device_id=torus_peer(source_y, my_x, nx), device_id_type=mesh_kind,
        ).wait_recv()
    out_ref[lower] = add_up(recv2[0]).astype(out_ref.dtype)
    for offset in range(1, nx):
        source_x = lax.rem(my_x + nx - offset, nx)
        pltpu.make_async_remote_copy(
            src_ref=mid.at[1, source_x], dst_ref=recv2.at[1, source_x],
            send_sem=send2.at[1, offset], recv_sem=got2.at[1, source_x],
            device_id=torus_peer(my_y, source_x, nx), device_id_type=mesh_kind,
        ).wait_recv()
    out_ref[upper] = add_up(recv2[1]).astype(out_ref.dtype)
    for copy in sends:
        copy.wait_send()


def scatter_sum_2d(x, nx, out_dtype, collective_id):
    n, rows, lanes = x.shape
    ny = n // nx
    half = rows // 2
    side = max(nx, ny)
    return pl.pallas_call(
        functools.partial(scatter_sum_2d_kernel, nx, ny),
        out_shape=jax.ShapeDtypeStruct((rows, lanes), out_dtype),
        in_specs=[pl.BlockSpec(memory_space=pl.ANY)],
        out_specs=pl.BlockSpec(memory_space=pltpu.VMEM),
        scratch_shapes=[
            pltpu.VMEM((2, side, side, half, lanes), x.dtype),
            pltpu.VMEM((2, side, half, lanes), x.dtype),
            pltpu.VMEM((2, side, half, lanes), x.dtype),
            (
                pltpu.SemaphoreType.DMA((2, side)),
                pltpu.SemaphoreType.DMA((2, side)),
                pltpu.SemaphoreType.DMA((2, side)),
                pltpu.SemaphoreType.DMA((2, side)),
                pltpu.SemaphoreType.DMA((2,)),
            ),
        ],
        compiler_params=pltpu.CompilerParams(
            collective_id=collective_id, has_side_effects=True,
            vmem_limit_bytes=48 * 1024 * 1024,
        ),
        cost_estimate=pl.CostEstimate(
            flops=x.size, transcendentals=0, bytes_accessed=3 * x.size * x.dtype.itemsize
        ),
    )(x.reshape(ny, nx, rows, lanes))


def row_peer(index):
    return (index, lax.axis_index("col"))


def greet_row(my_z, my_core, nz):
    barrier = pltpu.get_barrier_semaphore()
    mesh_kind = pl.DeviceIdType.MESH
    pl.semaphore_signal(barrier, 1, device_id=row_peer(my_z * 2 + 1 - my_core), device_id_type=mesh_kind)
    for offset in range(1, nz):
        peer_z = lax.rem(my_z + offset, nz)
        pl.semaphore_signal(barrier, 1, device_id=row_peer(peer_z * 2 + my_core), device_id_type=mesh_kind)
    pl.semaphore_wait(barrier, nz)


def scatter_sum_row_kernel(nz, x_hbm, out_ref, own1, recv1, mid, recv2, sems):
    send1, got1, send2, got2, own_sem = sems
    mesh_kind = pl.DeviceIdType.MESH
    me = lax.axis_index("row")
    my_z = me // 2
    my_core = lax.rem(me, 2)
    other_core = 1 - my_core
    partner = row_peer(my_z * 2 + other_core)
    greet_row(my_z, my_core, nz)
    own = pltpu.make_async_copy(x_hbm.at[:, my_core], own1, own_sem.at[0])
    own.start()
    sends = []
    for offset in range(nz):
        target_z = lax.rem(my_z + offset + 1, nz)
        copy = pltpu.make_async_remote_copy(
            src_ref=x_hbm.at[target_z, other_core], dst_ref=recv1.at[target_z],
            send_sem=send1.at[offset], recv_sem=got1.at[target_z],
            device_id=partner, device_id_type=mesh_kind,
        )
        copy.start()
        sends.append(copy)
    own.wait()
    for offset in range(nz - 1):
        target_z = lax.rem(my_z + offset + 1, nz)
        pltpu.make_async_remote_copy(
            src_ref=x_hbm.at[target_z, other_core], dst_ref=recv1.at[target_z],
            send_sem=send1.at[offset], recv_sem=got1.at[target_z],
            device_id=partner, device_id_type=mesh_kind,
        ).wait_recv()
        mid[target_z] = (own1[target_z].astype(jnp.float32) + recv1[target_z].astype(jnp.float32)).astype(mid.dtype)
        copy = pltpu.make_async_remote_copy(
            src_ref=mid.at[target_z], dst_ref=recv2.at[my_z],
            send_sem=send2.at[offset + 1], recv_sem=got2.at[my_z],
            device_id=row_peer(target_z * 2 + my_core), device_id_type=mesh_kind,
        )
        copy.start()
        sends.append(copy)
    pltpu.make_async_remote_copy(
        src_ref=x_hbm.at[my_z, other_core], dst_ref=recv1.at[my_z],
        send_sem=send1.at[nz - 1], recv_sem=got1.at[my_z],
        device_id=partner, device_id_type=mesh_kind,
    ).wait_recv()
    total = own1[my_z].astype(jnp.float32) + recv1[my_z].astype(jnp.float32)
    for offset in range(1, nz):
        source_z = lax.rem(my_z + nz - offset, nz)
        pltpu.make_async_remote_copy(
            src_ref=mid.at[source_z], dst_ref=recv2.at[source_z],
            send_sem=send2.at[offset], recv_sem=got2.at[source_z],
            device_id=row_peer(source_z * 2 + my_core), device_id_type=mesh_kind,
        ).wait_recv()
        total = total + recv2[source_z].astype(jnp.float32)
    out_ref[...] = total.astype(out_ref.dtype)
    for copy in sends:
        copy.wait_send()


def scatter_sum_row(x, out_dtype, collective_id):
    n, rows, lanes = x.shape
    nz = n // 2
    return pl.pallas_call(
        functools.partial(scatter_sum_row_kernel, nz),
        out_shape=jax.ShapeDtypeStruct((rows, lanes), out_dtype),
        in_specs=[pl.BlockSpec(memory_space=pl.ANY)],
        out_specs=pl.BlockSpec(memory_space=pltpu.VMEM),
        scratch_shapes=[
            pltpu.VMEM((nz, rows, lanes), x.dtype),
            pltpu.VMEM((nz, rows, lanes), x.dtype),
            pltpu.VMEM((nz, rows, lanes), x.dtype),
            pltpu.VMEM((nz, rows, lanes), x.dtype),
            (
                pltpu.SemaphoreType.DMA((nz,)),
                pltpu.SemaphoreType.DMA((nz,)),
                pltpu.SemaphoreType.DMA((nz,)),
                pltpu.SemaphoreType.DMA((nz,)),
                pltpu.SemaphoreType.DMA((1,)),
            ),
        ],
        compiler_params=pltpu.CompilerParams(
            collective_id=collective_id, has_side_effects=True,
            vmem_limit_bytes=48 * 1024 * 1024,
        ),
        cost_estimate=pl.CostEstimate(
            flops=x.size, transcendentals=0, bytes_accessed=3 * x.size * x.dtype.itemsize
        ),
    )(x.reshape(nz, 2, rows, lanes))


def gather_row_kernel(nz, x_ref, out_ref, full, sems):
    send1, got1, send2, got2, own_sem = sems
    mesh_kind = pl.DeviceIdType.MESH
    me = lax.axis_index("row")
    my_z = me // 2
    my_core = lax.rem(me, 2)
    other_core = 1 - my_core
    partner = row_peer(my_z * 2 + other_core)
    greet_row(my_z, my_core, nz)
    own = pltpu.make_async_copy(x_ref, full.at[my_z, my_core], own_sem.at[0])
    own.start()
    sends = []
    for offset in range(1, nz):
        peer_z = lax.rem(my_z + offset, nz)
        copy = pltpu.make_async_remote_copy(
            src_ref=x_ref, dst_ref=full.at[my_z, my_core],
            send_sem=send1.at[offset], recv_sem=got1.at[my_z],
            device_id=row_peer(peer_z * 2 + my_core), device_id_type=mesh_kind,
        )
        copy.start()
        sends.append(copy)

    def forward(block_z, slot):
        copy = pltpu.make_async_remote_copy(
            src_ref=full.at[block_z, my_core], dst_ref=full.at[block_z, my_core],
            send_sem=send2.at[slot], recv_sem=got2.at[block_z],
            device_id=partner, device_id_type=mesh_kind,
        )
        copy.start()
        sends.append(copy)

    own.wait()
    forward(my_z, 0)
    for offset in range(1, nz):
        source_z = lax.rem(my_z + nz - offset, nz)
        pltpu.make_async_remote_copy(
            src_ref=x_ref, dst_ref=full.at[source_z, my_core],
            send_sem=send1.at[offset], recv_sem=got1.at[source_z],
            device_id=row_peer(source_z * 2 + my_core), device_id_type=mesh_kind,
        ).wait_recv()
        forward(source_z, offset)
    for offset in range(nz):
        block_z = lax.rem(my_z + nz - offset, nz)
        pltpu.make_async_remote_copy(
            src_ref=full.at[block_z, other_core], dst_ref=full.at[block_z, other_core],
            send_sem=send2.at[offset], recv_sem=got2.at[block_z],
            device_id=partner, device_id_type=mesh_kind,
        ).wait_recv()
    for copy in sends:
        copy.wait_send()
    out_ref[...] = full[...]


def gather_row(x, collective_id):
    rows, lanes = x.shape
    nz = lax.axis_size("row") // 2
    out = pl.pallas_call(
        functools.partial(gather_row_kernel, nz),
        out_shape=jax.ShapeDtypeStruct((nz, 2, rows, lanes), x.dtype),
        in_specs=[pl.BlockSpec(memory_space=pltpu.VMEM)],
        out_specs=pl.BlockSpec(memory_space=pltpu.VMEM),
        scratch_shapes=[
            pltpu.VMEM((nz, 2, rows, lanes), x.dtype),
            (
                pltpu.SemaphoreType.DMA((nz,)),
                pltpu.SemaphoreType.DMA((nz,)),
                pltpu.SemaphoreType.DMA((nz,)),
                pltpu.SemaphoreType.DMA((nz,)),
                pltpu.SemaphoreType.DMA((1,)),
            ),
        ],
        compiler_params=pltpu.CompilerParams(
            collective_id=collective_id, has_side_effects=True,
            vmem_limit_bytes=48 * 1024 * 1024,
        ),
        cost_estimate=pl.CostEstimate(
            flops=0, transcendentals=0, bytes_accessed=3 * 2 * nz * x.size * x.dtype.itemsize
        ),
    )(x)
    return out.reshape(2 * nz * rows, lanes)


def gather_all_2d_kernel(nx, ny, x_ref, out_ref, full, sems):
    send, got, own_sem = sems
    mesh_kind = pl.DeviceIdType.MESH
    me = lax.axis_index("col")
    my_y = me // nx
    my_x = lax.rem(me, nx)
    half = x_ref.shape[0] // 2
    lower = pl.ds(0, half)
    upper = pl.ds(half, half)

    barrier = pltpu.get_barrier_semaphore()
    for offset in range(1, nx):
        pl.semaphore_signal(barrier, 1, device_id=torus_peer(my_y, lax.rem(my_x + offset, nx), nx),
                            device_id_type=mesh_kind)
    for offset in range(1, ny):
        pl.semaphore_signal(barrier, 1, device_id=torus_peer(lax.rem(my_y + offset, ny), my_x, nx),
                            device_id_type=mesh_kind)
    pl.semaphore_wait(barrier, nx + ny - 2)

    own = pltpu.make_async_copy(x_ref, full.at[my_y, my_x], own_sem.at[0])
    own.start()
    sends = []
    for offset in range(1, nx):
        peer_x = lax.rem(my_x + offset, nx)
        copy = pltpu.make_async_remote_copy(
            src_ref=x_ref.at[lower], dst_ref=full.at[my_y, my_x, lower],
            send_sem=send.at[0, offset], recv_sem=got.at[0, my_x],
            device_id=torus_peer(my_y, peer_x, nx), device_id_type=mesh_kind,
        )
        copy.start()
        sends.append(copy)
    for offset in range(1, ny):
        peer_y = lax.rem(my_y + offset, ny)
        copy = pltpu.make_async_remote_copy(
            src_ref=x_ref.at[upper], dst_ref=full.at[my_y, my_x, upper],
            send_sem=send.at[1, offset], recv_sem=got.at[1, my_y],
            device_id=torus_peer(peer_y, my_x, nx), device_id_type=mesh_kind,
        )
        copy.start()
        sends.append(copy)
    own.wait()
    for offset in range(1, nx):
        source_x = lax.rem(my_x + nx - offset, nx)
        pltpu.make_async_remote_copy(
            src_ref=x_ref.at[lower], dst_ref=full.at[my_y, source_x, lower],
            send_sem=send.at[0, offset], recv_sem=got.at[0, source_x],
            device_id=torus_peer(my_y, source_x, nx), device_id_type=mesh_kind,
        ).wait_recv()
    for offset in range(1, ny):
        peer_y = lax.rem(my_y + offset, ny)
        copy = pltpu.make_async_remote_copy(
            src_ref=full.at[my_y, :, lower], dst_ref=full.at[my_y, :, lower],
            send_sem=send.at[2, offset], recv_sem=got.at[2, my_y],
            device_id=torus_peer(peer_y, my_x, nx), device_id_type=mesh_kind,
        )
        copy.start()
        sends.append(copy)
    for offset in range(1, ny):
        source_y = lax.rem(my_y + ny - offset, ny)
        pltpu.make_async_remote_copy(
            src_ref=x_ref.at[upper], dst_ref=full.at[source_y, my_x, upper],
            send_sem=send.at[1, offset], recv_sem=got.at[1, source_y],
            device_id=torus_peer(source_y, my_x, nx), device_id_type=mesh_kind,
        ).wait_recv()
    for offset in range(1, nx):
        peer_x = lax.rem(my_x + offset, nx)
        copy = pltpu.make_async_remote_copy(
            src_ref=full.at[:, my_x, upper], dst_ref=full.at[:, my_x, upper],
            send_sem=send.at[3, offset], recv_sem=got.at[3, my_x],
            device_id=torus_peer(my_y, peer_x, nx), device_id_type=mesh_kind,
        )
        copy.start()
        sends.append(copy)
    for offset in range(1, ny):
        source_y = lax.rem(my_y + ny - offset, ny)
        pltpu.make_async_remote_copy(
            src_ref=full.at[source_y, :, lower], dst_ref=full.at[source_y, :, lower],
            send_sem=send.at[2, offset], recv_sem=got.at[2, source_y],
            device_id=torus_peer(source_y, my_x, nx), device_id_type=mesh_kind,
        ).wait_recv()
    for offset in range(1, nx):
        source_x = lax.rem(my_x + nx - offset, nx)
        pltpu.make_async_remote_copy(
            src_ref=full.at[:, source_x, upper], dst_ref=full.at[:, source_x, upper],
            send_sem=send.at[3, offset], recv_sem=got.at[3, source_x],
            device_id=torus_peer(my_y, source_x, nx), device_id_type=mesh_kind,
        ).wait_recv()
    for copy in sends:
        copy.wait_send()
    out_ref[...] = full[...]


def gather_all_2d(x, nx, collective_id):
    rows, lanes = x.shape
    n = lax.axis_size("col")
    ny = n // nx
    side = max(nx, ny)
    out = pl.pallas_call(
        functools.partial(gather_all_2d_kernel, nx, ny),
        out_shape=jax.ShapeDtypeStruct((ny, nx, rows, lanes), x.dtype),
        in_specs=[pl.BlockSpec(memory_space=pltpu.VMEM)],
        out_specs=pl.BlockSpec(memory_space=pltpu.VMEM),
        scratch_shapes=[
            pltpu.VMEM((ny, nx, rows, lanes), x.dtype),
            (
                pltpu.SemaphoreType.DMA((4, side)),
                pltpu.SemaphoreType.DMA((4, side)),
                pltpu.SemaphoreType.DMA((1,)),
            ),
        ],
        compiler_params=pltpu.CompilerParams(
            collective_id=collective_id, has_side_effects=True,
            vmem_limit_bytes=48 * 1024 * 1024,
        ),
        cost_estimate=pl.CostEstimate(
            flops=0, transcendentals=0, bytes_accessed=3 * n * x.size * x.dtype.itemsize
        ),
    )(x)
    return out.reshape(n, rows, lanes)


def fused_sum_kernel(nr, nc, x_ref, out_ref, recv1, recv2, recv3, sems):
    send1, got1, send2, got2, send3, got3 = sems
    mesh_kind = pl.DeviceIdType.MESH
    my_r = lax.axis_index("row")
    my_c = lax.axis_index("col")
    barrier = pltpu.get_barrier_semaphore()
    for offset in range(1, nc):
        pl.semaphore_signal(barrier, 1, device_id=(my_r, lax.rem(my_c + offset, nc)),
                            device_id_type=mesh_kind)
    for offset in range(1, nr):
        pl.semaphore_signal(barrier, 1, device_id=(lax.rem(my_r + offset, nr), my_c),
                            device_id_type=mesh_kind)
    pl.semaphore_wait(barrier, nc + nr - 2)

    def exchange(peers, axis_count, src_of, dst, send, got, me_index):
        started = []
        for offset in range(1, axis_count):
            peer = lax.rem(me_index + offset, axis_count)
            copy = pltpu.make_async_remote_copy(
                src_ref=src_of(peer), dst_ref=dst.at[me_index],
                send_sem=send.at[offset], recv_sem=got.at[me_index],
                device_id=peers(peer), device_id_type=mesh_kind,
            )
            copy.start()
            started.append(copy)
        for offset in range(1, axis_count):
            source = lax.rem(me_index + axis_count - offset, axis_count)
            pltpu.make_async_remote_copy(
                src_ref=src_of(source), dst_ref=dst.at[source],
                send_sem=send.at[offset], recv_sem=got.at[source],
                device_id=peers(source), device_id_type=mesh_kind,
            ).wait_recv()
        return started

    along_col = lambda peer: (my_r, peer)
    along_row = lambda peer: (peer, my_c)
    recv1[my_c] = x_ref[my_c]
    sends = exchange(along_col, nc, lambda peer: x_ref.at[peer], recv1, send1, got1, my_c)
    part = recv1[0]
    for j in range(1, nc):
        part = part + recv1[j]
    recv2[my_r] = part
    sends += exchange(along_row, nr, lambda peer: recv2.at[my_r], recv2, send2, got2, my_r)
    total = recv2[0]
    for j in range(1, nr):
        total = total + recv2[j]
    recv3[my_c] = total
    sends += exchange(along_col, nc, lambda peer: recv3.at[my_c], recv3, send3, got3, my_c)
    out_ref[...] = recv3[...]
    for copy in sends:
        copy.wait_send()


def fused_sum(local, collective_id):
    nr = lax.axis_size("row")
    nc = lax.axis_size("col")
    height, width = local.shape
    part = height // nc
    out = pl.pallas_call(
        functools.partial(fused_sum_kernel, nr, nc),
        out_shape=jax.ShapeDtypeStruct((nc, part, width), local.dtype),
        in_specs=[pl.BlockSpec(memory_space=pltpu.VMEM)],
        out_specs=pl.BlockSpec(memory_space=pltpu.VMEM),
        scratch_shapes=[
            pltpu.VMEM((nc, part, width), local.dtype),
            pltpu.VMEM((nr, part, width), local.dtype),
            pltpu.VMEM((nc, part, width), local.dtype),
            (
                pltpu.SemaphoreType.DMA((nc,)),
                pltpu.SemaphoreType.DMA((nc,)),
                pltpu.SemaphoreType.DMA((nr,)),
                pltpu.SemaphoreType.DMA((nr,)),
                pltpu.SemaphoreType.DMA((nc,)),
                pltpu.SemaphoreType.DMA((nc,)),
            ),
        ],
        compiler_params=pltpu.CompilerParams(
            collective_id=collective_id, has_side_effects=True,
            vmem_limit_bytes=48 * 1024 * 1024,
        ),
        cost_estimate=pl.CostEstimate(
            flops=local.size, transcendentals=0, bytes_accessed=3 * local.size * 4
        ),
    )(local.reshape(nc, part, width))
    return out.reshape(height, width)


def gather_and_sum_kernel(nx, ny, nr, x_ref, w_ref, out_ref, wout_ref, full, recv1, recv2, recv3, sems):
    send, got, own_sem, wsend1, wgot1, wsend2, wgot2, wsend3, wgot3 = sems
    mesh_kind = pl.DeviceIdType.MESH
    nc = nx * ny
    me = lax.axis_index("col")
    my_r = lax.axis_index("row")
    my_y = me // nx
    my_x = lax.rem(me, nx)
    half = x_ref.shape[0] // 2
    lower = pl.ds(0, half)
    upper = pl.ds(half, half)
    along_col = lambda peer: (my_r, peer)
    along_row = lambda peer: (peer, me)

    barrier = pltpu.get_barrier_semaphore()
    for offset in range(1, nc):
        pl.semaphore_signal(barrier, 1, device_id=along_col(lax.rem(me + offset, nc)),
                            device_id_type=mesh_kind)
    for offset in range(1, nr):
        pl.semaphore_signal(barrier, 1, device_id=along_row(lax.rem(my_r + offset, nr)),
                            device_id_type=mesh_kind)
    pl.semaphore_wait(barrier, nc + nr - 2)

    def start_all(peers, count, me_index, src_of, dst, sem_send, sem_got):
        started = []
        for offset in range(1, count):
            peer = lax.rem(me_index + offset, count)
            copy = pltpu.make_async_remote_copy(
                src_ref=src_of(peer), dst_ref=dst.at[me_index],
                send_sem=sem_send.at[offset], recv_sem=sem_got.at[me_index],
                device_id=peers(peer), device_id_type=mesh_kind,
            )
            copy.start()
            started.append(copy)
        return started

    def wait_all(peers, count, me_index, src_of, dst, sem_send, sem_got):
        for offset in range(1, count):
            source = lax.rem(me_index + count - offset, count)
            pltpu.make_async_remote_copy(
                src_ref=src_of(source), dst_ref=dst.at[source],
                send_sem=sem_send.at[offset], recv_sem=sem_got.at[source],
                device_id=peers(source), device_id_type=mesh_kind,
            ).wait_recv()

    own = pltpu.make_async_copy(x_ref, full.at[my_y, my_x], own_sem.at[0])
    own.start()
    sends = []
    for offset in range(1, nx):
        peer_x = lax.rem(my_x + offset, nx)
        copy = pltpu.make_async_remote_copy(
            src_ref=x_ref.at[lower], dst_ref=full.at[my_y, my_x, lower],
            send_sem=send.at[0, offset], recv_sem=got.at[0, my_x],
            device_id=torus_peer(my_y, peer_x, nx), device_id_type=mesh_kind,
        )
        copy.start()
        sends.append(copy)
    for offset in range(1, ny):
        peer_y = lax.rem(my_y + offset, ny)
        copy = pltpu.make_async_remote_copy(
            src_ref=x_ref.at[upper], dst_ref=full.at[my_y, my_x, upper],
            send_sem=send.at[1, offset], recv_sem=got.at[1, my_y],
            device_id=torus_peer(peer_y, my_x, nx), device_id_type=mesh_kind,
        )
        copy.start()
        sends.append(copy)
    recv1[me] = w_ref[me]
    weight_src = lambda peer: w_ref.at[peer]
    sends += start_all(along_col, nc, me, weight_src, recv1, wsend1, wgot1)
    own.wait()
    for offset in range(1, nx):
        source_x = lax.rem(my_x + nx - offset, nx)
        pltpu.make_async_remote_copy(
            src_ref=x_ref.at[lower], dst_ref=full.at[my_y, source_x, lower],
            send_sem=send.at[0, offset], recv_sem=got.at[0, source_x],
            device_id=torus_peer(my_y, source_x, nx), device_id_type=mesh_kind,
        ).wait_recv()
    for offset in range(1, ny):
        peer_y = lax.rem(my_y + offset, ny)
        copy = pltpu.make_async_remote_copy(
            src_ref=full.at[my_y, :, lower], dst_ref=full.at[my_y, :, lower],
            send_sem=send.at[2, offset], recv_sem=got.at[2, my_y],
            device_id=torus_peer(peer_y, my_x, nx), device_id_type=mesh_kind,
        )
        copy.start()
        sends.append(copy)
    for offset in range(1, ny):
        source_y = lax.rem(my_y + ny - offset, ny)
        pltpu.make_async_remote_copy(
            src_ref=x_ref.at[upper], dst_ref=full.at[source_y, my_x, upper],
            send_sem=send.at[1, offset], recv_sem=got.at[1, source_y],
            device_id=torus_peer(source_y, my_x, nx), device_id_type=mesh_kind,
        ).wait_recv()
    for offset in range(1, nx):
        peer_x = lax.rem(my_x + offset, nx)
        copy = pltpu.make_async_remote_copy(
            src_ref=full.at[:, my_x, upper], dst_ref=full.at[:, my_x, upper],
            send_sem=send.at[3, offset], recv_sem=got.at[3, my_x],
            device_id=torus_peer(my_y, peer_x, nx), device_id_type=mesh_kind,
        )
        copy.start()
        sends.append(copy)

    wait_all(along_col, nc, me, weight_src, recv1, wsend1, wgot1)
    part = recv1[0]
    for j in range(1, nc):
        part = part + recv1[j]
    recv2[my_r] = part
    row_src = lambda peer: recv2.at[my_r]
    sends += start_all(along_row, nr, my_r, row_src, recv2, wsend2, wgot2)
    wait_all(along_row, nr, my_r, row_src, recv2, wsend2, wgot2)
    total = recv2[0]
    for j in range(1, nr):
        total = total + recv2[j]
    recv3[me] = total
    back_src = lambda peer: recv3.at[me]
    sends += start_all(along_col, nc, me, back_src, recv3, wsend3, wgot3)

    for offset in range(1, ny):
        source_y = lax.rem(my_y + ny - offset, ny)
        pltpu.make_async_remote_copy(
            src_ref=full.at[source_y, :, lower], dst_ref=full.at[source_y, :, lower],
            send_sem=send.at[2, offset], recv_sem=got.at[2, source_y],
            device_id=torus_peer(source_y, my_x, nx), device_id_type=mesh_kind,
        ).wait_recv()
    for offset in range(1, nx):
        source_x = lax.rem(my_x + nx - offset, nx)
        pltpu.make_async_remote_copy(
            src_ref=full.at[:, source_x, upper], dst_ref=full.at[:, source_x, upper],
            send_sem=send.at[3, offset], recv_sem=got.at[3, source_x],
            device_id=torus_peer(my_y, source_x, nx), device_id_type=mesh_kind,
        ).wait_recv()
    out_ref[...] = full[...]
    wait_all(along_col, nc, me, back_src, recv3, wsend3, wgot3)
    wout_ref[...] = recv3[...]
    for copy in sends:
        copy.wait_send()


def gather_and_sum(x, local, nx, collective_id):
    rows, lanes = x.shape
    nc = lax.axis_size("col")
    nr = lax.axis_size("row")
    ny = nc // nx
    side = max(nx, ny)
    height, width = local.shape
    part = height // nc
    out, summed = pl.pallas_call(
        functools.partial(gather_and_sum_kernel, nx, ny, nr),
        out_shape=(
            jax.ShapeDtypeStruct((ny, nx, rows, lanes), x.dtype),
            jax.ShapeDtypeStruct((nc, part, width), local.dtype),
        ),
        in_specs=[pl.BlockSpec(memory_space=pltpu.VMEM)] * 2,
        out_specs=(pl.BlockSpec(memory_space=pltpu.VMEM),) * 2,
        scratch_shapes=[
            pltpu.VMEM((ny, nx, rows, lanes), x.dtype),
            pltpu.VMEM((nc, part, width), local.dtype),
            pltpu.VMEM((nr, part, width), local.dtype),
            pltpu.VMEM((nc, part, width), local.dtype),
            (
                pltpu.SemaphoreType.DMA((4, side)),
                pltpu.SemaphoreType.DMA((4, side)),
                pltpu.SemaphoreType.DMA((1,)),
                pltpu.SemaphoreType.DMA((nc,)),
                pltpu.SemaphoreType.DMA((nc,)),
                pltpu.SemaphoreType.DMA((nr,)),
                pltpu.SemaphoreType.DMA((nr,)),
                pltpu.SemaphoreType.DMA((nc,)),
                pltpu.SemaphoreType.DMA((nc,)),
            ),
        ],
        compiler_params=pltpu.CompilerParams(
            collective_id=collective_id, has_side_effects=True,
            vmem_limit_bytes=48 * 1024 * 1024,
        ),
        cost_estimate=pl.CostEstimate(
            flops=local.size, transcendentals=0,
            bytes_accessed=3 * nc * x.size * x.dtype.itemsize + 3 * local.size * 4,
        ),
    )(x, local.reshape(nc, part, width))
    return out.reshape(nc, rows, lanes), summed.reshape(height, width)


def all_sum(local, collective_base):
    row_count = lax.axis_size("row")
    col_count = lax.axis_size("col")
    height, width = local.shape
    by_col = scatter_sum(
        local.reshape(col_count, height // col_count, width), "col", "row", jnp.float32,
        collective_base,
    )
    part = height // col_count
    by_row = scatter_sum(
        by_col.reshape(row_count, part // row_count, width), "row", "col", jnp.float32,
        collective_base + 1,
    )
    back_row = gather_all(by_row, "row", "col", row_count, collective_base + 2)
    back_col = gather_all(back_row.reshape(part, width), "col", "row", col_count, collective_base + 3)
    return back_col.reshape(height, width)


def activation(aggregated, weight, cot_rows):
    hidden = jnp.dot(aggregated, weight, preferred_element_type=jnp.float32)
    sigmoid_value = jax.nn.sigmoid(hidden)
    output = (hidden * sigmoid_value).astype(jnp.bfloat16)
    silu_slope = sigmoid_value * (1.0 + hidden * (1.0 - sigmoid_value))
    hidden_grad = (cot_rows.astype(jnp.float32) * silu_slope).astype(jnp.bfloat16)
    return (output, hidden_grad)


def per_device(tile_values, tile_rows, tile_cols, tile_count, features, weight, cotangent):
    slot_total = tile_values.shape[2]
    tile_edge = tile_values.shape[3]
    tile_block = tile_values.reshape(slot_total, tile_edge, tile_edge)
    row_index = tile_rows.reshape(slot_total)
    col_index = tile_cols.reshape(slot_total)
    live_count = tile_count.reshape(1)
    own_rows = features.shape[0]
    feat_width = features.shape[1]
    row_count = lax.axis_size("row")
    col_count = lax.axis_size("col")
    row_tiles = col_count * own_rows // tile_edge
    col_tiles = row_count * own_rows // tile_edge
    column_block = gather_row(features, 8)
    source = column_block.reshape(col_tiles, tile_edge, feat_width)
    partial_rows = sparse_product(
        tile_block, row_index, col_index, live_count, source, row_tiles, False
    )
    partial_flat = partial_rows.reshape(row_tiles * tile_edge, feat_width)
    node_total = row_count * col_count * own_rows
    aggregated = scatter_sum_2d(
        partial_rows.reshape(col_count, own_rows, feat_width), TORUS_X, jnp.bfloat16, 0
    )
    output, hidden_grad = activation(aggregated, weight, cotangent)
    own_grad = lax.dot_general(
        hidden_grad, weight, (((1,), (1,)), ((), ())), preferred_element_type=jnp.float32
    ).astype(jnp.bfloat16)
    local_grad = lax.dot_general(
        aggregated, hidden_grad, (((0,), (0,)), ((), ())), preferred_element_type=jnp.float32
    )
    row_block, summed_grad = gather_and_sum(own_grad, local_grad, TORUS_X, 7)
    weight_grad = summed_grad * (1.0 / math.sqrt(node_total))
    source_back = row_block.reshape(row_tiles, tile_edge, feat_width)
    partial_cols = sparse_product(
        tile_block, col_index, row_index, live_count, source_back, col_tiles, True
    )
    input_grad = scatter_sum_row(
        partial_cols.reshape(row_count, own_rows, feat_width), jnp.float32, 9
    )
    return (output, weight_grad, input_grad)


def solution(mesh):
    placed = (
        P("row", "col", None, None, None),
        P("row", "col", None),
        P("row", "col", None),
        P("row", "col"),
        P(("row", "col"), None),
        P(),
        P(("row", "col"), None),
    )
    return jax.shard_map(
        per_device,
        mesh=mesh,
        in_specs=placed,
        out_specs=(P(("row", "col"), None), P(), P(("row", "col"), None)),
        check_vma=False,
    )
```
